32 devices in a mesh: dp: 16 (over z, x, core), tensor: 2 (over y).
Axes of the slice: x: 2, y: 2, z: 4, core: 2. Of those that a mesh axis runs over, the one named last changes fastest.
Arguments:
- tokens: bfloat16 [6144, 2048], P(('dp', 'tensor')), may hold values from -6 to 6
- routes: int32 [6144, 8], P('dp'), may hold values from 0 to 15, all different within a row; in each aligned block of 192 rows (0 to 191, 192 to 383, ...) at most 128 rows name the same one
- cotangent: bfloat16 [6144, 2048], P(('dp', 'tensor')), may hold values from -6 to 6
- attn_gain: float32 [2048], replicated, may hold values from 0.5 to 1.5
- q_gain: float32 [2048], replicated, may hold values from 0.5 to 1.5
- k_gain: float32 [2048], replicated, may hold values from 0.5 to 1.5
- w_query: bfloat16 [2048, 2048], P('dp', 'tensor'), may hold values from -0.125 to 0.125
- w_key: bfloat16 [2048, 2048], P('dp', 'tensor'), may hold values from -0.125 to 0.125
- w_value: bfloat16 [2048, 2048], P('dp', 'tensor'), may hold values from -0.125 to 0.125
- w_out: bfloat16 [2048, 2048], P('tensor', 'dp'), may hold values from -1 to 1
- mlp_gain: float32 [2048], replicated, may hold values from 0.5 to 1.5
- router: bfloat16 [2048, 16], replicated, may hold values from -0.0625 to 0.0625
- w_gate: bfloat16 [16, 2048, 1024], P('dp', None, 'tensor'), may hold values from -0.125 to 0.125
- w_up: bfloat16 [16, 2048, 1024], P('dp', None, 'tensor'), may hold values from -0.125 to 0.125
- w_down: bfloat16 [16, 1024, 2048], P('dp', 'tensor'), may hold values from -1.75 to 1.75
Outputs:
- layer_out: bfloat16 [6144, 2048], P(('dp', 'tensor'))
- tokens_grad: float32 [6144, 2048], P(('dp', 'tensor'))
- attn_gain_grad: float32 [2048], replicated
- q_gain_grad: float32 [2048], replicated
- k_gain_grad: float32 [2048], replicated
- w_query_grad: float32 [2048, 2048], P('dp', 'tensor')
- w_key_grad: float32 [2048, 2048], P('dp', 'tensor')
- w_value_grad: float32 [2048, 2048], P('dp', 'tensor')
- w_out_grad: float32 [2048, 2048], P('tensor', 'dp')
- mlp_gain_grad: float32 [2048], replicated
- router_grad: float32 [2048, 16], replicated
- w_gate_grad: float32 [16, 2048, 1024], P('dp', None, 'tensor')
- w_up_grad: float32 [16, 2048, 1024], P('dp', None, 'tensor')
- w_down_grad: float32 [16, 1024, 2048], P('dp', 'tensor')
The draws below stay inside these ranges and needn't reach their ends.
Inputs may be any that keep to these rules, and one draw needn't show every extreme that they name: `routes`: each row names 8 different experts; in each aligned block of 192 rows no expert is named by more than 128 rows, and in some block one expert is named by exactly 128 rows.
All inputs are finite; a program needn't handle non-finite values.
Results may differ from the reference program's by a relative error of at most 0.018.
Values may be sent and summed in bfloat16 or wider, within the bound.
A program may use at most 320 MiB of HBM per device.

```python
import math
import jax
import jax.numpy as jnp
import numpy as np
from jax import lax

D = 2048
HEADS = 16
HEAD = 128
FF = 1024
TOPK = 8
PROMPT = 256
CONT = 64
GROUP = 384
TOKENS = 6144
EXPERTS = 16
HALF_CAP = 128
CAP = 256
N_DP = 16
N_TENSOR = 2


def steps_of(own_key, extent, pieces, smallest, top_value):
    def one(dim, shards_of):
        draws = jax.random.uniform(jax.random.fold_in(jax.random.fold_in(own_key, 6), dim), (shards_of,), jnp.float32, smallest / len(pieces), top_value / len(pieces))
        return jnp.repeat(jnp.exp(draws), extent[dim] // shards_of).reshape((-1,) + (1,) * (len(extent) - dim - 1))

    level = one(*pieces[0])
    for cut in pieces[1:]:
        level = level * one(*cut)
    return level


def deal_out(stream_key, own, number, rows, count, top, most, slope):
    ranking = jax.random.permutation(stream_key, count)
    crowded, common = shares(count, rows * top, most, slope, True), shares(count, rows * top, most, slope, False)
    places = jnp.arange(count)

    def named(sizes, rotation):
        used = int((sizes > 0).sum())
        fixed = max(1, used // 4)
        moved = fixed + (places - fixed + rotation * (used - fixed)) % max(1, count - fixed)
        return jnp.zeros((count,), jnp.int32).at[ranking[jnp.where(places < fixed, places, moved)]].set(jnp.asarray(sizes, jnp.int32))

    sizes = jnp.where(number % 4 == 0, named(crowded, number // 4), named(common, number - number // 4 - 1))
    mixed = jax.random.permutation(jax.random.fold_in(own, 3), count)
    giver, receiver = mixed[0:count // 2 * 2:2], mixed[1:count // 2 * 2:2]
    margin = jnp.minimum(sizes[giver] - 1, most - sizes[receiver]) // 2
    margin = jnp.where((giver == ranking[0]) | (receiver == ranking[0]) | (sizes[receiver] == 0), 0, jnp.maximum(margin, 0))
    moved = jax.random.randint(jax.random.fold_in(own, 4), (count // 2,), 0, 1 << 20) % (margin + 1)
    sizes = sizes.at[giver].add(-moved).at[receiver].add(moved)
    items = jnp.searchsorted(jnp.cumsum(sizes), jnp.arange(rows * top), side="right").astype(jnp.int32)
    listing = items.reshape(top, rows).T
    listing = listing[jax.random.permutation(jax.random.fold_in(own, 1), rows)]
    rotation = jax.random.randint(jax.random.fold_in(own, 2), (rows, 1), 0, top)
    return jnp.take_along_axis(listing, (jnp.arange(top)[None, :] + rotation) % top, axis=1)


def shares(amount, total, limit, skew, full):
    portions = [(1 << 20) // math.isqrt(grade ** skew) + 1 for grade in range(1, amount + 1)]
    largest = limit if full else min(limit, max(-(-total // amount), total * portions[0] // sum(portions)))
    least = 1 if total - largest >= amount - 1 else 0
    counts, rest = [largest] + [least] * (amount - 1), total - largest - least * (amount - 1)
    while rest > 0:
        movable = [i for i in range(1, amount) if counts[i] < largest] or [i for i in range(1, amount) if counts[i] < limit]
        mass, budget = sum([portions[i] for i in movable]), rest
        for i in movable:
            addition = min(limit - counts[i], max(1, budget * portions[i] // mass), rest)
            counts[i] = counts[i] + addition
            rest = rest - addition
    return np.array(counts)


def normal_values(rng, dims, width, most, cuts=(), kind=jnp.bfloat16):
    values = jax.random.normal(rng, dims, jnp.float32) * width
    if len(cuts) > 0:
        values = steps_of(rng, dims, cuts, -0.22, 0.18) * values
    return jnp.clip(values, min=-most, max=most).astype(kind)


def setup_inputs(seed: int = 0) -> dict:
    key_of = jax.random.split(jax.random.key(seed), 16)
    tokens = normal_values(key_of[0], (TOKENS, D), 1.0, 6.0, ((0, 32),))
    routes_keys = jax.random.split(jax.random.fold_in(key_of[1], 1), TOKENS // (GROUP // N_TENSOR))
    routes_turns = jax.random.permutation(jax.random.fold_in(key_of[1], 3), TOKENS // (GROUP // N_TENSOR))
    routes = jax.vmap(lambda own, number: deal_out(jax.random.fold_in(key_of[1], 2), own, number, GROUP // N_TENSOR, EXPERTS, TOPK, HALF_CAP, 1))(routes_keys, routes_turns).reshape((TOKENS, TOPK))
    cotangent = normal_values(key_of[2], (TOKENS, D), 1.0, 6.0, ((0, 32),))
    attn_gain = jnp.clip(1.0 + 0.1 * jax.random.normal(key_of[3], (D,), jnp.float32), 0.5, 1.5)
    q_gain = jnp.clip(1.0 + 0.1 * jax.random.normal(key_of[4], (D,), jnp.float32), 0.5, 1.5)
    k_gain = jnp.clip(1.0 + 0.1 * jax.random.normal(key_of[5], (D,), jnp.float32), 0.5, 1.5)
    w_query = normal_values(key_of[6], (D, D), D ** -0.5, 0.125, ((0, 16), (1, 2)))
    w_key = normal_values(key_of[7], (D, D), D ** -0.5, 0.125, ((0, 16), (1, 2)))
    w_value = normal_values(key_of[8], (D, D), D ** -0.5, 0.125, ((0, 16), (1, 2)))
    w_out = normal_values(key_of[9], (D, D), (D // 64) ** -0.5, 1.0, ((0, 2), (1, 16)))
    mlp_gain = jnp.clip(1.0 + 0.1 * jax.random.normal(key_of[10], (D,), jnp.float32), 0.5, 1.5)
    router = normal_values(key_of[11], (D, EXPERTS), 0.011, 0.0625)
    w_gate = normal_values(key_of[12], (EXPERTS, D, FF), D ** -0.5, 0.125, ((0, 16), (2, 2)))
    w_up = normal_values(key_of[13], (EXPERTS, D, FF), D ** -0.5, 0.125, ((0, 16), (2, 2)))
    w_down = normal_values(key_of[14], (EXPERTS, FF, D), (EXPERTS * 0.018), 1.75, ((0, 16), (1, 2)))
    return dict(tokens=tokens, routes=routes, cotangent=cotangent, attn_gain=attn_gain, q_gain=q_gain, k_gain=k_gain, w_query=w_query, w_key=w_key, w_value=w_value, w_out=w_out, mlp_gain=mlp_gain, router=router, w_gate=w_gate, w_up=w_up, w_down=w_down)


@jax.custom_vjp
def low(v):
    return lax.optimization_barrier(v.astype(jnp.bfloat16)).astype(jnp.float32)

@jax.custom_vjp
def low_back(v):
    return v

def low_keep(v):
    return (low(v), None)

def low_pass(kept, grad):
    return (grad,)

def back_keep(v):
    return (v, None)

def back_low(kept, grad):
    return (low(grad),)
low.defvjp(low_keep, low_pass)
low_back.defvjp(back_keep, back_low)
EPSILON = 1e-05
ROPE_BASE = 10000.0
HIGHEST = lax.Precision.HIGHEST

def product(first_op, second_op):
    return jnp.dot(first_op, second_op, precision=HIGHEST)

def rms_norm(values, gain_vec):
    return values * lax.rsqrt(lax.optimization_barrier(jnp.mean(values * values, axis=-1, keepdims=True)) + EPSILON) * gain_vec

def group_positions():
    position = jnp.arange(GROUP, dtype=jnp.int32)
    return jnp.where(position < PROMPT, position, PROMPT + (position - PROMPT) % CONT)

def visible_keys():
    position = jnp.arange(GROUP, dtype=jnp.int32)
    member = jnp.where(position < PROMPT, -1, (position - PROMPT) // CONT)
    causal = position[None, :] <= position[:, None]
    return causal & ((member[None, :] == -1) | (member[None, :] == member[:, None]))

def rope_tables():
    half_head = HEAD // 2
    frequency = ROPE_BASE ** (-2.0 * jnp.arange(half_head, dtype=jnp.float32) / HEAD)
    angles = group_positions().astype(jnp.float32)[:, None] * frequency[None, :]
    angles = jnp.concatenate([angles, angles], axis=1)
    return (jnp.cos(angles), jnp.sin(angles))

def rotate(values, cosine_table, sine_table):
    half_head = HEAD // 2
    turned = jnp.concatenate([-values[..., half_head:], values[..., :half_head]], axis=-1)
    return values * cosine_table[:, None, :] + turned * sine_table[:, None, :]

def expert_slots(routes):
    flat_routes = routes.reshape(-1)
    one_hot = (flat_routes[:, None] == jnp.arange(EXPERTS, dtype=jnp.int32)[None, :]).astype(jnp.int32)
    earlier = jnp.cumsum(one_hot, axis=0) - one_hot
    return lax.optimization_barrier(jnp.sum(earlier * one_hot, axis=1)).astype(jnp.int32).reshape(routes.shape)

def group_forward(tokens, routes, attn_gain, q_gain, k_gain, w_query, w_key, w_value, w_out, mlp_gain, router, w_gate, w_up, w_down):
    head_shape = (GROUP, HEADS, HEAD)
    normed = low(rms_norm(tokens, attn_gain))
    queries = low_back(product(normed, w_query))
    keys_raw = low_back(product(normed, w_key))
    values = low(low_back(product(normed, w_value)))
    cosine_table, sine_table = rope_tables()
    query_rot = low(rotate(rms_norm(queries, q_gain).reshape(head_shape), cosine_table, sine_table))
    key_rot = low(rotate(rms_norm(keys_raw, k_gain).reshape(head_shape), cosine_table, sine_table))
    scores = low_back(jnp.einsum('qhd,khd->hqk', query_rot, key_rot, precision=HIGHEST) * HEAD ** (-0.5))
    scores = jnp.where(visible_keys()[None], scores, -1e+30)
    attn_weights = low(jax.nn.softmax(scores, axis=-1))
    mixed_heads = jnp.einsum('hqk,khd->qhd', attn_weights, values.reshape(head_shape), precision=HIGHEST)
    mixed_heads = low(low_back(mixed_heads.reshape(GROUP, D)))
    attended = low_back(product(mixed_heads, w_out))
    hidden_one = tokens + attended
    normed_two = low(rms_norm(hidden_one, mlp_gain))
    gates_all = jax.nn.softmax(product(normed_two, router), axis=-1)
    gate_weights = jnp.take_along_axis(gates_all, routes, axis=1)
    slot_index = expert_slots(routes)
    buffer = jnp.zeros((EXPERTS, CAP, D), jnp.float32).at[routes, slot_index].set(jnp.broadcast_to(normed_two[:, None, :], (GROUP, TOPK, D)))
    half_width = FF // N_TENSOR
    rows_in = low_back(buffer)
    partial_sum = jnp.zeros((EXPERTS, CAP, D), jnp.float32)
    for half_index in range(N_TENSOR):
        lower_col = half_index * half_width
        upper_col = lower_col + half_width
        gate_pre = low_back(jnp.einsum('ecd,edf->ecf', rows_in, w_gate[:, :, lower_col:upper_col], precision=HIGHEST))
        up_pre = low_back(jnp.einsum('ecd,edf->ecf', rows_in, w_up[:, :, lower_col:upper_col], precision=HIGHEST))
        hidden = low(jax.nn.silu(gate_pre) * up_pre)
        partial_sum = partial_sum + jnp.einsum('ecf,efd->ecd', hidden, w_down[:, lower_col:upper_col, :], precision=HIGHEST)
    returned = low(low_back(partial_sum))
    picked = returned[routes, slot_index]
    mixture = jnp.einsum('gk,gkd->gd', gate_weights, picked, precision=HIGHEST)
    return hidden_one + mixture

def reference(tokens, routes, cotangent, attn_gain, q_gain, k_gain, w_query, w_key, w_value, w_out, mlp_gain, router, w_gate, w_up, w_down):
    floats = tuple((array.astype(jnp.float32) for array in (tokens, attn_gain, q_gain, k_gain, w_query, w_key, w_value, w_out, mlp_gain, router, w_gate, w_up, w_down)))
    grouped_routes = routes.reshape(N_DP, GROUP, TOPK)

    def forward(inputs, *params):

        def one_group(carried, group_item):
            return (carried, group_forward(group_item[0], group_item[1], *params))
        carried, outputs = lax.scan(jax.checkpoint(one_group), jnp.zeros((), jnp.float32), (inputs.reshape(N_DP, GROUP, D), grouped_routes))
        return outputs.reshape(N_DP * GROUP, D)
    result, pullback = jax.vjp(forward, *floats)
    gradients = pullback(cotangent.astype(jnp.float32))
    return (result.astype(jnp.bfloat16), gradients[0], gradients[1], gradients[2], gradients[3], gradients[4], gradients[5], gradients[6], gradients[7], gradients[8], gradients[9], gradients[10], gradients[11], gradients[12])
```

```python
import jax
import jax.numpy as jnp
from jax import lax
from jax.experimental import pallas as pl
from jax.experimental.pallas import tpu as pltpu
from jax.sharding import PartitionSpec as P

D = 2048
HEAD = 128
TOPK = 8
PROMPT = 256
CONT = 64
GROUP = 384


EPSILON = 1e-05
ROPE_BASE = 10000.0
HIGHEST = lax.Precision.HIGHEST


def matmul(first_op, second_op):
    return jnp.dot(first_op, second_op, preferred_element_type=jnp.float32)


def gather_rows(values):
    return lax.all_gather(values, "tensor", axis=0, tiled=True)


def sum_rows(values):
    return lax.psum_scatter(values, "tensor", scatter_dimension=0, tiled=True)


def tensor_total(values):
    return lax.psum((values[0], values[1]), "tensor")


def expert_swap(values):
    return lax.all_to_all(values, "dp", split_axis=0, concat_axis=0, tiled=True)


def sum_slots(values):
    return lax.psum_scatter(values, "tensor", scatter_dimension=1, tiled=True)


def group_positions():
    position = jnp.arange(GROUP, dtype=jnp.int32)
    return jnp.where(position < PROMPT, position, PROMPT + (position - PROMPT) % CONT)


def visible_keys():
    position = jnp.arange(GROUP, dtype=jnp.int32)
    member = jnp.where(position < PROMPT, -1, (position - PROMPT) // CONT)
    causal = position[None, :] <= position[:, None]
    return causal & ((member[None, :] == -1) | (member[None, :] == member[:, None]))


def rope_tables():
    half_head = HEAD // 2
    frequency = ROPE_BASE ** (-2.0 * jnp.arange(half_head, dtype=jnp.float32) / HEAD)
    angles = group_positions().astype(jnp.float32)[:, None] * frequency[None, :]
    angles = jnp.concatenate([angles, angles], axis=1)
    return (jnp.cos(angles), jnp.sin(angles))


def rotate(values, cosine_table, sine_table):
    half_head = HEAD // 2
    turned = jnp.concatenate([-values[..., half_head:], values[..., :half_head]], axis=-1)
    return values * cosine_table[:, None, :] + turned * sine_table[:, None, :]


def unrotate(values, cosine_table, sine_table):
    half_head = HEAD // 2
    scaled = values * sine_table[:, None, :]
    turned = jnp.concatenate([scaled[..., half_head:], -scaled[..., :half_head]], axis=-1)
    return values * cosine_table[:, None, :] + turned


def gate_split(rows_in, hot_table, router):
    gates = jax.nn.softmax(matmul(rows_in, router), axis=1)
    weights = jnp.sum(jnp.where(hot_table, gates[:, None, :], 0.0), axis=2)
    return (gates, weights)


def routed_body(
    tokens,
    routes,
    cotangent,
    attn_gain,
    q_gain,
    k_gain,
    w_query,
    w_key,
    w_value,
    w_out,
    mlp_gain,
    router,
    w_gate,
    w_up,
    w_down,
):
    rank_index = lax.axis_index("tensor")
    tensor_count = lax.axis_size("tensor")
    own_rows = tokens.shape[0]
    head_cols = w_query.shape[1]
    local_heads = head_cols // HEAD
    col_start = rank_index * head_cols
    row_start = rank_index * own_rows
    experts = router.shape[1]
    half_cap = (own_rows * TOPK * 4 + 3 * experts - 1) // (3 * experts)
    capacity = tensor_count * half_cap
    attn_scale = HEAD ** (-0.5)
    head_shape = (GROUP, local_heads, HEAD)
    q_gain_local = lax.dynamic_slice_in_dim(q_gain, col_start, head_cols)
    k_gain_local = lax.dynamic_slice_in_dim(k_gain, col_start, head_cols)
    inputs = tokens.astype(jnp.float32)
    attn_inv = lax.rsqrt(jnp.mean(inputs * inputs, axis=1, keepdims=True) + EPSILON)
    normed = gather_rows((inputs * attn_inv * attn_gain).astype(jnp.bfloat16))
    pieces = (
        lax.all_gather(w_query, "dp", axis=0, tiled=True),
        lax.all_gather(w_key, "dp", axis=0, tiled=True),
        lax.all_gather(w_value, "dp", axis=0, tiled=True),
    )
    normed_part = normed
    queries = matmul(normed_part, pieces[0])
    keys_raw = matmul(normed_part, pieces[1])
    values_raw = matmul(normed_part, pieces[2])
    query_sq, key_sq = tensor_total(
        (jnp.sum(queries * queries, axis=1), jnp.sum(keys_raw * keys_raw, axis=1))
    )
    query_inv = lax.rsqrt(query_sq / D + EPSILON)[:, None]
    key_inv = lax.rsqrt(key_sq / D + EPSILON)[:, None]
    cosine_table, sine_table = rope_tables()
    query_rot = rotate(
        (queries * query_inv * q_gain_local).reshape(head_shape), cosine_table, sine_table
    ).astype(jnp.bfloat16)
    key_rot = rotate(
        (keys_raw * key_inv * k_gain_local).reshape(head_shape), cosine_table, sine_table
    ).astype(jnp.bfloat16)
    value_heads = values_raw.astype(jnp.bfloat16).reshape(head_shape)
    visible = visible_keys()[None]

    def masked_scores():
        raw_scores = (
            jnp.einsum("qhd,khd->hqk", query_rot, key_rot, preferred_element_type=jnp.float32)
            * attn_scale
        )
        return jnp.where(visible, raw_scores, -1e30)

    scores = masked_scores()
    row_max = jnp.max(scores, axis=2, keepdims=True)
    exponent = jnp.exp(scores - row_max)
    row_total = jnp.sum(exponent, axis=2, keepdims=True)
    log_total = row_max + jnp.log(row_total)
    mixed_heads = jnp.einsum(
        "hqk,khd->qhd",
        (exponent / row_total).astype(jnp.bfloat16),
        value_heads,
        preferred_element_type=jnp.float32,
    )
    mixed_heads = mixed_heads.reshape(GROUP, head_cols).astype(jnp.bfloat16)
    attn_part = matmul(mixed_heads, lax.all_gather(w_out, "dp", axis=1, tiled=True))
    attended = sum_rows(attn_part)
    hidden_one = inputs + attended
    mlp_inv = lax.rsqrt(jnp.mean(hidden_one * hidden_one, axis=1, keepdims=True) + EPSILON)
    normed_two = (hidden_one * mlp_inv * mlp_gain).astype(jnp.bfloat16)
    expert_ids = jnp.arange(experts, dtype=jnp.int32)
    route_hot = routes[:, :, None] == expert_ids[None, None, :]
    flat_hot = route_hot.astype(jnp.int32).reshape(tensor_count, own_rows * TOPK, experts)
    within = jnp.sum((jnp.cumsum(flat_hot, axis=1) - flat_hot) * flat_hot, axis=2).reshape(
        GROUP, TOPK
    )
    owner_of = (jnp.arange(GROUP, dtype=jnp.int32) // own_rows)[:, None]
    own_routes = lax.dynamic_slice_in_dim(routes, row_start, own_rows, 0)
    own_within = lax.dynamic_slice_in_dim(within, row_start, own_rows, 0)
    own_hot = lax.dynamic_slice_in_dim(route_hot, row_start, own_rows, 0)
    own_dest = own_routes * half_cap + own_within
    gate_weight = w_gate[0]
    up_weight = w_up[0]
    down_weight = w_down[0]
    normed_two_all = gather_rows(normed_two)
    gates_every, gate_every = gate_split(normed_two_all, route_hot, router)
    own_probs = lax.dynamic_slice_in_dim(gates_every, row_start, own_rows, 0)
    gate_weights = lax.dynamic_slice_in_dim(gate_every, row_start, own_rows, 0)
    destination = routes * capacity + owner_of * half_cap + within
    send_rows = (
        jnp.zeros((experts * capacity, D), jnp.bfloat16)
        .at[destination]
        .set(jnp.broadcast_to(normed_two_all[:, None, :], (GROUP, TOPK, D)))
        .reshape(experts, capacity, D)
    )
    received = lax.all_to_all(send_rows, "dp", split_axis=0, concat_axis=0, tiled=True)
    gate_pre = jnp.einsum("scd,df->scf", received, gate_weight, preferred_element_type=jnp.float32)
    up_pre = jnp.einsum("scd,df->scf", received, up_weight, preferred_element_type=jnp.float32)
    hidden = (jax.nn.silu(gate_pre) * up_pre).astype(jnp.bfloat16)
    expert_part = jnp.einsum("scf,fd->scd", hidden, down_weight, preferred_element_type=jnp.float32)
    expert_part, gate_pre, up_pre, hidden, received = (
        expert_part,
        gate_pre,
        up_pre,
        hidden,
        received,
    )
    back_rows = expert_swap(sum_slots(expert_part).astype(jnp.bfloat16)).reshape(
        experts * half_cap, D
    )
    picked = back_rows[own_dest].astype(jnp.float32)
    mixture = jnp.sum(gate_weights[:, :, None] * picked, axis=1)
    layer_out = (hidden_one + mixture).astype(jnp.bfloat16)
    upstream = cotangent.astype(jnp.float32)
    gate_grad = jnp.sum(upstream[:, None, :] * picked, axis=2)
    upstream_all = gather_rows(cotangent).astype(jnp.float32)
    send_grads = (
        jnp.zeros((experts * capacity, D), jnp.bfloat16)
        .at[destination]
        .set((gate_every[:, :, None] * upstream_all[:, None, :]).astype(jnp.bfloat16))
        .reshape(experts, capacity, D)
    )
    out_grads = expert_swap(send_grads)
    hidden_grad = jnp.einsum(
        "scd,fd->scf", out_grads, down_weight, preferred_element_type=jnp.float32
    )
    sigmoid = jax.nn.sigmoid(gate_pre)
    up_grad = (hidden_grad * gate_pre * sigmoid).astype(jnp.bfloat16)
    gate_pre_grad = (hidden_grad * up_pre * sigmoid * (1.0 + gate_pre * (1.0 - sigmoid))).astype(
        jnp.bfloat16
    )
    row_part = jnp.einsum(
        "scf,df->scd", gate_pre_grad, gate_weight, preferred_element_type=jnp.float32
    ) + jnp.einsum("scf,df->scd", up_grad, up_weight, preferred_element_type=jnp.float32)
    down_weight_grad = jnp.einsum(
        "scf,scd->fd", hidden, out_grads, preferred_element_type=jnp.float32
    )
    gate_weight_grad = jnp.einsum(
        "scd,scf->df", received, gate_pre_grad, preferred_element_type=jnp.float32
    )
    up_weight_grad = jnp.einsum(
        "scd,scf->df", received, up_grad, preferred_element_type=jnp.float32
    )
    returned_grads = expert_swap(sum_slots(row_part).astype(jnp.bfloat16)).reshape(
        experts * half_cap, D
    )
    normed_two_part = jnp.sum(returned_grads[own_dest].astype(jnp.float32), axis=1)
    expert_grad = jnp.sum(jnp.where(own_hot, gate_grad[:, :, None], 0.0), axis=1)
    logit_grad = own_probs * (expert_grad - jnp.sum(expert_grad * own_probs, axis=1, keepdims=True))
    router_grad = jnp.dot(normed_two.astype(jnp.float32).T, logit_grad, precision=HIGHEST)
    normed_two_grad = normed_two_part + jnp.dot(
        logit_grad, router.astype(jnp.float32).T, precision=HIGHEST
    )
    scaled_grad = normed_two_grad * mlp_gain
    hidden_one_grad = (
        upstream
        + mlp_inv * scaled_grad
        - hidden_one * mlp_inv**3 * jnp.mean(hidden_one * scaled_grad, axis=1, keepdims=True)
    )
    mlp_gain_grad = jnp.sum(normed_two_grad * hidden_one * mlp_inv, axis=0)
    attended_grad = gather_rows(hidden_one_grad.astype(jnp.bfloat16))
    mixed_grad = jnp.einsum(
        "gd,cd->gc",
        attended_grad,
        lax.all_gather(w_out, "dp", axis=1, tiled=True),
        preferred_element_type=jnp.float32,
    )
    mixed_grad = mixed_grad.astype(jnp.bfloat16).reshape(head_shape)
    attn_probs = jnp.exp(masked_scores() - log_total)
    prob_grad = jnp.einsum(
        "qhd,khd->hqk", mixed_grad, value_heads, preferred_element_type=jnp.float32
    )
    row_dot = jnp.sum(prob_grad * attn_probs, axis=2, keepdims=True)
    score_grad = (attn_probs * (prob_grad - row_dot)).astype(jnp.bfloat16)
    query_rot_grad = (
        jnp.einsum("hqk,khd->qhd", score_grad, key_rot, preferred_element_type=jnp.float32)
        * attn_scale
    )
    key_rot_grad = (
        jnp.einsum("hqk,qhd->khd", score_grad, query_rot, preferred_element_type=jnp.float32)
        * attn_scale
    )
    value_grad = (
        jnp.einsum(
            "hqk,qhd->khd",
            attn_probs.astype(jnp.bfloat16),
            mixed_grad,
            preferred_element_type=jnp.float32,
        )
        .reshape(GROUP, head_cols)
        .astype(jnp.bfloat16)
    )
    query_norm_grad = unrotate(query_rot_grad, cosine_table, sine_table).reshape(GROUP, head_cols)
    key_norm_grad = unrotate(key_rot_grad, cosine_table, sine_table).reshape(GROUP, head_cols)
    query_scaled = query_norm_grad * q_gain_local
    key_scaled = key_norm_grad * k_gain_local
    query_dot, key_dot = tensor_total(
        (jnp.sum(queries * query_scaled, axis=1), jnp.sum(keys_raw * key_scaled, axis=1))
    )
    query_grad = (
        query_inv * query_scaled - queries * query_inv**3 * (query_dot / D)[:, None]
    ).astype(jnp.bfloat16)
    key_grad = (key_inv * key_scaled - keys_raw * key_inv**3 * (key_dot / D)[:, None]).astype(
        jnp.bfloat16
    )
    q_gain_part = jnp.sum(query_norm_grad * queries * query_inv, axis=0)
    k_gain_part = jnp.sum(key_norm_grad * keys_raw * key_inv, axis=0)
    pieces = lax.all_gather((w_query, w_key, w_value), "dp", axis=0, tiled=True)
    normed_part = (
        jnp.einsum("gc,rc->gr", query_grad, pieces[0], preferred_element_type=jnp.float32)
        + jnp.einsum("gc,rc->gr", key_grad, pieces[1], preferred_element_type=jnp.float32)
        + jnp.einsum("gc,rc->gr", value_grad, pieces[2], preferred_element_type=jnp.float32)
    )
    weight_sums = lax.psum_scatter(
        jnp.concatenate(
            [
                jnp.einsum("gr,gc->rc", normed, query_grad, preferred_element_type=jnp.float32),
                jnp.einsum("gr,gc->rc", normed, key_grad, preferred_element_type=jnp.float32),
                jnp.einsum("gr,gc->rc", normed, value_grad, preferred_element_type=jnp.float32),
                jnp.einsum(
                    "gr,gc->rc", attended_grad, mixed_heads, preferred_element_type=jnp.float32
                ),
            ],
            axis=1,
        ),
        "dp",
        scatter_dimension=0,
        tiled=True,
    )
    normed_grad = sum_rows(normed_part)
    scaled_input = normed_grad * attn_gain
    tokens_grad = (
        hidden_one_grad
        + attn_inv * scaled_input
        - inputs * attn_inv**3 * jnp.mean(inputs * scaled_input, axis=1, keepdims=True)
    )
    attn_gain_grad = jnp.sum(normed_grad * inputs * attn_inv, axis=0)
    zero_width = jnp.zeros((D,), jnp.float32)
    q_gain_full = lax.dynamic_update_slice_in_dim(zero_width, q_gain_part, col_start, 0)
    k_gain_full = lax.dynamic_update_slice_in_dim(zero_width, k_gain_part, col_start, 0)
    attn_gain_grad, q_gain_grad, k_gain_grad, mlp_gain_grad, router_grad = lax.psum(
        (attn_gain_grad, q_gain_full, k_gain_full, mlp_gain_grad, router_grad), ("dp", "tensor")
    )
    return (
        layer_out,
        tokens_grad,
        attn_gain_grad,
        q_gain_grad,
        k_gain_grad,
        weight_sums[:, :head_cols],
        weight_sums[:, head_cols : 2 * head_cols],
        weight_sums[:, 2 * head_cols : 3 * head_cols],
        jnp.transpose(weight_sums[:, 3 * head_cols :]),
        mlp_gain_grad,
        router_grad,
        gate_weight_grad[None],
        up_weight_grad[None],
        down_weight_grad[None],
    )


def dot_nn(a, b):
    return lax.dot_general(a, b, (((1,), (0,)), ((), ())), preferred_element_type=jnp.float32)


def dot_nt(a, b):
    return lax.dot_general(a, b, (((1,), (1,)), ((), ())), preferred_element_type=jnp.float32)


def dot_tn(a, b):
    return lax.dot_general(a, b, (((0,), (0,)), ((), ())), preferred_element_type=jnp.float32)


def expert_kernel(
    x_ref,
    g_ref,
    gate_ref,
    wg_ref,
    wu_ref,
    wd_ref,
    y_ref,
    r_ref,
    gate_grad_ref,
    wg_grad_ref,
    wu_grad_ref,
    wd_grad_ref,
):
    @pl.when(pl.program_id(0) == 0)
    def _():
        wg_grad_ref[...] = jnp.zeros_like(wg_grad_ref)
        wu_grad_ref[...] = jnp.zeros_like(wu_grad_ref)
        wd_grad_ref[...] = jnp.zeros_like(wd_grad_ref)

    rows = x_ref[...]
    upstream = g_ref[...]
    gate = gate_ref[...]
    gate_pre = dot_nn(rows, wg_ref[...])
    up_pre = dot_nn(rows, wu_ref[...])
    raw_grad = dot_nt(upstream, wd_ref[...])
    sigmoid = jax.nn.sigmoid(gate_pre)
    silu = gate_pre * sigmoid
    hidden = silu * up_pre
    gate_grad_ref[...] = jnp.sum(hidden * raw_grad, axis=1, keepdims=True)
    hidden_gated = (gate * hidden).astype(jnp.bfloat16)
    y_ref[...] = dot_nn(hidden_gated, wd_ref[...]).astype(jnp.bfloat16)
    hidden_grad = gate * raw_grad
    up_grad = (hidden_grad * silu).astype(jnp.bfloat16)
    gate_pre_grad = (
        hidden_grad * up_pre * sigmoid * (1.0 + gate_pre * (1.0 - sigmoid))
    ).astype(jnp.bfloat16)
    r_ref[...] = (dot_nt(gate_pre_grad, wg_ref[...]) + dot_nt(up_grad, wu_ref[...])).astype(
        jnp.bfloat16
    )
    wg_grad_ref[...] += dot_tn(rows, gate_pre_grad)
    wu_grad_ref[...] += dot_tn(rows, up_grad)
    wd_grad_ref[...] += dot_tn(hidden_gated, upstream)


def expert_pass(rows, upstream, gate, w_gate, w_up, w_down):
    count, width = rows.shape
    units = w_gate.shape[1]
    tile = 512 if count % 512 == 0 else GROUP // 2

    def by_row(cols):
        return pl.BlockSpec((tile, cols), lambda i: (i, 0))

    def whole(first, second):
        return pl.BlockSpec((first, second), lambda i: (0, 0), pipeline_mode=pl.Buffered(1))

    weights = [whole(width, units), whole(width, units), whole(units, width)]
    return pl.pallas_call(
        expert_kernel,
        grid=(count // tile,),
        in_specs=[by_row(width), by_row(width), by_row(1)] + weights,
        out_specs=[by_row(width), by_row(width), by_row(1)] + weights,
        out_shape=[
            jax.ShapeDtypeStruct((count, width), jnp.bfloat16),
            jax.ShapeDtypeStruct((count, width), jnp.bfloat16),
            jax.ShapeDtypeStruct((count, 1), jnp.float32),
            jax.ShapeDtypeStruct((width, units), jnp.float32),
            jax.ShapeDtypeStruct((width, units), jnp.float32),
            jax.ShapeDtypeStruct((units, width), jnp.float32),
        ],
        cost_estimate=pl.CostEstimate(
            flops=18 * count * width * units,
            bytes_accessed=8 * count * width + 18 * width * units,
            transcendentals=count * units,
        ),
        compiler_params=pltpu.CompilerParams(vmem_limit_bytes=60 << 20),
    )(rows, upstream, gate, w_gate, w_up, w_down)


EVERY = ("dp", "tensor")


def dense_body(
    tokens,
    routes,
    cotangent,
    attn_gain,
    q_gain,
    k_gain,
    w_query,
    w_key,
    w_value,
    w_out,
    mlp_gain,
    router,
    w_gate,
    w_up,
    w_down,
):
    rank_index = lax.axis_index("tensor")
    own_rows = tokens.shape[0]
    head_cols = w_query.shape[1]
    local_heads = head_cols // HEAD
    col_start = rank_index * head_cols
    row_start = rank_index * own_rows
    experts = router.shape[1]
    attn_scale = HEAD ** (-0.5)
    head_shape = (GROUP, local_heads, HEAD)
    q_gain_local = lax.dynamic_slice_in_dim(q_gain, col_start, head_cols)
    k_gain_local = lax.dynamic_slice_in_dim(k_gain, col_start, head_cols)
    inputs = tokens.astype(jnp.float32)
    attn_inv = lax.rsqrt(jnp.mean(inputs * inputs, axis=1, keepdims=True) + EPSILON)
    normed = gather_rows((inputs * attn_inv * attn_gain).astype(jnp.bfloat16))
    q_all = lax.all_gather(w_query, "dp", axis=0, tiled=True)
    k_all = lax.all_gather(w_key, "dp", axis=0, tiled=True)
    v_all = lax.all_gather(w_value, "dp", axis=0, tiled=True)
    o_all = lax.all_gather(w_out, "dp", axis=1, tiled=True)
    upstream_all = lax.all_gather(cotangent, EVERY, axis=0, tiled=True)
    queries = matmul(normed, q_all)
    keys_raw = matmul(normed, k_all)
    values_raw = matmul(normed, v_all)
    query_sq, key_sq = tensor_total(
        (jnp.sum(queries * queries, axis=1), jnp.sum(keys_raw * keys_raw, axis=1))
    )
    query_inv = lax.rsqrt(query_sq / D + EPSILON)[:, None]
    key_inv = lax.rsqrt(key_sq / D + EPSILON)[:, None]
    cosine_table, sine_table = rope_tables()
    query_rot = rotate(
        (queries * query_inv * q_gain_local).reshape(head_shape), cosine_table, sine_table
    ).astype(jnp.bfloat16)
    key_rot = rotate(
        (keys_raw * key_inv * k_gain_local).reshape(head_shape), cosine_table, sine_table
    ).astype(jnp.bfloat16)
    value_heads = values_raw.astype(jnp.bfloat16).reshape(head_shape)
    visible = visible_keys()[None]

    def masked_scores():
        raw_scores = (
            jnp.einsum("qhd,khd->hqk", query_rot, key_rot, preferred_element_type=jnp.float32)
            * attn_scale
        )
        return jnp.where(visible, raw_scores, -1e30)

    scores = masked_scores()
    row_max = jnp.max(scores, axis=2, keepdims=True)
    exponent = jnp.exp(scores - row_max)
    row_total = jnp.sum(exponent, axis=2, keepdims=True)
    log_total = row_max + jnp.log(row_total)
    mixed_heads = jnp.einsum(
        "hqk,khd->qhd",
        (exponent / row_total).astype(jnp.bfloat16),
        value_heads,
        preferred_element_type=jnp.float32,
    )
    mixed_heads = mixed_heads.reshape(GROUP, head_cols).astype(jnp.bfloat16)
    attended = sum_rows(matmul(mixed_heads, o_all))
    hidden_one = inputs + attended
    mlp_inv = lax.rsqrt(jnp.mean(hidden_one * hidden_one, axis=1, keepdims=True) + EPSILON)
    normed_two = (hidden_one * mlp_inv * mlp_gain).astype(jnp.bfloat16)
    own_routes = lax.dynamic_slice_in_dim(routes, row_start, own_rows, 0)
    expert_ids = jnp.arange(experts, dtype=jnp.int32)
    own_hot = jnp.any(own_routes[:, :, None] == expert_ids[None, None, :], axis=1)
    own_probs = jax.nn.softmax(matmul(normed_two, router), axis=1)
    rows_all = lax.all_gather(normed_two, EVERY, axis=0, tiled=True)
    gates_all = lax.all_gather(jnp.where(own_hot, own_probs, 0.0), EVERY, axis=0, tiled=True)
    own_expert = lax.axis_index("dp")
    own_gate = lax.dynamic_slice_in_dim(gates_all, own_expert, 1, 1)
    y_part, r_part, gate_grad, gate_weight_grad, up_weight_grad, down_weight_grad = expert_pass(
        rows_all, upstream_all, own_gate, w_gate[0], w_up[0], w_down[0]
    )
    returned = lax.psum_scatter(r_part, EVERY, scatter_dimension=0, tiled=True)
    grad_table = jnp.where(expert_ids[None, :] == own_expert, gate_grad, 0.0)
    expert_grad = lax.psum_scatter(grad_table, EVERY, scatter_dimension=0, tiled=True)
    expert_grad = jnp.where(own_hot, expert_grad, 0.0)
    mixture = lax.psum_scatter(y_part, EVERY, scatter_dimension=0, tiled=True)
    layer_out = (hidden_one + mixture.astype(jnp.float32)).astype(jnp.bfloat16)
    upstream = cotangent.astype(jnp.float32)
    logit_grad = own_probs * (expert_grad - jnp.sum(expert_grad * own_probs, axis=1, keepdims=True))
    router_grad = jnp.dot(normed_two.astype(jnp.float32).T, logit_grad, precision=HIGHEST)
    normed_two_grad = returned.astype(jnp.float32) + jnp.dot(
        logit_grad, router.astype(jnp.float32).T, precision=HIGHEST
    )
    scaled_grad = normed_two_grad * mlp_gain
    hidden_one_grad = (
        upstream
        + mlp_inv * scaled_grad
        - hidden_one * mlp_inv**3 * jnp.mean(hidden_one * scaled_grad, axis=1, keepdims=True)
    )
    mlp_gain_grad = jnp.sum(normed_two_grad * hidden_one * mlp_inv, axis=0)
    attended_grad = gather_rows(hidden_one_grad.astype(jnp.bfloat16))
    mixed_grad = jnp.einsum("gd,cd->gc", attended_grad, o_all, preferred_element_type=jnp.float32)
    mixed_grad = mixed_grad.astype(jnp.bfloat16).reshape(head_shape)
    attn_probs = jnp.exp(masked_scores() - log_total)
    prob_grad = jnp.einsum(
        "qhd,khd->hqk", mixed_grad, value_heads, preferred_element_type=jnp.float32
    )
    row_dot = jnp.sum(prob_grad * attn_probs, axis=2, keepdims=True)
    score_grad = (attn_probs * (prob_grad - row_dot)).astype(jnp.bfloat16)
    query_rot_grad = (
        jnp.einsum("hqk,khd->qhd", score_grad, key_rot, preferred_element_type=jnp.float32)
        * attn_scale
    )
    key_rot_grad = (
        jnp.einsum("hqk,qhd->khd", score_grad, query_rot, preferred_element_type=jnp.float32)
        * attn_scale
    )
    value_grad = (
        jnp.einsum(
            "hqk,qhd->khd",
            attn_probs.astype(jnp.bfloat16),
            mixed_grad,
            preferred_element_type=jnp.float32,
        )
        .reshape(GROUP, head_cols)
        .astype(jnp.bfloat16)
    )
    query_norm_grad = unrotate(query_rot_grad, cosine_table, sine_table).reshape(GROUP, head_cols)
    key_norm_grad = unrotate(key_rot_grad, cosine_table, sine_table).reshape(GROUP, head_cols)
    query_scaled = query_norm_grad * q_gain_local
    key_scaled = key_norm_grad * k_gain_local
    query_dot, key_dot = tensor_total(
        (jnp.sum(queries * query_scaled, axis=1), jnp.sum(keys_raw * key_scaled, axis=1))
    )
    query_grad = (
        query_inv * query_scaled - queries * query_inv**3 * (query_dot / D)[:, None]
    ).astype(jnp.bfloat16)
    key_grad = (key_inv * key_scaled - keys_raw * key_inv**3 * (key_dot / D)[:, None]).astype(
        jnp.bfloat16
    )
    q_gain_part = jnp.sum(query_norm_grad * queries * query_inv, axis=0)
    k_gain_part = jnp.sum(key_norm_grad * keys_raw * key_inv, axis=0)
    normed_part = (
        jnp.einsum("gc,rc->gr", query_grad, q_all, preferred_element_type=jnp.float32)
        + jnp.einsum("gc,rc->gr", key_grad, k_all, preferred_element_type=jnp.float32)
        + jnp.einsum("gc,rc->gr", value_grad, v_all, preferred_element_type=jnp.float32)
    )
    weight_sums = [
        lax.psum_scatter(
            dot_tn(first, second).astype(jnp.bfloat16), "dp", scatter_dimension=0, tiled=True
        ).astype(jnp.float32)
        for first, second in (
            (normed, query_grad),
            (normed, key_grad),
            (normed, value_grad),
            (attended_grad, mixed_heads),
        )
    ]
    normed_grad = sum_rows(normed_part)
    scaled_input = normed_grad * attn_gain
    tokens_grad = (
        hidden_one_grad
        + attn_inv * scaled_input
        - inputs * attn_inv**3 * jnp.mean(inputs * scaled_input, axis=1, keepdims=True)
    )
    attn_gain_grad = jnp.sum(normed_grad * inputs * attn_inv, axis=0)
    zero_width = jnp.zeros((D,), jnp.float32)
    q_gain_full = lax.dynamic_update_slice_in_dim(zero_width, q_gain_part, col_start, 0)
    k_gain_full = lax.dynamic_update_slice_in_dim(zero_width, k_gain_part, col_start, 0)
    attn_gain_grad, q_gain_grad, k_gain_grad, mlp_gain_grad, router_grad = lax.psum(
        (attn_gain_grad, q_gain_full, k_gain_full, mlp_gain_grad, router_grad), EVERY
    )
    return (
        layer_out,
        tokens_grad,
        attn_gain_grad,
        q_gain_grad,
        k_gain_grad,
        weight_sums[0],
        weight_sums[1],
        weight_sums[2],
        jnp.transpose(weight_sums[3]),
        mlp_gain_grad,
        router_grad,
        gate_weight_grad[None],
        up_weight_grad[None],
        down_weight_grad[None],
    )


def solution(mesh):
    in_specs = (
        P(("dp", "tensor"), None),
        P("dp", None),
        P(("dp", "tensor"), None),
        P(),
        P(),
        P(),
        P("dp", "tensor"),
        P("dp", "tensor"),
        P("dp", "tensor"),
        P("tensor", "dp"),
        P(),
        P(),
        P("dp", None, "tensor"),
        P("dp", None, "tensor"),
        P("dp", "tensor", None),
    )
    out_specs = (
        P(("dp", "tensor"), None),
        P(("dp", "tensor"), None),
        P(),
        P(),
        P(),
        P("dp", "tensor"),
        P("dp", "tensor"),
        P("dp", "tensor"),
        P("tensor", "dp"),
        P(),
        P(),
        P("dp", None, "tensor"),
        P("dp", None, "tensor"),
        P("dp", "tensor", None),
    )
    experts = mesh.shape["dp"]
    body = dense_body if experts <= 2 * TOPK else routed_body
    return jax.shard_map(body, mesh=mesh, in_specs=in_specs, out_specs=out_specs, check_vma=False)
```

```python
import functools

import jax
import jax.numpy as jnp
from jax import lax
from jax.experimental import pallas as pl
from jax.experimental.pallas import tpu as pltpu
from jax.sharding import PartitionSpec as P

D = 2048
HEAD = 128
TOPK = 8
PROMPT = 256
CONT = 64
GROUP = 384


EPSILON = 1e-05
ROPE_BASE = 10000.0
HIGHEST = lax.Precision.HIGHEST


def matmul(first_op, second_op):
    return jnp.dot(first_op, second_op, preferred_element_type=jnp.float32)


def gather_rows(values):
    return lax.all_gather(values, "tensor", axis=0, tiled=True)


def sum_rows(values):
    return lax.psum_scatter(values, "tensor", scatter_dimension=0, tiled=True)


def tensor_total(values):
    return lax.psum((values[0], values[1]), "tensor")


def expert_swap(values):
    return lax.all_to_all(values, "dp", split_axis=0, concat_axis=0, tiled=True)


def sum_slots(values):
    return lax.psum_scatter(values, "tensor", scatter_dimension=1, tiled=True)


def group_positions():
    position = jnp.arange(GROUP, dtype=jnp.int32)
    return jnp.where(position < PROMPT, position, PROMPT + (position - PROMPT) % CONT)


def visible_keys():
    position = jnp.arange(GROUP, dtype=jnp.int32)
    member = jnp.where(position < PROMPT, -1, (position - PROMPT) // CONT)
    causal = position[None, :] <= position[:, None]
    return causal & ((member[None, :] == -1) | (member[None, :] == member[:, None]))


def rope_tables():
    half_head = HEAD // 2
    frequency = ROPE_BASE ** (-2.0 * jnp.arange(half_head, dtype=jnp.float32) / HEAD)
    angles = group_positions().astype(jnp.float32)[:, None] * frequency[None, :]
    angles = jnp.concatenate([angles, angles], axis=1)
    return (jnp.cos(angles), jnp.sin(angles))


def rotate(values, cosine_table, sine_table):
    half_head = HEAD // 2
    turned = jnp.concatenate([-values[..., half_head:], values[..., :half_head]], axis=-1)
    return values * cosine_table[:, None, :] + turned * sine_table[:, None, :]


def unrotate(values, cosine_table, sine_table):
    half_head = HEAD // 2
    scaled = values * sine_table[:, None, :]
    turned = jnp.concatenate([scaled[..., half_head:], -scaled[..., :half_head]], axis=-1)
    return values * cosine_table[:, None, :] + turned


def gate_split(rows_in, hot_table, router):
    gates = jax.nn.softmax(matmul(rows_in, router), axis=1)
    weights = jnp.sum(jnp.where(hot_table, gates[:, None, :], 0.0), axis=2)
    return (gates, weights)


def routed_body(
    tokens,
    routes,
    cotangent,
    attn_gain,
    q_gain,
    k_gain,
    w_query,
    w_key,
    w_value,
    w_out,
    mlp_gain,
    router,
    w_gate,
    w_up,
    w_down,
):
    rank_index = lax.axis_index("tensor")
    tensor_count = lax.axis_size("tensor")
    own_rows = tokens.shape[0]
    head_cols = w_query.shape[1]
    local_heads = head_cols // HEAD
    col_start = rank_index * head_cols
    row_start = rank_index * own_rows
    experts = router.shape[1]
    half_cap = (own_rows * TOPK * 4 + 3 * experts - 1) // (3 * experts)
    capacity = tensor_count * half_cap
    attn_scale = HEAD ** (-0.5)
    head_shape = (GROUP, local_heads, HEAD)
    q_gain_local = lax.dynamic_slice_in_dim(q_gain, col_start, head_cols)
    k_gain_local = lax.dynamic_slice_in_dim(k_gain, col_start, head_cols)
    inputs = tokens.astype(jnp.float32)
    attn_inv = lax.rsqrt(jnp.mean(inputs * inputs, axis=1, keepdims=True) + EPSILON)
    normed = gather_rows((inputs * attn_inv * attn_gain).astype(jnp.bfloat16))
    pieces = (
        lax.all_gather(w_query, "dp", axis=0, tiled=True),
        lax.all_gather(w_key, "dp", axis=0, tiled=True),
        lax.all_gather(w_value, "dp", axis=0, tiled=True),
    )
    normed_part = normed
    queries = matmul(normed_part, pieces[0])
    keys_raw = matmul(normed_part, pieces[1])
    values_raw = matmul(normed_part, pieces[2])
    query_sq, key_sq = tensor_total(
        (jnp.sum(queries * queries, axis=1), jnp.sum(keys_raw * keys_raw, axis=1))
    )
    query_inv = lax.rsqrt(query_sq / D + EPSILON)[:, None]
    key_inv = lax.rsqrt(key_sq / D + EPSILON)[:, None]
    cosine_table, sine_table = rope_tables()
    query_rot = rotate(
        (queries * query_inv * q_gain_local).reshape(head_shape), cosine_table, sine_table
    ).astype(jnp.bfloat16)
    key_rot = rotate(
        (keys_raw * key_inv * k_gain_local).reshape(head_shape), cosine_table, sine_table
    ).astype(jnp.bfloat16)
    value_heads = values_raw.astype(jnp.bfloat16).reshape(head_shape)
    visible = visible_keys()[None]

    def masked_scores():
        raw_scores = (
            jnp.einsum("qhd,khd->hqk", query_rot, key_rot, preferred_element_type=jnp.float32)
            * attn_scale
        )
        return jnp.where(visible, raw_scores, -1e30)

    scores = masked_scores()
    row_max = jnp.max(scores, axis=2, keepdims=True)
    exponent = jnp.exp(scores - row_max)
    row_total = jnp.sum(exponent, axis=2, keepdims=True)
    log_total = row_max + jnp.log(row_total)
    mixed_heads = jnp.einsum(
        "hqk,khd->qhd",
        (exponent / row_total).astype(jnp.bfloat16),
        value_heads,
        preferred_element_type=jnp.float32,
    )
    mixed_heads = mixed_heads.reshape(GROUP, head_cols).astype(jnp.bfloat16)
    attn_part = matmul(mixed_heads, lax.all_gather(w_out, "dp", axis=1, tiled=True))
    attended = sum_rows(attn_part)
    hidden_one = inputs + attended
    mlp_inv = lax.rsqrt(jnp.mean(hidden_one * hidden_one, axis=1, keepdims=True) + EPSILON)
    normed_two = (hidden_one * mlp_inv * mlp_gain).astype(jnp.bfloat16)
    expert_ids = jnp.arange(experts, dtype=jnp.int32)
    route_hot = routes[:, :, None] == expert_ids[None, None, :]
    flat_hot = route_hot.astype(jnp.int32).reshape(tensor_count, own_rows * TOPK, experts)
    within = jnp.sum((jnp.cumsum(flat_hot, axis=1) - flat_hot) * flat_hot, axis=2).reshape(
        GROUP, TOPK
    )
    owner_of = (jnp.arange(GROUP, dtype=jnp.int32) // own_rows)[:, None]
    own_routes = lax.dynamic_slice_in_dim(routes, row_start, own_rows, 0)
    own_within = lax.dynamic_slice_in_dim(within, row_start, own_rows, 0)
    own_hot = lax.dynamic_slice_in_dim(route_hot, row_start, own_rows, 0)
    own_dest = own_routes * half_cap + own_within
    gate_weight = w_gate[0]
    up_weight = w_up[0]
    down_weight = w_down[0]
    normed_two_all = gather_rows(normed_two)
    gates_every, gate_every = gate_split(normed_two_all, route_hot, router)
    own_probs = lax.dynamic_slice_in_dim(gates_every, row_start, own_rows, 0)
    gate_weights = lax.dynamic_slice_in_dim(gate_every, row_start, own_rows, 0)
    destination = routes * capacity + owner_of * half_cap + within
    send_rows = (
        jnp.zeros((experts * capacity, D), jnp.bfloat16)
        .at[destination]
        .set(jnp.broadcast_to(normed_two_all[:, None, :], (GROUP, TOPK, D)))
        .reshape(experts, capacity, D)
    )
    received = lax.all_to_all(send_rows, "dp", split_axis=0, concat_axis=0, tiled=True)
    gate_pre = jnp.einsum("scd,df->scf", received, gate_weight, preferred_element_type=jnp.float32)
    up_pre = jnp.einsum("scd,df->scf", received, up_weight, preferred_element_type=jnp.float32)
    hidden = (jax.nn.silu(gate_pre) * up_pre).astype(jnp.bfloat16)
    expert_part = jnp.einsum("scf,fd->scd", hidden, down_weight, preferred_element_type=jnp.float32)
    expert_part, gate_pre, up_pre, hidden, received = (
        expert_part,
        gate_pre,
        up_pre,
        hidden,
        received,
    )
    back_rows = expert_swap(sum_slots(expert_part).astype(jnp.bfloat16)).reshape(
        experts * half_cap, D
    )
    picked = back_rows[own_dest].astype(jnp.float32)
    mixture = jnp.sum(gate_weights[:, :, None] * picked, axis=1)
    layer_out = (hidden_one + mixture).astype(jnp.bfloat16)
    upstream = cotangent.astype(jnp.float32)
    gate_grad = jnp.sum(upstream[:, None, :] * picked, axis=2)
    upstream_all = gather_rows(cotangent).astype(jnp.float32)
    send_grads = (
        jnp.zeros((experts * capacity, D), jnp.bfloat16)
        .at[destination]
        .set((gate_every[:, :, None] * upstream_all[:, None, :]).astype(jnp.bfloat16))
        .reshape(experts, capacity, D)
    )
    out_grads = expert_swap(send_grads)
    hidden_grad = jnp.einsum(
        "scd,fd->scf", out_grads, down_weight, preferred_element_type=jnp.float32
    )
    sigmoid = jax.nn.sigmoid(gate_pre)
    up_grad = (hidden_grad * gate_pre * sigmoid).astype(jnp.bfloat16)
    gate_pre_grad = (hidden_grad * up_pre * sigmoid * (1.0 + gate_pre * (1.0 - sigmoid))).astype(
        jnp.bfloat16
    )
    row_part = jnp.einsum(
        "scf,df->scd", gate_pre_grad, gate_weight, preferred_element_type=jnp.float32
    ) + jnp.einsum("scf,df->scd", up_grad, up_weight, preferred_element_type=jnp.float32)
    down_weight_grad = jnp.einsum(
        "scf,scd->fd", hidden, out_grads, preferred_element_type=jnp.float32
    )
    gate_weight_grad = jnp.einsum(
        "scd,scf->df", received, gate_pre_grad, preferred_element_type=jnp.float32
    )
    up_weight_grad = jnp.einsum(
        "scd,scf->df", received, up_grad, preferred_element_type=jnp.float32
    )
    returned_grads = expert_swap(sum_slots(row_part).astype(jnp.bfloat16)).reshape(
        experts * half_cap, D
    )
    normed_two_part = jnp.sum(returned_grads[own_dest].astype(jnp.float32), axis=1)
    expert_grad = jnp.sum(jnp.where(own_hot, gate_grad[:, :, None], 0.0), axis=1)
    logit_grad = own_probs * (expert_grad - jnp.sum(expert_grad * own_probs, axis=1, keepdims=True))
    router_grad = jnp.dot(normed_two.astype(jnp.float32).T, logit_grad, precision=HIGHEST)
    normed_two_grad = normed_two_part + jnp.dot(
        logit_grad, router.astype(jnp.float32).T, precision=HIGHEST
    )
    scaled_grad = normed_two_grad * mlp_gain
    hidden_one_grad = (
        upstream
        + mlp_inv * scaled_grad
        - hidden_one * mlp_inv**3 * jnp.mean(hidden_one * scaled_grad, axis=1, keepdims=True)
    )
    mlp_gain_grad = jnp.sum(normed_two_grad * hidden_one * mlp_inv, axis=0)
    attended_grad = gather_rows(hidden_one_grad.astype(jnp.bfloat16))
    mixed_grad = jnp.einsum(
        "gd,cd->gc",
        attended_grad,
        lax.all_gather(w_out, "dp", axis=1, tiled=True),
        preferred_element_type=jnp.float32,
    )
    mixed_grad = mixed_grad.astype(jnp.bfloat16).reshape(head_shape)
    attn_probs = jnp.exp(masked_scores() - log_total)
    prob_grad = jnp.einsum(
        "qhd,khd->hqk", mixed_grad, value_heads, preferred_element_type=jnp.float32
    )
    row_dot = jnp.sum(prob_grad * attn_probs, axis=2, keepdims=True)
    score_grad = (attn_probs * (prob_grad - row_dot)).astype(jnp.bfloat16)
    query_rot_grad = (
        jnp.einsum("hqk,khd->qhd", score_grad, key_rot, preferred_element_type=jnp.float32)
        * attn_scale
    )
    key_rot_grad = (
        jnp.einsum("hqk,qhd->khd", score_grad, query_rot, preferred_element_type=jnp.float32)
        * attn_scale
    )
    value_grad = (
        jnp.einsum(
            "hqk,qhd->khd",
            attn_probs.astype(jnp.bfloat16),
            mixed_grad,
            preferred_element_type=jnp.float32,
        )
        .reshape(GROUP, head_cols)
        .astype(jnp.bfloat16)
    )
    query_norm_grad = unrotate(query_rot_grad, cosine_table, sine_table).reshape(GROUP, head_cols)
    key_norm_grad = unrotate(key_rot_grad, cosine_table, sine_table).reshape(GROUP, head_cols)
    query_scaled = query_norm_grad * q_gain_local
    key_scaled = key_norm_grad * k_gain_local
    query_dot, key_dot = tensor_total(
        (jnp.sum(queries * query_scaled, axis=1), jnp.sum(keys_raw * key_scaled, axis=1))
    )
    query_grad = (
        query_inv * query_scaled - queries * query_inv**3 * (query_dot / D)[:, None]
    ).astype(jnp.bfloat16)
    key_grad = (key_inv * key_scaled - keys_raw * key_inv**3 * (key_dot / D)[:, None]).astype(
        jnp.bfloat16
    )
    q_gain_part = jnp.sum(query_norm_grad * queries * query_inv, axis=0)
    k_gain_part = jnp.sum(key_norm_grad * keys_raw * key_inv, axis=0)
    pieces = lax.all_gather((w_query, w_key, w_value), "dp", axis=0, tiled=True)
    normed_part = (
        jnp.einsum("gc,rc->gr", query_grad, pieces[0], preferred_element_type=jnp.float32)
        + jnp.einsum("gc,rc->gr", key_grad, pieces[1], preferred_element_type=jnp.float32)
        + jnp.einsum("gc,rc->gr", value_grad, pieces[2], preferred_element_type=jnp.float32)
    )
    weight_sums = lax.psum_scatter(
        jnp.concatenate(
            [
                jnp.einsum("gr,gc->rc", normed, query_grad, preferred_element_type=jnp.float32),
                jnp.einsum("gr,gc->rc", normed, key_grad, preferred_element_type=jnp.float32),
                jnp.einsum("gr,gc->rc", normed, value_grad, preferred_element_type=jnp.float32),
                jnp.einsum(
                    "gr,gc->rc", attended_grad, mixed_heads, preferred_element_type=jnp.float32
                ),
            ],
            axis=1,
        ),
        "dp",
        scatter_dimension=0,
        tiled=True,
    )
    normed_grad = sum_rows(normed_part)
    scaled_input = normed_grad * attn_gain
    tokens_grad = (
        hidden_one_grad
        + attn_inv * scaled_input
        - inputs * attn_inv**3 * jnp.mean(inputs * scaled_input, axis=1, keepdims=True)
    )
    attn_gain_grad = jnp.sum(normed_grad * inputs * attn_inv, axis=0)
    zero_width = jnp.zeros((D,), jnp.float32)
    q_gain_full = lax.dynamic_update_slice_in_dim(zero_width, q_gain_part, col_start, 0)
    k_gain_full = lax.dynamic_update_slice_in_dim(zero_width, k_gain_part, col_start, 0)
    attn_gain_grad, q_gain_grad, k_gain_grad, mlp_gain_grad, router_grad = lax.psum(
        (attn_gain_grad, q_gain_full, k_gain_full, mlp_gain_grad, router_grad), ("dp", "tensor")
    )
    return (
        layer_out,
        tokens_grad,
        attn_gain_grad,
        q_gain_grad,
        k_gain_grad,
        weight_sums[:, :head_cols],
        weight_sums[:, head_cols : 2 * head_cols],
        weight_sums[:, 2 * head_cols : 3 * head_cols],
        jnp.transpose(weight_sums[:, 3 * head_cols :]),
        mlp_gain_grad,
        router_grad,
        gate_weight_grad[None],
        up_weight_grad[None],
        down_weight_grad[None],
    )


MESH_ID = pl.DeviceIdType.MESH
EVERY = ("dp", "tensor")
LANES = 128
ANYWHERE = pl.BlockSpec(memory_space=pl.ANY)
IN_VMEM = pl.BlockSpec(memory_space=pltpu.VMEM)


class Place:
    def __init__(self):
        dp = lax.axis_index("dp")
        self.y = lax.axis_index("tensor")
        self.z, self.x, self.c = dp // 4, (dp // 2) % 2, dp % 2
        self.z_count = lax.axis_size("dp") // 4

    def device(self, z=None, x=None, c=None, y=None):
        z = self.z if z is None else z
        x = self.x if x is None else x
        c = self.c if c is None else c
        y = self.y if y is None else y
        return (z * 4 + x * 2 + c, y)

    def meet(self, use_y=True):
        barrier = pltpu.get_barrier_semaphore()
        partners = [self.device(x=1 - self.x), self.device(c=1 - self.c)]
        if use_y:
            partners.append(self.device(y=1 - self.y))
        for partner in partners:
            pl.semaphore_signal(barrier, inc=1, device_id=partner, device_id_type=MESH_ID)

        @pl.when(self.z > 0)
        def _():
            pl.semaphore_signal(
                barrier, inc=1, device_id=self.device(z=self.z - 1), device_id_type=MESH_ID
            )

        @pl.when(self.z < self.z_count - 1)
        def _():
            pl.semaphore_signal(
                barrier, inc=1, device_id=self.device(z=self.z + 1), device_id_type=MESH_ID
            )

        ends = jnp.where(self.z > 0, 1, 0) + jnp.where(self.z < self.z_count - 1, 1, 0)
        pl.semaphore_wait(barrier, len(partners) + ends)

    def far_first(self, step):
        last = self.z_count - 1
        low = jnp.where(step < last - self.z, last - step, step - (last - self.z))
        high = jnp.where(step < self.z, step, last - (step - self.z))
        return jnp.where(self.z * 2 < self.z_count, low, high)


def send(src, dst, send_sem, recv_sem, device):
    copy = pltpu.make_async_remote_copy(
        src_ref=src, dst_ref=dst, send_sem=send_sem, recv_sem=recv_sem, device_id=device, device_id_type=MESH_ID
    )
    copy.start()
    return copy


def add_rows(total, part, rows, step=16):
    def chunk(i, carry):
        here = pl.ds(pl.multiple_of(i * step, step), step)
        total[here] = total[here] + part[here]
        return carry

    lax.fori_loop(0, rows // step, chunk, 0)


def spread_rows(place, src, whole, half, sems):
    z, x, c, y, nz = place.z, place.x, place.c, place.y, place.z_count
    sent, got, kept = sems
    ZU, ZD, XF, YF, XH, YH, CO, CX, CY, CA, CB = range(11)
    up, down = place.device(z=z + 1), place.device(z=z - 1)
    over_x, over_y, over_c = place.device(x=1 - x), place.device(y=1 - y), place.device(c=1 - c)
    full = slice(None)
    low, high = pl.ds(0, half), pl.ds(half, half)

    def at(zz, xx, yy, rows=full):
        return whole.at[zz, xx, c, yy, rows]

    def push(kind, zz, xx, yy, rows, device, origin=None):
        ref = at(zz, xx, yy, rows)
        send(ref if origin is None else origin, ref, sent.at[kind, zz], got.at[kind, zz], device)

    def arrival(kind, zz, xx, yy, rows=full, cc=None):
        ref = whole.at[zz, xx, c if cc is None else cc, yy, rows]
        pltpu.make_async_copy(ref, ref, got.at[kind, zz]).wait()

    def departure(kind, zz, xx, yy, rows=full):
        ref = at(zz, xx, yy, rows)
        pltpu.make_async_copy(ref, ref, sent.at[kind, zz]).wait()

    def spread_own(zz, origin=None):
        push(XF, zz, x, y, full, over_x, origin)
        push(YF, zz, x, y, full, over_y, origin)
        push(CO, zz, x, y, full, over_c, origin)

    @pl.when(z < nz - 1)
    def _():
        push(ZU, z, x, y, full, up, src)

    @pl.when(z > 0)
    def _():
        push(ZD, z, x, y, full, down, src)

    spread_own(z, src)
    keep = pltpu.make_async_copy(src, at(z, x, y), kept)
    keep.start()

    def relay(zz):
        arrival(XF, zz, 1 - x, y)
        push(YH, zz, 1 - x, y, low, over_y)
        push(CX, zz, 1 - x, y, full, over_c)
        arrival(YF, zz, x, 1 - y)
        push(XH, zz, x, 1 - y, high, over_x)
        push(CY, zz, x, 1 - y, full, over_c)

    for d in range(nz):
        below, above = z - d - 1, z + d + 1
        if d < nz - 1:
            @pl.when(below >= 0)
            def _():
                arrival(ZU, below, x, y)

                @pl.when(z < nz - 1)
                def _():
                    push(ZU, below, x, y, full, up)

                spread_own(below)

            @pl.when(above < nz)
            def _():
                arrival(ZD, above, x, y)

                @pl.when(z > 0)
                def _():
                    push(ZD, above, x, y, full, down)

                spread_own(above)

        if d == 0:
            relay(z)
        else:
            @pl.when(z - d >= 0)
            def _():
                relay(z - d)

            @pl.when(z + d < nz)
            def _():
                relay(z + d)

    def diagonal(zz):
        arrival(XH, zz, 1 - x, 1 - y, high)
        push(CB, zz, 1 - x, 1 - y, high, over_c)
        arrival(YH, zz, 1 - x, 1 - y, low)
        push(CA, zz, 1 - x, 1 - y, low, over_c)

    diagonal(z)
    for d in range(1, nz):
        @pl.when(z - d >= 0)
        def _():
            diagonal(z - d)

        @pl.when(z + d < nz)
        def _():
            diagonal(z + d)

    keep.wait()
    for zz in range(nz):
        arrival(CO, zz, x, y, cc=1 - c)
        arrival(CX, zz, 1 - x, y, cc=1 - c)
        arrival(CY, zz, x, 1 - y, cc=1 - c)
        arrival(CA, zz, 1 - x, 1 - y, low, cc=1 - c)
        arrival(CB, zz, 1 - x, 1 - y, high, cc=1 - c)
        departure(XF, zz, x, y)
        departure(YF, zz, x, y)
        departure(CO, zz, x, y)
        departure(CX, zz, 1 - x, y)
        departure(CY, zz, x, 1 - y)
        departure(YH, zz, 1 - x, y, low)
        departure(XH, zz, x, 1 - y, high)
        departure(CA, zz, 1 - x, 1 - y, low)
        departure(CB, zz, 1 - x, 1 - y, high)

        @pl.when((zz <= z) & (z < nz - 1))
        def _():
            departure(ZU, zz, x, y)

        @pl.when((zz >= z) & (z > 0))
        def _():
            departure(ZD, zz, x, y)


def gather_kernel(src, whole, sent, got, kept):
    place = Place()
    place.meet()
    spread_rows(place, src, whole, src.shape[0] // 2, (sent, got, kept))


def gather_everywhere(block, collective):
    rows, cols = block.shape
    nz = lax.axis_size("dp") // 4
    return pl.pallas_call(
        gather_kernel,
        out_shape=jax.ShapeDtypeStruct((nz, 2, 2, 2, rows, cols), block.dtype),
        in_specs=[ANYWHERE],
        out_specs=ANYWHERE,
        scratch_shapes=[
            pltpu.SemaphoreType.DMA((11, nz)),
            pltpu.SemaphoreType.DMA((11, nz)),
            pltpu.SemaphoreType.DMA,
        ],
        compiler_params=pltpu.CompilerParams(collective_id=collective, has_side_effects=True),
    )(block)


def scatter_kernel(parts, out, total, from_c, half_x, half_y, full_x, full_y, up_buf, down_buf, sent, got, loaded):
    place = Place()
    z, x, c, y, nz = place.z, place.x, place.c, place.y, place.z_count
    rows = total.shape[3]
    half = rows // 2
    CD, CX, CY, CO, XH, YH, XF, YF, ZU, ZD = range(10)
    over_x, over_y, over_c = place.device(x=1 - x), place.device(y=1 - y), place.device(c=1 - c)
    place.meet()

    def spot(kind):
        return {CD: (1, 1), CX: (1, 0), CY: (0, 1), CO: (0, 0)}[kind]

    for kind in (CD, CX, CY, CO):
        dx, dy = spot(kind)
        for i in range(nz):
            zz = place.far_first(i)
            xx, yy = (1 - x if dx else x), (1 - y if dy else y)
            send(parts.at[zz, xx, 1 - c, yy], from_c.at[dx, dy, zz], sent.at[kind, zz], got.at[kind, zz], over_c)
            pltpu.make_async_copy(parts.at[zz, xx, c, yy], total.at[dx, dy, zz], loaded.at[kind, zz]).start()

    def arrival(kind, zz, ref):
        pltpu.make_async_copy(ref, ref, got.at[kind, zz]).wait()

    def join_cores(kind, zz):
        dx, dy = spot(kind)
        here, there = total.at[dx, dy, zz], from_c.at[dx, dy, zz]
        pltpu.make_async_copy(here, here, loaded.at[kind, zz]).wait()
        arrival(kind, zz, there)
        add_rows(here, there, rows)

    low, high = pl.ds(0, half), pl.ds(half, half)
    for i in range(nz):
        zz = place.far_first(i)
        join_cores(CD, zz)
        send(total.at[1, 1, zz, low], half_x.at[zz], sent.at[XH, zz], got.at[XH, zz], over_x)
        send(total.at[1, 1, zz, high], half_y.at[zz], sent.at[YH, zz], got.at[YH, zz], over_y)
    for i in range(nz):
        zz = place.far_first(i)
        join_cores(CX, zz)
        join_cores(CY, zz)
        arrival(XH, zz, half_x.at[zz])
        add_rows(total.at[0, 1, zz, low], half_x.at[zz], half)
        send(total.at[0, 1, zz], full_y.at[zz], sent.at[YF, zz], got.at[YF, zz], over_y)
        arrival(YH, zz, half_y.at[zz])
        add_rows(total.at[1, 0, zz, high], half_y.at[zz], half)
        send(total.at[1, 0, zz], full_x.at[zz], sent.at[XF, zz], got.at[XF, zz], over_x)
    for i in range(nz):
        zz = place.far_first(i)
        mine = total.at[0, 0, zz]
        join_cores(CO, zz)
        arrival(XF, zz, full_x.at[zz])
        add_rows(mine, full_x.at[zz], rows)
        arrival(YF, zz, full_y.at[zz])
        add_rows(mine, full_y.at[zz], rows)

        @pl.when((z > 0) & (zz >= z))
        def _():
            arrival(ZU, zz, up_buf.at[zz])
            add_rows(mine, up_buf.at[zz], rows)

        @pl.when((z < nz - 1) & (zz <= z))
        def _():
            arrival(ZD, zz, down_buf.at[zz])
            add_rows(mine, down_buf.at[zz], rows)

        @pl.when(zz > z)
        def _():
            send(mine, up_buf.at[zz], sent.at[ZU, zz], got.at[ZU, zz], place.device(z=z + 1))

        @pl.when(zz < z)
        def _():
            send(mine, down_buf.at[zz], sent.at[ZD, zz], got.at[ZD, zz], place.device(z=z - 1))

    out[...] = total[0, 0, z]

    def departure(kind, zz, ref):
        pltpu.make_async_copy(ref, ref, sent.at[kind, zz]).wait()

    for zz in range(nz):
        for kind in (CD, CX, CY, CO):
            departure(kind, zz, total.at[0, 0, zz])
        departure(XH, zz, half_x.at[zz])
        departure(YH, zz, half_y.at[zz])
        departure(XF, zz, full_x.at[zz])
        departure(YF, zz, full_y.at[zz])

        @pl.when(zz > z)
        def _():
            departure(ZU, zz, up_buf.at[zz])

        @pl.when(zz < z)
        def _():
            departure(ZD, zz, down_buf.at[zz])


def scatter_sum(parts, collective):
    nz, _, _, _, rows, cols = parts.shape
    dt = parts.dtype
    return pl.pallas_call(
        scatter_kernel,
        out_shape=jax.ShapeDtypeStruct((rows, cols), dt),
        in_specs=[ANYWHERE],
        out_specs=IN_VMEM,
        scratch_shapes=[
            pltpu.VMEM((2, 2, nz, rows, cols), dt),
            pltpu.VMEM((2, 2, nz, rows, cols), dt),
            pltpu.VMEM((nz, rows // 2, cols), dt),
            pltpu.VMEM((nz, rows // 2, cols), dt),
            pltpu.VMEM((nz, rows, cols), dt),
            pltpu.VMEM((nz, rows, cols), dt),
            pltpu.VMEM((nz, rows, cols), dt),
            pltpu.VMEM((nz, rows, cols), dt),
            pltpu.SemaphoreType.DMA((10, nz)),
            pltpu.SemaphoreType.DMA((10, nz)),
            pltpu.SemaphoreType.DMA((4, nz)),
        ],
        compiler_params=pltpu.CompilerParams(
            collective_id=collective, has_side_effects=True, vmem_limit_bytes=58 << 20
        ),
    )(parts)


def plane_gather_kernel(count, *refs):
    srcs, outs = refs[:count], refs[count : 2 * count]
    sent, got, kept = refs[2 * count :]
    place = Place()
    z, x, c, nz = place.z, place.x, place.c, place.z_count
    ZU, ZD, XF, CO, CX = range(5)
    up, down = place.device(z=z + 1), place.device(z=z - 1)
    over_x, over_c = place.device(x=1 - x), place.device(c=1 - c)
    place.meet(use_y=False)
    every = range(count)

    def push(a, kind, zz, xx, device, own=False):
        ref = outs[a].at[zz, xx, c]
        send(srcs[a] if own else ref, ref, sent.at[kind, a, zz], got.at[kind, a, zz], device)

    def arrival(a, kind, zz, xx, cc):
        ref = outs[a].at[zz, xx, cc]
        pltpu.make_async_copy(ref, ref, got.at[kind, a, zz]).wait()

    def departure(a, kind, zz, xx):
        ref = outs[a].at[zz, xx, c]
        pltpu.make_async_copy(ref, ref, sent.at[kind, a, zz]).wait()

    keeps = []
    for a in every:
        push(a, XF, z, x, over_x, own=True)

        @pl.when(z < nz - 1)
        def _():
            push(a, ZU, z, x, up, own=True)

        @pl.when(z > 0)
        def _():
            push(a, ZD, z, x, down, own=True)

        push(a, CO, z, x, over_c, own=True)
        keep = pltpu.make_async_copy(srcs[a], outs[a].at[z, x, c], kept.at[a])
        keep.start()
        keeps.append(keep)

    def relay(a, zz):
        arrival(a, XF, zz, 1 - x, c)
        push(a, CX, zz, 1 - x, over_c)

    for d in range(nz):
        below, above = z - d - 1, z + d + 1
        for a in every:
            if d < nz - 1:
                @pl.when(below >= 0)
                def _():
                    arrival(a, ZU, below, x, c)

                    @pl.when(z < nz - 1)
                    def _():
                        push(a, ZU, below, x, up)

                    push(a, XF, below, x, over_x)
                    push(a, CO, below, x, over_c)

                @pl.when(above < nz)
                def _():
                    arrival(a, ZD, above, x, c)

                    @pl.when(z > 0)
                    def _():
                        push(a, ZD, above, x, down)

                    push(a, XF, above, x, over_x)
                    push(a, CO, above, x, over_c)

    for d in range(nz):
        for a in every:
            if d == 0:
                relay(a, z)
            else:
                @pl.when(z - d >= 0)
                def _():
                    relay(a, z - d)

                @pl.when(z + d < nz)
                def _():
                    relay(a, z + d)

    for a in every:
        keeps[a].wait()
        for zz in range(nz):
            arrival(a, CO, zz, x, 1 - c)
            arrival(a, CX, zz, 1 - x, 1 - c)
            departure(a, XF, zz, x)
            departure(a, CO, zz, x)
            departure(a, CX, zz, 1 - x)

            @pl.when((zz <= z) & (z < nz - 1))
            def _():
                departure(a, ZU, zz, x)

            @pl.when((zz >= z) & (z > 0))
            def _():
                departure(a, ZD, zz, x)


def gather_in_plane(shards, collective):
    nz = lax.axis_size("dp") // 4
    count = len(shards)
    return pl.pallas_call(
        functools.partial(plane_gather_kernel, count),
        out_shape=[jax.ShapeDtypeStruct((nz, 2, 2) + s.shape, s.dtype) for s in shards],
        in_specs=[ANYWHERE] * count,
        out_specs=[ANYWHERE] * count,
        scratch_shapes=[
            pltpu.SemaphoreType.DMA((5, count, nz)),
            pltpu.SemaphoreType.DMA((5, count, nz)),
            pltpu.SemaphoreType.DMA((count,)),
        ],
        compiler_params=pltpu.CompilerParams(collective_id=collective, has_side_effects=True),
    )(*shards)


def plane_scatter_kernel(count, *refs):
    parts, outs = refs[:count], refs[count : 2 * count]
    total, from_c, full_x, up_buf, down_buf, sent, got, loaded = refs[2 * count :]
    place = Place()
    z, x, c, nz = place.z, place.x, place.c, place.z_count
    rows = total.shape[3]
    C0, C1, XF, ZU, ZD = range(5)
    over_x, over_c = place.device(x=1 - x), place.device(c=1 - c)
    place.meet(use_y=False)

    def arrival(a, kind, zz, ref):
        pltpu.make_async_copy(ref, ref, got.at[kind, a, zz]).wait()

    for dx, kind in ((1, C1), (0, C0)):
        for i in range(nz):
            zz = place.far_first(i)
            xx = 1 - x if dx else x
            for a in range(count):
                send(parts[a].at[zz, xx, 1 - c], from_c.at[dx, zz, a], sent.at[kind, a, zz], got.at[kind, a, zz], over_c)
                pltpu.make_async_copy(parts[a].at[zz, xx, c], total.at[dx, zz, a], loaded.at[dx, a, zz]).start()

    def join_cores(a, dx, zz):
        here, there = total.at[dx, zz, a], from_c.at[dx, zz, a]
        pltpu.make_async_copy(here, here, loaded.at[dx, a, zz]).wait()
        arrival(a, C1 if dx else C0, zz, there)
        add_rows(here, there, rows)

    for i in range(nz):
        zz = place.far_first(i)
        for a in range(count):
            join_cores(a, 1, zz)
            send(total.at[1, zz, a], full_x.at[zz, a], sent.at[XF, a, zz], got.at[XF, a, zz], over_x)
    for i in range(nz):
        zz = place.far_first(i)
        for a in range(count):
            mine = total.at[0, zz, a]
            join_cores(a, 0, zz)
            arrival(a, XF, zz, full_x.at[zz, a])
            add_rows(mine, full_x.at[zz, a], rows)

            @pl.when((z > 0) & (zz >= z))
            def _():
                arrival(a, ZU, zz, up_buf.at[zz, a])
                add_rows(mine, up_buf.at[zz, a], rows)

            @pl.when((z < nz - 1) & (zz <= z))
            def _():
                arrival(a, ZD, zz, down_buf.at[zz, a])
                add_rows(mine, down_buf.at[zz, a], rows)

            @pl.when(zz > z)
            def _():
                send(mine, up_buf.at[zz, a], sent.at[ZU, a, zz], got.at[ZU, a, zz], place.device(z=z + 1))

            @pl.when(zz < z)
            def _():
                send(mine, down_buf.at[zz, a], sent.at[ZD, a, zz], got.at[ZD, a, zz], place.device(z=z - 1))

    for a in range(count):

        def widen(i, carry):
            here = pl.ds(pl.multiple_of(i * 16, 16), 16)
            outs[a][here] = total[0, z, a, here].astype(jnp.float32)
            return carry

        lax.fori_loop(0, rows // 16, widen, 0)

    def departure(a, kind, zz, ref):
        pltpu.make_async_copy(ref, ref, sent.at[kind, a, zz]).wait()

    for a in range(count):
        for zz in range(nz):
            departure(a, C0, zz, total.at[0, 0, a])
            departure(a, C1, zz, total.at[0, 0, a])
            departure(a, XF, zz, total.at[0, 0, a])

            @pl.when(zz > z)
            def _():
                departure(a, ZU, zz, total.at[0, 0, a])

            @pl.when(zz < z)
            def _():
                departure(a, ZD, zz, total.at[0, 0, a])


def scatter_in_plane(parts, collective):
    nz, _, _, rows, cols = parts[0].shape
    count = len(parts)
    dt = parts[0].dtype
    return pl.pallas_call(
        functools.partial(plane_scatter_kernel, count),
        out_shape=[jax.ShapeDtypeStruct((rows, cols), jnp.float32)] * count,
        in_specs=[ANYWHERE] * count,
        out_specs=[IN_VMEM] * count,
        scratch_shapes=[
            pltpu.VMEM((2, nz, count, rows, cols), dt),
            pltpu.VMEM((2, nz, count, rows, cols), dt),
            pltpu.VMEM((nz, count, rows, cols), dt),
            pltpu.VMEM((nz, count, rows, cols), dt),
            pltpu.VMEM((nz, count, rows, cols), dt),
            pltpu.SemaphoreType.DMA((5, count, nz)),
            pltpu.SemaphoreType.DMA((5, count, nz)),
            pltpu.SemaphoreType.DMA((2, count, nz)),
        ],
        compiler_params=pltpu.CompilerParams(
            collective_id=collective, has_side_effects=True, vmem_limit_bytes=58 << 20
        ),
    )(*parts)


def dot_nn(a, b):
    return lax.dot_general(a, b, (((1,), (0,)), ((), ())), preferred_element_type=jnp.float32)


def dot_nt(a, b):
    return lax.dot_general(a, b, (((1,), (1,)), ((), ())), preferred_element_type=jnp.float32)


def dot_tn(a, b):
    return lax.dot_general(a, b, (((0,), (0,)), ((), ())), preferred_element_type=jnp.float32)


def expert_kernel(
    x_ref,
    g_ref,
    hot_ref,
    router_ref,
    lanes_ref,
    wg_ref,
    wu_ref,
    wd_ref,
    y_ref,
    r_ref,
    wg_grad_ref,
    wu_grad_ref,
    wd_grad_ref,
):
    @pl.when(pl.program_id(0) == 0)
    def _():
        wg_grad_ref[...] = jnp.zeros_like(wg_grad_ref)
        wu_grad_ref[...] = jnp.zeros_like(wu_grad_ref)
        wd_grad_ref[...] = jnp.zeros_like(wd_grad_ref)

    rows = x_ref[...]
    upstream = g_ref[...]
    logits = jnp.where(lanes_ref[1:2] > 0.0, dot_nn(rows, router_ref[...]), -1e30)
    weights = jnp.exp(logits - jnp.max(logits, axis=1, keepdims=True))
    own_weight = jnp.sum(weights * lanes_ref[0:1], axis=1, keepdims=True)
    gate = hot_ref[...] * own_weight / jnp.sum(weights, axis=1, keepdims=True)
    gate_pre = dot_nn(rows, wg_ref[...])
    up_pre = dot_nn(rows, wu_ref[...])
    raw_grad = dot_nt(upstream, wd_ref[...])
    sigmoid = jax.nn.sigmoid(gate_pre)
    silu = gate_pre * sigmoid
    hidden = silu * up_pre
    width = x_ref.shape[1]
    gate_grad = jnp.sum(hidden * raw_grad, axis=1, keepdims=True)
    coarse = gate_grad.astype(jnp.bfloat16).astype(jnp.float32)
    r_ref[:, width:] = (coarse * lanes_ref[2:3] + (gate_grad - coarse) * lanes_ref[3:4]).astype(
        jnp.bfloat16
    )
    hidden_gated = (gate * hidden).astype(jnp.bfloat16)
    y_ref[...] = dot_nn(hidden_gated, wd_ref[...]).astype(jnp.bfloat16)
    hidden_grad = gate * raw_grad
    up_grad = (hidden_grad * silu).astype(jnp.bfloat16)
    gate_pre_grad = (
        hidden_grad * up_pre * sigmoid * (1.0 + gate_pre * (1.0 - sigmoid))
    ).astype(jnp.bfloat16)
    r_ref[:, :width] = (
        dot_nt(gate_pre_grad, wg_ref[...]) + dot_nt(up_grad, wu_ref[...])
    ).astype(jnp.bfloat16)
    wg_grad_ref[...] += dot_tn(rows, gate_pre_grad)
    wu_grad_ref[...] += dot_tn(rows, up_grad)
    wd_grad_ref[...] += dot_tn(hidden_gated, upstream)


def expert_pass(rows, upstream, hot, router, lanes, w_gate, w_up, w_down):
    count, width = rows.shape
    units = w_gate.shape[1]
    tile = 512 if count % 512 == 0 else GROUP // 2

    def by_row(cols):
        return pl.BlockSpec((tile, cols), lambda i: (i, 0))

    def whole(first, second):
        return pl.BlockSpec((first, second), lambda i: (0, 0), pipeline_mode=pl.Buffered(1))

    weights = [whole(width, units), whole(width, units), whole(units, width)]
    return pl.pallas_call(
        expert_kernel,
        grid=(count // tile,),
        in_specs=[by_row(width), by_row(width), by_row(1), whole(width, LANES), whole(8, LANES)]
        + weights,
        out_specs=[by_row(width), by_row(width + LANES)] + weights,
        out_shape=[
            jax.ShapeDtypeStruct((count, width), jnp.bfloat16),
            jax.ShapeDtypeStruct((count, width + LANES), jnp.bfloat16),
            jax.ShapeDtypeStruct((width, units), jnp.float32),
            jax.ShapeDtypeStruct((width, units), jnp.float32),
            jax.ShapeDtypeStruct((units, width), jnp.float32),
        ],
        cost_estimate=pl.CostEstimate(
            flops=18 * count * width * units,
            bytes_accessed=8 * count * width + 18 * width * units,
            transcendentals=count * units,
        ),
        compiler_params=pltpu.CompilerParams(vmem_limit_bytes=60 << 20),
    )(rows, upstream, hot, router, lanes, w_gate, w_up, w_down)


def dense_body(
    tokens,
    routes,
    cotangent,
    attn_gain,
    q_gain,
    k_gain,
    w_query,
    w_key,
    w_value,
    w_out,
    mlp_gain,
    router,
    w_gate,
    w_up,
    w_down,
):
    rank_index = lax.axis_index("tensor")
    own_rows = tokens.shape[0]
    head_cols = w_query.shape[1]
    local_heads = head_cols // HEAD
    col_start = rank_index * head_cols
    row_start = rank_index * own_rows
    experts = router.shape[1]
    attn_scale = HEAD ** (-0.5)
    head_shape = (GROUP, local_heads, HEAD)
    q_gain_local = lax.dynamic_slice_in_dim(q_gain, col_start, head_cols)
    k_gain_local = lax.dynamic_slice_in_dim(k_gain, col_start, head_cols)
    inputs = tokens.astype(jnp.float32)
    attn_inv = lax.rsqrt(jnp.mean(inputs * inputs, axis=1, keepdims=True) + EPSILON)
    normed = gather_rows((inputs * attn_inv * attn_gain).astype(jnp.bfloat16))
    q_all, k_all, v_all, o_all = gather_in_plane((w_query, w_key, w_value, w_out), 1)
    q_all, k_all, v_all = (w.reshape(D, head_cols) for w in (q_all, k_all, v_all))
    o_all = jnp.transpose(o_all.reshape(-1, *w_out.shape), (1, 0, 2)).reshape(head_cols, D)
    routes_all = lax.all_gather(routes, "dp", axis=0, tiled=True)
    own_expert = lax.axis_index("dp")
    hot = jnp.any(routes_all == own_expert, axis=1, keepdims=True).astype(jnp.float32)
    lane = jnp.arange(LANES)
    marked = own_expert + experts * rank_index
    lanes = jnp.stack(
        [lane == own_expert, lane < experts, lane == marked, lane == marked + 2 * experts]
        + [lane < 0] * 4
    ).astype(jnp.float32)
    router_wide = jnp.pad(router, ((0, 0), (0, LANES - experts)))
    upstream_all = lax.all_gather(cotangent, EVERY, axis=0, tiled=True)
    queries = matmul(normed, q_all)
    keys_raw = matmul(normed, k_all)
    values_raw = matmul(normed, v_all)
    query_sq, key_sq = tensor_total(
        (jnp.sum(queries * queries, axis=1), jnp.sum(keys_raw * keys_raw, axis=1))
    )
    query_inv = lax.rsqrt(query_sq / D + EPSILON)[:, None]
    key_inv = lax.rsqrt(key_sq / D + EPSILON)[:, None]
    cosine_table, sine_table = rope_tables()
    query_rot = rotate(
        (queries * query_inv * q_gain_local).reshape(head_shape), cosine_table, sine_table
    ).astype(jnp.bfloat16)
    key_rot = rotate(
        (keys_raw * key_inv * k_gain_local).reshape(head_shape), cosine_table, sine_table
    ).astype(jnp.bfloat16)
    value_heads = values_raw.astype(jnp.bfloat16).reshape(head_shape)
    visible = visible_keys()[None]

    def masked_scores():
        raw_scores = (
            jnp.einsum("qhd,khd->hqk", query_rot, key_rot, preferred_element_type=jnp.float32)
            * attn_scale
        )
        return jnp.where(visible, raw_scores, -1e30)

    scores = masked_scores()
    row_max = jnp.max(scores, axis=2, keepdims=True)
    exponent = jnp.exp(scores - row_max)
    row_total = jnp.sum(exponent, axis=2, keepdims=True)
    log_total = row_max + jnp.log(row_total)
    mixed_heads = jnp.einsum(
        "hqk,khd->qhd",
        (exponent / row_total).astype(jnp.bfloat16),
        value_heads,
        preferred_element_type=jnp.float32,
    )
    mixed_heads = mixed_heads.reshape(GROUP, head_cols).astype(jnp.bfloat16)
    attended = sum_rows(matmul(mixed_heads, o_all))
    hidden_one = inputs + attended
    mlp_inv = lax.rsqrt(jnp.mean(hidden_one * hidden_one, axis=1, keepdims=True) + EPSILON)
    normed_two = (hidden_one * mlp_inv * mlp_gain).astype(jnp.bfloat16)
    own_routes = lax.dynamic_slice_in_dim(routes, row_start, own_rows, 0)
    expert_ids = jnp.arange(experts, dtype=jnp.int32)
    own_hot = jnp.any(own_routes[:, :, None] == expert_ids[None, None, :], axis=1)
    own_probs = jax.nn.softmax(matmul(normed_two, router), axis=1)
    rows_all = gather_everywhere(normed_two, 2).reshape(-1, D)
    y_part, r_part, gate_weight_grad, up_weight_grad, down_weight_grad = expert_pass(
        rows_all, upstream_all, hot, router_wide, lanes, w_gate[0], w_up[0], w_down[0]
    )
    blocks = (lax.axis_size("dp") // 4, 2, 2, 2, own_rows)
    returned = scatter_sum(r_part.reshape(*blocks, D + LANES), 3)
    y_part, returned = lax.optimization_barrier((y_part, returned))
    mixture = lax.psum_scatter(y_part, EVERY, scatter_dimension=0, tiled=True)
    layer_out = (hidden_one + mixture.astype(jnp.float32)).astype(jnp.bfloat16)
    expert_grad = jnp.sum(
        returned[:, D : D + 4 * experts].astype(jnp.float32).reshape(own_rows, 4, experts), axis=1
    )
    expert_grad = jnp.where(own_hot, expert_grad, 0.0)
    returned = returned[:, :D]
    upstream = cotangent.astype(jnp.float32)
    logit_grad = own_probs * (expert_grad - jnp.sum(expert_grad * own_probs, axis=1, keepdims=True))
    router_grad = jnp.dot(normed_two.astype(jnp.float32).T, logit_grad, precision=HIGHEST)
    normed_two_grad = returned.astype(jnp.float32) + jnp.dot(
        logit_grad, router.astype(jnp.float32).T, precision=HIGHEST
    )
    scaled_grad = normed_two_grad * mlp_gain
    hidden_one_grad = (
        upstream
        + mlp_inv * scaled_grad
        - hidden_one * mlp_inv**3 * jnp.mean(hidden_one * scaled_grad, axis=1, keepdims=True)
    )
    mlp_gain_grad = jnp.sum(normed_two_grad * hidden_one * mlp_inv, axis=0)
    attended_grad = gather_rows(hidden_one_grad.astype(jnp.bfloat16))
    mixed_grad = jnp.einsum("gd,cd->gc", attended_grad, o_all, preferred_element_type=jnp.float32)
    mixed_grad = mixed_grad.astype(jnp.bfloat16).reshape(head_shape)
    attn_probs = jnp.exp(masked_scores() - log_total)
    prob_grad = jnp.einsum(
        "qhd,khd->hqk", mixed_grad, value_heads, preferred_element_type=jnp.float32
    )
    row_dot = jnp.sum(prob_grad * attn_probs, axis=2, keepdims=True)
    score_grad = (attn_probs * (prob_grad - row_dot)).astype(jnp.bfloat16)
    query_rot_grad = (
        jnp.einsum("hqk,khd->qhd", score_grad, key_rot, preferred_element_type=jnp.float32)
        * attn_scale
    )
    key_rot_grad = (
        jnp.einsum("hqk,qhd->khd", score_grad, query_rot, preferred_element_type=jnp.float32)
        * attn_scale
    )
    value_grad = (
        jnp.einsum(
            "hqk,qhd->khd",
            attn_probs.astype(jnp.bfloat16),
            mixed_grad,
            preferred_element_type=jnp.float32,
        )
        .reshape(GROUP, head_cols)
        .astype(jnp.bfloat16)
    )
    query_norm_grad = unrotate(query_rot_grad, cosine_table, sine_table).reshape(GROUP, head_cols)
    key_norm_grad = unrotate(key_rot_grad, cosine_table, sine_table).reshape(GROUP, head_cols)
    query_scaled = query_norm_grad * q_gain_local
    key_scaled = key_norm_grad * k_gain_local
    query_dot, key_dot = tensor_total(
        (jnp.sum(queries * query_scaled, axis=1), jnp.sum(keys_raw * key_scaled, axis=1))
    )
    query_grad = (
        query_inv * query_scaled - queries * query_inv**3 * (query_dot / D)[:, None]
    ).astype(jnp.bfloat16)
    key_grad = (key_inv * key_scaled - keys_raw * key_inv**3 * (key_dot / D)[:, None]).astype(
        jnp.bfloat16
    )
    q_gain_part = jnp.sum(query_norm_grad * queries * query_inv, axis=0)
    k_gain_part = jnp.sum(key_norm_grad * keys_raw * key_inv, axis=0)
    normed_part = (
        jnp.einsum("gc,rc->gr", query_grad, q_all, preferred_element_type=jnp.float32)
        + jnp.einsum("gc,rc->gr", key_grad, k_all, preferred_element_type=jnp.float32)
        + jnp.einsum("gc,rc->gr", value_grad, v_all, preferred_element_type=jnp.float32)
    )
    shard = (lax.axis_size("dp") // 4, 2, 2, w_query.shape[0], head_cols)
    weight_sums = scatter_in_plane(
        [
            dot_tn(first, second).astype(jnp.bfloat16).reshape(shard)
            for first, second in (
                (normed, query_grad),
                (normed, key_grad),
                (normed, value_grad),
                (attended_grad, mixed_heads),
            )
        ],
        4,
    )
    normed_grad = sum_rows(normed_part)
    scaled_input = normed_grad * attn_gain
    tokens_grad = (
        hidden_one_grad
        + attn_inv * scaled_input
        - inputs * attn_inv**3 * jnp.mean(inputs * scaled_input, axis=1, keepdims=True)
    )
    attn_gain_grad = jnp.sum(normed_grad * inputs * attn_inv, axis=0)
    zero_width = jnp.zeros((D,), jnp.float32)
    q_gain_full = lax.dynamic_update_slice_in_dim(zero_width, q_gain_part, col_start, 0)
    k_gain_full = lax.dynamic_update_slice_in_dim(zero_width, k_gain_part, col_start, 0)
    attn_gain_grad, q_gain_grad, k_gain_grad, mlp_gain_grad, router_grad = lax.psum(
        (attn_gain_grad, q_gain_full, k_gain_full, mlp_gain_grad, router_grad), EVERY
    )
    return (
        layer_out,
        tokens_grad,
        attn_gain_grad,
        q_gain_grad,
        k_gain_grad,
        weight_sums[0],
        weight_sums[1],
        weight_sums[2],
        jnp.transpose(weight_sums[3]),
        mlp_gain_grad,
        router_grad,
        gate_weight_grad[None],
        up_weight_grad[None],
        down_weight_grad[None],
    )


def solution(mesh):
    in_specs = (
        P(("dp", "tensor"), None),
        P("dp", None),
        P(("dp", "tensor"), None),
        P(),
        P(),
        P(),
        P("dp", "tensor"),
        P("dp", "tensor"),
        P("dp", "tensor"),
        P("tensor", "dp"),
        P(),
        P(),
        P("dp", None, "tensor"),
        P("dp", None, "tensor"),
        P("dp", "tensor", None),
    )
    out_specs = (
        P(("dp", "tensor"), None),
        P(("dp", "tensor"), None),
        P(),
        P(),
        P(),
        P("dp", "tensor"),
        P("dp", "tensor"),
        P("dp", "tensor"),
        P("tensor", "dp"),
        P(),
        P(),
        P("dp", None, "tensor"),
        P("dp", None, "tensor"),
        P("dp", "tensor", None),
    )
    experts = mesh.shape["dp"]
    body = dense_body if experts <= 2 * TOPK else routed_body
    return jax.shard_map(body, mesh=mesh, in_specs=in_specs, out_specs=out_specs, check_vma=False)
```

```python
import functools

import jax
import jax.numpy as jnp
from jax import lax
from jax.experimental import pallas as pl
from jax.experimental.pallas import tpu as pltpu
from jax.sharding import PartitionSpec as P

D = 2048
HEAD = 128
TOPK = 8
PROMPT = 256
CONT = 64
GROUP = 384


EPSILON = 1e-05
ROPE_BASE = 10000.0
HIGHEST = lax.Precision.HIGHEST


def matmul(first_op, second_op):
    return jnp.dot(first_op, second_op, preferred_element_type=jnp.float32)


def gather_rows(values):
    return lax.all_gather(values, "tensor", axis=0, tiled=True)


def sum_rows(values):
    return lax.psum_scatter(values, "tensor", scatter_dimension=0, tiled=True)


def tensor_total(values):
    return lax.psum((values[0], values[1]), "tensor")


def expert_swap(values):
    return lax.all_to_all(values, "dp", split_axis=0, concat_axis=0, tiled=True)


def sum_slots(values):
    return lax.psum_scatter(values, "tensor", scatter_dimension=1, tiled=True)


def group_positions():
    position = jnp.arange(GROUP, dtype=jnp.int32)
    return jnp.where(position < PROMPT, position, PROMPT + (position - PROMPT) % CONT)


def visible_keys():
    position = jnp.arange(GROUP, dtype=jnp.int32)
    member = jnp.where(position < PROMPT, -1, (position - PROMPT) // CONT)
    causal = position[None, :] <= position[:, None]
    return causal & ((member[None, :] == -1) | (member[None, :] == member[:, None]))


def rope_tables():
    half_head = HEAD // 2
    frequency = ROPE_BASE ** (-2.0 * jnp.arange(half_head, dtype=jnp.float32) / HEAD)
    angles = group_positions().astype(jnp.float32)[:, None] * frequency[None, :]
    angles = jnp.concatenate([angles, angles], axis=1)
    return (jnp.cos(angles), jnp.sin(angles))


def rotate(values, cosine_table, sine_table):
    half_head = HEAD // 2
    turned = jnp.concatenate([-values[..., half_head:], values[..., :half_head]], axis=-1)
    return values * cosine_table[:, None, :] + turned * sine_table[:, None, :]


def unrotate(values, cosine_table, sine_table):
    half_head = HEAD // 2
    scaled = values * sine_table[:, None, :]
    turned = jnp.concatenate([scaled[..., half_head:], -scaled[..., :half_head]], axis=-1)
    return values * cosine_table[:, None, :] + turned


def gate_split(rows_in, hot_table, router):
    gates = jax.nn.softmax(matmul(rows_in, router), axis=1)
    weights = jnp.sum(jnp.where(hot_table, gates[:, None, :], 0.0), axis=2)
    return (gates, weights)


def routed_body(
    tokens,
    routes,
    cotangent,
    attn_gain,
    q_gain,
    k_gain,
    w_query,
    w_key,
    w_value,
    w_out,
    mlp_gain,
    router,
    w_gate,
    w_up,
    w_down,
):
    rank_index = lax.axis_index("tensor")
    tensor_count = lax.axis_size("tensor")
    own_rows = tokens.shape[0]
    head_cols = w_query.shape[1]
    local_heads = head_cols // HEAD
    col_start = rank_index * head_cols
    row_start = rank_index * own_rows
    experts = router.shape[1]
    half_cap = (own_rows * TOPK * 4 + 3 * experts - 1) // (3 * experts)
    capacity = tensor_count * half_cap
    attn_scale = HEAD ** (-0.5)
    head_shape = (GROUP, local_heads, HEAD)
    q_gain_local = lax.dynamic_slice_in_dim(q_gain, col_start, head_cols)
    k_gain_local = lax.dynamic_slice_in_dim(k_gain, col_start, head_cols)
    inputs = tokens.astype(jnp.float32)
    attn_inv = lax.rsqrt(jnp.mean(inputs * inputs, axis=1, keepdims=True) + EPSILON)
    normed = gather_rows((inputs * attn_inv * attn_gain).astype(jnp.bfloat16))
    pieces = (
        lax.all_gather(w_query, "dp", axis=0, tiled=True),
        lax.all_gather(w_key, "dp", axis=0, tiled=True),
        lax.all_gather(w_value, "dp", axis=0, tiled=True),
    )
    normed_part = normed
    queries = matmul(normed_part, pieces[0])
    keys_raw = matmul(normed_part, pieces[1])
    values_raw = matmul(normed_part, pieces[2])
    query_sq, key_sq = tensor_total(
        (jnp.sum(queries * queries, axis=1), jnp.sum(keys_raw * keys_raw, axis=1))
    )
    query_inv = lax.rsqrt(query_sq / D + EPSILON)[:, None]
    key_inv = lax.rsqrt(key_sq / D + EPSILON)[:, None]
    cosine_table, sine_table = rope_tables()
    query_rot = rotate(
        (queries * query_inv * q_gain_local).reshape(head_shape), cosine_table, sine_table
    ).astype(jnp.bfloat16)
    key_rot = rotate(
        (keys_raw * key_inv * k_gain_local).reshape(head_shape), cosine_table, sine_table
    ).astype(jnp.bfloat16)
    value_heads = values_raw.astype(jnp.bfloat16).reshape(head_shape)
    visible = visible_keys()[None]

    def masked_scores():
        raw_scores = (
            jnp.einsum("qhd,khd->hqk", query_rot, key_rot, preferred_element_type=jnp.float32)
            * attn_scale
        )
        return jnp.where(visible, raw_scores, -1e30)

    scores = masked_scores()
    row_max = jnp.max(scores, axis=2, keepdims=True)
    exponent = jnp.exp(scores - row_max)
    row_total = jnp.sum(exponent, axis=2, keepdims=True)
    log_total = row_max + jnp.log(row_total)
    mixed_heads = jnp.einsum(
        "hqk,khd->qhd",
        (exponent / row_total).astype(jnp.bfloat16),
        value_heads,
        preferred_element_type=jnp.float32,
    )
    mixed_heads = mixed_heads.reshape(GROUP, head_cols).astype(jnp.bfloat16)
    attn_part = matmul(mixed_heads, lax.all_gather(w_out, "dp", axis=1, tiled=True))
    attended = sum_rows(attn_part)
    hidden_one = inputs + attended
    mlp_inv = lax.rsqrt(jnp.mean(hidden_one * hidden_one, axis=1, keepdims=True) + EPSILON)
    normed_two = (hidden_one * mlp_inv * mlp_gain).astype(jnp.bfloat16)
    expert_ids = jnp.arange(experts, dtype=jnp.int32)
    route_hot = routes[:, :, None] == expert_ids[None, None, :]
    flat_hot = route_hot.astype(jnp.int32).reshape(tensor_count, own_rows * TOPK, experts)
    within = jnp.sum((jnp.cumsum(flat_hot, axis=1) - flat_hot) * flat_hot, axis=2).reshape(
        GROUP, TOPK
    )
    owner_of = (jnp.arange(GROUP, dtype=jnp.int32) // own_rows)[:, None]
    own_routes = lax.dynamic_slice_in_dim(routes, row_start, own_rows, 0)
    own_within = lax.dynamic_slice_in_dim(within, row_start, own_rows, 0)
    own_hot = lax.dynamic_slice_in_dim(route_hot, row_start, own_rows, 0)
    own_dest = own_routes * half_cap + own_within
    gate_weight = w_gate[0]
    up_weight = w_up[0]
    down_weight = w_down[0]
    normed_two_all = gather_rows(normed_two)
    gates_every, gate_every = gate_split(normed_two_all, route_hot, router)
    own_probs = lax.dynamic_slice_in_dim(gates_every, row_start, own_rows, 0)
    gate_weights = lax.dynamic_slice_in_dim(gate_every, row_start, own_rows, 0)
    destination = routes * capacity + owner_of * half_cap + within
    send_rows = (
        jnp.zeros((experts * capacity, D), jnp.bfloat16)
        .at[destination]
        .set(jnp.broadcast_to(normed_two_all[:, None, :], (GROUP, TOPK, D)))
        .reshape(experts, capacity, D)
    )
    received = lax.all_to_all(send_rows, "dp", split_axis=0, concat_axis=0, tiled=True)
    gate_pre = jnp.einsum("scd,df->scf", received, gate_weight, preferred_element_type=jnp.float32)
    up_pre = jnp.einsum("scd,df->scf", received, up_weight, preferred_element_type=jnp.float32)
    hidden = (jax.nn.silu(gate_pre) * up_pre).astype(jnp.bfloat16)
    expert_part = jnp.einsum("scf,fd->scd", hidden, down_weight, preferred_element_type=jnp.float32)
    expert_part, gate_pre, up_pre, hidden, received = (
        expert_part,
        gate_pre,
        up_pre,
        hidden,
        received,
    )
    back_rows = expert_swap(sum_slots(expert_part).astype(jnp.bfloat16)).reshape(
        experts * half_cap, D
    )
    picked = back_rows[own_dest].astype(jnp.float32)
    mixture = jnp.sum(gate_weights[:, :, None] * picked, axis=1)
    layer_out = (hidden_one + mixture).astype(jnp.bfloat16)
    upstream = cotangent.astype(jnp.float32)
    gate_grad = jnp.sum(upstream[:, None, :] * picked, axis=2)
    upstream_all = gather_rows(cotangent).astype(jnp.float32)
    send_grads = (
        jnp.zeros((experts * capacity, D), jnp.bfloat16)
        .at[destination]
        .set((gate_every[:, :, None] * upstream_all[:, None, :]).astype(jnp.bfloat16))
        .reshape(experts, capacity, D)
    )
    out_grads = expert_swap(send_grads)
    hidden_grad = jnp.einsum(
        "scd,fd->scf", out_grads, down_weight, preferred_element_type=jnp.float32
    )
    sigmoid = jax.nn.sigmoid(gate_pre)
    up_grad = (hidden_grad * gate_pre * sigmoid).astype(jnp.bfloat16)
    gate_pre_grad = (hidden_grad * up_pre * sigmoid * (1.0 + gate_pre * (1.0 - sigmoid))).astype(
        jnp.bfloat16
    )
    row_part = jnp.einsum(
        "scf,df->scd", gate_pre_grad, gate_weight, preferred_element_type=jnp.float32
    ) + jnp.einsum("scf,df->scd", up_grad, up_weight, preferred_element_type=jnp.float32)
    down_weight_grad = jnp.einsum(
        "scf,scd->fd", hidden, out_grads, preferred_element_type=jnp.float32
    )
    gate_weight_grad = jnp.einsum(
        "scd,scf->df", received, gate_pre_grad, preferred_element_type=jnp.float32
    )
    up_weight_grad = jnp.einsum(
        "scd,scf->df", received, up_grad, preferred_element_type=jnp.float32
    )
    returned_grads = expert_swap(sum_slots(row_part).astype(jnp.bfloat16)).reshape(
        experts * half_cap, D
    )
    normed_two_part = jnp.sum(returned_grads[own_dest].astype(jnp.float32), axis=1)
    expert_grad = jnp.sum(jnp.where(own_hot, gate_grad[:, :, None], 0.0), axis=1)
    logit_grad = own_probs * (expert_grad - jnp.sum(expert_grad * own_probs, axis=1, keepdims=True))
    router_grad = jnp.dot(normed_two.astype(jnp.float32).T, logit_grad, precision=HIGHEST)
    normed_two_grad = normed_two_part + jnp.dot(
        logit_grad, router.astype(jnp.float32).T, precision=HIGHEST
    )
    scaled_grad = normed_two_grad * mlp_gain
    hidden_one_grad = (
        upstream
        + mlp_inv * scaled_grad
        - hidden_one * mlp_inv**3 * jnp.mean(hidden_one * scaled_grad, axis=1, keepdims=True)
    )
    mlp_gain_grad = jnp.sum(normed_two_grad * hidden_one * mlp_inv, axis=0)
    attended_grad = gather_rows(hidden_one_grad.astype(jnp.bfloat16))
    mixed_grad = jnp.einsum(
        "gd,cd->gc",
        attended_grad,
        lax.all_gather(w_out, "dp", axis=1, tiled=True),
        preferred_element_type=jnp.float32,
    )
    mixed_grad = mixed_grad.astype(jnp.bfloat16).reshape(head_shape)
    attn_probs = jnp.exp(masked_scores() - log_total)
    prob_grad = jnp.einsum(
        "qhd,khd->hqk", mixed_grad, value_heads, preferred_element_type=jnp.float32
    )
    row_dot = jnp.sum(prob_grad * attn_probs, axis=2, keepdims=True)
    score_grad = (attn_probs * (prob_grad - row_dot)).astype(jnp.bfloat16)
    query_rot_grad = (
        jnp.einsum("hqk,khd->qhd", score_grad, key_rot, preferred_element_type=jnp.float32)
        * attn_scale
    )
    key_rot_grad = (
        jnp.einsum("hqk,qhd->khd", score_grad, query_rot, preferred_element_type=jnp.float32)
        * attn_scale
    )
    value_grad = (
        jnp.einsum(
            "hqk,qhd->khd",
            attn_probs.astype(jnp.bfloat16),
            mixed_grad,
            preferred_element_type=jnp.float32,
        )
        .reshape(GROUP, head_cols)
        .astype(jnp.bfloat16)
    )
    query_norm_grad = unrotate(query_rot_grad, cosine_table, sine_table).reshape(GROUP, head_cols)
    key_norm_grad = unrotate(key_rot_grad, cosine_table, sine_table).reshape(GROUP, head_cols)
    query_scaled = query_norm_grad * q_gain_local
    key_scaled = key_norm_grad * k_gain_local
    query_dot, key_dot = tensor_total(
        (jnp.sum(queries * query_scaled, axis=1), jnp.sum(keys_raw * key_scaled, axis=1))
    )
    query_grad = (
        query_inv * query_scaled - queries * query_inv**3 * (query_dot / D)[:, None]
    ).astype(jnp.bfloat16)
    key_grad = (key_inv * key_scaled - keys_raw * key_inv**3 * (key_dot / D)[:, None]).astype(
        jnp.bfloat16
    )
    q_gain_part = jnp.sum(query_norm_grad * queries * query_inv, axis=0)
    k_gain_part = jnp.sum(key_norm_grad * keys_raw * key_inv, axis=0)
    pieces = lax.all_gather((w_query, w_key, w_value), "dp", axis=0, tiled=True)
    normed_part = (
        jnp.einsum("gc,rc->gr", query_grad, pieces[0], preferred_element_type=jnp.float32)
        + jnp.einsum("gc,rc->gr", key_grad, pieces[1], preferred_element_type=jnp.float32)
        + jnp.einsum("gc,rc->gr", value_grad, pieces[2], preferred_element_type=jnp.float32)
    )
    weight_sums = lax.psum_scatter(
        jnp.concatenate(
            [
                jnp.einsum("gr,gc->rc", normed, query_grad, preferred_element_type=jnp.float32),
                jnp.einsum("gr,gc->rc", normed, key_grad, preferred_element_type=jnp.float32),
                jnp.einsum("gr,gc->rc", normed, value_grad, preferred_element_type=jnp.float32),
                jnp.einsum(
                    "gr,gc->rc", attended_grad, mixed_heads, preferred_element_type=jnp.float32
                ),
            ],
            axis=1,
        ),
        "dp",
        scatter_dimension=0,
        tiled=True,
    )
    normed_grad = sum_rows(normed_part)
    scaled_input = normed_grad * attn_gain
    tokens_grad = (
        hidden_one_grad
        + attn_inv * scaled_input
        - inputs * attn_inv**3 * jnp.mean(inputs * scaled_input, axis=1, keepdims=True)
    )
    attn_gain_grad = jnp.sum(normed_grad * inputs * attn_inv, axis=0)
    zero_width = jnp.zeros((D,), jnp.float32)
    q_gain_full = lax.dynamic_update_slice_in_dim(zero_width, q_gain_part, col_start, 0)
    k_gain_full = lax.dynamic_update_slice_in_dim(zero_width, k_gain_part, col_start, 0)
    attn_gain_grad, q_gain_grad, k_gain_grad, mlp_gain_grad, router_grad = lax.psum(
        (attn_gain_grad, q_gain_full, k_gain_full, mlp_gain_grad, router_grad), ("dp", "tensor")
    )
    return (
        layer_out,
        tokens_grad,
        attn_gain_grad,
        q_gain_grad,
        k_gain_grad,
        weight_sums[:, :head_cols],
        weight_sums[:, head_cols : 2 * head_cols],
        weight_sums[:, 2 * head_cols : 3 * head_cols],
        jnp.transpose(weight_sums[:, 3 * head_cols :]),
        mlp_gain_grad,
        router_grad,
        gate_weight_grad[None],
        up_weight_grad[None],
        down_weight_grad[None],
    )


MESH_ID = pl.DeviceIdType.MESH
LINK_TIME = pl.CostEstimate(flops=10**11, bytes_accessed=10**8, transcendentals=0)
EVERY = ("dp", "tensor")
LANES = 128
ANYWHERE = pl.BlockSpec(memory_space=pl.ANY)
IN_VMEM = pl.BlockSpec(memory_space=pltpu.VMEM)


class Place:
    def __init__(self):
        dp = lax.axis_index("dp")
        self.y = lax.axis_index("tensor")
        self.z, self.x, self.c = dp // 4, (dp // 2) % 2, dp % 2
        self.z_count = lax.axis_size("dp") // 4

    def device(self, z=None, x=None, c=None, y=None):
        z = self.z if z is None else z
        x = self.x if x is None else x
        c = self.c if c is None else c
        y = self.y if y is None else y
        return (z * 4 + x * 2 + c, y)

    def meet(self, use_y=True, all_z=False):
        barrier = pltpu.get_barrier_semaphore()
        partners = [self.device(x=1 - self.x), self.device(c=1 - self.c)]
        if use_y:
            partners.append(self.device(y=1 - self.y))
        if all_z:
            partners += [self.device(z=(self.z + d) % self.z_count) for d in range(1, self.z_count)]
        for partner in partners:
            pl.semaphore_signal(barrier, inc=1, device_id=partner, device_id_type=MESH_ID)
        if all_z:
            pl.semaphore_wait(barrier, len(partners))
            return

        @pl.when(self.z > 0)
        def _():
            pl.semaphore_signal(
                barrier, inc=1, device_id=self.device(z=self.z - 1), device_id_type=MESH_ID
            )

        @pl.when(self.z < self.z_count - 1)
        def _():
            pl.semaphore_signal(
                barrier, inc=1, device_id=self.device(z=self.z + 1), device_id_type=MESH_ID
            )

        ends = jnp.where(self.z > 0, 1, 0) + jnp.where(self.z < self.z_count - 1, 1, 0)
        pl.semaphore_wait(barrier, len(partners) + ends)

    def far_first(self, step):
        last = self.z_count - 1
        low = jnp.where(step < last - self.z, last - step, step - (last - self.z))
        high = jnp.where(step < self.z, step, last - (step - self.z))
        return jnp.where(self.z * 2 < self.z_count, low, high)


def send(src, dst, send_sem, recv_sem, device):
    copy = pltpu.make_async_remote_copy(
        src_ref=src, dst_ref=dst, send_sem=send_sem, recv_sem=recv_sem, device_id=device, device_id_type=MESH_ID
    )
    copy.start()
    return copy


def add_rows(total, part, rows, step=16):
    def chunk(i, carry):
        here = pl.ds(pl.multiple_of(i * step, step), step)
        total[here] = total[here] + part[here]
        return carry

    lax.fori_loop(0, rows // step, chunk, 0)


class Spread:
    ZU, ZD, XF, YF, XH, YH, CO, CX, CY, CA, CB = range(11)

    def __init__(self, place, src, whole, sent, got, kept):
        self.place, self.src, self.whole, self.sent, self.got = place, src, whole, sent, got
        half = src.shape[0] // 2
        self.low, self.high = pl.ds(0, half), pl.ds(half, half)
        z, x, c, y = place.z, place.x, place.c, place.y
        self.up, self.down = place.device(z=z + 1), place.device(z=z - 1)
        self.over_x, self.over_y = place.device(x=1 - x), place.device(y=1 - y)
        self.over_c = place.device(c=1 - c)
        self.keep = pltpu.make_async_copy(src, whole.at[z, x, c, y], kept)

    def push(self, kind, zz, xx, yy, rows, device, origin=None):
        ref = self.whole.at[zz, xx, self.place.c, yy, rows]
        send(
            ref if origin is None else origin,
            ref,
            self.sent.at[kind, zz],
            self.got.at[kind, zz],
            device,
        )

    def arrival(self, kind, zz, xx, yy, rows=slice(None), sibling=False):
        cc = 1 - self.place.c if sibling else self.place.c
        ref = self.whole.at[zz, xx, cc, yy, rows]
        pltpu.make_async_copy(ref, ref, self.got.at[kind, zz]).wait()

    def departure(self, kind, zz, xx, yy, rows=slice(None)):
        ref = self.whole.at[zz, xx, self.place.c, yy, rows]
        pltpu.make_async_copy(ref, ref, self.sent.at[kind, zz]).wait()

    def spread_own(self, zz, origin=None):
        x, y, every = self.place.x, self.place.y, slice(None)
        self.push(self.XF, zz, x, y, every, self.over_x, origin)
        self.push(self.YF, zz, x, y, every, self.over_y, origin)
        self.push(self.CO, zz, x, y, every, self.over_c, origin)

    def begin(self):
        z, x, y, nz = self.place.z, self.place.x, self.place.y, self.place.z_count

        @pl.when(z < nz - 1)
        def _():
            self.push(self.ZU, z, x, y, slice(None), self.up, self.src)

        @pl.when(z > 0)
        def _():
            self.push(self.ZD, z, x, y, slice(None), self.down, self.src)

        self.spread_own(z, self.src)
        self.keep.start()

    def along_z(self, d):
        z, x, y, nz = self.place.z, self.place.x, self.place.y, self.place.z_count
        below, above = z - d, z + d

        @pl.when(below >= 0)
        def _():
            self.arrival(self.ZU, below, x, y)

            @pl.when(z < nz - 1)
            def _():
                self.push(self.ZU, below, x, y, slice(None), self.up)

            self.spread_own(below)

        @pl.when(above < nz)
        def _():
            self.arrival(self.ZD, above, x, y)

            @pl.when(z > 0)
            def _():
                self.push(self.ZD, above, x, y, slice(None), self.down)

            self.spread_own(above)

    def relay(self, zz):
        x, y, every = self.place.x, self.place.y, slice(None)
        self.arrival(self.XF, zz, 1 - x, y)
        self.push(self.YH, zz, 1 - x, y, self.low, self.over_y)
        self.push(self.CX, zz, 1 - x, y, every, self.over_c)
        self.arrival(self.YF, zz, x, 1 - y)
        self.push(self.XH, zz, x, 1 - y, self.high, self.over_x)
        self.push(self.CY, zz, x, 1 - y, every, self.over_c)

    def diagonal(self, zz):
        x, y = self.place.x, self.place.y
        self.arrival(self.XH, zz, 1 - x, 1 - y, self.high)
        self.push(self.CB, zz, 1 - x, 1 - y, self.high, self.over_c)
        self.arrival(self.YH, zz, 1 - x, 1 - y, self.low)
        self.push(self.CA, zz, 1 - x, 1 - y, self.low, self.over_c)

    def sibling_near(self, zz):
        x, y = self.place.x, self.place.y
        self.arrival(self.CO, zz, x, y, sibling=True)
        self.arrival(self.CY, zz, x, 1 - y, sibling=True)

    def sibling_far(self, zz):
        x, y = self.place.x, self.place.y
        self.arrival(self.CX, zz, 1 - x, y, sibling=True)
        self.arrival(self.CA, zz, 1 - x, 1 - y, self.low, sibling=True)
        self.arrival(self.CB, zz, 1 - x, 1 - y, self.high, sibling=True)

    def finish(self):
        z, x, y, nz = self.place.z, self.place.x, self.place.y, self.place.z_count

        def one(zz, carry):
            self.departure(self.XF, zz, x, y)
            self.departure(self.YF, zz, x, y)
            self.departure(self.CO, zz, x, y)
            self.departure(self.CX, zz, 1 - x, y)
            self.departure(self.CY, zz, x, 1 - y)
            self.departure(self.YH, zz, 1 - x, y, self.low)
            self.departure(self.XH, zz, x, 1 - y, self.high)
            self.departure(self.CA, zz, 1 - x, 1 - y, self.low)
            self.departure(self.CB, zz, 1 - x, 1 - y, self.high)

            @pl.when((zz <= z) & (z < nz - 1))
            def _():
                self.departure(self.ZU, zz, x, y)

            @pl.when((zz >= z) & (z > 0))
            def _():
                self.departure(self.ZD, zz, x, y)

            return carry

        lax.fori_loop(0, nz, one, 0)


def scatter_kernel(parts, out, total, from_c, half_x, half_y, full_x, full_y, up_buf, down_buf, sent, got, loaded):
    place = Place()
    z, x, c, y, nz = place.z, place.x, place.c, place.y, place.z_count
    rows = total.shape[3]
    half = rows // 2
    CD, CX, CY, CO, XH, YH, XF, YF, ZU, ZD = range(10)
    over_x, over_y, over_c = place.device(x=1 - x), place.device(y=1 - y), place.device(c=1 - c)
    place.meet()

    def spot(kind):
        return {CD: (1, 1), CX: (1, 0), CY: (0, 1), CO: (0, 0)}[kind]

    for kind in (CD, CX, CY, CO):
        dx, dy = spot(kind)
        for i in range(nz):
            zz = place.far_first(i)
            xx, yy = (1 - x if dx else x), (1 - y if dy else y)
            send(parts.at[zz, xx, 1 - c, yy], from_c.at[dx, dy, zz], sent.at[kind, zz], got.at[kind, zz], over_c)
            pltpu.make_async_copy(parts.at[zz, xx, c, yy], total.at[dx, dy, zz], loaded.at[kind, zz]).start()

    def arrival(kind, zz, ref):
        pltpu.make_async_copy(ref, ref, got.at[kind, zz]).wait()

    def join_cores(kind, zz):
        dx, dy = spot(kind)
        here, there = total.at[dx, dy, zz], from_c.at[dx, dy, zz]
        pltpu.make_async_copy(here, here, loaded.at[kind, zz]).wait()
        arrival(kind, zz, there)
        add_rows(here, there, rows)

    low, high = pl.ds(0, half), pl.ds(half, half)
    for i in range(nz):
        zz = place.far_first(i)
        join_cores(CD, zz)
        send(total.at[1, 1, zz, low], half_x.at[zz], sent.at[XH, zz], got.at[XH, zz], over_x)
        send(total.at[1, 1, zz, high], half_y.at[zz], sent.at[YH, zz], got.at[YH, zz], over_y)
    for i in range(nz):
        zz = place.far_first(i)
        join_cores(CX, zz)
        join_cores(CY, zz)
        arrival(XH, zz, half_x.at[zz])
        add_rows(total.at[0, 1, zz, low], half_x.at[zz], half)
        send(total.at[0, 1, zz], full_y.at[zz], sent.at[YF, zz], got.at[YF, zz], over_y)
        arrival(YH, zz, half_y.at[zz])
        add_rows(total.at[1, 0, zz, high], half_y.at[zz], half)
        send(total.at[1, 0, zz], full_x.at[zz], sent.at[XF, zz], got.at[XF, zz], over_x)
    for i in range(nz):
        zz = place.far_first(i)
        mine = total.at[0, 0, zz]
        join_cores(CO, zz)
        arrival(XF, zz, full_x.at[zz])
        add_rows(mine, full_x.at[zz], rows)
        arrival(YF, zz, full_y.at[zz])
        add_rows(mine, full_y.at[zz], rows)

        @pl.when((z > 0) & (zz >= z))
        def _():
            arrival(ZU, zz, up_buf.at[zz])
            add_rows(mine, up_buf.at[zz], rows)

        @pl.when((z < nz - 1) & (zz <= z))
        def _():
            arrival(ZD, zz, down_buf.at[zz])
            add_rows(mine, down_buf.at[zz], rows)

        @pl.when(zz > z)
        def _():
            send(mine, up_buf.at[zz], sent.at[ZU, zz], got.at[ZU, zz], place.device(z=z + 1))

        @pl.when(zz < z)
        def _():
            send(mine, down_buf.at[zz], sent.at[ZD, zz], got.at[ZD, zz], place.device(z=z - 1))

    out[...] = total[0, 0, z]

    def departure(kind, zz, ref):
        pltpu.make_async_copy(ref, ref, sent.at[kind, zz]).wait()

    for zz in range(nz):
        for kind in (CD, CX, CY, CO):
            departure(kind, zz, total.at[0, 0, zz])
        departure(XH, zz, half_x.at[zz])
        departure(YH, zz, half_y.at[zz])
        departure(XF, zz, full_x.at[zz])
        departure(YF, zz, full_y.at[zz])

        @pl.when(zz > z)
        def _():
            departure(ZU, zz, up_buf.at[zz])

        @pl.when(zz < z)
        def _():
            departure(ZD, zz, down_buf.at[zz])


def scatter_sum(parts, collective):
    nz, _, _, _, rows, cols = parts.shape
    dt = parts.dtype
    return pl.pallas_call(
        scatter_kernel,
        out_shape=jax.ShapeDtypeStruct((rows, cols), dt),
        in_specs=[ANYWHERE],
        out_specs=IN_VMEM,
        scratch_shapes=[
            pltpu.VMEM((2, 2, nz, rows, cols), dt),
            pltpu.VMEM((2, 2, nz, rows, cols), dt),
            pltpu.VMEM((nz, rows // 2, cols), dt),
            pltpu.VMEM((nz, rows // 2, cols), dt),
            pltpu.VMEM((nz, rows, cols), dt),
            pltpu.VMEM((nz, rows, cols), dt),
            pltpu.VMEM((nz, rows, cols), dt),
            pltpu.VMEM((nz, rows, cols), dt),
            pltpu.SemaphoreType.DMA((10, nz)),
            pltpu.SemaphoreType.DMA((10, nz)),
            pltpu.SemaphoreType.DMA((4, nz)),
        ],
        cost_estimate=LINK_TIME,
        compiler_params=pltpu.CompilerParams(
            collective_id=collective, has_side_effects=True, vmem_limit_bytes=58 << 20
        ),
    )(parts)


def swap_kernel(src, out, sent, got):
    dp, y = lax.axis_index("dp"), lax.axis_index("tensor")
    other = (dp, 1 - y)
    barrier = pltpu.get_barrier_semaphore()
    pl.semaphore_signal(barrier, inc=1, device_id=other, device_id_type=MESH_ID)
    pl.semaphore_wait(barrier, 1)
    send(src, out, sent, got, other).wait()


def swap_tensor(block, collective):
    return pl.pallas_call(
        swap_kernel,
        out_shape=jax.ShapeDtypeStruct(block.shape, block.dtype),
        in_specs=[ANYWHERE],
        out_specs=ANYWHERE,
        scratch_shapes=[pltpu.SemaphoreType.DMA, pltpu.SemaphoreType.DMA],
        compiler_params=pltpu.CompilerParams(collective_id=collective, has_side_effects=True),
    )(block)


def both_rows(block, collective):
    other = swap_tensor(block, collective)
    first = lax.axis_index("tensor") == 0
    return jnp.concatenate([jnp.where(first, block, other), jnp.where(first, other, block)], axis=0)


def own_rows_sum(part, collective):
    rows = part.shape[0] // 2
    index = lax.axis_index("tensor")
    other = lax.dynamic_slice_in_dim(part, (1 - index) * rows, rows, 0).astype(jnp.bfloat16)
    mine = lax.dynamic_slice_in_dim(part, index * rows, rows, 0)
    return mine + swap_tensor(other, collective).astype(jnp.float32)


def plane_gather_kernel(count, *refs):
    srcs, outs = refs[:count], refs[count : 2 * count]
    sent, got, kept = refs[2 * count :]
    place = Place()
    z, x, c, nz = place.z, place.x, place.c, place.z_count
    ZU, ZD, XF, CO, CX = range(5)
    up, down = place.device(z=z + 1), place.device(z=z - 1)
    over_x, over_c = place.device(x=1 - x), place.device(c=1 - c)
    place.meet(use_y=False)
    every = range(count)

    def push(a, kind, zz, xx, device, own=False):
        ref = outs[a].at[zz, xx, c]
        send(srcs[a] if own else ref, ref, sent.at[kind, a, zz], got.at[kind, a, zz], device)

    def arrival(a, kind, zz, xx, cc):
        ref = outs[a].at[zz, xx, cc]
        pltpu.make_async_copy(ref, ref, got.at[kind, a, zz]).wait()

    def departure(a, kind, zz, xx):
        ref = outs[a].at[zz, xx, c]
        pltpu.make_async_copy(ref, ref, sent.at[kind, a, zz]).wait()

    keeps = []
    for a in every:
        push(a, XF, z, x, over_x, own=True)

        @pl.when(z < nz - 1)
        def _():
            push(a, ZU, z, x, up, own=True)

        @pl.when(z > 0)
        def _():
            push(a, ZD, z, x, down, own=True)

        push(a, CO, z, x, over_c, own=True)
        keep = pltpu.make_async_copy(srcs[a], outs[a].at[z, x, c], kept.at[a])
        keep.start()
        keeps.append(keep)

    def relay(a, zz):
        arrival(a, XF, zz, 1 - x, c)
        push(a, CX, zz, 1 - x, over_c)

    for d in range(nz):
        below, above = z - d - 1, z + d + 1
        for a in every:
            if d < nz - 1:
                @pl.when(below >= 0)
                def _():
                    arrival(a, ZU, below, x, c)

                    @pl.when(z < nz - 1)
                    def _():
                        push(a, ZU, below, x, up)

                    push(a, XF, below, x, over_x)
                    push(a, CO, below, x, over_c)

                @pl.when(above < nz)
                def _():
                    arrival(a, ZD, above, x, c)

                    @pl.when(z > 0)
                    def _():
                        push(a, ZD, above, x, down)

                    push(a, XF, above, x, over_x)
                    push(a, CO, above, x, over_c)

    for d in range(nz):
        for a in every:
            if d == 0:
                relay(a, z)
            else:
                @pl.when(z - d >= 0)
                def _():
                    relay(a, z - d)

                @pl.when(z + d < nz)
                def _():
                    relay(a, z + d)

    for a in every:
        keeps[a].wait()
        for zz in range(nz):
            arrival(a, CO, zz, x, 1 - c)
            arrival(a, CX, zz, 1 - x, 1 - c)
            departure(a, XF, zz, x)
            departure(a, CO, zz, x)
            departure(a, CX, zz, 1 - x)

            @pl.when((zz <= z) & (z < nz - 1))
            def _():
                departure(a, ZU, zz, x)

            @pl.when((zz >= z) & (z > 0))
            def _():
                departure(a, ZD, zz, x)


def gather_in_plane(shards, collective):
    nz = lax.axis_size("dp") // 4
    count = len(shards)
    return pl.pallas_call(
        functools.partial(plane_gather_kernel, count),
        out_shape=[jax.ShapeDtypeStruct((nz, 2, 2) + s.shape, s.dtype) for s in shards],
        in_specs=[ANYWHERE] * count,
        out_specs=[ANYWHERE] * count,
        scratch_shapes=[
            pltpu.SemaphoreType.DMA((5, count, nz)),
            pltpu.SemaphoreType.DMA((5, count, nz)),
            pltpu.SemaphoreType.DMA((count,)),
        ],
        cost_estimate=LINK_TIME,
        compiler_params=pltpu.CompilerParams(collective_id=collective, has_side_effects=True),
    )(*shards)


def plane_scatter_kernel(count, *refs):
    parts, small = refs[:count], refs[count]
    outs, small_out = refs[count + 1 : 2 * count + 1], refs[2 * count + 1]
    (
        total,
        from_c,
        full_x,
        up_buf,
        down_buf,
        small_sum,
        small_got,
        sent,
        got,
        loaded,
        small_sems,
    ) = refs[2 * count + 2 :]
    place = Place()
    z, x, c, nz = place.z, place.x, place.c, place.z_count
    rows = total.shape[3]
    C0, C1, XF, ZU, ZD = range(5)
    over_x, over_c = place.device(x=1 - x), place.device(c=1 - c)
    place.meet(all_z=True)

    def arrival(a, kind, zz, ref):
        pltpu.make_async_copy(ref, ref, got.at[kind, a, zz]).wait()

    for dx, kind in ((1, C1), (0, C0)):
        for i in range(nz):
            zz = place.far_first(i)
            xx = 1 - x if dx else x
            for a in range(count):
                send(parts[a].at[zz, xx, 1 - c], from_c.at[dx, zz, a], sent.at[kind, a, zz], got.at[kind, a, zz], over_c)
                pltpu.make_async_copy(parts[a].at[zz, xx, c], total.at[dx, zz, a], loaded.at[dx, a, zz]).start()

    def join_cores(a, dx, zz):
        here, there = total.at[dx, zz, a], from_c.at[dx, zz, a]
        pltpu.make_async_copy(here, here, loaded.at[dx, a, zz]).wait()
        arrival(a, C1 if dx else C0, zz, there)
        add_rows(here, there, rows)

    small_sum[0] = small[...]

    def small_step(i):
        if i < 3:
            partner = (over_c, place.device(y=1 - place.y), over_x)[i]
            copy = send(small_sum.at[i], small_got.at[i], small_sems.at[0, i], small_sems.at[1, i], partner)
            copy.wait()
            small_sum[i + 1] = small_sum[i] + small_got[i]
            return
        copies = [
            send(
                small_sum.at[3],
                small_got.at[2 + d],
                small_sems.at[0, 2 + d],
                small_sems.at[1, 2 + d],
                place.device(z=(z + d) % nz),
            )
            for d in range(1, nz)
        ]
        for copy in copies:
            copy.wait()
        result = jnp.zeros_like(small_out)
        for zz in range(nz):
            away = (z - zz) % nz
            result = result + jnp.where(away == 0, small_sum[3], small_got[jnp.maximum(2 + away, 3)])
        small_out[...] = result

    for i in range(nz):
        zz = place.far_first(i)
        small_step(min(i, 3))
        for a in range(count):
            join_cores(a, 1, zz)
            send(total.at[1, zz, a], full_x.at[zz, a], sent.at[XF, a, zz], got.at[XF, a, zz], over_x)
    for i in range(nz):
        zz = place.far_first(i)
        for a in range(count):
            mine = total.at[0, zz, a]
            join_cores(a, 0, zz)
            arrival(a, XF, zz, full_x.at[zz, a])
            add_rows(mine, full_x.at[zz, a], rows)

            @pl.when((z > 0) & (zz >= z))
            def _():
                arrival(a, ZU, zz, up_buf.at[zz, a])
                add_rows(mine, up_buf.at[zz, a], rows)

            @pl.when((z < nz - 1) & (zz <= z))
            def _():
                arrival(a, ZD, zz, down_buf.at[zz, a])
                add_rows(mine, down_buf.at[zz, a], rows)

            @pl.when(zz > z)
            def _():
                send(mine, up_buf.at[zz, a], sent.at[ZU, a, zz], got.at[ZU, a, zz], place.device(z=z + 1))

            @pl.when(zz < z)
            def _():
                send(mine, down_buf.at[zz, a], sent.at[ZD, a, zz], got.at[ZD, a, zz], place.device(z=z - 1))

    for a in range(count):

        def widen(i, carry):
            here = pl.ds(pl.multiple_of(i * 16, 16), 16)
            outs[a][here] = total[0, z, a, here].astype(jnp.float32)
            return carry

        lax.fori_loop(0, rows // 16, widen, 0)

    def departure(a, kind, zz, ref):
        pltpu.make_async_copy(ref, ref, sent.at[kind, a, zz]).wait()

    for a in range(count):
        for zz in range(nz):
            departure(a, C0, zz, total.at[0, 0, a])
            departure(a, C1, zz, total.at[0, 0, a])
            departure(a, XF, zz, total.at[0, 0, a])

            @pl.when(zz > z)
            def _():
                departure(a, ZU, zz, total.at[0, 0, a])

            @pl.when(zz < z)
            def _():
                departure(a, ZD, zz, total.at[0, 0, a])


def scatter_in_plane(parts, small, collective):
    nz, _, _, rows, cols = parts[0].shape
    count = len(parts)
    dt = parts[0].dtype
    return pl.pallas_call(
        functools.partial(plane_scatter_kernel, count),
        out_shape=[jax.ShapeDtypeStruct((rows, cols), jnp.float32)] * count
        + [jax.ShapeDtypeStruct(small.shape, small.dtype)],
        in_specs=[ANYWHERE] * count + [IN_VMEM],
        out_specs=[IN_VMEM] * (count + 1),
        scratch_shapes=[
            pltpu.VMEM((2, nz, count, rows, cols), dt),
            pltpu.VMEM((2, nz, count, rows, cols), dt),
            pltpu.VMEM((nz, count, rows, cols), dt),
            pltpu.VMEM((nz, count, rows, cols), dt),
            pltpu.VMEM((nz, count, rows, cols), dt),
            pltpu.VMEM((4,) + small.shape, small.dtype),
            pltpu.VMEM((2 + nz,) + small.shape, small.dtype),
            pltpu.SemaphoreType.DMA((5, count, nz)),
            pltpu.SemaphoreType.DMA((5, count, nz)),
            pltpu.SemaphoreType.DMA((2, count, nz)),
            pltpu.SemaphoreType.DMA((2, 2 + nz)),
        ],
        cost_estimate=LINK_TIME,
        compiler_params=pltpu.CompilerParams(
            collective_id=collective, has_side_effects=True, vmem_limit_bytes=58 << 20
        ),
    )(*parts, small)


def dot_nn(a, b):
    return lax.dot_general(a, b, (((1,), (0,)), ((), ())), preferred_element_type=jnp.float32)


def dot_nt(a, b):
    return lax.dot_general(a, b, (((1,), (1,)), ((), ())), preferred_element_type=jnp.float32)


def dot_tn(a, b):
    return lax.dot_general(a, b, (((0,), (0,)), ((), ())), preferred_element_type=jnp.float32)


def pick(table, index):
    return sum(jnp.where(index == i, value, 0) for i, value in enumerate(table))


def expert_kernel(
    z_count,
    src,
    g_all,
    hot_ref,
    router_ref,
    lanes_ref,
    wg_ref,
    wu_ref,
    wd_ref,
    x_all,
    y_all,
    r_all,
    hidden_all,
    gate_pre_grad_all,
    up_grad_all,
    x_tile,
    g_tile,
    y_tile,
    r_tile,
    hidden_tile,
    gate_pre_grad_tile,
    up_grad_tile,
    load_sems,
    store_sems,
    sent,
    got,
    kept,
):
    place = Place()
    place.meet()
    spread = Spread(place, src, x_all, sent, got, kept)
    spread.begin()
    width = src.shape[1]
    tile = x_tile.shape[1]
    pairs = sorted(
        ((k, dx) for k in range(z_count) for dx in (0, 1)), key=lambda p: p[0] + 1.3 * p[1]
    )
    tiles = 2 * len(pairs)
    near_table, across_table = [p[0] for p in pairs], [p[1] for p in pairs]

    def near(k):
        return place.far_first(z_count - 1 - k)

    def tile_at(i):
        pair, second = i // 2, i % 2
        zz = near(pick(near_table, pair))
        xx = jnp.where(pick(across_table, pair) == 1, 1 - place.x, place.x)
        cc = jnp.where(second == 1, 1 - place.c, place.c)
        return zz, xx, cc

    stores = (
        (y_tile, y_all),
        (r_tile, r_all),
        (hidden_tile, hidden_all),
        (gate_pre_grad_tile, gate_pre_grad_all),
        (up_grad_tile, up_grad_all),
    )

    def loads(i, slot):
        zz, xx, cc = tile_at(i)
        copies = []
        for yy in range(2):
            rows = pl.ds(yy * (tile // 2), tile // 2)
            copies.append(
                pltpu.make_async_copy(
                    x_all.at[zz, xx, cc, yy], x_tile.at[slot, rows], load_sems.at[slot, yy]
                )
            )
        copies.append(
            pltpu.make_async_copy(g_all.at[zz, xx, cc], g_tile.at[slot], load_sems.at[slot, 2])
        )
        return copies

    def store(i, slot):
        zz, xx, cc = tile_at(i)
        return [
            pltpu.make_async_copy(here.at[slot], there.at[zz, xx, cc], store_sems.at[slot, n])
            for n, (here, there) in enumerate(stores)
        ]

    z_done, steps = 0, {}
    for position, (k, dx) in enumerate(pairs):
        todo = []
        if dx == 0:
            todo.append(("relay", k))
            while z_done < min(k + 1, z_count - 1):
                z_done += 1
                todo.insert(0, ("z", z_done))
        else:
            todo.append(("diagonal", k))
        steps[2 * position] = todo

    def prepare(i):
        for position in range(tiles):
            pair = position // 2
            k, dx = pairs[pair]

            @pl.when(i == position)
            def _():
                if position % 2 == 0:
                    for kind, number in steps[position]:
                        if kind == "z":
                            spread.along_z(number)
                        elif kind == "relay":
                            spread.relay(near(number))
                        else:
                            spread.diagonal(near(number))
                    if position == 0:
                        spread.keep.wait()
                elif dx == 0:
                    spread.sibling_near(near(k))
                else:
                    spread.sibling_far(near(k))

        for copy in loads(i, i % 2):
            copy.start()

    def compute(i, carry):
        slot = i % 2
        for copy in loads(i, slot):
            copy.wait()

        @pl.when(i >= 2)
        def _():
            for copy in store(i - 2, slot):
                copy.wait()

        zz, xx, cc = tile_at(i)
        first_row = pl.multiple_of(((zz * 2 + xx) * 2 + cc) * tile, tile)
        rows = x_tile[slot]
        logits = jnp.where(lanes_ref[1:2] > 0.0, dot_nn(rows, router_ref[...]), -1e30)
        weights = jnp.exp(logits - jnp.max(logits, axis=1, keepdims=True))
        own_weight = jnp.sum(weights * lanes_ref[0:1], axis=1, keepdims=True)
        gate = hot_ref[pl.ds(first_row, tile)] * own_weight / jnp.sum(weights, axis=1, keepdims=True)
        gate_pre = dot_nn(rows, wg_ref[...])
        up_pre = dot_nn(rows, wu_ref[...])
        raw_grad = dot_nt(g_tile[slot], wd_ref[...])

        @pl.when(i < tiles - 1)
        def _():
            prepare(i + 1)

        sigmoid = jax.nn.sigmoid(gate_pre)
        silu = gate_pre * sigmoid
        hidden = silu * up_pre
        gate_grad = jnp.sum(hidden * raw_grad, axis=1, keepdims=True)
        coarse = gate_grad.astype(jnp.bfloat16).astype(jnp.float32)
        r_tile[slot, :, width:] = (
            coarse * lanes_ref[2:3] + (gate_grad - coarse) * lanes_ref[3:4]
        ).astype(jnp.bfloat16)
        hidden_gated = (gate * hidden).astype(jnp.bfloat16)
        hidden_tile[slot] = hidden_gated
        hidden_grad = gate * raw_grad
        up_grad = (hidden_grad * silu).astype(jnp.bfloat16)
        up_grad_tile[slot] = up_grad
        gate_pre_grad = (
            hidden_grad * up_pre * sigmoid * (1.0 + gate_pre * (1.0 - sigmoid))
        ).astype(jnp.bfloat16)
        gate_pre_grad_tile[slot] = gate_pre_grad
        y_tile[slot] = dot_nn(hidden_gated, wd_ref[...]).astype(jnp.bfloat16)
        r_tile[slot, :, :width] = (
            dot_nt(gate_pre_grad, wg_ref[...]) + dot_nt(up_grad, wu_ref[...])
        ).astype(jnp.bfloat16)
        for copy in store(i, slot):
            copy.start()
        return carry

    prepare(0)
    lax.fori_loop(0, tiles, compute, 0)
    for i in (tiles - 2, tiles - 1):
        for copy in store(i, i % 2):
            copy.wait()
    spread.finish()


def expert_pass(block, upstream, hot, router, lanes, w_gate, w_up, w_down, collective):
    rows, width = block.shape
    units = w_gate.shape[1]
    nz = lax.axis_size("dp") // 4
    tile = 2 * rows
    out = (nz, 2, 2, tile)
    return pl.pallas_call(
        functools.partial(expert_kernel, nz),
        in_specs=[ANYWHERE] * 2 + [IN_VMEM] * 6,
        out_specs=[ANYWHERE] * 6,
        out_shape=[
            jax.ShapeDtypeStruct((nz, 2, 2, 2, rows, width), jnp.bfloat16),
            jax.ShapeDtypeStruct(out + (width,), jnp.bfloat16),
            jax.ShapeDtypeStruct(out + (width + LANES,), jnp.bfloat16),
        ]
        + [jax.ShapeDtypeStruct(out + (units,), jnp.bfloat16)] * 3,
        scratch_shapes=[
            pltpu.VMEM((2, tile, width), jnp.bfloat16),
            pltpu.VMEM((2, tile, width), jnp.bfloat16),
            pltpu.VMEM((2, tile, width), jnp.bfloat16),
            pltpu.VMEM((2, tile, width + LANES), jnp.bfloat16),
            pltpu.VMEM((2, tile, units), jnp.bfloat16),
            pltpu.VMEM((2, tile, units), jnp.bfloat16),
            pltpu.VMEM((2, tile, units), jnp.bfloat16),
            pltpu.SemaphoreType.DMA((2, 3)),
            pltpu.SemaphoreType.DMA((2, 5)),
            pltpu.SemaphoreType.DMA((11, nz)),
            pltpu.SemaphoreType.DMA((11, nz)),
            pltpu.SemaphoreType.DMA,
        ],
        cost_estimate=LINK_TIME,
        compiler_params=pltpu.CompilerParams(
            collective_id=collective, has_side_effects=True, vmem_limit_bytes=60 << 20
        ),
    )(block, upstream.reshape(out + (width,)), hot, router, lanes, w_gate, w_up, w_down)


def expert_weights_kernel(
    x_ref, g_ref, hidden_ref, gate_pre_grad_ref, up_grad_ref, wg_grad_ref, wu_grad_ref, wd_grad_ref
):
    @pl.when(pl.program_id(0) == 0)
    def _():
        wg_grad_ref[...] = jnp.zeros_like(wg_grad_ref)
        wu_grad_ref[...] = jnp.zeros_like(wu_grad_ref)
        wd_grad_ref[...] = jnp.zeros_like(wd_grad_ref)

    rows = x_ref[...]
    wg_grad_ref[...] += dot_tn(rows, gate_pre_grad_ref[...])
    wu_grad_ref[...] += dot_tn(rows, up_grad_ref[...])
    wd_grad_ref[...] += dot_tn(hidden_ref[...], g_ref[...])


def expert_weights_pass(rows, upstream, hidden, gate_pre_grad, up_grad):
    count, width = rows.shape
    units = hidden.shape[1]
    tile = 512 if count % 512 == 0 else GROUP // 2

    def by_row(cols):
        return pl.BlockSpec((tile, cols), lambda i: (i, 0))

    def whole(first, second):
        return pl.BlockSpec((first, second), lambda i: (0, 0), pipeline_mode=pl.Buffered(1))

    shapes = [(width, units), (width, units), (units, width)]
    return pl.pallas_call(
        expert_weights_kernel,
        grid=(count // tile,),
        in_specs=[by_row(width)] * 2 + [by_row(units)] * 3,
        out_specs=[whole(*shape) for shape in shapes],
        out_shape=[jax.ShapeDtypeStruct(shape, jnp.float32) for shape in shapes],
        cost_estimate=pl.CostEstimate(
            flops=6 * count * width * units,
            bytes_accessed=4 * count * width + 12 * width * units,
            transcendentals=0,
        ),
        compiler_params=pltpu.CompilerParams(vmem_limit_bytes=60 << 20),
    )(rows, upstream, hidden, gate_pre_grad, up_grad)


def dense_body(
    tokens,
    routes,
    cotangent,
    attn_gain,
    q_gain,
    k_gain,
    w_query,
    w_key,
    w_value,
    w_out,
    mlp_gain,
    router,
    w_gate,
    w_up,
    w_down,
):
    rank_index = lax.axis_index("tensor")
    own_rows = tokens.shape[0]
    head_cols = w_query.shape[1]
    local_heads = head_cols // HEAD
    col_start = rank_index * head_cols
    row_start = rank_index * own_rows
    experts = router.shape[1]
    attn_scale = HEAD ** (-0.5)
    head_shape = (GROUP, local_heads, HEAD)
    q_gain_local = lax.dynamic_slice_in_dim(q_gain, col_start, head_cols)
    k_gain_local = lax.dynamic_slice_in_dim(k_gain, col_start, head_cols)
    inputs = tokens.astype(jnp.float32)
    attn_inv = lax.rsqrt(jnp.mean(inputs * inputs, axis=1, keepdims=True) + EPSILON)
    normed = both_rows((inputs * attn_inv * attn_gain).astype(jnp.bfloat16), 5)
    q_all, k_all, v_all, o_all, routes_all = gather_in_plane(
        (w_query, w_key, w_value, w_out, routes), 1
    )
    q_all, k_all, v_all = (w.reshape(D, head_cols) for w in (q_all, k_all, v_all))
    o_all = jnp.transpose(o_all.reshape(-1, *w_out.shape), (1, 0, 2)).reshape(head_cols, D)
    routes_all = routes_all.reshape(-1, TOPK)
    own_expert = lax.axis_index("dp")
    hot = jnp.any(routes_all == own_expert, axis=1, keepdims=True).astype(jnp.float32)
    lane = jnp.arange(LANES)
    marked = own_expert + experts * rank_index
    lanes = jnp.stack(
        [lane == own_expert, lane < experts, lane == marked, lane == marked + 2 * experts]
        + [lane < 0] * 4
    ).astype(jnp.float32)
    router_wide = jnp.pad(router, ((0, 0), (0, LANES - experts)))
    upstream_all = lax.all_gather(cotangent, EVERY, axis=0, tiled=True)
    queries = matmul(normed, q_all)
    keys_raw = matmul(normed, k_all)
    values_raw = matmul(normed, v_all)
    query_sq, key_sq = tensor_total(
        (jnp.sum(queries * queries, axis=1), jnp.sum(keys_raw * keys_raw, axis=1))
    )
    query_inv = lax.rsqrt(query_sq / D + EPSILON)[:, None]
    key_inv = lax.rsqrt(key_sq / D + EPSILON)[:, None]
    cosine_table, sine_table = rope_tables()
    query_rot = rotate(
        (queries * query_inv * q_gain_local).reshape(head_shape), cosine_table, sine_table
    ).astype(jnp.bfloat16)
    key_rot = rotate(
        (keys_raw * key_inv * k_gain_local).reshape(head_shape), cosine_table, sine_table
    ).astype(jnp.bfloat16)
    value_heads = values_raw.astype(jnp.bfloat16).reshape(head_shape)
    visible = visible_keys()[None]

    def masked_scores():
        raw_scores = (
            jnp.einsum("qhd,khd->hqk", query_rot, key_rot, preferred_element_type=jnp.float32)
            * attn_scale
        )
        return jnp.where(visible, raw_scores, -1e30)

    scores = masked_scores()
    row_max = jnp.max(scores, axis=2, keepdims=True)
    exponent = jnp.exp(scores - row_max)
    row_total = jnp.sum(exponent, axis=2, keepdims=True)
    log_total = row_max + jnp.log(row_total)
    mixed_heads = jnp.einsum(
        "hqk,khd->qhd",
        (exponent / row_total).astype(jnp.bfloat16),
        value_heads,
        preferred_element_type=jnp.float32,
    )
    mixed_heads = mixed_heads.reshape(GROUP, head_cols).astype(jnp.bfloat16)
    attended = own_rows_sum(matmul(mixed_heads, o_all), 6)
    hidden_one = inputs + attended
    mlp_inv = lax.rsqrt(jnp.mean(hidden_one * hidden_one, axis=1, keepdims=True) + EPSILON)
    normed_two = (hidden_one * mlp_inv * mlp_gain).astype(jnp.bfloat16)
    own_routes = lax.dynamic_slice_in_dim(routes, row_start, own_rows, 0)
    expert_ids = jnp.arange(experts, dtype=jnp.int32)
    own_hot = jnp.any(own_routes[:, :, None] == expert_ids[None, None, :], axis=1)
    own_probs = jax.nn.softmax(matmul(normed_two, router), axis=1)
    rows_all, y_part, r_part, *for_weights = expert_pass(
        normed_two, upstream_all, hot, router_wide, lanes, w_gate[0], w_up[0], w_down[0], 2
    )
    rows_all, y_part = rows_all.reshape(-1, D), y_part.reshape(-1, D)
    for_weights = [array.reshape(rows_all.shape[0], -1) for array in for_weights]
    blocks = (lax.axis_size("dp") // 4, 2, 2, 2, own_rows)
    returned = scatter_sum(r_part.reshape(*blocks, D + LANES), 3)
    y_part, returned, for_weights = lax.optimization_barrier((y_part, returned, for_weights))
    gate_weight_grad, up_weight_grad, down_weight_grad = expert_weights_pass(
        rows_all, upstream_all, *for_weights
    )
    mixture = lax.psum_scatter(y_part, EVERY, scatter_dimension=0, tiled=True)
    expert_grad = jnp.sum(
        returned[:, D : D + 4 * experts].astype(jnp.float32).reshape(own_rows, 4, experts), axis=1
    )
    expert_grad = jnp.where(own_hot, expert_grad, 0.0)
    returned = returned[:, :D]
    upstream = cotangent.astype(jnp.float32)
    logit_grad = own_probs * (expert_grad - jnp.sum(expert_grad * own_probs, axis=1, keepdims=True))
    router_grad = jnp.dot(normed_two.astype(jnp.float32).T, logit_grad, precision=HIGHEST)
    normed_two_grad = returned.astype(jnp.float32) + jnp.dot(
        logit_grad, router.astype(jnp.float32).T, precision=HIGHEST
    )
    scaled_grad = normed_two_grad * mlp_gain
    hidden_one_grad = (
        upstream
        + mlp_inv * scaled_grad
        - hidden_one * mlp_inv**3 * jnp.mean(hidden_one * scaled_grad, axis=1, keepdims=True)
    )
    mlp_gain_grad = jnp.sum(normed_two_grad * hidden_one * mlp_inv, axis=0)
    attended_grad = both_rows(hidden_one_grad.astype(jnp.bfloat16), 7)
    mixed_grad = jnp.einsum("gd,cd->gc", attended_grad, o_all, preferred_element_type=jnp.float32)
    mixed_grad = mixed_grad.astype(jnp.bfloat16).reshape(head_shape)
    attn_probs = jnp.exp(masked_scores() - log_total)
    prob_grad = jnp.einsum(
        "qhd,khd->hqk", mixed_grad, value_heads, preferred_element_type=jnp.float32
    )
    row_dot = jnp.sum(prob_grad * attn_probs, axis=2, keepdims=True)
    score_grad = (attn_probs * (prob_grad - row_dot)).astype(jnp.bfloat16)
    query_rot_grad = (
        jnp.einsum("hqk,khd->qhd", score_grad, key_rot, preferred_element_type=jnp.float32)
        * attn_scale
    )
    key_rot_grad = (
        jnp.einsum("hqk,qhd->khd", score_grad, query_rot, preferred_element_type=jnp.float32)
        * attn_scale
    )
    value_grad = (
        jnp.einsum(
            "hqk,qhd->khd",
            attn_probs.astype(jnp.bfloat16),
            mixed_grad,
            preferred_element_type=jnp.float32,
        )
        .reshape(GROUP, head_cols)
        .astype(jnp.bfloat16)
    )
    query_norm_grad = unrotate(query_rot_grad, cosine_table, sine_table).reshape(GROUP, head_cols)
    key_norm_grad = unrotate(key_rot_grad, cosine_table, sine_table).reshape(GROUP, head_cols)
    query_scaled = query_norm_grad * q_gain_local
    key_scaled = key_norm_grad * k_gain_local
    query_dot, key_dot = tensor_total(
        (jnp.sum(queries * query_scaled, axis=1), jnp.sum(keys_raw * key_scaled, axis=1))
    )
    query_grad = (
        query_inv * query_scaled - queries * query_inv**3 * (query_dot / D)[:, None]
    ).astype(jnp.bfloat16)
    key_grad = (key_inv * key_scaled - keys_raw * key_inv**3 * (key_dot / D)[:, None]).astype(
        jnp.bfloat16
    )
    q_gain_part = jnp.sum(query_norm_grad * queries * query_inv, axis=0)
    k_gain_part = jnp.sum(key_norm_grad * keys_raw * key_inv, axis=0)
    normed_part = (
        jnp.einsum("gc,rc->gr", query_grad, q_all, preferred_element_type=jnp.float32)
        + jnp.einsum("gc,rc->gr", key_grad, k_all, preferred_element_type=jnp.float32)
        + jnp.einsum("gc,rc->gr", value_grad, v_all, preferred_element_type=jnp.float32)
    )
    normed_grad = own_rows_sum(normed_part, 8)
    scaled_input = normed_grad * attn_gain
    tokens_grad = (
        hidden_one_grad
        + attn_inv * scaled_input
        - inputs * attn_inv**3 * jnp.mean(inputs * scaled_input, axis=1, keepdims=True)
    )
    attn_gain_grad = jnp.sum(normed_grad * inputs * attn_inv, axis=0)
    zero_width = jnp.zeros((D,), jnp.float32)
    q_gain_full = lax.dynamic_update_slice_in_dim(zero_width, q_gain_part, col_start, 0)
    k_gain_full = lax.dynamic_update_slice_in_dim(zero_width, k_gain_part, col_start, 0)
    small_grads = jnp.concatenate(
        [
            jnp.stack([attn_gain_grad, q_gain_full, k_gain_full, mlp_gain_grad]),
            jnp.zeros((4, D), jnp.float32),
            jnp.transpose(router_grad),
        ],
        axis=0,
    )
    shard = (lax.axis_size("dp") // 4, 2, 2, w_query.shape[0], head_cols)
    products = [
        dot_tn(first, second).astype(jnp.bfloat16).reshape(shard)
        for first, second in (
            (normed, query_grad),
            (normed, key_grad),
            (normed, value_grad),
            (attended_grad, mixed_heads),
        )
    ]
    products, gate_weight_grad = lax.optimization_barrier((products, gate_weight_grad))
    *weight_sums, small_sums = scatter_in_plane(products, small_grads, 4)
    attn_gain_grad, q_gain_grad, k_gain_grad, mlp_gain_grad = (small_sums[i] for i in range(4))
    router_grad = jnp.transpose(small_sums[8:])
    mixture, weight_sums = lax.optimization_barrier((mixture, weight_sums))
    layer_out = (hidden_one + mixture.astype(jnp.float32)).astype(jnp.bfloat16)
    return (
        layer_out,
        tokens_grad,
        attn_gain_grad,
        q_gain_grad,
        k_gain_grad,
        weight_sums[0],
        weight_sums[1],
        weight_sums[2],
        jnp.transpose(weight_sums[3]),
        mlp_gain_grad,
        router_grad,
        gate_weight_grad[None],
        up_weight_grad[None],
        down_weight_grad[None],
    )


def solution(mesh):
    in_specs = (
        P(("dp", "tensor"), None),
        P("dp", None),
        P(("dp", "tensor"), None),
        P(),
        P(),
        P(),
        P("dp", "tensor"),
        P("dp", "tensor"),
        P("dp", "tensor"),
        P("tensor", "dp"),
        P(),
        P(),
        P("dp", None, "tensor"),
        P("dp", None, "tensor"),
        P("dp", "tensor", None),
    )
    out_specs = (
        P(("dp", "tensor"), None),
        P(("dp", "tensor"), None),
        P(),
        P(),
        P(),
        P("dp", "tensor"),
        P("dp", "tensor"),
        P("dp", "tensor"),
        P("tensor", "dp"),
        P(),
        P(),
        P("dp", None, "tensor"),
        P("dp", None, "tensor"),
        P("dp", "tensor", None),
    )
    experts = mesh.shape["dp"]
    body = dense_body if experts <= 2 * TOPK else routed_body
    return jax.shard_map(body, mesh=mesh, in_specs=in_specs, out_specs=out_specs, check_vma=False)
```

```python
import functools

import jax
import jax.numpy as jnp
from jax import lax
from jax.experimental import pallas as pl
from jax.experimental.pallas import tpu as pltpu
from jax.sharding import PartitionSpec as P

D = 2048
HEAD = 128
TOPK = 8
PROMPT = 256
CONT = 64
GROUP = 384


EPSILON = 1e-05
ROPE_BASE = 10000.0
HIGHEST = lax.Precision.HIGHEST


def matmul(first_op, second_op):
    return jnp.dot(first_op, second_op, preferred_element_type=jnp.float32)


def gather_rows(values):
    return lax.all_gather(values, "tensor", axis=0, tiled=True)


def sum_rows(values):
    return lax.psum_scatter(values, "tensor", scatter_dimension=0, tiled=True)


def tensor_total(values):
    return lax.psum((values[0], values[1]), "tensor")


def expert_swap(values):
    return lax.all_to_all(values, "dp", split_axis=0, concat_axis=0, tiled=True)


def sum_slots(values):
    return lax.psum_scatter(values, "tensor", scatter_dimension=1, tiled=True)


def group_positions():
    position = jnp.arange(GROUP, dtype=jnp.int32)
    return jnp.where(position < PROMPT, position, PROMPT + (position - PROMPT) % CONT)


def visible_keys():
    position = jnp.arange(GROUP, dtype=jnp.int32)
    member = jnp.where(position < PROMPT, -1, (position - PROMPT) // CONT)
    causal = position[None, :] <= position[:, None]
    return causal & ((member[None, :] == -1) | (member[None, :] == member[:, None]))


def rope_tables():
    half_head = HEAD // 2
    frequency = ROPE_BASE ** (-2.0 * jnp.arange(half_head, dtype=jnp.float32) / HEAD)
    angles = group_positions().astype(jnp.float32)[:, None] * frequency[None, :]
    angles = jnp.concatenate([angles, angles], axis=1)
    return (jnp.cos(angles), jnp.sin(angles))


def rotate(values, cosine_table, sine_table):
    half_head = HEAD // 2
    turned = jnp.concatenate([-values[..., half_head:], values[..., :half_head]], axis=-1)
    return values * cosine_table[:, None, :] + turned * sine_table[:, None, :]


def unrotate(values, cosine_table, sine_table):
    half_head = HEAD // 2
    scaled = values * sine_table[:, None, :]
    turned = jnp.concatenate([scaled[..., half_head:], -scaled[..., :half_head]], axis=-1)
    return values * cosine_table[:, None, :] + turned


def gate_split(rows_in, hot_table, router):
    gates = jax.nn.softmax(matmul(rows_in, router), axis=1)
    weights = jnp.sum(jnp.where(hot_table, gates[:, None, :], 0.0), axis=2)
    return (gates, weights)


def routed_body(
    tokens,
    routes,
    cotangent,
    attn_gain,
    q_gain,
    k_gain,
    w_query,
    w_key,
    w_value,
    w_out,
    mlp_gain,
    router,
    w_gate,
    w_up,
    w_down,
):
    rank_index = lax.axis_index("tensor")
    tensor_count = lax.axis_size("tensor")
    own_rows = tokens.shape[0]
    head_cols = w_query.shape[1]
    local_heads = head_cols // HEAD
    col_start = rank_index * head_cols
    row_start = rank_index * own_rows
    experts = router.shape[1]
    half_cap = (own_rows * TOPK * 4 + 3 * experts - 1) // (3 * experts)
    capacity = tensor_count * half_cap
    attn_scale = HEAD ** (-0.5)
    head_shape = (GROUP, local_heads, HEAD)
    q_gain_local = lax.dynamic_slice_in_dim(q_gain, col_start, head_cols)
    k_gain_local = lax.dynamic_slice_in_dim(k_gain, col_start, head_cols)
    inputs = tokens.astype(jnp.float32)
    attn_inv = lax.rsqrt(jnp.mean(inputs * inputs, axis=1, keepdims=True) + EPSILON)
    normed = gather_rows((inputs * attn_inv * attn_gain).astype(jnp.bfloat16))
    pieces = (
        lax.all_gather(w_query, "dp", axis=0, tiled=True),
        lax.all_gather(w_key, "dp", axis=0, tiled=True),
        lax.all_gather(w_value, "dp", axis=0, tiled=True),
    )
    normed_part = normed
    queries = matmul(normed_part, pieces[0])
    keys_raw = matmul(normed_part, pieces[1])
    values_raw = matmul(normed_part, pieces[2])
    query_sq, key_sq = tensor_total(
        (jnp.sum(queries * queries, axis=1), jnp.sum(keys_raw * keys_raw, axis=1))
    )
    query_inv = lax.rsqrt(query_sq / D + EPSILON)[:, None]
    key_inv = lax.rsqrt(key_sq / D + EPSILON)[:, None]
    cosine_table, sine_table = rope_tables()
    query_rot = rotate(
        (queries * query_inv * q_gain_local).reshape(head_shape), cosine_table, sine_table
    ).astype(jnp.bfloat16)
    key_rot = rotate(
        (keys_raw * key_inv * k_gain_local).reshape(head_shape), cosine_table, sine_table
    ).astype(jnp.bfloat16)
    value_heads = values_raw.astype(jnp.bfloat16).reshape(head_shape)
    visible = visible_keys()[None]

    def masked_scores():
        raw_scores = (
            jnp.einsum("qhd,khd->hqk", query_rot, key_rot, preferred_element_type=jnp.float32)
            * attn_scale
        )
        return jnp.where(visible, raw_scores, -1e30)

    scores = masked_scores()
    row_max = jnp.max(scores, axis=2, keepdims=True)
    exponent = jnp.exp(scores - row_max)
    row_total = jnp.sum(exponent, axis=2, keepdims=True)
    log_total = row_max + jnp.log(row_total)
    mixed_heads = jnp.einsum(
        "hqk,khd->qhd",
        (exponent / row_total).astype(jnp.bfloat16),
        value_heads,
        preferred_element_type=jnp.float32,
    )
    mixed_heads = mixed_heads.reshape(GROUP, head_cols).astype(jnp.bfloat16)
    attn_part = matmul(mixed_heads, lax.all_gather(w_out, "dp", axis=1, tiled=True))
    attended = sum_rows(attn_part)
    hidden_one = inputs + attended
    mlp_inv = lax.rsqrt(jnp.mean(hidden_one * hidden_one, axis=1, keepdims=True) + EPSILON)
    normed_two = (hidden_one * mlp_inv * mlp_gain).astype(jnp.bfloat16)
    expert_ids = jnp.arange(experts, dtype=jnp.int32)
    route_hot = routes[:, :, None] == expert_ids[None, None, :]
    flat_hot = route_hot.astype(jnp.int32).reshape(tensor_count, own_rows * TOPK, experts)
    within = jnp.sum((jnp.cumsum(flat_hot, axis=1) - flat_hot) * flat_hot, axis=2).reshape(
        GROUP, TOPK
    )
    owner_of = (jnp.arange(GROUP, dtype=jnp.int32) // own_rows)[:, None]
    own_routes = lax.dynamic_slice_in_dim(routes, row_start, own_rows, 0)
    own_within = lax.dynamic_slice_in_dim(within, row_start, own_rows, 0)
    own_hot = lax.dynamic_slice_in_dim(route_hot, row_start, own_rows, 0)
    own_dest = own_routes * half_cap + own_within
    gate_weight = w_gate[0]
    up_weight = w_up[0]
    down_weight = w_down[0]
    normed_two_all = gather_rows(normed_two)
    gates_every, gate_every = gate_split(normed_two_all, route_hot, router)
    own_probs = lax.dynamic_slice_in_dim(gates_every, row_start, own_rows, 0)
    gate_weights = lax.dynamic_slice_in_dim(gate_every, row_start, own_rows, 0)
    destination = routes * capacity + owner_of * half_cap + within
    send_rows = (
        jnp.zeros((experts * capacity, D), jnp.bfloat16)
        .at[destination]
        .set(jnp.broadcast_to(normed_two_all[:, None, :], (GROUP, TOPK, D)))
        .reshape(experts, capacity, D)
    )
    received = lax.all_to_all(send_rows, "dp", split_axis=0, concat_axis=0, tiled=True)
    gate_pre = jnp.einsum("scd,df->scf", received, gate_weight, preferred_element_type=jnp.float32)
    up_pre = jnp.einsum("scd,df->scf", received, up_weight, preferred_element_type=jnp.float32)
    hidden = (jax.nn.silu(gate_pre) * up_pre).astype(jnp.bfloat16)
    expert_part = jnp.einsum("scf,fd->scd", hidden, down_weight, preferred_element_type=jnp.float32)
    expert_part, gate_pre, up_pre, hidden, received = (
        expert_part,
        gate_pre,
        up_pre,
        hidden,
        received,
    )
    back_rows = expert_swap(sum_slots(expert_part).astype(jnp.bfloat16)).reshape(
        experts * half_cap, D
    )
    picked = back_rows[own_dest].astype(jnp.float32)
    mixture = jnp.sum(gate_weights[:, :, None] * picked, axis=1)
    layer_out = (hidden_one + mixture).astype(jnp.bfloat16)
    upstream = cotangent.astype(jnp.float32)
    gate_grad = jnp.sum(upstream[:, None, :] * picked, axis=2)
    upstream_all = gather_rows(cotangent).astype(jnp.float32)
    send_grads = (
        jnp.zeros((experts * capacity, D), jnp.bfloat16)
        .at[destination]
        .set((gate_every[:, :, None] * upstream_all[:, None, :]).astype(jnp.bfloat16))
        .reshape(experts, capacity, D)
    )
    out_grads = expert_swap(send_grads)
    hidden_grad = jnp.einsum(
        "scd,fd->scf", out_grads, down_weight, preferred_element_type=jnp.float32
    )
    sigmoid = jax.nn.sigmoid(gate_pre)
    up_grad = (hidden_grad * gate_pre * sigmoid).astype(jnp.bfloat16)
    gate_pre_grad = (hidden_grad * up_pre * sigmoid * (1.0 + gate_pre * (1.0 - sigmoid))).astype(
        jnp.bfloat16
    )
    row_part = jnp.einsum(
        "scf,df->scd", gate_pre_grad, gate_weight, preferred_element_type=jnp.float32
    ) + jnp.einsum("scf,df->scd", up_grad, up_weight, preferred_element_type=jnp.float32)
    down_weight_grad = jnp.einsum(
        "scf,scd->fd", hidden, out_grads, preferred_element_type=jnp.float32
    )
    gate_weight_grad = jnp.einsum(
        "scd,scf->df", received, gate_pre_grad, preferred_element_type=jnp.float32
    )
    up_weight_grad = jnp.einsum(
        "scd,scf->df", received, up_grad, preferred_element_type=jnp.float32
    )
    returned_grads = expert_swap(sum_slots(row_part).astype(jnp.bfloat16)).reshape(
        experts * half_cap, D
    )
    normed_two_part = jnp.sum(returned_grads[own_dest].astype(jnp.float32), axis=1)
    expert_grad = jnp.sum(jnp.where(own_hot, gate_grad[:, :, None], 0.0), axis=1)
    logit_grad = own_probs * (expert_grad - jnp.sum(expert_grad * own_probs, axis=1, keepdims=True))
    router_grad = jnp.dot(normed_two.astype(jnp.float32).T, logit_grad, precision=HIGHEST)
    normed_two_grad = normed_two_part + jnp.dot(
        logit_grad, router.astype(jnp.float32).T, precision=HIGHEST
    )
    scaled_grad = normed_two_grad * mlp_gain
    hidden_one_grad = (
        upstream
        + mlp_inv * scaled_grad
        - hidden_one * mlp_inv**3 * jnp.mean(hidden_one * scaled_grad, axis=1, keepdims=True)
    )
    mlp_gain_grad = jnp.sum(normed_two_grad * hidden_one * mlp_inv, axis=0)
    attended_grad = gather_rows(hidden_one_grad.astype(jnp.bfloat16))
    mixed_grad = jnp.einsum(
        "gd,cd->gc",
        attended_grad,
        lax.all_gather(w_out, "dp", axis=1, tiled=True),
        preferred_element_type=jnp.float32,
    )
    mixed_grad = mixed_grad.astype(jnp.bfloat16).reshape(head_shape)
    attn_probs = jnp.exp(masked_scores() - log_total)
    prob_grad = jnp.einsum(
        "qhd,khd->hqk", mixed_grad, value_heads, preferred_element_type=jnp.float32
    )
    row_dot = jnp.sum(prob_grad * attn_probs, axis=2, keepdims=True)
    score_grad = (attn_probs * (prob_grad - row_dot)).astype(jnp.bfloat16)
    query_rot_grad = (
        jnp.einsum("hqk,khd->qhd", score_grad, key_rot, preferred_element_type=jnp.float32)
        * attn_scale
    )
    key_rot_grad = (
        jnp.einsum("hqk,qhd->khd", score_grad, query_rot, preferred_element_type=jnp.float32)
        * attn_scale
    )
    value_grad = (
        jnp.einsum(
            "hqk,qhd->khd",
            attn_probs.astype(jnp.bfloat16),
            mixed_grad,
            preferred_element_type=jnp.float32,
        )
        .reshape(GROUP, head_cols)
        .astype(jnp.bfloat16)
    )
    query_norm_grad = unrotate(query_rot_grad, cosine_table, sine_table).reshape(GROUP, head_cols)
    key_norm_grad = unrotate(key_rot_grad, cosine_table, sine_table).reshape(GROUP, head_cols)
    query_scaled = query_norm_grad * q_gain_local
    key_scaled = key_norm_grad * k_gain_local
    query_dot, key_dot = tensor_total(
        (jnp.sum(queries * query_scaled, axis=1), jnp.sum(keys_raw * key_scaled, axis=1))
    )
    query_grad = (
        query_inv * query_scaled - queries * query_inv**3 * (query_dot / D)[:, None]
    ).astype(jnp.bfloat16)
    key_grad = (key_inv * key_scaled - keys_raw * key_inv**3 * (key_dot / D)[:, None]).astype(
        jnp.bfloat16
    )
    q_gain_part = jnp.sum(query_norm_grad * queries * query_inv, axis=0)
    k_gain_part = jnp.sum(key_norm_grad * keys_raw * key_inv, axis=0)
    pieces = lax.all_gather((w_query, w_key, w_value), "dp", axis=0, tiled=True)
    normed_part = (
        jnp.einsum("gc,rc->gr", query_grad, pieces[0], preferred_element_type=jnp.float32)
        + jnp.einsum("gc,rc->gr", key_grad, pieces[1], preferred_element_type=jnp.float32)
        + jnp.einsum("gc,rc->gr", value_grad, pieces[2], preferred_element_type=jnp.float32)
    )
    weight_sums = lax.psum_scatter(
        jnp.concatenate(
            [
                jnp.einsum("gr,gc->rc", normed, query_grad, preferred_element_type=jnp.float32),
                jnp.einsum("gr,gc->rc", normed, key_grad, preferred_element_type=jnp.float32),
                jnp.einsum("gr,gc->rc", normed, value_grad, preferred_element_type=jnp.float32),
                jnp.einsum(
                    "gr,gc->rc", attended_grad, mixed_heads, preferred_element_type=jnp.float32
                ),
            ],
            axis=1,
        ),
        "dp",
        scatter_dimension=0,
        tiled=True,
    )
    normed_grad = sum_rows(normed_part)
    scaled_input = normed_grad * attn_gain
    tokens_grad = (
        hidden_one_grad
        + attn_inv * scaled_input
        - inputs * attn_inv**3 * jnp.mean(inputs * scaled_input, axis=1, keepdims=True)
    )
    attn_gain_grad = jnp.sum(normed_grad * inputs * attn_inv, axis=0)
    zero_width = jnp.zeros((D,), jnp.float32)
    q_gain_full = lax.dynamic_update_slice_in_dim(zero_width, q_gain_part, col_start, 0)
    k_gain_full = lax.dynamic_update_slice_in_dim(zero_width, k_gain_part, col_start, 0)
    attn_gain_grad, q_gain_grad, k_gain_grad, mlp_gain_grad, router_grad = lax.psum(
        (attn_gain_grad, q_gain_full, k_gain_full, mlp_gain_grad, router_grad), ("dp", "tensor")
    )
    return (
        layer_out,
        tokens_grad,
        attn_gain_grad,
        q_gain_grad,
        k_gain_grad,
        weight_sums[:, :head_cols],
        weight_sums[:, head_cols : 2 * head_cols],
        weight_sums[:, 2 * head_cols : 3 * head_cols],
        jnp.transpose(weight_sums[:, 3 * head_cols :]),
        mlp_gain_grad,
        router_grad,
        gate_weight_grad[None],
        up_weight_grad[None],
        down_weight_grad[None],
    )


MESH_ID = pl.DeviceIdType.MESH
LINK_TIME = pl.CostEstimate(flops=10**11, bytes_accessed=10**8, transcendentals=0)
EVERY = ("dp", "tensor")
LANES = 128
ANYWHERE = pl.BlockSpec(memory_space=pl.ANY)
IN_VMEM = pl.BlockSpec(memory_space=pltpu.VMEM)


class Place:
    def __init__(self):
        dp = lax.axis_index("dp")
        self.y = lax.axis_index("tensor")
        self.z, self.x, self.c = dp // 4, (dp // 2) % 2, dp % 2
        self.z_count = lax.axis_size("dp") // 4

    def device(self, z=None, x=None, c=None, y=None):
        z = self.z if z is None else z
        x = self.x if x is None else x
        c = self.c if c is None else c
        y = self.y if y is None else y
        return (z * 4 + x * 2 + c, y)

    def meet(self, use_y=True, all_z=False):
        barrier = pltpu.get_barrier_semaphore()
        partners = [self.device(x=1 - self.x), self.device(c=1 - self.c)]
        if use_y:
            partners.append(self.device(y=1 - self.y))
        if all_z:
            partners += [self.device(z=(self.z + d) % self.z_count) for d in range(1, self.z_count)]
        for partner in partners:
            pl.semaphore_signal(barrier, inc=1, device_id=partner, device_id_type=MESH_ID)
        if all_z:
            pl.semaphore_wait(barrier, len(partners))
            return

        @pl.when(self.z > 0)
        def _():
            pl.semaphore_signal(
                barrier, inc=1, device_id=self.device(z=self.z - 1), device_id_type=MESH_ID
            )

        @pl.when(self.z < self.z_count - 1)
        def _():
            pl.semaphore_signal(
                barrier, inc=1, device_id=self.device(z=self.z + 1), device_id_type=MESH_ID
            )

        ends = jnp.where(self.z > 0, 1, 0) + jnp.where(self.z < self.z_count - 1, 1, 0)
        pl.semaphore_wait(barrier, len(partners) + ends)

    def far_first(self, step):
        last = self.z_count - 1
        low = jnp.where(step < last - self.z, last - step, step - (last - self.z))
        high = jnp.where(step < self.z, step, last - (step - self.z))
        return jnp.where(self.z * 2 < self.z_count, low, high)


def send(src, dst, send_sem, recv_sem, device):
    copy = pltpu.make_async_remote_copy(
        src_ref=src, dst_ref=dst, send_sem=send_sem, recv_sem=recv_sem, device_id=device, device_id_type=MESH_ID
    )
    copy.start()
    return copy


def add_rows(total, part, rows, step=16):
    def chunk(i, carry):
        here = pl.ds(pl.multiple_of(i * step, step), step)
        total[here] = total[here] + part[here]
        return carry

    lax.fori_loop(0, rows // step, chunk, 0)


class Spread:
    ZU, ZD, XF, YF, XH, YH, CO, CX, CY, CA, CB = range(11)

    def __init__(self, place, src, whole, sent, got, kept):
        self.place, self.src, self.whole, self.sent, self.got = place, src, whole, sent, got
        half = src.shape[0] // 2
        self.low, self.high = pl.ds(0, half), pl.ds(half, half)
        z, x, c, y = place.z, place.x, place.c, place.y
        self.up, self.down = place.device(z=z + 1), place.device(z=z - 1)
        self.over_x, self.over_y = place.device(x=1 - x), place.device(y=1 - y)
        self.over_c = place.device(c=1 - c)
        self.keep = pltpu.make_async_copy(src, whole.at[z, x, c, y], kept)

    def push(self, kind, zz, xx, yy, rows, device, origin=None):
        ref = self.whole.at[zz, xx, self.place.c, yy, rows]
        send(
            ref if origin is None else origin,
            ref,
            self.sent.at[kind, zz],
            self.got.at[kind, zz],
            device,
        )

    def arrival(self, kind, zz, xx, yy, rows=slice(None), sibling=False):
        cc = 1 - self.place.c if sibling else self.place.c
        ref = self.whole.at[zz, xx, cc, yy, rows]
        pltpu.make_async_copy(ref, ref, self.got.at[kind, zz]).wait()

    def departure(self, kind, zz, xx, yy, rows=slice(None)):
        ref = self.whole.at[zz, xx, self.place.c, yy, rows]
        pltpu.make_async_copy(ref, ref, self.sent.at[kind, zz]).wait()

    def spread_own(self, zz, origin=None):
        x, y, every = self.place.x, self.place.y, slice(None)
        self.push(self.XF, zz, x, y, every, self.over_x, origin)
        self.push(self.YF, zz, x, y, every, self.over_y, origin)
        self.push(self.CO, zz, x, y, every, self.over_c, origin)

    def begin(self):
        z, x, y, nz = self.place.z, self.place.x, self.place.y, self.place.z_count

        @pl.when(z < nz - 1)
        def _():
            self.push(self.ZU, z, x, y, slice(None), self.up, self.src)

        @pl.when(z > 0)
        def _():
            self.push(self.ZD, z, x, y, slice(None), self.down, self.src)

        self.spread_own(z, self.src)
        self.keep.start()

    def along_z(self, d):
        z, x, y, nz = self.place.z, self.place.x, self.place.y, self.place.z_count
        below, above = z - d, z + d

        @pl.when(below >= 0)
        def _():
            self.arrival(self.ZU, below, x, y)

            @pl.when(z < nz - 1)
            def _():
                self.push(self.ZU, below, x, y, slice(None), self.up)

            self.spread_own(below)

        @pl.when(above < nz)
        def _():
            self.arrival(self.ZD, above, x, y)

            @pl.when(z > 0)
            def _():
                self.push(self.ZD, above, x, y, slice(None), self.down)

            self.spread_own(above)

    def relay(self, zz):
        x, y, every = self.place.x, self.place.y, slice(None)
        self.arrival(self.XF, zz, 1 - x, y)
        self.push(self.YH, zz, 1 - x, y, self.low, self.over_y)
        self.push(self.CX, zz, 1 - x, y, every, self.over_c)
        self.arrival(self.YF, zz, x, 1 - y)
        self.push(self.XH, zz, x, 1 - y, self.high, self.over_x)
        self.push(self.CY, zz, x, 1 - y, every, self.over_c)

    def diagonal(self, zz):
        x, y = self.place.x, self.place.y
        self.arrival(self.XH, zz, 1 - x, 1 - y, self.high)
        self.push(self.CB, zz, 1 - x, 1 - y, self.high, self.over_c)
        self.arrival(self.YH, zz, 1 - x, 1 - y, self.low)
        self.push(self.CA, zz, 1 - x, 1 - y, self.low, self.over_c)

    def sibling_near(self, zz):
        x, y = self.place.x, self.place.y
        self.arrival(self.CO, zz, x, y, sibling=True)
        self.arrival(self.CY, zz, x, 1 - y, sibling=True)

    def sibling_far(self, zz):
        x, y = self.place.x, self.place.y
        self.arrival(self.CX, zz, 1 - x, y, sibling=True)
        self.arrival(self.CA, zz, 1 - x, 1 - y, self.low, sibling=True)
        self.arrival(self.CB, zz, 1 - x, 1 - y, self.high, sibling=True)

    def finish(self):
        z, x, y, nz = self.place.z, self.place.x, self.place.y, self.place.z_count

        def one(zz, carry):
            self.departure(self.XF, zz, x, y)
            self.departure(self.YF, zz, x, y)
            self.departure(self.CO, zz, x, y)
            self.departure(self.CX, zz, 1 - x, y)
            self.departure(self.CY, zz, x, 1 - y)
            self.departure(self.YH, zz, 1 - x, y, self.low)
            self.departure(self.XH, zz, x, 1 - y, self.high)
            self.departure(self.CA, zz, 1 - x, 1 - y, self.low)
            self.departure(self.CB, zz, 1 - x, 1 - y, self.high)

            @pl.when((zz <= z) & (z < nz - 1))
            def _():
                self.departure(self.ZU, zz, x, y)

            @pl.when((zz >= z) & (z > 0))
            def _():
                self.departure(self.ZD, zz, x, y)

            return carry

        lax.fori_loop(0, nz, one, 0)


class Fold:
    CD, CX, CY, CO, XH, YH, XF, YF, ZU, ZD = range(10)
    SPOT = {CD: (1, 1), CX: (1, 0), CY: (0, 1), CO: (0, 0)}

    def __init__(self, place, parts, total, from_c, half_x, half_y, z_buf, sent, got, loaded):
        self.place, self.parts, self.total, self.from_c = place, parts, total, from_c
        self.half_x, self.half_y, self.z_buf = half_x, half_y, z_buf
        self.sent, self.got, self.loaded = sent, got, loaded
        self.rows = total.shape[3]
        self.split = half_x.shape[1]
        self.low, self.high = pl.ds(0, self.split), pl.ds(self.split, self.rows - self.split)
        z, x, c, y = place.z, place.x, place.c, place.y
        self.over_x, self.over_y = place.device(x=1 - x), place.device(y=1 - y)
        self.over_c = place.device(c=1 - c)

    def push(self, kind, zz, src, dst, device):
        send(src, dst, self.sent.at[kind, zz], self.got.at[kind, zz], device)

    def arrival(self, kind, zz, ref):
        pltpu.make_async_copy(ref, ref, self.got.at[kind, zz]).wait()

    def begin(self):
        x, c, y, nz = self.place.x, self.place.c, self.place.y, self.place.z_count

        def start(kind, i):
            dx, dy = self.SPOT[kind]
            zz = self.place.far_first(i)
            xx, yy = (1 - x if dx else x), (1 - y if dy else y)
            self.push(
                kind, zz, self.parts.at[zz, xx, 1 - c, yy], self.from_c.at[dx, dy, zz], self.over_c
            )
            pltpu.make_async_copy(
                self.parts.at[zz, xx, c, yy], self.total.at[dx, dy, zz], self.loaded.at[kind, zz]
            ).start()

        for i in range(nz):
            start(self.CD, i)
            start(self.CX, i)
        for kind in (self.CY, self.CO):
            for i in range(nz):
                start(kind, i)

    def join_cores(self, kind, zz):
        dx, dy = self.SPOT[kind]
        here, there = self.total.at[dx, dy, zz], self.from_c.at[dx, dy, zz]
        pltpu.make_async_copy(here, here, self.loaded.at[kind, zz]).wait()
        self.arrival(kind, zz, there)
        add_rows(here, there, self.rows)

    def halves(self, i):
        zz = self.place.far_first(i)
        self.join_cores(self.CD, zz)
        self.join_cores(self.CX, zz)
        self.push(self.XH, zz, self.total.at[1, 1, zz, self.low], self.half_x.at[zz], self.over_x)
        self.push(self.YH, zz, self.total.at[1, 1, zz, self.high], self.half_y.at[zz], self.over_y)

    def columns(self, i):
        zz = self.place.far_first(i)
        self.join_cores(self.CY, zz)
        self.arrival(self.XH, zz, self.half_x.at[zz])
        add_rows(self.total.at[0, 1, zz, self.low], self.half_x.at[zz], self.split)
        self.arrival(self.YH, zz, self.half_y.at[zz])
        add_rows(self.total.at[1, 0, zz, self.high], self.half_y.at[zz], self.rows - self.split)
        self.push(self.XF, zz, self.total.at[1, 0, zz], self.from_c.at[1, 1, zz], self.over_x)
        self.push(self.YF, zz, self.total.at[0, 1, zz], self.from_c.at[1, 0, zz], self.over_y)

    def along_z(self, i):
        z, nz = self.place.z, self.place.z_count
        zz = self.place.far_first(i)
        mine = self.total.at[0, 0, zz]
        self.join_cores(self.CO, zz)
        self.arrival(self.XF, zz, self.from_c.at[1, 1, zz])
        add_rows(mine, self.from_c.at[1, 1, zz], self.rows)
        self.arrival(self.YF, zz, self.from_c.at[1, 0, zz])
        add_rows(mine, self.from_c.at[1, 0, zz], self.rows)
        above = jnp.where(zz == z, nz, zz)

        @pl.when((z > 0) & (zz >= z))
        def _():
            self.arrival(self.ZU, zz, self.z_buf.at[zz])
            add_rows(mine, self.z_buf.at[zz], self.rows)

        @pl.when((z < nz - 1) & (zz <= z))
        def _():
            self.arrival(self.ZD, zz, self.z_buf.at[above])
            add_rows(mine, self.z_buf.at[above], self.rows)

        @pl.when(zz > z)
        def _():
            self.push(self.ZU, zz, mine, self.z_buf.at[zz], self.place.device(z=z + 1))

        @pl.when(zz < z)
        def _():
            landing = jnp.where(zz == z - 1, nz, zz)
            self.push(self.ZD, zz, mine, self.z_buf.at[landing], self.place.device(z=z - 1))

    def result(self):
        return self.total[0, 0, self.place.z]

    def finish(self):
        z, nz = self.place.z, self.place.z_count

        def departure(kind, zz, ref):
            pltpu.make_async_copy(ref, ref, self.sent.at[kind, zz]).wait()

        def one(zz, carry):
            for kind in (self.CD, self.CX, self.CY, self.CO, self.XF, self.YF):
                departure(kind, zz, self.total.at[0, 0, zz])
            departure(self.XH, zz, self.half_x.at[zz])
            departure(self.YH, zz, self.half_y.at[zz])

            @pl.when(zz > z)
            def _():
                departure(self.ZU, zz, self.total.at[0, 0, zz])

            @pl.when(zz < z)
            def _():
                departure(self.ZD, zz, self.total.at[0, 0, zz])

            return carry

        lax.fori_loop(0, nz, one, 0)


def fold_scratch(nz, rows, cols, split, dt):
    return [
        pltpu.VMEM((2, 2, nz, rows, cols), dt),
        pltpu.VMEM((2, 2, nz, rows, cols), dt),
        pltpu.VMEM((nz, split, cols), dt),
        pltpu.VMEM((nz, rows - split, cols), dt),
        pltpu.VMEM((nz + 1, rows, cols), dt),
        pltpu.SemaphoreType.DMA((10, nz)),
        pltpu.SemaphoreType.DMA((10, nz)),
        pltpu.SemaphoreType.DMA((4, nz)),
    ]


def scatter_kernel(parts, out, *scratch):
    place = Place()
    fold = Fold(place, parts, *scratch)
    place.meet()
    fold.begin()
    for step in (fold.halves, fold.columns, fold.along_z):
        for i in range(place.z_count):
            step(i)
    out[...] = fold.result()
    fold.finish()


def scatter_sum(parts, collective):
    nz, _, _, _, rows, cols = parts.shape
    dt = parts.dtype
    return pl.pallas_call(
        scatter_kernel,
        out_shape=jax.ShapeDtypeStruct((rows, cols), dt),
        in_specs=[ANYWHERE],
        out_specs=IN_VMEM,
        scratch_shapes=fold_scratch(nz, rows, cols, rows // 2, dt),
        cost_estimate=LINK_TIME,
        compiler_params=pltpu.CompilerParams(
            collective_id=collective, has_side_effects=True, vmem_limit_bytes=58 << 20
        ),
    )(parts)


def swap_kernel(src, out, sent, got):
    dp, y = lax.axis_index("dp"), lax.axis_index("tensor")
    other = (dp, 1 - y)
    barrier = pltpu.get_barrier_semaphore()
    pl.semaphore_signal(barrier, inc=1, device_id=other, device_id_type=MESH_ID)
    pl.semaphore_wait(barrier, 1)
    send(src, out, sent, got, other).wait()


def swap_tensor(block, collective):
    return pl.pallas_call(
        swap_kernel,
        out_shape=jax.ShapeDtypeStruct(block.shape, block.dtype),
        in_specs=[ANYWHERE],
        out_specs=ANYWHERE,
        scratch_shapes=[pltpu.SemaphoreType.DMA, pltpu.SemaphoreType.DMA],
        compiler_params=pltpu.CompilerParams(collective_id=collective, has_side_effects=True),
    )(block)


def both_rows(block, collective):
    other = swap_tensor(block, collective)
    first = lax.axis_index("tensor") == 0
    return jnp.concatenate([jnp.where(first, block, other), jnp.where(first, other, block)], axis=0)


def own_rows_sum(part, collective):
    rows = part.shape[0] // 2
    index = lax.axis_index("tensor")
    other = lax.dynamic_slice_in_dim(part, (1 - index) * rows, rows, 0).astype(jnp.bfloat16)
    mine = lax.dynamic_slice_in_dim(part, index * rows, rows, 0)
    return mine + swap_tensor(other, collective).astype(jnp.float32)


def turn(values):
    return pltpu.roll(values, HEAD // 2, 1)


def seen_keys():
    row = lax.broadcasted_iota(jnp.int32, (GROUP, GROUP), 0)
    col = lax.broadcasted_iota(jnp.int32, (GROUP, GROUP), 1)
    return (col <= row) & ((col < PROMPT) | (col >= row - row % CONT))


def signed_rope_tables():
    cosine_table, sine_table = rope_tables()
    sign = jnp.where(jnp.arange(HEAD) < HEAD // 2, -1.0, 1.0)
    return cosine_table, sine_table * sign[None, :]


def attend_kernel(
    queries, keys, values, q_inv, k_inv, q_gain, k_gain, cosine, sine, q_rot, k_rot, mixed, log_total
):
    visible = seen_keys()

    def head(h, carry):
        here = pl.ds(pl.multiple_of(h * HEAD, HEAD), HEAD)
        for raw, inv, gain, rotated in ((queries, q_inv, q_gain, q_rot), (keys, k_inv, k_gain, k_rot)):
            normal = raw[:, here] * inv[...] * gain[:, here]
            rotated[:, here] = (normal * cosine[...] + turn(normal) * sine[...]).astype(jnp.bfloat16)
        scores = dot_nt(q_rot[:, here], k_rot[:, here]) * HEAD**-0.5
        scores = jnp.where(visible, scores, -1e30)
        row_max = jnp.max(scores, axis=1, keepdims=True)
        exponent = jnp.exp(scores - row_max)
        row_total = jnp.sum(exponent, axis=1, keepdims=True)
        log_total[h] = row_max + jnp.log(row_total)
        weights = (exponent / row_total).astype(jnp.bfloat16)
        mixed[:, here] = dot_nn(weights, values[:, here]).astype(jnp.bfloat16)
        return carry

    lax.fori_loop(0, queries.shape[1] // HEAD, head, 0)


def attend(queries, keys, values, q_inv, k_inv, q_gain, k_gain, tables):
    rows, cols = queries.shape
    half = jax.ShapeDtypeStruct((rows, cols), jnp.bfloat16)
    return pl.pallas_call(
        attend_kernel,
        out_shape=[half, half, half, jax.ShapeDtypeStruct((cols // HEAD, rows, 1), jnp.float32)],
        in_specs=[IN_VMEM] * 9,
        out_specs=[IN_VMEM] * 4,
        cost_estimate=pl.CostEstimate(
            flops=4 * rows * rows * cols, bytes_accessed=16 * rows * cols, transcendentals=rows * rows * 8
        ),
        compiler_params=pltpu.CompilerParams(vmem_limit_bytes=40 << 20),
    )(queries, keys, values, q_inv, k_inv, q_gain, k_gain, *tables)


def attend_back_kernel(
    parts,
    own_grad,
    o_all,
    queries,
    keys,
    q_rot,
    k_rot,
    values,
    q_inv,
    k_inv,
    log_total,
    q_gain,
    k_gain,
    cosine,
    sine,
    mixture,
    attended_grad,
    q_grad,
    k_grad,
    v_grad,
    gain_grads,
    landed,
    mixed_grad,
    q_scaled,
    k_scaled,
    dots,
    dots_got,
    swap_sems,
    *scratch,
):
    place = Place()
    nz = place.z_count
    fold = Fold(place, parts, *scratch)
    place.meet()
    over_y = place.device(y=1 - place.y)
    rows = own_grad.shape[0]
    swap = send(own_grad, landed, swap_sems.at[0, 0], swap_sems.at[1, 0], over_y)
    fold.begin()

    def take(block, index):
        where = pl.ds(pl.multiple_of(index * rows, rows), rows)
        attended_grad[where] = block[...]
        mixed_grad[where] = dot_nt(block[...], o_all[...]).astype(jnp.bfloat16)

    take(own_grad, place.y)
    for i in range(nz):
        fold.halves(i)
    swap.wait()
    take(landed, 1 - place.y)
    visible = seen_keys()
    lane = lax.broadcasted_iota(jnp.int32, dots.shape, 1)
    dots[...] = jnp.zeros_like(dots)

    def head(h, carry):
        here = pl.ds(pl.multiple_of(h * HEAD, HEAD), HEAD)
        upstream = mixed_grad[:, here]
        scores = dot_nt(q_rot[:, here], k_rot[:, here]) * HEAD**-0.5
        probs = jnp.exp(jnp.where(visible, scores, -1e30) - log_total[h])
        prob_grad = dot_nt(upstream, values[:, here])
        row_dot = jnp.sum(prob_grad * probs, axis=1, keepdims=True)
        score_grad = (probs * (prob_grad - row_dot)).astype(jnp.bfloat16)
        v_grad[:, here] = dot_tn(probs.astype(jnp.bfloat16), upstream).astype(jnp.bfloat16)
        for index, (rot_grad, raw, inv, gain, scaled) in enumerate(
            (
                (dot_nn(score_grad, k_rot[:, here]), queries, q_inv, q_gain, q_scaled),
                (dot_tn(score_grad, q_rot[:, here]), keys, k_inv, k_gain, k_scaled),
            )
        ):
            rot_grad = rot_grad * HEAD**-0.5
            norm_grad = rot_grad * cosine[...] - turn(rot_grad) * sine[...]
            with_raw = norm_grad * raw[:, here]
            gain_grads[index : index + 1, here] = jnp.sum(with_raw * inv[...], axis=0, keepdims=True)
            scaled[:, here] = norm_grad * gain[:, here]
            part = jnp.sum(with_raw * gain[:, here], axis=1, keepdims=True)
            dots[...] += jnp.where(lane == index, part, 0.0)
        return carry

    heads = queries.shape[1] // HEAD
    cuts = [heads * (i + 1) // nz for i in range(nz)]
    for i in range(nz):
        fold.columns(i)
        lax.fori_loop(cuts[i - 1] if i else 0, cuts[i], head, 0)
    dots_swap = send(dots, dots_got, swap_sems.at[0, 1], swap_sems.at[1, 1], over_y)
    for i in range(nz):
        fold.along_z(i)
    mixture[...] = fold.result()
    dots_swap.wait()

    def grads(h, carry):
        here = pl.ds(pl.multiple_of(h * HEAD, HEAD), HEAD)
        for index, (raw, inv, scaled, grad) in enumerate(
            ((queries, q_inv, q_scaled, q_grad), (keys, k_inv, k_scaled, k_grad))
        ):
            mean = (dots[:, index : index + 1] + dots_got[:, index : index + 1]) / D
            scale = inv[...]
            grad[:, here] = (
                scale * scaled[:, here] - raw[:, here] * (scale * scale * scale * mean)
            ).astype(jnp.bfloat16)
        return carry

    lax.fori_loop(0, heads, grads, 0)
    fold.finish()


def attend_back(parts, own_grad, o_all, saved, gains, tables, collective):
    nz, _, _, _, rows, cols = parts.shape
    queries = saved[0]
    group, head_cols = queries.shape
    half = jax.ShapeDtypeStruct((group, head_cols), jnp.bfloat16)
    wide = pltpu.VMEM((group, head_cols), jnp.float32)
    split = rows * 2 // 3
    return pl.pallas_call(
        attend_back_kernel,
        out_shape=[
            jax.ShapeDtypeStruct((rows, cols), jnp.bfloat16),
            jax.ShapeDtypeStruct((group, cols), jnp.bfloat16),
            half,
            half,
            half,
            jax.ShapeDtypeStruct((8, head_cols), jnp.float32),
        ],
        in_specs=[ANYWHERE] + [IN_VMEM] * 14,
        out_specs=[IN_VMEM] * 6,
        scratch_shapes=[
            pltpu.VMEM((rows, cols), jnp.bfloat16),
            pltpu.VMEM((group, head_cols), jnp.bfloat16),
            wide,
            wide,
            pltpu.VMEM((group, LANES), jnp.float32),
            pltpu.VMEM((group, LANES), jnp.float32),
            pltpu.SemaphoreType.DMA((2, 2)),
        ]
        + fold_scratch(nz, rows, cols, split, parts.dtype),
        cost_estimate=LINK_TIME,
        compiler_params=pltpu.CompilerParams(
            collective_id=collective, has_side_effects=True, vmem_limit_bytes=62 << 20
        ),
    )(parts, own_grad, o_all, *saved, *gains, *tables)


def plane_gather_kernel(count, *refs):
    srcs, outs = refs[:count], refs[count : 2 * count]
    sent, got, kept = refs[2 * count :]
    place = Place()
    z, x, c, nz = place.z, place.x, place.c, place.z_count
    ZU, ZD, XF, CO, CX = range(5)
    up, down = place.device(z=z + 1), place.device(z=z - 1)
    over_x, over_c = place.device(x=1 - x), place.device(c=1 - c)
    place.meet(use_y=False)
    every = range(count)

    def push(a, kind, zz, xx, device, own=False):
        ref = outs[a].at[zz, xx, c]
        send(srcs[a] if own else ref, ref, sent.at[kind, a, zz], got.at[kind, a, zz], device)

    def arrival(a, kind, zz, xx, cc):
        ref = outs[a].at[zz, xx, cc]
        pltpu.make_async_copy(ref, ref, got.at[kind, a, zz]).wait()

    def departure(a, kind, zz, xx):
        ref = outs[a].at[zz, xx, c]
        pltpu.make_async_copy(ref, ref, sent.at[kind, a, zz]).wait()

    keeps = []
    for a in every:
        push(a, XF, z, x, over_x, own=True)

        @pl.when(z < nz - 1)
        def _():
            push(a, ZU, z, x, up, own=True)

        @pl.when(z > 0)
        def _():
            push(a, ZD, z, x, down, own=True)

        push(a, CO, z, x, over_c, own=True)
        keep = pltpu.make_async_copy(srcs[a], outs[a].at[z, x, c], kept.at[a])
        keep.start()
        keeps.append(keep)

    def relay(a, zz):
        arrival(a, XF, zz, 1 - x, c)
        push(a, CX, zz, 1 - x, over_c)

    for d in range(nz):
        below, above = z - d - 1, z + d + 1
        for a in every:
            if d < nz - 1:
                @pl.when(below >= 0)
                def _():
                    arrival(a, ZU, below, x, c)

                    @pl.when(z < nz - 1)
                    def _():
                        push(a, ZU, below, x, up)

                    push(a, XF, below, x, over_x)
                    push(a, CO, below, x, over_c)

                @pl.when(above < nz)
                def _():
                    arrival(a, ZD, above, x, c)

                    @pl.when(z > 0)
                    def _():
                        push(a, ZD, above, x, down)

                    push(a, XF, above, x, over_x)
                    push(a, CO, above, x, over_c)

    for d in range(nz):
        for a in every:
            if d == 0:
                relay(a, z)
            else:
                @pl.when(z - d >= 0)
                def _():
                    relay(a, z - d)

                @pl.when(z + d < nz)
                def _():
                    relay(a, z + d)

    for a in every:
        keeps[a].wait()
        for zz in range(nz):
            arrival(a, CO, zz, x, 1 - c)
            arrival(a, CX, zz, 1 - x, 1 - c)
            departure(a, XF, zz, x)
            departure(a, CO, zz, x)
            departure(a, CX, zz, 1 - x)

            @pl.when((zz <= z) & (z < nz - 1))
            def _():
                departure(a, ZU, zz, x)

            @pl.when((zz >= z) & (z > 0))
            def _():
                departure(a, ZD, zz, x)


def gather_in_plane(shards, collective):
    nz = lax.axis_size("dp") // 4
    count = len(shards)
    return pl.pallas_call(
        functools.partial(plane_gather_kernel, count),
        out_shape=[jax.ShapeDtypeStruct((nz, 2, 2) + s.shape, s.dtype) for s in shards],
        in_specs=[ANYWHERE] * count,
        out_specs=[ANYWHERE] * count,
        scratch_shapes=[
            pltpu.SemaphoreType.DMA((5, count, nz)),
            pltpu.SemaphoreType.DMA((5, count, nz)),
            pltpu.SemaphoreType.DMA((count,)),
        ],
        cost_estimate=LINK_TIME,
        compiler_params=pltpu.CompilerParams(collective_id=collective, has_side_effects=True),
    )(*shards)


def plane_scatter_kernel(count, *refs):
    parts, small, row_part = refs[:count], refs[count], refs[count + 1]
    streams = refs[count + 2 : count + 7]
    refs = refs[count + 7 :]
    outs, small_out, row_landed = refs[:count], refs[count], refs[count + 1]
    wg_grad, wu_grad, wd_grad = refs[count + 2 : count + 5]
    total, from_c, full_x, z_buf, small_sum, small_got = refs[count + 5 : count + 11]
    tiles = refs[count + 11 : count + 16]
    sent, got, loaded, small_sems, row_sems, tile_sems = refs[count + 16 :]
    place = Place()
    z, x, c, nz = place.z, place.x, place.c, place.z_count
    rows = total.shape[3]
    C0, C1, XF, ZU, ZD = range(5)
    over_x, over_c = place.device(x=1 - x), place.device(c=1 - c)
    over_y = place.device(y=1 - place.y)
    place.meet(all_z=True)

    small_sum[0] = small[...]

    def small_start(i):
        return send(
            small_sum.at[i],
            small_got.at[i],
            small_sems.at[0, i],
            small_sems.at[1, i],
            (over_x, over_c, over_y)[i],
        )

    def small_end(i, copy):
        copy.wait()
        small_sum[i + 1] = small_sum[i] + small_got[i]

    def small_z_start():
        return [
            send(
                small_sum.at[3],
                small_got.at[2 + d],
                small_sems.at[0, 2 + d],
                small_sems.at[1, 2 + d],
                place.device(z=(z + d) % nz),
            )
            for d in range(1, nz)
        ]

    def small_z_end(copies):
        for copy in copies:
            copy.wait()
        result = jnp.zeros_like(small_out)
        for zz in range(nz):
            away = (z - zz) % nz
            result = result + jnp.where(away == 0, small_sum[3], small_got[jnp.maximum(2 + away, 3)])
        small_out[...] = result

    count_tiles = streams[0].shape[0]

    def tile_loads(t, slot):
        return [
            pltpu.make_async_copy(stream.at[t], tile.at[slot], tile_sems.at[slot, n])
            for n, (stream, tile) in enumerate(zip(streams, tiles))
        ]

    def tile_step(t, carry):
        slot = t % 2
        for copy in tile_loads(t, slot):
            copy.wait()

        @pl.when(t + 1 < count_tiles)
        def _():
            for copy in tile_loads(t + 1, 1 - slot):
                copy.start()

        x_tile, g_tile, hidden, gate_pre_grad, up_grad = (tile[slot] for tile in tiles)
        wg_grad[...] += dot_tn(x_tile, gate_pre_grad)
        wu_grad[...] += dot_tn(x_tile, up_grad)
        wd_grad[...] += dot_tn(hidden, g_tile)
        return carry

    def arrival(a, kind, zz, ref):
        pltpu.make_async_copy(ref, ref, got.at[kind, a, zz]).wait()

    small_copy = small_start(0)
    for dx, kind in ((1, C1), (0, C0)):
        for i in range(nz):
            zz = place.far_first(i)
            xx = 1 - x if dx else x
            for a in range(count):
                send(
                    parts[a].at[zz, xx, 1 - c],
                    from_c.at[dx, zz, a],
                    sent.at[kind, a, zz],
                    got.at[kind, a, zz],
                    over_c,
                )
                pltpu.make_async_copy(
                    parts[a].at[zz, xx, c], total.at[dx, zz, a], loaded.at[dx, a, zz]
                ).start()
    for copy in tile_loads(0, 0):
        copy.start()

    def join_cores(a, dx, zz):
        here, there = total.at[dx, zz, a], from_c.at[dx, zz, a]
        pltpu.make_async_copy(here, here, loaded.at[dx, a, zz]).wait()
        arrival(a, C1 if dx else C0, zz, there)
        add_rows(here, there, rows)

    def over_the_x(i):
        zz = place.far_first(i)
        for a in range(count):
            join_cores(a, 1, zz)
            send(total.at[1, zz, a], full_x.at[zz, a], sent.at[XF, a, zz], got.at[XF, a, zz], over_x)

    def along_z(i):
        zz = place.far_first(i)
        above = jnp.where(zz == z, nz, zz)
        landing = jnp.where(zz == z - 1, nz, zz)
        for a in range(count):
            mine = total.at[0, zz, a]
            join_cores(a, 0, zz)
            arrival(a, XF, zz, full_x.at[zz, a])
            add_rows(mine, full_x.at[zz, a], rows)

            @pl.when((z > 0) & (zz >= z))
            def _():
                arrival(a, ZU, zz, z_buf.at[zz, a])
                add_rows(mine, z_buf.at[zz, a], rows)

            @pl.when((z < nz - 1) & (zz <= z))
            def _():
                arrival(a, ZD, zz, z_buf.at[above, a])
                add_rows(mine, z_buf.at[above, a], rows)

            @pl.when(zz > z)
            def _():
                send(
                    mine,
                    z_buf.at[zz, a],
                    sent.at[ZU, a, zz],
                    got.at[ZU, a, zz],
                    place.device(z=z + 1),
                )

            @pl.when(zz < z)
            def _():
                send(
                    mine,
                    z_buf.at[landing, a],
                    sent.at[ZD, a, zz],
                    got.at[ZD, a, zz],
                    place.device(z=z - 1),
                )

    small_end(0, small_copy)
    over_the_x(0)
    small_copy = small_start(1)
    small_end(1, small_copy)
    small_copy = small_start(2)
    row_copy = send(row_part, row_landed, row_sems.at[0], row_sems.at[1], over_y)
    wg_grad[...] = jnp.zeros_like(wg_grad)
    wu_grad[...] = jnp.zeros_like(wu_grad)
    wd_grad[...] = jnp.zeros_like(wd_grad)
    for i in range(1, nz - 1):
        over_the_x(i)
    small_end(2, small_copy)
    small_copies = small_z_start()
    over_the_x(nz - 1)
    for i in range(nz):
        lax.fori_loop(count_tiles * i // nz, count_tiles * (i + 1) // nz, tile_step, 0)
        if i == 0:
            small_z_end(small_copies)
        along_z(i)
    row_copy.wait()

    for a in range(count):

        def widen(i, carry):
            here = pl.ds(pl.multiple_of(i * 16, 16), 16)
            outs[a][here] = total[0, z, a, here].astype(jnp.float32)
            return carry

        lax.fori_loop(0, rows // 16, widen, 0)

    def departure(a, kind, zz):
        ref = total.at[0, 0, a]
        pltpu.make_async_copy(ref, ref, sent.at[kind, a, zz]).wait()

    for a in range(count):
        for zz in range(nz):
            departure(a, C0, zz)
            departure(a, C1, zz)
            departure(a, XF, zz)

            @pl.when(zz > z)
            def _():
                departure(a, ZU, zz)

            @pl.when(zz < z)
            def _():
                departure(a, ZD, zz)


def scatter_in_plane(parts, small, row_part, streams, collective):
    nz, _, _, rows, cols = parts[0].shape
    count = len(parts)
    dt = parts[0].dtype
    width, units = streams[0].shape[1], streams[2].shape[1]
    tile = 256 if streams[0].shape[0] % 256 == 0 else GROUP // 2
    streams = [stream.reshape(-1, tile, stream.shape[1]) for stream in streams]
    return pl.pallas_call(
        functools.partial(plane_scatter_kernel, count),
        out_shape=[jax.ShapeDtypeStruct((rows, cols), jnp.float32)] * count
        + [
            jax.ShapeDtypeStruct(small.shape, small.dtype),
            jax.ShapeDtypeStruct(row_part.shape, row_part.dtype),
            jax.ShapeDtypeStruct((width, units), jnp.float32),
            jax.ShapeDtypeStruct((width, units), jnp.float32),
            jax.ShapeDtypeStruct((units, width), jnp.float32),
        ],
        in_specs=[ANYWHERE] * count + [IN_VMEM] + [ANYWHERE] * 6,
        out_specs=[IN_VMEM] * (count + 1) + [ANYWHERE] + [IN_VMEM] * 3,
        scratch_shapes=[
            pltpu.VMEM((2, nz, count, rows, cols), dt),
            pltpu.VMEM((2, nz, count, rows, cols), dt),
            pltpu.VMEM((nz, count, rows, cols), dt),
            pltpu.VMEM((nz + 1, count, rows, cols), dt),
            pltpu.VMEM((4,) + small.shape, small.dtype),
            pltpu.VMEM((2 + nz,) + small.shape, small.dtype),
        ]
        + [pltpu.VMEM((2,) + stream.shape[1:], stream.dtype) for stream in streams]
        + [
            pltpu.SemaphoreType.DMA((5, count, nz)),
            pltpu.SemaphoreType.DMA((5, count, nz)),
            pltpu.SemaphoreType.DMA((2, count, nz)),
            pltpu.SemaphoreType.DMA((2, 2 + nz)),
            pltpu.SemaphoreType.DMA((2,)),
            pltpu.SemaphoreType.DMA((2, 5)),
        ],
        cost_estimate=LINK_TIME,
        compiler_params=pltpu.CompilerParams(
            collective_id=collective, has_side_effects=True, vmem_limit_bytes=62 << 20
        ),
    )(*parts, small, row_part, *streams)


def dot_nn(a, b):
    return lax.dot_general(a, b, (((1,), (0,)), ((), ())), preferred_element_type=jnp.float32)


def dot_nt(a, b):
    return lax.dot_general(a, b, (((1,), (1,)), ((), ())), preferred_element_type=jnp.float32)


def dot_tn(a, b):
    return lax.dot_general(a, b, (((0,), (0,)), ((), ())), preferred_element_type=jnp.float32)


def pick(table, index):
    return sum(jnp.where(index == i, value, 0) for i, value in enumerate(table))


def expert_kernel(
    z_count,
    src,
    g_all,
    hot_ref,
    router_ref,
    lanes_ref,
    wg_ref,
    wu_ref,
    wd_ref,
    x_all,
    y_all,
    r_all,
    hidden_all,
    gate_pre_grad_all,
    up_grad_all,
    x_tile,
    g_tile,
    y_tile,
    r_tile,
    hidden_tile,
    gate_pre_grad_tile,
    up_grad_tile,
    load_sems,
    store_sems,
    sent,
    got,
    kept,
):
    place = Place()
    place.meet()
    spread = Spread(place, src, x_all, sent, got, kept)
    spread.begin()
    width = src.shape[1]
    tile = x_tile.shape[1]
    pairs = sorted(
        ((k, dx) for k in range(z_count) for dx in (0, 1)), key=lambda p: p[0] + 1.3 * p[1]
    )
    tiles = 2 * len(pairs)
    near_table, across_table = [p[0] for p in pairs], [p[1] for p in pairs]

    def near(k):
        return place.far_first(z_count - 1 - k)

    def tile_at(i):
        pair, second = i // 2, i % 2
        zz = near(pick(near_table, pair))
        xx = jnp.where(pick(across_table, pair) == 1, 1 - place.x, place.x)
        cc = jnp.where(second == 1, 1 - place.c, place.c)
        return zz, xx, cc

    stores = (
        (y_tile, y_all),
        (r_tile, r_all),
        (hidden_tile, hidden_all),
        (gate_pre_grad_tile, gate_pre_grad_all),
        (up_grad_tile, up_grad_all),
    )

    def loads(i, slot):
        zz, xx, cc = tile_at(i)
        copies = []
        for yy in range(2):
            rows = pl.ds(yy * (tile // 2), tile // 2)
            copies.append(
                pltpu.make_async_copy(
                    x_all.at[zz, xx, cc, yy], x_tile.at[slot, rows], load_sems.at[slot, yy]
                )
            )
        copies.append(
            pltpu.make_async_copy(g_all.at[zz, xx, cc], g_tile.at[slot], load_sems.at[slot, 2])
        )
        return copies

    def store(i, slot):
        zz, xx, cc = tile_at(i)
        return [
            pltpu.make_async_copy(here.at[slot], there.at[zz, xx, cc], store_sems.at[slot, n])
            for n, (here, there) in enumerate(stores)
        ]

    z_done, steps = 0, {}
    for position, (k, dx) in enumerate(pairs):
        todo = []
        if dx == 0:
            todo.append(("relay", k))
            while z_done < min(k + 1, z_count - 1):
                z_done += 1
                todo.insert(0, ("z", z_done))
        else:
            todo.append(("diagonal", k))
        steps[2 * position] = todo

    def prepare(i):
        for position in range(tiles):
            pair = position // 2
            k, dx = pairs[pair]

            @pl.when(i == position)
            def _():
                if position % 2 == 0:
                    for kind, number in steps[position]:
                        if kind == "z":
                            spread.along_z(number)
                        elif kind == "relay":
                            spread.relay(near(number))
                        else:
                            spread.diagonal(near(number))
                    if position == 0:
                        spread.keep.wait()
                elif dx == 0:
                    spread.sibling_near(near(k))
                else:
                    spread.sibling_far(near(k))

        for copy in loads(i, i % 2):
            copy.start()

    def compute(i, carry):
        slot = i % 2
        for copy in loads(i, slot):
            copy.wait()

        @pl.when(i >= 2)
        def _():
            for copy in store(i - 2, slot):
                copy.wait()

        zz, xx, cc = tile_at(i)
        first_row = pl.multiple_of(((zz * 2 + xx) * 2 + cc) * tile, tile)
        rows = x_tile[slot]
        logits = jnp.where(lanes_ref[1:2] > 0.0, dot_nn(rows, router_ref[...]), -1e30)
        weights = jnp.exp(logits - jnp.max(logits, axis=1, keepdims=True))
        own_weight = jnp.sum(weights * lanes_ref[0:1], axis=1, keepdims=True)
        gate = hot_ref[pl.ds(first_row, tile)] * own_weight / jnp.sum(weights, axis=1, keepdims=True)
        gate_pre = dot_nn(rows, wg_ref[...])
        up_pre = dot_nn(rows, wu_ref[...])
        raw_grad = dot_nt(g_tile[slot], wd_ref[...])

        @pl.when(i < tiles - 1)
        def _():
            prepare(i + 1)

        sigmoid = jax.nn.sigmoid(gate_pre)
        silu = gate_pre * sigmoid
        hidden = silu * up_pre
        gate_grad = jnp.sum(hidden * raw_grad, axis=1, keepdims=True)
        coarse = gate_grad.astype(jnp.bfloat16).astype(jnp.float32)
        r_tile[slot, :, width:] = (
            coarse * lanes_ref[2:3] + (gate_grad - coarse) * lanes_ref[3:4]
        ).astype(jnp.bfloat16)
        hidden_gated = (gate * hidden).astype(jnp.bfloat16)
        hidden_tile[slot] = hidden_gated
        hidden_grad = gate * raw_grad
        up_grad = (hidden_grad * silu).astype(jnp.bfloat16)
        up_grad_tile[slot] = up_grad
        gate_pre_grad = (
            hidden_grad * up_pre * sigmoid * (1.0 + gate_pre * (1.0 - sigmoid))
        ).astype(jnp.bfloat16)
        gate_pre_grad_tile[slot] = gate_pre_grad
        y_tile[slot] = dot_nn(hidden_gated, wd_ref[...]).astype(jnp.bfloat16)
        r_tile[slot, :, :width] = (
            dot_nt(gate_pre_grad, wg_ref[...]) + dot_nt(up_grad, wu_ref[...])
        ).astype(jnp.bfloat16)
        for copy in store(i, slot):
            copy.start()
        return carry

    prepare(0)
    lax.fori_loop(0, tiles, compute, 0)
    for i in (tiles - 2, tiles - 1):
        for copy in store(i, i % 2):
            copy.wait()
    spread.finish()


def expert_pass(block, upstream, hot, router, lanes, w_gate, w_up, w_down, collective):
    rows, width = block.shape
    units = w_gate.shape[1]
    nz = lax.axis_size("dp") // 4
    tile = 2 * rows
    out = (nz, 2, 2, tile)
    return pl.pallas_call(
        functools.partial(expert_kernel, nz),
        in_specs=[ANYWHERE] * 2 + [IN_VMEM] * 6,
        out_specs=[ANYWHERE] * 6,
        out_shape=[
            jax.ShapeDtypeStruct((nz, 2, 2, 2, rows, width), jnp.bfloat16),
            jax.ShapeDtypeStruct(out + (width,), jnp.bfloat16),
            jax.ShapeDtypeStruct(out + (width + LANES,), jnp.bfloat16),
        ]
        + [jax.ShapeDtypeStruct(out + (units,), jnp.bfloat16)] * 3,
        scratch_shapes=[
            pltpu.VMEM((2, tile, width), jnp.bfloat16),
            pltpu.VMEM((2, tile, width), jnp.bfloat16),
            pltpu.VMEM((2, tile, width), jnp.bfloat16),
            pltpu.VMEM((2, tile, width + LANES), jnp.bfloat16),
            pltpu.VMEM((2, tile, units), jnp.bfloat16),
            pltpu.VMEM((2, tile, units), jnp.bfloat16),
            pltpu.VMEM((2, tile, units), jnp.bfloat16),
            pltpu.SemaphoreType.DMA((2, 3)),
            pltpu.SemaphoreType.DMA((2, 5)),
            pltpu.SemaphoreType.DMA((11, nz)),
            pltpu.SemaphoreType.DMA((11, nz)),
            pltpu.SemaphoreType.DMA,
        ],
        cost_estimate=LINK_TIME,
        compiler_params=pltpu.CompilerParams(
            collective_id=collective, has_side_effects=True, vmem_limit_bytes=60 << 20
        ),
    )(block, upstream.reshape(out + (width,)), hot, router, lanes, w_gate, w_up, w_down)


def dense_body(
    tokens,
    routes,
    cotangent,
    attn_gain,
    q_gain,
    k_gain,
    w_query,
    w_key,
    w_value,
    w_out,
    mlp_gain,
    router,
    w_gate,
    w_up,
    w_down,
):
    rank_index = lax.axis_index("tensor")
    own_rows = tokens.shape[0]
    head_cols = w_query.shape[1]
    col_start = rank_index * head_cols
    row_start = rank_index * own_rows
    experts = router.shape[1]
    q_gain_local = lax.dynamic_slice_in_dim(q_gain, col_start, head_cols)
    k_gain_local = lax.dynamic_slice_in_dim(k_gain, col_start, head_cols)
    inputs_both = both_rows(tokens, 5).astype(jnp.float32)
    unit_both = inputs_both * lax.rsqrt(
        jnp.mean(inputs_both * inputs_both, axis=1, keepdims=True) + EPSILON
    )
    normed = (unit_both * attn_gain).astype(jnp.bfloat16)
    inputs = tokens.astype(jnp.float32)
    attn_inv = lax.rsqrt(jnp.mean(inputs * inputs, axis=1, keepdims=True) + EPSILON)
    q_all, k_all, v_all, o_all, routes_all = gather_in_plane(
        (w_query, w_key, w_value, w_out, routes), 1
    )
    q_all, k_all, v_all = (w.reshape(D, head_cols) for w in (q_all, k_all, v_all))
    o_all = jnp.transpose(o_all.reshape(-1, *w_out.shape), (1, 0, 2)).reshape(head_cols, D)
    routes_all = routes_all.reshape(-1, TOPK)
    own_expert = lax.axis_index("dp")
    hot = jnp.any(routes_all == own_expert, axis=1, keepdims=True).astype(jnp.float32)
    lane = jnp.arange(LANES)
    marked = own_expert + experts * rank_index
    lanes = jnp.stack(
        [lane == own_expert, lane < experts, lane == marked, lane == marked + 2 * experts]
        + [lane < 0] * 4
    ).astype(jnp.float32)
    router_wide = jnp.pad(router, ((0, 0), (0, LANES - experts)))
    upstream_all = lax.all_gather(cotangent, EVERY, axis=0, tiled=True)
    queries = matmul(normed, q_all)
    keys_raw = matmul(normed, k_all)
    values_raw = matmul(normed, v_all)
    query_sq, key_sq = tensor_total(
        (jnp.sum(queries * queries, axis=1), jnp.sum(keys_raw * keys_raw, axis=1))
    )
    query_inv = lax.rsqrt(query_sq / D + EPSILON)[:, None]
    key_inv = lax.rsqrt(key_sq / D + EPSILON)[:, None]
    tables = signed_rope_tables()
    values = values_raw.astype(jnp.bfloat16)
    gains = (q_gain_local[None], k_gain_local[None])
    query_rot, key_rot, mixed_heads, log_total = attend(
        queries, keys_raw, values, query_inv, key_inv, *gains, tables
    )
    attended = own_rows_sum(matmul(mixed_heads, o_all), 6)
    hidden_one = inputs + attended
    mlp_inv = lax.rsqrt(jnp.mean(hidden_one * hidden_one, axis=1, keepdims=True) + EPSILON)
    normed_two = (hidden_one * mlp_inv * mlp_gain).astype(jnp.bfloat16)
    own_routes = lax.dynamic_slice_in_dim(routes, row_start, own_rows, 0)
    expert_ids = jnp.arange(experts, dtype=jnp.int32)
    own_hot = jnp.any(own_routes[:, :, None] == expert_ids[None, None, :], axis=1)
    own_probs = jax.nn.softmax(matmul(normed_two, router), axis=1)
    rows_all, y_part, r_part, *for_weights = expert_pass(
        normed_two, upstream_all, hot, router_wide, lanes, w_gate[0], w_up[0], w_down[0], 2
    )
    rows_all, y_part = rows_all.reshape(-1, D), y_part.reshape(-1, D)
    for_weights = [array.reshape(rows_all.shape[0], -1) for array in for_weights]
    blocks = (lax.axis_size("dp") // 4, 2, 2, 2, own_rows)
    returned = scatter_sum(r_part.reshape(*blocks, D + LANES), 3)
    expert_grad = jnp.sum(
        returned[:, D : D + 4 * experts].astype(jnp.float32).reshape(own_rows, 4, experts), axis=1
    )
    expert_grad = jnp.where(own_hot, expert_grad, 0.0)
    returned = returned[:, :D]
    upstream = cotangent.astype(jnp.float32)
    logit_grad = own_probs * (expert_grad - jnp.sum(expert_grad * own_probs, axis=1, keepdims=True))
    router_grad = jnp.dot(normed_two.astype(jnp.float32).T, logit_grad, precision=HIGHEST)
    normed_two_grad = returned.astype(jnp.float32) + jnp.dot(
        logit_grad, router.astype(jnp.float32).T, precision=HIGHEST
    )
    scaled_grad = normed_two_grad * mlp_gain
    hidden_one_grad = (
        upstream
        + mlp_inv * scaled_grad
        - hidden_one * mlp_inv**3 * jnp.mean(hidden_one * scaled_grad, axis=1, keepdims=True)
    )
    mlp_gain_grad = jnp.sum(normed_two_grad * hidden_one * mlp_inv, axis=0)
    saved = (queries, keys_raw, query_rot, key_rot, values, query_inv, key_inv, log_total)
    mixture, attended_grad, query_grad, key_grad, value_grad, gain_grads = attend_back(
        y_part.reshape(*blocks, D), hidden_one_grad.astype(jnp.bfloat16), o_all, saved, gains, tables, 7
    )
    layer_out = (hidden_one + mixture.astype(jnp.float32)).astype(jnp.bfloat16)
    q_gain_part, k_gain_part = gain_grads[0], gain_grads[1]
    normed_part = (
        jnp.einsum("gc,rc->gr", query_grad, q_all, preferred_element_type=jnp.float32)
        + jnp.einsum("gc,rc->gr", key_grad, k_all, preferred_element_type=jnp.float32)
        + jnp.einsum("gc,rc->gr", value_grad, v_all, preferred_element_type=jnp.float32)
    )
    attn_gain_grad = jnp.sum(normed_part * unit_both, axis=0)
    zero_width = jnp.zeros((D,), jnp.float32)
    q_gain_full = lax.dynamic_update_slice_in_dim(zero_width, q_gain_part, col_start, 0)
    k_gain_full = lax.dynamic_update_slice_in_dim(zero_width, k_gain_part, col_start, 0)
    small_grads = jnp.concatenate(
        [
            jnp.stack([attn_gain_grad, q_gain_full, k_gain_full, mlp_gain_grad]),
            jnp.zeros((4, D), jnp.float32),
            jnp.transpose(router_grad),
        ],
        axis=0,
    )
    shard = (lax.axis_size("dp") // 4, 2, 2, w_query.shape[0], head_cols)
    products = [
        dot_tn(first, second).astype(jnp.bfloat16).reshape(shard)
        for first, second in (
            (normed, query_grad),
            (normed, key_grad),
            (normed, value_grad),
            (attended_grad, mixed_heads),
        )
    ]
    row_part = lax.dynamic_slice_in_dim(
        normed_part, (1 - rank_index) * own_rows, own_rows, 0
    ).astype(jnp.bfloat16)
    own_part = lax.dynamic_slice_in_dim(normed_part, row_start, own_rows, 0)
    streams = [rows_all, upstream_all, *for_weights]
    *weight_sums, small_sums, other_part, gate_weight_grad, up_weight_grad, down_weight_grad = (
        scatter_in_plane(products, small_grads, row_part, streams, 4)
    )
    normed_grad = own_part + other_part.astype(jnp.float32)
    scaled_input = normed_grad * attn_gain
    tokens_grad = (
        hidden_one_grad
        + attn_inv * scaled_input
        - inputs * attn_inv**3 * jnp.mean(inputs * scaled_input, axis=1, keepdims=True)
    )
    attn_gain_grad, q_gain_grad, k_gain_grad, mlp_gain_grad = (small_sums[i] for i in range(4))
    router_grad = jnp.transpose(small_sums[8:])
    return (
        layer_out,
        tokens_grad,
        attn_gain_grad,
        q_gain_grad,
        k_gain_grad,
        weight_sums[0],
        weight_sums[1],
        weight_sums[2],
        jnp.transpose(weight_sums[3]),
        mlp_gain_grad,
        router_grad,
        gate_weight_grad[None],
        up_weight_grad[None],
        down_weight_grad[None],
    )


def solution(mesh):
    in_specs = (
        P(("dp", "tensor"), None),
        P("dp", None),
        P(("dp", "tensor"), None),
        P(),
        P(),
        P(),
        P("dp", "tensor"),
        P("dp", "tensor"),
        P("dp", "tensor"),
        P("tensor", "dp"),
        P(),
        P(),
        P("dp", None, "tensor"),
        P("dp", None, "tensor"),
        P("dp", "tensor", None),
    )
    out_specs = (
        P(("dp", "tensor"), None),
        P(("dp", "tensor"), None),
        P(),
        P(),
        P(),
        P("dp", "tensor"),
        P("dp", "tensor"),
        P("dp", "tensor"),
        P("tensor", "dp"),
        P(),
        P(),
        P("dp", None, "tensor"),
        P("dp", None, "tensor"),
        P("dp", "tensor", None),
    )
    experts = mesh.shape["dp"]
    body = dense_body if experts <= 2 * TOPK else routed_body
    return jax.shard_map(body, mesh=mesh, in_specs=in_specs, out_specs=out_specs, check_vma=False)
```

```python
import functools

import jax
import jax.numpy as jnp
from jax import lax
from jax.experimental import pallas as pl
from jax.experimental.pallas import tpu as pltpu
from jax.sharding import PartitionSpec as P

D = 2048
HEAD = 128
TOPK = 8
PROMPT = 256
CONT = 64
GROUP = 384


EPSILON = 1e-05
ROPE_BASE = 10000.0
HIGHEST = lax.Precision.HIGHEST


def matmul(first_op, second_op):
    return jnp.dot(first_op, second_op, preferred_element_type=jnp.float32)


def gather_rows(values):
    return lax.all_gather(values, "tensor", axis=0, tiled=True)


def sum_rows(values):
    return lax.psum_scatter(values, "tensor", scatter_dimension=0, tiled=True)


def tensor_total(values):
    return lax.psum((values[0], values[1]), "tensor")


def expert_swap(values):
    return lax.all_to_all(values, "dp", split_axis=0, concat_axis=0, tiled=True)


def sum_slots(values):
    return lax.psum_scatter(values, "tensor", scatter_dimension=1, tiled=True)


def group_positions():
    position = jnp.arange(GROUP, dtype=jnp.int32)
    return jnp.where(position < PROMPT, position, PROMPT + (position - PROMPT) % CONT)


def visible_keys():
    position = jnp.arange(GROUP, dtype=jnp.int32)
    member = jnp.where(position < PROMPT, -1, (position - PROMPT) // CONT)
    causal = position[None, :] <= position[:, None]
    return causal & ((member[None, :] == -1) | (member[None, :] == member[:, None]))


def rope_tables():
    half_head = HEAD // 2
    frequency = ROPE_BASE ** (-2.0 * jnp.arange(half_head, dtype=jnp.float32) / HEAD)
    angles = group_positions().astype(jnp.float32)[:, None] * frequency[None, :]
    angles = jnp.concatenate([angles, angles], axis=1)
    return (jnp.cos(angles), jnp.sin(angles))


def rotate(values, cosine_table, sine_table):
    half_head = HEAD // 2
    turned = jnp.concatenate([-values[..., half_head:], values[..., :half_head]], axis=-1)
    return values * cosine_table[:, None, :] + turned * sine_table[:, None, :]


def unrotate(values, cosine_table, sine_table):
    half_head = HEAD // 2
    scaled = values * sine_table[:, None, :]
    turned = jnp.concatenate([scaled[..., half_head:], -scaled[..., :half_head]], axis=-1)
    return values * cosine_table[:, None, :] + turned


def gate_split(rows_in, hot_table, router):
    gates = jax.nn.softmax(matmul(rows_in, router), axis=1)
    weights = jnp.sum(jnp.where(hot_table, gates[:, None, :], 0.0), axis=2)
    return (gates, weights)


def routed_body(
    tokens,
    routes,
    cotangent,
    attn_gain,
    q_gain,
    k_gain,
    w_query,
    w_key,
    w_value,
    w_out,
    mlp_gain,
    router,
    w_gate,
    w_up,
    w_down,
):
    rank_index = lax.axis_index("tensor")
    tensor_count = lax.axis_size("tensor")
    own_rows = tokens.shape[0]
    head_cols = w_query.shape[1]
    local_heads = head_cols // HEAD
    col_start = rank_index * head_cols
    row_start = rank_index * own_rows
    experts = router.shape[1]
    half_cap = (own_rows * TOPK * 4 + 3 * experts - 1) // (3 * experts)
    capacity = tensor_count * half_cap
    attn_scale = HEAD ** (-0.5)
    head_shape = (GROUP, local_heads, HEAD)
    q_gain_local = lax.dynamic_slice_in_dim(q_gain, col_start, head_cols)
    k_gain_local = lax.dynamic_slice_in_dim(k_gain, col_start, head_cols)
    inputs = tokens.astype(jnp.float32)
    attn_inv = lax.rsqrt(jnp.mean(inputs * inputs, axis=1, keepdims=True) + EPSILON)
    normed = gather_rows((inputs * attn_inv * attn_gain).astype(jnp.bfloat16))
    pieces = (
        lax.all_gather(w_query, "dp", axis=0, tiled=True),
        lax.all_gather(w_key, "dp", axis=0, tiled=True),
        lax.all_gather(w_value, "dp", axis=0, tiled=True),
    )
    normed_part = normed
    queries = matmul(normed_part, pieces[0])
    keys_raw = matmul(normed_part, pieces[1])
    values_raw = matmul(normed_part, pieces[2])
    query_sq, key_sq = tensor_total(
        (jnp.sum(queries * queries, axis=1), jnp.sum(keys_raw * keys_raw, axis=1))
    )
    query_inv = lax.rsqrt(query_sq / D + EPSILON)[:, None]
    key_inv = lax.rsqrt(key_sq / D + EPSILON)[:, None]
    cosine_table, sine_table = rope_tables()
    query_rot = rotate(
        (queries * query_inv * q_gain_local).reshape(head_shape), cosine_table, sine_table
    ).astype(jnp.bfloat16)
    key_rot = rotate(
        (keys_raw * key_inv * k_gain_local).reshape(head_shape), cosine_table, sine_table
    ).astype(jnp.bfloat16)
    value_heads = values_raw.astype(jnp.bfloat16).reshape(head_shape)
    visible = visible_keys()[None]

    def masked_scores():
        raw_scores = (
            jnp.einsum("qhd,khd->hqk", query_rot, key_rot, preferred_element_type=jnp.float32)
            * attn_scale
        )
        return jnp.where(visible, raw_scores, -1e30)

    scores = masked_scores()
    row_max = jnp.max(scores, axis=2, keepdims=True)
    exponent = jnp.exp(scores - row_max)
    row_total = jnp.sum(exponent, axis=2, keepdims=True)
    log_total = row_max + jnp.log(row_total)
    mixed_heads = jnp.einsum(
        "hqk,khd->qhd",
        (exponent / row_total).astype(jnp.bfloat16),
        value_heads,
        preferred_element_type=jnp.float32,
    )
    mixed_heads = mixed_heads.reshape(GROUP, head_cols).astype(jnp.bfloat16)
    attn_part = matmul(mixed_heads, lax.all_gather(w_out, "dp", axis=1, tiled=True))
    attended = sum_rows(attn_part)
    hidden_one = inputs + attended
    mlp_inv = lax.rsqrt(jnp.mean(hidden_one * hidden_one, axis=1, keepdims=True) + EPSILON)
    normed_two = (hidden_one * mlp_inv * mlp_gain).astype(jnp.bfloat16)
    expert_ids = jnp.arange(experts, dtype=jnp.int32)
    route_hot = routes[:, :, None] == expert_ids[None, None, :]
    flat_hot = route_hot.astype(jnp.int32).reshape(tensor_count, own_rows * TOPK, experts)
    within = jnp.sum((jnp.cumsum(flat_hot, axis=1) - flat_hot) * flat_hot, axis=2).reshape(
        GROUP, TOPK
    )
    owner_of = (jnp.arange(GROUP, dtype=jnp.int32) // own_rows)[:, None]
    own_routes = lax.dynamic_slice_in_dim(routes, row_start, own_rows, 0)
    own_within = lax.dynamic_slice_in_dim(within, row_start, own_rows, 0)
    own_hot = lax.dynamic_slice_in_dim(route_hot, row_start, own_rows, 0)
    own_dest = own_routes * half_cap + own_within
    gate_weight = w_gate[0]
    up_weight = w_up[0]
    down_weight = w_down[0]
    normed_two_all = gather_rows(normed_two)
    gates_every, gate_every = gate_split(normed_two_all, route_hot, router)
    own_probs = lax.dynamic_slice_in_dim(gates_every, row_start, own_rows, 0)
    gate_weights = lax.dynamic_slice_in_dim(gate_every, row_start, own_rows, 0)
    destination = routes * capacity + owner_of * half_cap + within
    send_rows = (
        jnp.zeros((experts * capacity, D), jnp.bfloat16)
        .at[destination]
        .set(jnp.broadcast_to(normed_two_all[:, None, :], (GROUP, TOPK, D)))
        .reshape(experts, capacity, D)
    )
    received = lax.all_to_all(send_rows, "dp", split_axis=0, concat_axis=0, tiled=True)
    gate_pre = jnp.einsum("scd,df->scf", received, gate_weight, preferred_element_type=jnp.float32)
    up_pre = jnp.einsum("scd,df->scf", received, up_weight, preferred_element_type=jnp.float32)
    hidden = (jax.nn.silu(gate_pre) * up_pre).astype(jnp.bfloat16)
    expert_part = jnp.einsum("scf,fd->scd", hidden, down_weight, preferred_element_type=jnp.float32)
    expert_part, gate_pre, up_pre, hidden, received = (
        expert_part,
        gate_pre,
        up_pre,
        hidden,
        received,
    )
    back_rows = expert_swap(sum_slots(expert_part).astype(jnp.bfloat16)).reshape(
        experts * half_cap, D
    )
    picked = back_rows[own_dest].astype(jnp.float32)
    mixture = jnp.sum(gate_weights[:, :, None] * picked, axis=1)
    layer_out = (hidden_one + mixture).astype(jnp.bfloat16)
    upstream = cotangent.astype(jnp.float32)
    gate_grad = jnp.sum(upstream[:, None, :] * picked, axis=2)
    upstream_all = gather_rows(cotangent).astype(jnp.float32)
    send_grads = (
        jnp.zeros((experts * capacity, D), jnp.bfloat16)
        .at[destination]
        .set((gate_every[:, :, None] * upstream_all[:, None, :]).astype(jnp.bfloat16))
        .reshape(experts, capacity, D)
    )
    out_grads = expert_swap(send_grads)
    hidden_grad = jnp.einsum(
        "scd,fd->scf", out_grads, down_weight, preferred_element_type=jnp.float32
    )
    sigmoid = jax.nn.sigmoid(gate_pre)
    up_grad = (hidden_grad * gate_pre * sigmoid).astype(jnp.bfloat16)
    gate_pre_grad = (hidden_grad * up_pre * sigmoid * (1.0 + gate_pre * (1.0 - sigmoid))).astype(
        jnp.bfloat16
    )
    row_part = jnp.einsum(
        "scf,df->scd", gate_pre_grad, gate_weight, preferred_element_type=jnp.float32
    ) + jnp.einsum("scf,df->scd", up_grad, up_weight, preferred_element_type=jnp.float32)
    down_weight_grad = jnp.einsum(
        "scf,scd->fd", hidden, out_grads, preferred_element_type=jnp.float32
    )
    gate_weight_grad = jnp.einsum(
        "scd,scf->df", received, gate_pre_grad, preferred_element_type=jnp.float32
    )
    up_weight_grad = jnp.einsum(
        "scd,scf->df", received, up_grad, preferred_element_type=jnp.float32
    )
    returned_grads = expert_swap(sum_slots(row_part).astype(jnp.bfloat16)).reshape(
        experts * half_cap, D
    )
    normed_two_part = jnp.sum(returned_grads[own_dest].astype(jnp.float32), axis=1)
    expert_grad = jnp.sum(jnp.where(own_hot, gate_grad[:, :, None], 0.0), axis=1)
    logit_grad = own_probs * (expert_grad - jnp.sum(expert_grad * own_probs, axis=1, keepdims=True))
    router_grad = jnp.dot(normed_two.astype(jnp.float32).T, logit_grad, precision=HIGHEST)
    normed_two_grad = normed_two_part + jnp.dot(
        logit_grad, router.astype(jnp.float32).T, precision=HIGHEST
    )
    scaled_grad = normed_two_grad * mlp_gain
    hidden_one_grad = (
        upstream
        + mlp_inv * scaled_grad
        - hidden_one * mlp_inv**3 * jnp.mean(hidden_one * scaled_grad, axis=1, keepdims=True)
    )
    mlp_gain_grad = jnp.sum(normed_two_grad * hidden_one * mlp_inv, axis=0)
    attended_grad = gather_rows(hidden_one_grad.astype(jnp.bfloat16))
    mixed_grad = jnp.einsum(
        "gd,cd->gc",
        attended_grad,
        lax.all_gather(w_out, "dp", axis=1, tiled=True),
        preferred_element_type=jnp.float32,
    )
    mixed_grad = mixed_grad.astype(jnp.bfloat16).reshape(head_shape)
    attn_probs = jnp.exp(masked_scores() - log_total)
    prob_grad = jnp.einsum(
        "qhd,khd->hqk", mixed_grad, value_heads, preferred_element_type=jnp.float32
    )
    row_dot = jnp.sum(prob_grad * attn_probs, axis=2, keepdims=True)
    score_grad = (attn_probs * (prob_grad - row_dot)).astype(jnp.bfloat16)
    query_rot_grad = (
        jnp.einsum("hqk,khd->qhd", score_grad, key_rot, preferred_element_type=jnp.float32)
        * attn_scale
    )
    key_rot_grad = (
        jnp.einsum("hqk,qhd->khd", score_grad, query_rot, preferred_element_type=jnp.float32)
        * attn_scale
    )
    value_grad = (
        jnp.einsum(
            "hqk,qhd->khd",
            attn_probs.astype(jnp.bfloat16),
            mixed_grad,
            preferred_element_type=jnp.float32,
        )
        .reshape(GROUP, head_cols)
        .astype(jnp.bfloat16)
    )
    query_norm_grad = unrotate(query_rot_grad, cosine_table, sine_table).reshape(GROUP, head_cols)
    key_norm_grad = unrotate(key_rot_grad, cosine_table, sine_table).reshape(GROUP, head_cols)
    query_scaled = query_norm_grad * q_gain_local
    key_scaled = key_norm_grad * k_gain_local
    query_dot, key_dot = tensor_total(
        (jnp.sum(queries * query_scaled, axis=1), jnp.sum(keys_raw * key_scaled, axis=1))
    )
    query_grad = (
        query_inv * query_scaled - queries * query_inv**3 * (query_dot / D)[:, None]
    ).astype(jnp.bfloat16)
    key_grad = (key_inv * key_scaled - keys_raw * key_inv**3 * (key_dot / D)[:, None]).astype(
        jnp.bfloat16
    )
    q_gain_part = jnp.sum(query_norm_grad * queries * query_inv, axis=0)
    k_gain_part = jnp.sum(key_norm_grad * keys_raw * key_inv, axis=0)
    pieces = lax.all_gather((w_query, w_key, w_value), "dp", axis=0, tiled=True)
    normed_part = (
        jnp.einsum("gc,rc->gr", query_grad, pieces[0], preferred_element_type=jnp.float32)
        + jnp.einsum("gc,rc->gr", key_grad, pieces[1], preferred_element_type=jnp.float32)
        + jnp.einsum("gc,rc->gr", value_grad, pieces[2], preferred_element_type=jnp.float32)
    )
    weight_sums = lax.psum_scatter(
        jnp.concatenate(
            [
                jnp.einsum("gr,gc->rc", normed, query_grad, preferred_element_type=jnp.float32),
                jnp.einsum("gr,gc->rc", normed, key_grad, preferred_element_type=jnp.float32),
                jnp.einsum("gr,gc->rc", normed, value_grad, preferred_element_type=jnp.float32),
                jnp.einsum(
                    "gr,gc->rc", attended_grad, mixed_heads, preferred_element_type=jnp.float32
                ),
            ],
            axis=1,
        ),
        "dp",
        scatter_dimension=0,
        tiled=True,
    )
    normed_grad = sum_rows(normed_part)
    scaled_input = normed_grad * attn_gain
    tokens_grad = (
        hidden_one_grad
        + attn_inv * scaled_input
        - inputs * attn_inv**3 * jnp.mean(inputs * scaled_input, axis=1, keepdims=True)
    )
    attn_gain_grad = jnp.sum(normed_grad * inputs * attn_inv, axis=0)
    zero_width = jnp.zeros((D,), jnp.float32)
    q_gain_full = lax.dynamic_update_slice_in_dim(zero_width, q_gain_part, col_start, 0)
    k_gain_full = lax.dynamic_update_slice_in_dim(zero_width, k_gain_part, col_start, 0)
    attn_gain_grad, q_gain_grad, k_gain_grad, mlp_gain_grad, router_grad = lax.psum(
        (attn_gain_grad, q_gain_full, k_gain_full, mlp_gain_grad, router_grad), ("dp", "tensor")
    )
    return (
        layer_out,
        tokens_grad,
        attn_gain_grad,
        q_gain_grad,
        k_gain_grad,
        weight_sums[:, :head_cols],
        weight_sums[:, head_cols : 2 * head_cols],
        weight_sums[:, 2 * head_cols : 3 * head_cols],
        jnp.transpose(weight_sums[:, 3 * head_cols :]),
        mlp_gain_grad,
        router_grad,
        gate_weight_grad[None],
        up_weight_grad[None],
        down_weight_grad[None],
    )


MESH_ID = pl.DeviceIdType.MESH
LINK_TIME = pl.CostEstimate(flops=10**11, bytes_accessed=10**8, transcendentals=0)
EVERY = ("dp", "tensor")
LANES = 128
ANYWHERE = pl.BlockSpec(memory_space=pl.ANY)
IN_VMEM = pl.BlockSpec(memory_space=pltpu.VMEM)


class Place:
    def __init__(self):
        dp = lax.axis_index("dp")
        self.y = lax.axis_index("tensor")
        self.z, self.x, self.c = dp // 4, (dp // 2) % 2, dp % 2
        self.z_count = lax.axis_size("dp") // 4

    def device(self, z=None, x=None, c=None, y=None):
        z = self.z if z is None else z
        x = self.x if x is None else x
        c = self.c if c is None else c
        y = self.y if y is None else y
        return (z * 4 + x * 2 + c, y)

    def meet(self, use_y=True, all_z=False):
        barrier = pltpu.get_barrier_semaphore()
        partners = [self.device(x=1 - self.x), self.device(c=1 - self.c)]
        if use_y:
            partners.append(self.device(y=1 - self.y))
        if all_z:
            partners += [self.device(z=(self.z + d) % self.z_count) for d in range(1, self.z_count)]
        for partner in partners:
            pl.semaphore_signal(barrier, inc=1, device_id=partner, device_id_type=MESH_ID)
        if all_z:
            pl.semaphore_wait(barrier, len(partners))
            return

        @pl.when(self.z > 0)
        def _():
            pl.semaphore_signal(
                barrier, inc=1, device_id=self.device(z=self.z - 1), device_id_type=MESH_ID
            )

        @pl.when(self.z < self.z_count - 1)
        def _():
            pl.semaphore_signal(
                barrier, inc=1, device_id=self.device(z=self.z + 1), device_id_type=MESH_ID
            )

        ends = jnp.where(self.z > 0, 1, 0) + jnp.where(self.z < self.z_count - 1, 1, 0)
        pl.semaphore_wait(barrier, len(partners) + ends)

    def far_first(self, step):
        last = self.z_count - 1
        low = jnp.where(step < last - self.z, last - step, step - (last - self.z))
        high = jnp.where(step < self.z, step, last - (step - self.z))
        return jnp.where(self.z * 2 < self.z_count, low, high)


def send(src, dst, send_sem, recv_sem, device):
    copy = pltpu.make_async_remote_copy(
        src_ref=src, dst_ref=dst, send_sem=send_sem, recv_sem=recv_sem, device_id=device, device_id_type=MESH_ID
    )
    copy.start()
    return copy


def add_rows(total, part, rows, step=16):
    def chunk(i, carry):
        here = pl.ds(pl.multiple_of(i * step, step), step)
        total[here] = total[here] + part[here]
        return carry

    lax.fori_loop(0, rows // step, chunk, 0)


class Spread:
    ZU, ZD, XF, YF, XH, YH, CO, CX, CY, CA, CB = range(11)

    def __init__(self, place, src, whole, sent, got, kept, split=None):
        self.place, self.src, self.whole, self.sent, self.got = place, src, whole, sent, got
        rows = src.shape[0]
        split = rows // 2 if split is None else split
        self.low, self.high = pl.ds(0, split), pl.ds(split, rows - split)
        z, x, c, y = place.z, place.x, place.c, place.y
        self.up, self.down = place.device(z=z + 1), place.device(z=z - 1)
        self.over_x, self.over_y = place.device(x=1 - x), place.device(y=1 - y)
        self.over_c = place.device(c=1 - c)
        self.keep = pltpu.make_async_copy(src, whole.at[z, x, c, y], kept)

    def push(self, kind, zz, xx, yy, rows, device, origin=None):
        ref = self.whole.at[zz, xx, self.place.c, yy, rows]
        send(
            ref if origin is None else origin,
            ref,
            self.sent.at[kind, zz],
            self.got.at[kind, zz],
            device,
        )

    def arrival(self, kind, zz, xx, yy, rows=slice(None), sibling=False):
        cc = 1 - self.place.c if sibling else self.place.c
        ref = self.whole.at[zz, xx, cc, yy, rows]
        pltpu.make_async_copy(ref, ref, self.got.at[kind, zz]).wait()

    def departure(self, kind, zz, xx, yy, rows=slice(None)):
        ref = self.whole.at[zz, xx, self.place.c, yy, rows]
        pltpu.make_async_copy(ref, ref, self.sent.at[kind, zz]).wait()

    def column(self, zz, origin=None):
        x, y, every = self.place.x, self.place.y, slice(None)
        self.push(self.XF, zz, x, y, every, self.over_x, origin)
        self.push(self.YF, zz, x, y, every, self.over_y, origin)
        self.push(self.CO, zz, x, y, every, self.over_c, origin)

    def begin(self):
        z, x, y, nz = self.place.z, self.place.x, self.place.y, self.place.z_count

        @pl.when(z < nz - 1)
        def _():
            self.push(self.ZU, z, x, y, slice(None), self.up, self.src)

        @pl.when(z > 0)
        def _():
            self.push(self.ZD, z, x, y, slice(None), self.down, self.src)

        self.column(z, self.src)
        self.keep.start()

    def along_z(self, d):
        z, x, y, nz = self.place.z, self.place.x, self.place.y, self.place.z_count
        below, above = z - d, z + d

        @pl.when(below >= 0)
        def _():
            self.arrival(self.ZU, below, x, y)

            @pl.when(z < nz - 1)
            def _():
                self.push(self.ZU, below, x, y, slice(None), self.up)

        @pl.when(above < nz)
        def _():
            self.arrival(self.ZD, above, x, y)

            @pl.when(z > 0)
            def _():
                self.push(self.ZD, above, x, y, slice(None), self.down)

    def relay(self, zz):
        x, y, every = self.place.x, self.place.y, slice(None)
        self.arrival(self.XF, zz, 1 - x, y)
        self.push(self.YH, zz, 1 - x, y, self.low, self.over_y)
        self.push(self.CX, zz, 1 - x, y, every, self.over_c)
        self.arrival(self.YF, zz, x, 1 - y)
        self.push(self.XH, zz, x, 1 - y, self.high, self.over_x)
        self.push(self.CY, zz, x, 1 - y, every, self.over_c)

    def diagonal(self, zz):
        x, y = self.place.x, self.place.y
        self.arrival(self.XH, zz, 1 - x, 1 - y, self.high)
        self.push(self.CB, zz, 1 - x, 1 - y, self.high, self.over_c)
        self.arrival(self.YH, zz, 1 - x, 1 - y, self.low)
        self.push(self.CA, zz, 1 - x, 1 - y, self.low, self.over_c)

    def sibling_near(self, zz):
        x, y = self.place.x, self.place.y
        self.arrival(self.CO, zz, x, y, sibling=True)
        self.arrival(self.CY, zz, x, 1 - y, sibling=True)

    def sibling_far(self, zz):
        x, y = self.place.x, self.place.y
        self.arrival(self.CX, zz, 1 - x, y, sibling=True)
        self.arrival(self.CA, zz, 1 - x, 1 - y, self.low, sibling=True)
        self.arrival(self.CB, zz, 1 - x, 1 - y, self.high, sibling=True)

    def finish(self):
        z, x, y, nz = self.place.z, self.place.x, self.place.y, self.place.z_count

        def one(zz, carry):
            self.departure(self.XF, zz, x, y)
            self.departure(self.YF, zz, x, y)
            self.departure(self.CO, zz, x, y)
            self.departure(self.CX, zz, 1 - x, y)
            self.departure(self.CY, zz, x, 1 - y)
            self.departure(self.YH, zz, 1 - x, y, self.low)
            self.departure(self.XH, zz, x, 1 - y, self.high)
            self.departure(self.CA, zz, 1 - x, 1 - y, self.low)
            self.departure(self.CB, zz, 1 - x, 1 - y, self.high)

            @pl.when((zz <= z) & (z < nz - 1))
            def _():
                self.departure(self.ZU, zz, x, y)

            @pl.when((zz >= z) & (z > 0))
            def _():
                self.departure(self.ZD, zz, x, y)

            return carry

        lax.fori_loop(0, nz, one, 0)


class Fold:
    CD, CX, CY, CO, XH, YH, XF, YF, ZU, ZD = range(10)
    SPOT = {CD: (1, 1), CX: (1, 0), CY: (0, 1), CO: (0, 0)}

    def __init__(self, place, parts, total, from_c, half_x, half_y, z_buf, sent, got, loaded):
        self.place, self.parts, self.total, self.from_c = place, parts, total, from_c
        self.half_x, self.half_y, self.z_buf = half_x, half_y, z_buf
        self.sent, self.got, self.loaded = sent, got, loaded
        self.rows = total.shape[3]
        self.split = half_x.shape[1]
        self.low, self.high = pl.ds(0, self.split), pl.ds(self.split, self.rows - self.split)
        z, x, c, y = place.z, place.x, place.c, place.y
        self.over_x, self.over_y = place.device(x=1 - x), place.device(y=1 - y)
        self.over_c = place.device(c=1 - c)

    def push(self, kind, zz, src, dst, device):
        send(src, dst, self.sent.at[kind, zz], self.got.at[kind, zz], device)

    def arrival(self, kind, zz, ref):
        pltpu.make_async_copy(ref, ref, self.got.at[kind, zz]).wait()

    def begin(self):
        x, c, y, nz = self.place.x, self.place.c, self.place.y, self.place.z_count

        def start(kind, i):
            dx, dy = self.SPOT[kind]
            zz = self.place.far_first(i)
            xx, yy = (1 - x if dx else x), (1 - y if dy else y)
            self.push(
                kind, zz, self.parts.at[zz, xx, 1 - c, yy], self.from_c.at[dx, dy, zz], self.over_c
            )
            pltpu.make_async_copy(
                self.parts.at[zz, xx, c, yy], self.total.at[dx, dy, zz], self.loaded.at[kind, zz]
            ).start()

        for i in range(nz):
            start(self.CD, i)
            start(self.CX, i)
        for kind in (self.CY, self.CO):
            for i in range(nz):
                start(kind, i)

    def join_cores(self, kind, zz):
        dx, dy = self.SPOT[kind]
        here, there = self.total.at[dx, dy, zz], self.from_c.at[dx, dy, zz]
        pltpu.make_async_copy(here, here, self.loaded.at[kind, zz]).wait()
        self.arrival(kind, zz, there)
        add_rows(here, there, self.rows)

    def halves(self, i):
        zz = self.place.far_first(i)
        self.join_cores(self.CD, zz)
        self.join_cores(self.CX, zz)
        self.push(self.XH, zz, self.total.at[1, 1, zz, self.low], self.half_x.at[zz], self.over_x)
        self.push(self.YH, zz, self.total.at[1, 1, zz, self.high], self.half_y.at[zz], self.over_y)

    def columns(self, i):
        zz = self.place.far_first(i)
        self.join_cores(self.CY, zz)
        self.arrival(self.XH, zz, self.half_x.at[zz])
        add_rows(self.total.at[0, 1, zz, self.low], self.half_x.at[zz], self.split)
        self.arrival(self.YH, zz, self.half_y.at[zz])
        add_rows(self.total.at[1, 0, zz, self.high], self.half_y.at[zz], self.rows - self.split)
        self.push(self.XF, zz, self.total.at[1, 0, zz], self.from_c.at[1, 1, zz], self.over_x)
        self.push(self.YF, zz, self.total.at[0, 1, zz], self.from_c.at[1, 0, zz], self.over_y)

    def along_z(self, i):
        z, nz = self.place.z, self.place.z_count
        zz = self.place.far_first(i)
        mine = self.total.at[0, 0, zz]
        self.join_cores(self.CO, zz)
        self.arrival(self.XF, zz, self.from_c.at[1, 1, zz])
        add_rows(mine, self.from_c.at[1, 1, zz], self.rows)
        self.arrival(self.YF, zz, self.from_c.at[1, 0, zz])
        add_rows(mine, self.from_c.at[1, 0, zz], self.rows)
        above = jnp.where(zz == z, nz, zz)

        @pl.when((z > 0) & (zz >= z))
        def _():
            self.arrival(self.ZU, zz, self.z_buf.at[zz])
            add_rows(mine, self.z_buf.at[zz], self.rows)

        @pl.when((z < nz - 1) & (zz <= z))
        def _():
            self.arrival(self.ZD, zz, self.z_buf.at[above])
            add_rows(mine, self.z_buf.at[above], self.rows)

        @pl.when(zz > z)
        def _():
            self.push(self.ZU, zz, mine, self.z_buf.at[zz], self.place.device(z=z + 1))

        @pl.when(zz < z)
        def _():
            landing = jnp.where(zz == z - 1, nz, zz)
            self.push(self.ZD, zz, mine, self.z_buf.at[landing], self.place.device(z=z - 1))

    def result(self):
        return self.total[0, 0, self.place.z]

    def finish(self):
        z, nz = self.place.z, self.place.z_count

        def departure(kind, zz, ref):
            pltpu.make_async_copy(ref, ref, self.sent.at[kind, zz]).wait()

        def one(zz, carry):
            for kind in (self.CD, self.CX, self.CY, self.CO, self.XF, self.YF):
                departure(kind, zz, self.total.at[0, 0, zz])
            departure(self.XH, zz, self.half_x.at[zz])
            departure(self.YH, zz, self.half_y.at[zz])

            @pl.when(zz > z)
            def _():
                departure(self.ZU, zz, self.total.at[0, 0, zz])

            @pl.when(zz < z)
            def _():
                departure(self.ZD, zz, self.total.at[0, 0, zz])

            return carry

        lax.fori_loop(0, nz, one, 0)


def fold_scratch(nz, rows, cols, split, dt):
    return [
        pltpu.VMEM((2, 2, nz, rows, cols), dt),
        pltpu.VMEM((2, 2, nz, rows, cols), dt),
        pltpu.VMEM((nz, split, cols), dt),
        pltpu.VMEM((nz, rows - split, cols), dt),
        pltpu.VMEM((nz + 1, rows, cols), dt),
        pltpu.SemaphoreType.DMA((10, nz)),
        pltpu.SemaphoreType.DMA((10, nz)),
        pltpu.SemaphoreType.DMA((4, nz)),
    ]


def scatter_kernel(parts, *refs):
    streams, refs = refs[:5], refs[5:]
    out, wg_grad, wu_grad, wd_grad = refs[:4]
    tiles, tile_sems, scratch = refs[4:9], refs[9], refs[10:]
    place = Place()
    nz = place.z_count
    fold = Fold(place, parts, *scratch)
    count = streams[0].shape[0]
    place.meet()
    fold.begin()

    def loads(t, slot):
        return [
            pltpu.make_async_copy(stream.at[t], tile.at[slot], tile_sems.at[slot, n])
            for n, (stream, tile) in enumerate(zip(streams, tiles))
        ]

    def tile_step(t, carry):
        slot = t % 2
        for copy in loads(t, slot):
            copy.wait()

        @pl.when(t + 1 < count)
        def _():
            for copy in loads(t + 1, 1 - slot):
                copy.start()

        x_tile, g_tile, hidden, gate_pre_grad, up_grad = (tile[slot] for tile in tiles)
        wg_grad[...] += dot_tn(x_tile, gate_pre_grad)
        wu_grad[...] += dot_tn(x_tile, up_grad)
        wd_grad[...] += dot_tn(hidden, g_tile)
        return carry

    for copy in loads(0, 0):
        copy.start()
    for grad in (wg_grad, wu_grad, wd_grad):
        grad[...] = jnp.zeros_like(grad)
    for i in range(nz):
        fold.halves(i)
    steps = [functools.partial(fold.columns, i) for i in range(nz)]
    steps += [functools.partial(fold.along_z, i) for i in range(nz)]
    done = 0
    for n, step in enumerate(steps):
        share = (n + 1) / (2 * nz) if n < nz else 0.5 + (n - nz + 1) / (2 * nz)
        until = min(count, round(count * share))
        lax.fori_loop(done, until, tile_step, 0)
        done = until
        step()
    out[...] = fold.result()
    fold.finish()


def scatter_sum(parts, streams, collective):
    nz, _, _, _, rows, cols = parts.shape
    dt = parts.dtype
    width, units = streams[0].shape[1], streams[2].shape[1]
    tile = 256 if streams[0].shape[0] % 256 == 0 else GROUP // 2
    streams = [stream.reshape(-1, tile, stream.shape[1]) for stream in streams]
    shapes = [(width, units), (width, units), (units, width)]
    return pl.pallas_call(
        scatter_kernel,
        out_shape=[jax.ShapeDtypeStruct((rows, cols), dt)]
        + [jax.ShapeDtypeStruct(shape, jnp.float32) for shape in shapes],
        in_specs=[ANYWHERE] * 6,
        out_specs=[IN_VMEM] * 4,
        scratch_shapes=[pltpu.VMEM((2,) + stream.shape[1:], stream.dtype) for stream in streams]
        + [pltpu.SemaphoreType.DMA((2, 5))]
        + fold_scratch(nz, rows, cols, rows // 2, dt),
        cost_estimate=LINK_TIME,
        compiler_params=pltpu.CompilerParams(
            collective_id=collective, has_side_effects=True, vmem_limit_bytes=62 << 20
        ),
    )(parts, *streams)


def turn(values):
    return pltpu.roll(values, HEAD // 2, 1)


def seen_keys():
    row = lax.broadcasted_iota(jnp.int32, (GROUP, GROUP), 0)
    col = lax.broadcasted_iota(jnp.int32, (GROUP, GROUP), 1)
    return (col <= row) & ((col < PROMPT) | (col >= row - row % CONT))


def signed_rope_tables():
    cosine_table, sine_table = rope_tables()
    sign = jnp.where(jnp.arange(HEAD) < HEAD // 2, -1.0, 1.0)
    return cosine_table, sine_table * sign[None, :]


def attend_kernel(
    src,
    normed,
    w_query,
    w_key,
    w_value,
    w_out,
    q_gain,
    k_gain,
    cosine,
    sine,
    whole,
    queries,
    keys,
    values,
    q_rot,
    k_rot,
    mixed,
    q_inv,
    k_inv,
    log_total,
    attended,
    stats,
    stats_got,
    leaving,
    landed,
    swap_sems,
    sent,
    got,
    kept,
):
    place = Place()
    nz = place.z_count
    rows = leaving.shape[0]
    spread = Spread(place, src, whole, sent, got, kept, src.shape[0] // 3)
    place.meet()
    over_y = place.device(y=1 - place.y)
    spread.begin()

    def near(k):
        return place.far_first(nz - 1 - k)

    lane = lax.broadcasted_iota(jnp.int32, stats.shape, 1)
    stats[...] = jnp.zeros_like(stats)
    chunk = 2 * HEAD

    def project(i, carry):
        here = pl.ds(pl.multiple_of(i * chunk, chunk), chunk)
        for index, (weight, raw) in enumerate(((w_query, queries), (w_key, keys))):
            product = dot_nn(normed[...], weight[:, here])
            raw[:, here] = product
            squares = jnp.sum(product * product, axis=1, keepdims=True)
            stats[...] += jnp.where(lane == index, squares, 0.0)
        values[:, here] = dot_nn(normed[...], w_value[:, here]).astype(jnp.bfloat16)
        return carry

    lax.fori_loop(0, queries.shape[1] // chunk, project, 0)
    stats_swap = send(stats, stats_got, swap_sems.at[0, 0], swap_sems.at[1, 0], over_y)
    if nz > 1:
        spread.along_z(1)
        spread.column(near(1))
    spread.relay(near(0))
    stats_swap.wait()
    for index, inv in enumerate((q_inv, k_inv)):
        total = stats[:, index : index + 1] + stats_got[:, index : index + 1]
        inv[...] = lax.rsqrt(total / D + EPSILON)
    visible = seen_keys()

    def head(h, carry):
        here = pl.ds(pl.multiple_of(h * HEAD, HEAD), HEAD)
        for raw, inv, gain, rotated in ((queries, q_inv, q_gain, q_rot), (keys, k_inv, k_gain, k_rot)):
            normal = raw[:, here] * inv[...] * gain[:, here]
            rotated[:, here] = (normal * cosine[...] + turn(normal) * sine[...]).astype(jnp.bfloat16)
        scores = dot_nt(q_rot[:, here], k_rot[:, here]) * HEAD**-0.5
        scores = jnp.where(visible, scores, -1e30)
        row_max = jnp.max(scores, axis=1, keepdims=True)
        exponent = jnp.exp(scores - row_max)
        row_total = jnp.sum(exponent, axis=1, keepdims=True)
        log_total[h] = row_max + jnp.log(row_total)
        weights = (exponent / row_total).astype(jnp.bfloat16)
        mixed[:, here] = dot_nn(weights, values[:, here]).astype(jnp.bfloat16)
        return carry

    heads = queries.shape[1] // HEAD
    lax.fori_loop(0, heads // 2, head, 0)
    if nz > 2:
        spread.along_z(2)
        spread.column(near(2))
    lax.fori_loop(heads // 2, heads, head, 0)

    def joined(target, index):
        where = pl.ds(pl.multiple_of(index * rows, rows), rows)

        def columns(b, carry):
            here = pl.ds(pl.multiple_of(b * w_out.shape[2], w_out.shape[2]), w_out.shape[2])
            target[:, here] = dot_nn(mixed[where], w_out[b]).astype(target.dtype)
            return carry

        lax.fori_loop(0, w_out.shape[0], columns, 0)

    joined(leaving, 1 - place.y)
    swap = send(leaving, landed, swap_sems.at[0, 1], swap_sems.at[1, 1], over_y)
    if nz > 1:
        spread.relay(near(1))
    joined(attended, place.y)
    for d in range(3, nz):
        spread.along_z(d)
        spread.column(near(d))
    spread.diagonal(near(0))
    for k in range(2, nz):
        spread.relay(near(k))
        spread.diagonal(near(k - 1))
    if nz > 1:
        spread.diagonal(near(nz - 1))
    swap.wait()
    attended[...] += landed[...].astype(jnp.float32)
    spread.keep.wait()
    for zz in range(nz):
        spread.sibling_near(zz)
        spread.sibling_far(zz)
    spread.finish()


def attend(block, normed, weights, gains, tables, collective):
    nz = lax.axis_size("dp") // 4
    rows, width = block.shape
    group, cols = normed.shape[0], weights[0].shape[1]
    half = jax.ShapeDtypeStruct((group, cols), jnp.bfloat16)
    wide = jax.ShapeDtypeStruct((group, cols), jnp.float32)
    thin = jax.ShapeDtypeStruct((group, 1), jnp.float32)
    return pl.pallas_call(
        attend_kernel,
        out_shape=[
            jax.ShapeDtypeStruct((nz, 2, 2, 2, rows, width), block.dtype),
            wide,
            wide,
            half,
            half,
            half,
            half,
            thin,
            thin,
            jax.ShapeDtypeStruct((cols // HEAD, group, 1), jnp.float32),
            jax.ShapeDtypeStruct((rows, width), jnp.float32),
        ],
        in_specs=[ANYWHERE] + [IN_VMEM] * 9,
        out_specs=[ANYWHERE] + [IN_VMEM] * 10,
        scratch_shapes=[
            pltpu.VMEM((group, LANES), jnp.float32),
            pltpu.VMEM((group, LANES), jnp.float32),
            pltpu.VMEM((rows, width), jnp.bfloat16),
            pltpu.VMEM((rows, width), jnp.bfloat16),
            pltpu.SemaphoreType.DMA((2, 2)),
            pltpu.SemaphoreType.DMA((11, nz)),
            pltpu.SemaphoreType.DMA((11, nz)),
            pltpu.SemaphoreType.DMA,
        ],
        cost_estimate=LINK_TIME,
        compiler_params=pltpu.CompilerParams(
            collective_id=collective, has_side_effects=True, vmem_limit_bytes=60 << 20
        ),
    )(block, normed, *weights, *gains, *tables)


def attend_back_kernel(
    parts,
    own_grad,
    w_out,
    queries,
    keys,
    q_rot,
    k_rot,
    values,
    q_inv,
    k_inv,
    log_total,
    q_gain,
    k_gain,
    cosine,
    sine,
    mixture,
    attended_grad,
    q_grad,
    k_grad,
    v_grad,
    gain_grads,
    landed,
    mixed_grad,
    q_scaled,
    k_scaled,
    dots,
    dots_got,
    swap_sems,
    *scratch,
):
    place = Place()
    nz = place.z_count
    fold = Fold(place, parts, *scratch)
    place.meet()
    over_y = place.device(y=1 - place.y)
    rows = own_grad.shape[0]
    swap = send(own_grad, landed, swap_sems.at[0, 0], swap_sems.at[1, 0], over_y)
    fold.begin()

    def take(block, index):
        where = pl.ds(pl.multiple_of(index * rows, rows), rows)
        attended_grad[where] = block[...]
        step = w_out.shape[2]

        def columns(b, total):
            here = pl.ds(pl.multiple_of(b * step, step), step)
            return total + dot_nt(block[:, here], w_out[b])

        total = jnp.zeros((rows, mixed_grad.shape[1]), jnp.float32)
        total = lax.fori_loop(0, w_out.shape[0], columns, total)
        mixed_grad[where] = total.astype(jnp.bfloat16)

    take(own_grad, place.y)
    for i in range(nz):
        fold.halves(i)
    swap.wait()
    take(landed, 1 - place.y)
    visible = seen_keys()
    lane = lax.broadcasted_iota(jnp.int32, dots.shape, 1)
    dots[...] = jnp.zeros_like(dots)

    def head(h, carry):
        here = pl.ds(pl.multiple_of(h * HEAD, HEAD), HEAD)
        upstream = mixed_grad[:, here]
        scores = dot_nt(q_rot[:, here], k_rot[:, here]) * HEAD**-0.5
        probs = jnp.exp(jnp.where(visible, scores, -1e30) - log_total[h])
        prob_grad = dot_nt(upstream, values[:, here])
        row_dot = jnp.sum(prob_grad * probs, axis=1, keepdims=True)
        score_grad = (probs * (prob_grad - row_dot)).astype(jnp.bfloat16)
        v_grad[:, here] = dot_tn(probs.astype(jnp.bfloat16), upstream).astype(jnp.bfloat16)
        for index, (rot_grad, raw, inv, gain, scaled) in enumerate(
            (
                (dot_nn(score_grad, k_rot[:, here]), queries, q_inv, q_gain, q_scaled),
                (dot_tn(score_grad, q_rot[:, here]), keys, k_inv, k_gain, k_scaled),
            )
        ):
            rot_grad = rot_grad * HEAD**-0.5
            norm_grad = rot_grad * cosine[...] - turn(rot_grad) * sine[...]
            with_raw = norm_grad * raw[:, here]
            gain_grads[index : index + 1, here] = jnp.sum(with_raw * inv[...], axis=0, keepdims=True)
            scaled[:, here] = norm_grad * gain[:, here]
            part = jnp.sum(with_raw * gain[:, here], axis=1, keepdims=True)
            dots[...] += jnp.where(lane == index, part, 0.0)
        return carry

    heads = queries.shape[1] // HEAD
    cuts = [heads * (i + 1) // nz for i in range(nz)]
    for i in range(nz):
        fold.columns(i)
        lax.fori_loop(cuts[i - 1] if i else 0, cuts[i], head, 0)
    dots_swap = send(dots, dots_got, swap_sems.at[0, 1], swap_sems.at[1, 1], over_y)
    for i in range(nz):
        fold.along_z(i)
    mixture[...] = fold.result()
    dots_swap.wait()

    def grads(h, carry):
        here = pl.ds(pl.multiple_of(h * HEAD, HEAD), HEAD)
        for index, (raw, inv, scaled, grad) in enumerate(
            ((queries, q_inv, q_scaled, q_grad), (keys, k_inv, k_scaled, k_grad))
        ):
            mean = (dots[:, index : index + 1] + dots_got[:, index : index + 1]) / D
            scale = inv[...]
            grad[:, here] = (
                scale * scaled[:, here] - raw[:, here] * (scale * scale * scale * mean)
            ).astype(jnp.bfloat16)
        return carry

    lax.fori_loop(0, heads, grads, 0)
    fold.finish()


def attend_back(parts, own_grad, w_out, saved, gains, tables, collective):
    nz, _, _, _, rows, cols = parts.shape
    queries = saved[0]
    group, head_cols = queries.shape
    half = jax.ShapeDtypeStruct((group, head_cols), jnp.bfloat16)
    wide = pltpu.VMEM((group, head_cols), jnp.float32)
    split = rows * 2 // 3
    return pl.pallas_call(
        attend_back_kernel,
        out_shape=[
            jax.ShapeDtypeStruct((rows, cols), jnp.bfloat16),
            jax.ShapeDtypeStruct((group, cols), jnp.bfloat16),
            half,
            half,
            half,
            jax.ShapeDtypeStruct((8, head_cols), jnp.float32),
        ],
        in_specs=[ANYWHERE] + [IN_VMEM] * 14,
        out_specs=[IN_VMEM] * 6,
        scratch_shapes=[
            pltpu.VMEM((rows, cols), jnp.bfloat16),
            pltpu.VMEM((group, head_cols), jnp.bfloat16),
            wide,
            wide,
            pltpu.VMEM((group, LANES), jnp.float32),
            pltpu.VMEM((group, LANES), jnp.float32),
            pltpu.SemaphoreType.DMA((2, 2)),
        ]
        + fold_scratch(nz, rows, cols, split, parts.dtype),
        cost_estimate=LINK_TIME,
        compiler_params=pltpu.CompilerParams(
            collective_id=collective, has_side_effects=True, vmem_limit_bytes=62 << 20
        ),
    )(parts, own_grad, w_out, *saved, *gains, *tables)


def plane_gather_kernel(count, *refs):
    srcs, block = refs[:count], refs[count]
    outs, landed = refs[count + 1 : 2 * count + 1], refs[2 * count + 1]
    sent, got, kept, swap_sems = refs[2 * count + 2 :]
    place = Place()
    z, x, c, nz = place.z, place.x, place.c, place.z_count
    ZU, ZD, XF, CO, CX = range(5)
    up, down = place.device(z=z + 1), place.device(z=z - 1)
    over_x, over_c = place.device(x=1 - x), place.device(c=1 - c)
    place.meet()
    every = range(count)
    swap = send(block, landed, swap_sems.at[0], swap_sems.at[1], place.device(y=1 - place.y))

    def push(a, kind, zz, xx, device, own=False):
        ref = outs[a].at[zz, xx, c]
        send(srcs[a] if own else ref, ref, sent.at[kind, a, zz], got.at[kind, a, zz], device)

    def arrival(a, kind, zz, xx, cc):
        ref = outs[a].at[zz, xx, cc]
        pltpu.make_async_copy(ref, ref, got.at[kind, a, zz]).wait()

    def departure(a, kind, zz, xx):
        ref = outs[a].at[zz, xx, c]
        pltpu.make_async_copy(ref, ref, sent.at[kind, a, zz]).wait()

    keeps = []
    for a in every:
        push(a, XF, z, x, over_x, own=True)

        @pl.when(z < nz - 1)
        def _():
            push(a, ZU, z, x, up, own=True)

        @pl.when(z > 0)
        def _():
            push(a, ZD, z, x, down, own=True)

        push(a, CO, z, x, over_c, own=True)
        keep = pltpu.make_async_copy(srcs[a], outs[a].at[z, x, c], kept.at[a])
        keep.start()
        keeps.append(keep)

    def relay(a, zz):
        arrival(a, XF, zz, 1 - x, c)
        push(a, CX, zz, 1 - x, over_c)

    for d in range(nz):
        below, above = z - d - 1, z + d + 1
        for a in every:
            if d < nz - 1:
                @pl.when(below >= 0)
                def _():
                    arrival(a, ZU, below, x, c)

                    @pl.when(z < nz - 1)
                    def _():
                        push(a, ZU, below, x, up)

                    push(a, XF, below, x, over_x)
                    push(a, CO, below, x, over_c)

                @pl.when(above < nz)
                def _():
                    arrival(a, ZD, above, x, c)

                    @pl.when(z > 0)
                    def _():
                        push(a, ZD, above, x, down)

                    push(a, XF, above, x, over_x)
                    push(a, CO, above, x, over_c)

    for d in range(nz):
        for a in every:
            if d == 0:
                relay(a, z)
            else:
                @pl.when(z - d >= 0)
                def _():
                    relay(a, z - d)

                @pl.when(z + d < nz)
                def _():
                    relay(a, z + d)

    for a in every:
        keeps[a].wait()
        for zz in range(nz):
            arrival(a, CO, zz, x, 1 - c)
            arrival(a, CX, zz, 1 - x, 1 - c)
            departure(a, XF, zz, x)
            departure(a, CO, zz, x)
            departure(a, CX, zz, 1 - x)

            @pl.when((zz <= z) & (z < nz - 1))
            def _():
                departure(a, ZU, zz, x)

            @pl.when((zz >= z) & (z > 0))
            def _():
                departure(a, ZD, zz, x)

    swap.wait()


def gather_in_plane(shards, block, collective):
    nz = lax.axis_size("dp") // 4
    count = len(shards)
    return pl.pallas_call(
        functools.partial(plane_gather_kernel, count),
        out_shape=[jax.ShapeDtypeStruct((nz, 2, 2) + s.shape, s.dtype) for s in shards]
        + [jax.ShapeDtypeStruct(block.shape, block.dtype)],
        in_specs=[ANYWHERE] * (count + 1),
        out_specs=[ANYWHERE] * (count + 1),
        scratch_shapes=[
            pltpu.SemaphoreType.DMA((5, count, nz)),
            pltpu.SemaphoreType.DMA((5, count, nz)),
            pltpu.SemaphoreType.DMA((count,)),
            pltpu.SemaphoreType.DMA((2,)),
        ],
        cost_estimate=LINK_TIME,
        compiler_params=pltpu.CompilerParams(collective_id=collective, has_side_effects=True),
    )(*shards, block)


def plane_scatter_kernel(count, *refs):
    lefts, rights = refs[:count], refs[count : 2 * count]
    small, row_part = refs[2 * count : 2 * count + 2]
    refs = refs[2 * count + 2 :]
    outs, small_out, row_landed = refs[:count], refs[count], refs[count + 1]
    total, leaving, from_c, full_x, z_buf, small_sum, small_got = refs[count + 2 : count + 9]
    sent, got, small_sems, row_sems = refs[count + 9 :]
    place = Place()
    z, x, c, nz = place.z, place.x, place.c, place.z_count
    rows = total.shape[3]
    C0, C1, XF, ZU, ZD = range(5)
    over_x, over_c = place.device(x=1 - x), place.device(c=1 - c)
    over_y = place.device(y=1 - place.y)
    place.meet(all_z=True)

    small_sum[0] = small[...]

    def small_start(i):
        return send(
            small_sum.at[i],
            small_got.at[i],
            small_sems.at[0, i],
            small_sems.at[1, i],
            (over_x, over_c, over_y)[i],
        )

    def small_end(i, copy):
        copy.wait()
        small_sum[i + 1] = small_sum[i] + small_got[i]

    def small_z_start():
        return [
            send(
                small_sum.at[3],
                small_got.at[2 + d],
                small_sems.at[0, 2 + d],
                small_sems.at[1, 2 + d],
                place.device(z=(z + d) % nz),
            )
            for d in range(1, nz)
        ]

    def small_z_end(copies):
        for copy in copies:
            copy.wait()
        result = jnp.zeros_like(small_out)
        for zz in range(nz):
            away = (z - zz) % nz
            result = result + jnp.where(away == 0, small_sum[3], small_got[jnp.maximum(2 + away, 3)])
        small_out[...] = result

    def arrival(a, kind, zz, ref):
        pltpu.make_async_copy(ref, ref, got.at[kind, a, zz]).wait()

    small_copy = small_start(0)

    def make(dx, i):
        zz = place.far_first(i)
        xx = 1 - x if dx else x
        for a in range(count):

            def product(cc):
                shard = (zz * 2 + xx) * 2 + cc
                here = pl.ds(pl.multiple_of(shard * rows, rows), rows)
                return dot_tn(lefts[a][:, here], rights[a][...]).astype(total.dtype)

            leaving[dx, zz, a] = product(1 - c)
            send(
                leaving.at[dx, zz, a],
                from_c.at[dx, zz, a],
                sent.at[C1 if dx else C0, a, zz],
                got.at[C1 if dx else C0, a, zz],
                over_c,
            )
            total[dx, zz, a] = product(c)

    def join_cores(a, dx, zz):
        there = from_c.at[dx, zz, a]
        arrival(a, C1 if dx else C0, zz, there)
        add_rows(total.at[dx, zz, a], there, rows)

    def over_the_x(i):
        zz = place.far_first(i)
        for a in range(count):
            join_cores(a, 1, zz)
            send(total.at[1, zz, a], full_x.at[zz, a], sent.at[XF, a, zz], got.at[XF, a, zz], over_x)

    def along_z(i):
        zz = place.far_first(i)
        above = jnp.where(zz == z, nz, zz)
        landing = jnp.where(zz == z - 1, nz, zz)
        for a in range(count):
            mine = total.at[0, zz, a]
            join_cores(a, 0, zz)
            arrival(a, XF, zz, full_x.at[zz, a])
            add_rows(mine, full_x.at[zz, a], rows)

            @pl.when((z > 0) & (zz >= z))
            def _():
                arrival(a, ZU, zz, z_buf.at[zz, a])
                add_rows(mine, z_buf.at[zz, a], rows)

            @pl.when((z < nz - 1) & (zz <= z))
            def _():
                arrival(a, ZD, zz, z_buf.at[above, a])
                add_rows(mine, z_buf.at[above, a], rows)

            @pl.when(zz > z)
            def _():
                send(
                    mine,
                    z_buf.at[zz, a],
                    sent.at[ZU, a, zz],
                    got.at[ZU, a, zz],
                    place.device(z=z + 1),
                )

            @pl.when(zz < z)
            def _():
                send(
                    mine,
                    z_buf.at[landing, a],
                    sent.at[ZD, a, zz],
                    got.at[ZD, a, zz],
                    place.device(z=z - 1),
                )

    make(1, 0)
    row_copy = send(row_part, row_landed, row_sems.at[0], row_sems.at[1], over_y)
    small_end(0, small_copy)
    small_copy = small_start(1)
    for i in range(1, nz):
        make(1, i)
        over_the_x(i - 1)
        if i == 1:
            small_end(1, small_copy)
            small_copy = small_start(2)
    over_the_x(nz - 1)

    def own_chips(i, carry):
        make(0, i)
        return carry

    lax.fori_loop(0, nz, own_chips, 0)
    small_end(2, small_copy)
    small_copies = small_z_start()
    for i in range(nz):
        along_z(i)
        if i == 0:
            small_z_end(small_copies)
    row_copy.wait()

    for a in range(count):

        def widen(i, carry):
            here = pl.ds(pl.multiple_of(i * 16, 16), 16)
            outs[a][here] = total[0, z, a, here].astype(jnp.float32)
            return carry

        lax.fori_loop(0, rows // 16, widen, 0)

    def departure(a, kind, zz):
        ref = total.at[0, 0, a]
        pltpu.make_async_copy(ref, ref, sent.at[kind, a, zz]).wait()

    for a in range(count):
        for zz in range(nz):
            departure(a, C0, zz)
            departure(a, C1, zz)
            departure(a, XF, zz)

            @pl.when(zz > z)
            def _():
                departure(a, ZU, zz)

            @pl.when(zz < z)
            def _():
                departure(a, ZD, zz)


def scatter_in_plane(lefts, rights, small, row_part, collective):
    count = len(lefts)
    nz = lax.axis_size("dp") // 4
    cols, dt = rights[0].shape[1], rights[0].dtype
    rows = lefts[0].shape[1] // (4 * nz)
    blocks = pltpu.VMEM((2, nz, count, rows, cols), dt)
    return pl.pallas_call(
        functools.partial(plane_scatter_kernel, count),
        out_shape=[jax.ShapeDtypeStruct((rows, cols), jnp.float32)] * count
        + [
            jax.ShapeDtypeStruct(small.shape, small.dtype),
            jax.ShapeDtypeStruct(row_part.shape, row_part.dtype),
        ],
        in_specs=[IN_VMEM] * (2 * count + 1) + [ANYWHERE],
        out_specs=[IN_VMEM] * (count + 1) + [ANYWHERE],
        scratch_shapes=[
            blocks,
            blocks,
            blocks,
            pltpu.VMEM((nz, count, rows, cols), dt),
            pltpu.VMEM((nz + 1, count, rows, cols), dt),
            pltpu.VMEM((4,) + small.shape, small.dtype),
            pltpu.VMEM((2 + nz,) + small.shape, small.dtype),
            pltpu.SemaphoreType.DMA((5, count, nz)),
            pltpu.SemaphoreType.DMA((5, count, nz)),
            pltpu.SemaphoreType.DMA((2, 2 + nz)),
            pltpu.SemaphoreType.DMA((2,)),
        ],
        cost_estimate=LINK_TIME,
        compiler_params=pltpu.CompilerParams(
            collective_id=collective, has_side_effects=True, vmem_limit_bytes=62 << 20
        ),
    )(*lefts, *rights, small, row_part)


def dot_nn(a, b):
    return lax.dot_general(a, b, (((1,), (0,)), ((), ())), preferred_element_type=jnp.float32)


def dot_nt(a, b):
    return lax.dot_general(a, b, (((1,), (1,)), ((), ())), preferred_element_type=jnp.float32)


def dot_tn(a, b):
    return lax.dot_general(a, b, (((0,), (0,)), ((), ())), preferred_element_type=jnp.float32)


def pick(table, index):
    return sum(jnp.where(index == i, value, 0) for i, value in enumerate(table))


def expert_kernel(
    z_count,
    src,
    g_all,
    hot_ref,
    router_ref,
    lanes_ref,
    wg_ref,
    wu_ref,
    wd_ref,
    x_all,
    y_all,
    r_all,
    hidden_all,
    gate_pre_grad_all,
    up_grad_all,
    x_tile,
    g_tile,
    y_tile,
    r_tile,
    hidden_tile,
    gate_pre_grad_tile,
    up_grad_tile,
    load_sems,
    store_sems,
    sent,
    got,
    kept,
):
    place = Place()
    place.meet()
    spread = Spread(place, src, x_all, sent, got, kept)
    spread.begin()
    width = src.shape[1]
    tile = x_tile.shape[1]
    pairs = sorted(
        ((k, dx) for k in range(z_count) for dx in (0, 1)), key=lambda p: p[0] + 1.3 * p[1]
    )
    tiles = 2 * len(pairs)
    near_table, across_table = [p[0] for p in pairs], [p[1] for p in pairs]

    def near(k):
        return place.far_first(z_count - 1 - k)

    def tile_at(i):
        pair, second = i // 2, i % 2
        zz = near(pick(near_table, pair))
        xx = jnp.where(pick(across_table, pair) == 1, 1 - place.x, place.x)
        cc = jnp.where(second == 1, 1 - place.c, place.c)
        return zz, xx, cc

    stores = (
        (y_tile, y_all),
        (r_tile, r_all),
        (hidden_tile, hidden_all),
        (gate_pre_grad_tile, gate_pre_grad_all),
        (up_grad_tile, up_grad_all),
    )

    def loads(i, slot):
        zz, xx, cc = tile_at(i)
        copies = []
        for yy in range(2):
            rows = pl.ds(yy * (tile // 2), tile // 2)
            copies.append(
                pltpu.make_async_copy(
                    x_all.at[zz, xx, cc, yy], x_tile.at[slot, rows], load_sems.at[slot, yy]
                )
            )
        copies.append(
            pltpu.make_async_copy(g_all.at[zz, xx, cc], g_tile.at[slot], load_sems.at[slot, 2])
        )
        return copies

    def store(i, slot):
        zz, xx, cc = tile_at(i)
        return [
            pltpu.make_async_copy(here.at[slot], there.at[zz, xx, cc], store_sems.at[slot, n])
            for n, (here, there) in enumerate(stores)
        ]

    steps = {}
    for position, (k, dx) in enumerate(pairs):
        todo = []
        if dx == 0:
            if k + 1 < z_count:
                todo += [("z", k + 1), ("column", k + 1)]
            todo.append(("relay", k))
        else:
            todo.append(("diagonal", k))
        steps[2 * position] = todo

    def prepare(i):
        for position in range(tiles):
            pair = position // 2
            k, dx = pairs[pair]

            @pl.when(i == position)
            def _():
                if position % 2 == 0:
                    for kind, number in steps[position]:
                        if kind == "z":
                            spread.along_z(number)
                        elif kind == "column":
                            spread.column(near(number))
                        elif kind == "relay":
                            spread.relay(near(number))
                        else:
                            spread.diagonal(near(number))
                    if position == 0:
                        spread.keep.wait()
                elif dx == 0:
                    spread.sibling_near(near(k))
                else:
                    spread.sibling_far(near(k))

        for copy in loads(i, i % 2):
            copy.start()

    def compute(i, carry):
        slot = i % 2
        for copy in loads(i, slot):
            copy.wait()

        @pl.when(i >= 2)
        def _():
            for copy in store(i - 2, slot):
                copy.wait()

        zz, xx, cc = tile_at(i)
        rows = x_tile[slot]
        logits = jnp.where(lanes_ref[1:2] > 0.0, dot_nn(rows, router_ref[...]), -1e30)
        weights = jnp.exp(logits - jnp.max(logits, axis=1, keepdims=True))
        own_weight = jnp.sum(weights * lanes_ref[0:1], axis=1, keepdims=True)
        named = jnp.transpose(hot_ref[(zz * 2 + xx) * 2 + cc].astype(jnp.float32))
        hot = jnp.sum(named * lanes_ref[0:1, : named.shape[1]], axis=1, keepdims=True)
        gate = hot * own_weight / jnp.sum(weights, axis=1, keepdims=True)
        gate_pre = dot_nn(rows, wg_ref[...])
        up_pre = dot_nn(rows, wu_ref[...])
        raw_grad = dot_nt(g_tile[slot], wd_ref[...])

        @pl.when(i < tiles - 1)
        def _():
            prepare(i + 1)

        sigmoid = jax.nn.sigmoid(gate_pre)
        silu = gate_pre * sigmoid
        hidden = silu * up_pre
        gate_grad = jnp.sum(hidden * raw_grad, axis=1, keepdims=True)
        coarse = gate_grad.astype(jnp.bfloat16).astype(jnp.float32)
        r_tile[slot, :, width:] = (
            coarse * lanes_ref[2:3] + (gate_grad - coarse) * lanes_ref[3:4]
        ).astype(jnp.bfloat16)
        hidden_gated = (gate * hidden).astype(jnp.bfloat16)
        hidden_tile[slot] = hidden_gated
        hidden_grad = gate * raw_grad
        up_grad = (hidden_grad * silu).astype(jnp.bfloat16)
        up_grad_tile[slot] = up_grad
        gate_pre_grad = (
            hidden_grad * up_pre * sigmoid * (1.0 + gate_pre * (1.0 - sigmoid))
        ).astype(jnp.bfloat16)
        gate_pre_grad_tile[slot] = gate_pre_grad
        y_tile[slot] = dot_nn(hidden_gated, wd_ref[...]).astype(jnp.bfloat16)
        r_tile[slot, :, :width] = (
            dot_nt(gate_pre_grad, wg_ref[...]) + dot_nt(up_grad, wu_ref[...])
        ).astype(jnp.bfloat16)
        for copy in store(i, slot):
            copy.start()
        return carry

    prepare(0)
    lax.fori_loop(0, tiles, compute, 0)
    for i in (tiles - 2, tiles - 1):
        for copy in store(i, i % 2):
            copy.wait()
    spread.finish()


def expert_pass(block, upstream, hot, router, lanes, w_gate, w_up, w_down, collective):
    rows, width = block.shape
    units = w_gate.shape[1]
    nz = lax.axis_size("dp") // 4
    tile = 2 * rows
    out = (nz, 2, 2, tile)
    return pl.pallas_call(
        functools.partial(expert_kernel, nz),
        in_specs=[ANYWHERE] * 2 + [IN_VMEM] * 6,
        out_specs=[ANYWHERE] * 6,
        out_shape=[
            jax.ShapeDtypeStruct((nz, 2, 2, 2, rows, width), jnp.bfloat16),
            jax.ShapeDtypeStruct(out + (width,), jnp.bfloat16),
            jax.ShapeDtypeStruct(out + (width + LANES,), jnp.bfloat16),
        ]
        + [jax.ShapeDtypeStruct(out + (units,), jnp.bfloat16)] * 3,
        scratch_shapes=[
            pltpu.VMEM((2, tile, width), jnp.bfloat16),
            pltpu.VMEM((2, tile, width), jnp.bfloat16),
            pltpu.VMEM((2, tile, width), jnp.bfloat16),
            pltpu.VMEM((2, tile, width + LANES), jnp.bfloat16),
            pltpu.VMEM((2, tile, units), jnp.bfloat16),
            pltpu.VMEM((2, tile, units), jnp.bfloat16),
            pltpu.VMEM((2, tile, units), jnp.bfloat16),
            pltpu.SemaphoreType.DMA((2, 3)),
            pltpu.SemaphoreType.DMA((2, 5)),
            pltpu.SemaphoreType.DMA((11, nz)),
            pltpu.SemaphoreType.DMA((11, nz)),
            pltpu.SemaphoreType.DMA,
        ],
        cost_estimate=LINK_TIME,
        compiler_params=pltpu.CompilerParams(
            collective_id=collective, has_side_effects=True, vmem_limit_bytes=60 << 20
        ),
    )(block, upstream.reshape(out + (width,)), hot, router, lanes, w_gate, w_up, w_down)


def dense_body(
    tokens,
    routes,
    cotangent,
    attn_gain,
    q_gain,
    k_gain,
    w_query,
    w_key,
    w_value,
    w_out,
    mlp_gain,
    router,
    w_gate,
    w_up,
    w_down,
):
    rank_index = lax.axis_index("tensor")
    own_rows = tokens.shape[0]
    head_cols = w_query.shape[1]
    col_start = rank_index * head_cols
    row_start = rank_index * own_rows
    experts = router.shape[1]
    q_gain_local = lax.dynamic_slice_in_dim(q_gain, col_start, head_cols)
    k_gain_local = lax.dynamic_slice_in_dim(k_gain, col_start, head_cols)
    expert_ids = jnp.arange(experts, dtype=jnp.int32)
    named = jnp.any(routes[None] == expert_ids[:, None, None], axis=2).astype(jnp.bfloat16)
    q_all, k_all, v_all, o_all, hot, other_tokens = gather_in_plane(
        (w_query, w_key, w_value, w_out, named), tokens, 1
    )
    hot = hot.reshape(-1, *named.shape)
    q_all, k_all, v_all = (w.reshape(D, head_cols) for w in (q_all, k_all, v_all))
    o_all = o_all.reshape(-1, *w_out.shape)
    first = rank_index == 0
    inputs_both = jnp.concatenate(
        [jnp.where(first, tokens, other_tokens), jnp.where(first, other_tokens, tokens)], axis=0
    ).astype(jnp.float32)
    unit_both = inputs_both * lax.rsqrt(
        jnp.mean(inputs_both * inputs_both, axis=1, keepdims=True) + EPSILON
    )
    normed = (unit_both * attn_gain).astype(jnp.bfloat16)
    inputs = tokens.astype(jnp.float32)
    attn_inv = lax.rsqrt(jnp.mean(inputs * inputs, axis=1, keepdims=True) + EPSILON)
    own_expert = lax.axis_index("dp")
    lane = jnp.arange(LANES)
    marked = own_expert + experts * rank_index
    lanes = jnp.stack(
        [lane == own_expert, lane < experts, lane == marked, lane == marked + 2 * experts]
        + [lane < 0] * 4
    ).astype(jnp.float32)
    router_wide = jnp.pad(router, ((0, 0), (0, LANES - experts)))
    tables = signed_rope_tables()
    gains = (q_gain_local[None], k_gain_local[None])
    (
        upstream_all,
        queries,
        keys_raw,
        values,
        query_rot,
        key_rot,
        mixed_heads,
        query_inv,
        key_inv,
        log_total,
        attended,
    ) = attend(cotangent, normed, (q_all, k_all, v_all, o_all), gains, tables, 6)
    upstream_all = upstream_all.reshape(-1, D)
    hidden_one = inputs + attended
    mlp_inv = lax.rsqrt(jnp.mean(hidden_one * hidden_one, axis=1, keepdims=True) + EPSILON)
    normed_two = (hidden_one * mlp_inv * mlp_gain).astype(jnp.bfloat16)
    own_routes = lax.dynamic_slice_in_dim(routes, row_start, own_rows, 0)
    own_hot = jnp.any(own_routes[:, :, None] == expert_ids[None, None, :], axis=1)
    own_probs = jax.nn.softmax(matmul(normed_two, router), axis=1)
    rows_all, y_part, r_part, *for_weights = expert_pass(
        normed_two, upstream_all, hot, router_wide, lanes, w_gate[0], w_up[0], w_down[0], 2
    )
    rows_all, y_part = rows_all.reshape(-1, D), y_part.reshape(-1, D)
    for_weights = [array.reshape(rows_all.shape[0], -1) for array in for_weights]
    blocks = (lax.axis_size("dp") // 4, 2, 2, 2, own_rows)
    returned, gate_weight_grad, up_weight_grad, down_weight_grad = scatter_sum(
        r_part.reshape(*blocks, D + LANES), [rows_all, upstream_all, *for_weights], 3
    )
    expert_grad = jnp.sum(
        returned[:, D : D + 4 * experts].astype(jnp.float32).reshape(own_rows, 4, experts), axis=1
    )
    expert_grad = jnp.where(own_hot, expert_grad, 0.0)
    returned = returned[:, :D]
    upstream = cotangent.astype(jnp.float32)
    logit_grad = own_probs * (expert_grad - jnp.sum(expert_grad * own_probs, axis=1, keepdims=True))
    router_grad = jnp.dot(normed_two.astype(jnp.float32).T, logit_grad, precision=HIGHEST)
    normed_two_grad = returned.astype(jnp.float32) + jnp.dot(
        logit_grad, router.astype(jnp.float32).T, precision=HIGHEST
    )
    scaled_grad = normed_two_grad * mlp_gain
    hidden_one_grad = (
        upstream
        + mlp_inv * scaled_grad
        - hidden_one * mlp_inv**3 * jnp.mean(hidden_one * scaled_grad, axis=1, keepdims=True)
    )
    mlp_gain_grad = jnp.sum(normed_two_grad * hidden_one * mlp_inv, axis=0)
    saved = (queries, keys_raw, query_rot, key_rot, values, query_inv, key_inv, log_total)
    mixture, attended_grad, query_grad, key_grad, value_grad, gain_grads = attend_back(
        y_part.reshape(*blocks, D), hidden_one_grad.astype(jnp.bfloat16), o_all, saved, gains, tables, 7
    )
    layer_out = (hidden_one + mixture.astype(jnp.float32)).astype(jnp.bfloat16)
    q_gain_part, k_gain_part = gain_grads[0], gain_grads[1]
    normed_part = (
        jnp.einsum("gc,rc->gr", query_grad, q_all, preferred_element_type=jnp.float32)
        + jnp.einsum("gc,rc->gr", key_grad, k_all, preferred_element_type=jnp.float32)
        + jnp.einsum("gc,rc->gr", value_grad, v_all, preferred_element_type=jnp.float32)
    )
    attn_gain_grad = jnp.sum(normed_part * unit_both, axis=0)
    zero_width = jnp.zeros((D,), jnp.float32)
    q_gain_full = lax.dynamic_update_slice_in_dim(zero_width, q_gain_part, col_start, 0)
    k_gain_full = lax.dynamic_update_slice_in_dim(zero_width, k_gain_part, col_start, 0)
    small_grads = jnp.concatenate(
        [
            jnp.stack([attn_gain_grad, q_gain_full, k_gain_full, mlp_gain_grad]),
            jnp.zeros((4, D), jnp.float32),
            jnp.transpose(router_grad),
        ],
        axis=0,
    )
    row_part = lax.dynamic_slice_in_dim(
        normed_part, (1 - rank_index) * own_rows, own_rows, 0
    ).astype(jnp.bfloat16)
    own_part = lax.dynamic_slice_in_dim(normed_part, row_start, own_rows, 0)
    *weight_sums, small_sums, other_part = scatter_in_plane(
        (normed, normed, normed, attended_grad),
        (query_grad, key_grad, value_grad, mixed_heads),
        small_grads,
        row_part,
        4,
    )
    normed_grad = own_part + other_part.astype(jnp.float32)
    scaled_input = normed_grad * attn_gain
    tokens_grad = (
        hidden_one_grad
        + attn_inv * scaled_input
        - inputs * attn_inv**3 * jnp.mean(inputs * scaled_input, axis=1, keepdims=True)
    )
    attn_gain_grad, q_gain_grad, k_gain_grad, mlp_gain_grad = (small_sums[i] for i in range(4))
    router_grad = jnp.transpose(small_sums[8:])
    return (
        layer_out,
        tokens_grad,
        attn_gain_grad,
        q_gain_grad,
        k_gain_grad,
        weight_sums[0],
        weight_sums[1],
        weight_sums[2],
        jnp.transpose(weight_sums[3]),
        mlp_gain_grad,
        router_grad,
        gate_weight_grad[None],
        up_weight_grad[None],
        down_weight_grad[None],
    )


def solution(mesh):
    in_specs = (
        P(("dp", "tensor"), None),
        P("dp", None),
        P(("dp", "tensor"), None),
        P(),
        P(),
        P(),
        P("dp", "tensor"),
        P("dp", "tensor"),
        P("dp", "tensor"),
        P("tensor", "dp"),
        P(),
        P(),
        P("dp", None, "tensor"),
        P("dp", None, "tensor"),
        P("dp", "tensor", None),
    )
    out_specs = (
        P(("dp", "tensor"), None),
        P(("dp", "tensor"), None),
        P(),
        P(),
        P(),
        P("dp", "tensor"),
        P("dp", "tensor"),
        P("dp", "tensor"),
        P("tensor", "dp"),
        P(),
        P(),
        P("dp", None, "tensor"),
        P("dp", None, "tensor"),
        P("dp", "tensor", None),
    )
    experts = mesh.shape["dp"]
    body = dense_body if experts <= 2 * TOPK else routed_body
    return jax.shard_map(body, mesh=mesh, in_specs=in_specs, out_specs=out_specs, check_vma=False)
```

```python
import functools

import jax
import jax.numpy as jnp
from jax import lax
from jax.experimental import pallas as pl
from jax.experimental.pallas import tpu as pltpu
from jax.sharding import PartitionSpec as P

D = 2048
HEAD = 128
TOPK = 8
PROMPT = 256
CONT = 64
GROUP = 384


EPSILON = 1e-05
ROPE_BASE = 10000.0
HIGHEST = lax.Precision.HIGHEST


def matmul(first_op, second_op):
    return jnp.dot(first_op, second_op, preferred_element_type=jnp.float32)


def gather_rows(values):
    return lax.all_gather(values, "tensor", axis=0, tiled=True)


def sum_rows(values):
    return lax.psum_scatter(values, "tensor", scatter_dimension=0, tiled=True)


def tensor_total(values):
    return lax.psum((values[0], values[1]), "tensor")


def expert_swap(values):
    return lax.all_to_all(values, "dp", split_axis=0, concat_axis=0, tiled=True)


def sum_slots(values):
    return lax.psum_scatter(values, "tensor", scatter_dimension=1, tiled=True)


def group_positions():
    position = jnp.arange(GROUP, dtype=jnp.int32)
    return jnp.where(position < PROMPT, position, PROMPT + (position - PROMPT) % CONT)


def visible_keys():
    position = jnp.arange(GROUP, dtype=jnp.int32)
    member = jnp.where(position < PROMPT, -1, (position - PROMPT) // CONT)
    causal = position[None, :] <= position[:, None]
    return causal & ((member[None, :] == -1) | (member[None, :] == member[:, None]))


def rope_tables():
    half_head = HEAD // 2
    frequency = ROPE_BASE ** (-2.0 * jnp.arange(half_head, dtype=jnp.float32) / HEAD)
    angles = group_positions().astype(jnp.float32)[:, None] * frequency[None, :]
    angles = jnp.concatenate([angles, angles], axis=1)
    return (jnp.cos(angles), jnp.sin(angles))


def rotate(values, cosine_table, sine_table):
    half_head = HEAD // 2
    turned = jnp.concatenate([-values[..., half_head:], values[..., :half_head]], axis=-1)
    return values * cosine_table[:, None, :] + turned * sine_table[:, None, :]


def unrotate(values, cosine_table, sine_table):
    half_head = HEAD // 2
    scaled = values * sine_table[:, None, :]
    turned = jnp.concatenate([scaled[..., half_head:], -scaled[..., :half_head]], axis=-1)
    return values * cosine_table[:, None, :] + turned


def gate_split(rows_in, hot_table, router):
    gates = jax.nn.softmax(matmul(rows_in, router), axis=1)
    weights = jnp.sum(jnp.where(hot_table, gates[:, None, :], 0.0), axis=2)
    return (gates, weights)


def routed_body(
    tokens,
    routes,
    cotangent,
    attn_gain,
    q_gain,
    k_gain,
    w_query,
    w_key,
    w_value,
    w_out,
    mlp_gain,
    router,
    w_gate,
    w_up,
    w_down,
):
    rank_index = lax.axis_index("tensor")
    tensor_count = lax.axis_size("tensor")
    own_rows = tokens.shape[0]
    head_cols = w_query.shape[1]
    local_heads = head_cols // HEAD
    col_start = rank_index * head_cols
    row_start = rank_index * own_rows
    experts = router.shape[1]
    half_cap = (own_rows * TOPK * 4 + 3 * experts - 1) // (3 * experts)
    capacity = tensor_count * half_cap
    attn_scale = HEAD ** (-0.5)
    head_shape = (GROUP, local_heads, HEAD)
    q_gain_local = lax.dynamic_slice_in_dim(q_gain, col_start, head_cols)
    k_gain_local = lax.dynamic_slice_in_dim(k_gain, col_start, head_cols)
    inputs = tokens.astype(jnp.float32)
    attn_inv = lax.rsqrt(jnp.mean(inputs * inputs, axis=1, keepdims=True) + EPSILON)
    normed = gather_rows((inputs * attn_inv * attn_gain).astype(jnp.bfloat16))
    pieces = (
        lax.all_gather(w_query, "dp", axis=0, tiled=True),
        lax.all_gather(w_key, "dp", axis=0, tiled=True),
        lax.all_gather(w_value, "dp", axis=0, tiled=True),
    )
    normed_part = normed
    queries = matmul(normed_part, pieces[0])
    keys_raw = matmul(normed_part, pieces[1])
    values_raw = matmul(normed_part, pieces[2])
    query_sq, key_sq = tensor_total(
        (jnp.sum(queries * queries, axis=1), jnp.sum(keys_raw * keys_raw, axis=1))
    )
    query_inv = lax.rsqrt(query_sq / D + EPSILON)[:, None]
    key_inv = lax.rsqrt(key_sq / D + EPSILON)[:, None]
    cosine_table, sine_table = rope_tables()
    query_rot = rotate(
        (queries * query_inv * q_gain_local).reshape(head_shape), cosine_table, sine_table
    ).astype(jnp.bfloat16)
    key_rot = rotate(
        (keys_raw * key_inv * k_gain_local).reshape(head_shape), cosine_table, sine_table
    ).astype(jnp.bfloat16)
    value_heads = values_raw.astype(jnp.bfloat16).reshape(head_shape)
    visible = visible_keys()[None]

    def masked_scores():
        raw_scores = (
            jnp.einsum("qhd,khd->hqk", query_rot, key_rot, preferred_element_type=jnp.float32)
            * attn_scale
        )
        return jnp.where(visible, raw_scores, -1e30)

    scores = masked_scores()
    row_max = jnp.max(scores, axis=2, keepdims=True)
    exponent = jnp.exp(scores - row_max)
    row_total = jnp.sum(exponent, axis=2, keepdims=True)
    log_total = row_max + jnp.log(row_total)
    mixed_heads = jnp.einsum(
        "hqk,khd->qhd",
        (exponent / row_total).astype(jnp.bfloat16),
        value_heads,
        preferred_element_type=jnp.float32,
    )
    mixed_heads = mixed_heads.reshape(GROUP, head_cols).astype(jnp.bfloat16)
    attn_part = matmul(mixed_heads, lax.all_gather(w_out, "dp", axis=1, tiled=True))
    attended = sum_rows(attn_part)
    hidden_one = inputs + attended
    mlp_inv = lax.rsqrt(jnp.mean(hidden_one * hidden_one, axis=1, keepdims=True) + EPSILON)
    normed_two = (hidden_one * mlp_inv * mlp_gain).astype(jnp.bfloat16)
    expert_ids = jnp.arange(experts, dtype=jnp.int32)
    route_hot = routes[:, :, None] == expert_ids[None, None, :]
    flat_hot = route_hot.astype(jnp.int32).reshape(tensor_count, own_rows * TOPK, experts)
    within = jnp.sum((jnp.cumsum(flat_hot, axis=1) - flat_hot) * flat_hot, axis=2).reshape(
        GROUP, TOPK
    )
    owner_of = (jnp.arange(GROUP, dtype=jnp.int32) // own_rows)[:, None]
    own_routes = lax.dynamic_slice_in_dim(routes, row_start, own_rows, 0)
    own_within = lax.dynamic_slice_in_dim(within, row_start, own_rows, 0)
    own_hot = lax.dynamic_slice_in_dim(route_hot, row_start, own_rows, 0)
    own_dest = own_routes * half_cap + own_within
    gate_weight = w_gate[0]
    up_weight = w_up[0]
    down_weight = w_down[0]
    normed_two_all = gather_rows(normed_two)
    gates_every, gate_every = gate_split(normed_two_all, route_hot, router)
    own_probs = lax.dynamic_slice_in_dim(gates_every, row_start, own_rows, 0)
    gate_weights = lax.dynamic_slice_in_dim(gate_every, row_start, own_rows, 0)
    destination = routes * capacity + owner_of * half_cap + within
    send_rows = (
        jnp.zeros((experts * capacity, D), jnp.bfloat16)
        .at[destination]
        .set(jnp.broadcast_to(normed_two_all[:, None, :], (GROUP, TOPK, D)))
        .reshape(experts, capacity, D)
    )
    received = lax.all_to_all(send_rows, "dp", split_axis=0, concat_axis=0, tiled=True)
    gate_pre = jnp.einsum("scd,df->scf", received, gate_weight, preferred_element_type=jnp.float32)
    up_pre = jnp.einsum("scd,df->scf", received, up_weight, preferred_element_type=jnp.float32)
    hidden = (jax.nn.silu(gate_pre) * up_pre).astype(jnp.bfloat16)
    expert_part = jnp.einsum("scf,fd->scd", hidden, down_weight, preferred_element_type=jnp.float32)
    expert_part, gate_pre, up_pre, hidden, received = (
        expert_part,
        gate_pre,
        up_pre,
        hidden,
        received,
    )
    back_rows = expert_swap(sum_slots(expert_part).astype(jnp.bfloat16)).reshape(
        experts * half_cap, D
    )
    picked = back_rows[own_dest].astype(jnp.float32)
    mixture = jnp.sum(gate_weights[:, :, None] * picked, axis=1)
    layer_out = (hidden_one + mixture).astype(jnp.bfloat16)
    upstream = cotangent.astype(jnp.float32)
    gate_grad = jnp.sum(upstream[:, None, :] * picked, axis=2)
    upstream_all = gather_rows(cotangent).astype(jnp.float32)
    send_grads = (
        jnp.zeros((experts * capacity, D), jnp.bfloat16)
        .at[destination]
        .set((gate_every[:, :, None] * upstream_all[:, None, :]).astype(jnp.bfloat16))
        .reshape(experts, capacity, D)
    )
    out_grads = expert_swap(send_grads)
    hidden_grad = jnp.einsum(
        "scd,fd->scf", out_grads, down_weight, preferred_element_type=jnp.float32
    )
    sigmoid = jax.nn.sigmoid(gate_pre)
    up_grad = (hidden_grad * gate_pre * sigmoid).astype(jnp.bfloat16)
    gate_pre_grad = (hidden_grad * up_pre * sigmoid * (1.0 + gate_pre * (1.0 - sigmoid))).astype(
        jnp.bfloat16
    )
    row_part = jnp.einsum(
        "scf,df->scd", gate_pre_grad, gate_weight, preferred_element_type=jnp.float32
    ) + jnp.einsum("scf,df->scd", up_grad, up_weight, preferred_element_type=jnp.float32)
    down_weight_grad = jnp.einsum(
        "scf,scd->fd", hidden, out_grads, preferred_element_type=jnp.float32
    )
    gate_weight_grad = jnp.einsum(
        "scd,scf->df", received, gate_pre_grad, preferred_element_type=jnp.float32
    )
    up_weight_grad = jnp.einsum(
        "scd,scf->df", received, up_grad, preferred_element_type=jnp.float32
    )
    returned_grads = expert_swap(sum_slots(row_part).astype(jnp.bfloat16)).reshape(
        experts * half_cap, D
    )
    normed_two_part = jnp.sum(returned_grads[own_dest].astype(jnp.float32), axis=1)
    expert_grad = jnp.sum(jnp.where(own_hot, gate_grad[:, :, None], 0.0), axis=1)
    logit_grad = own_probs * (expert_grad - jnp.sum(expert_grad * own_probs, axis=1, keepdims=True))
    router_grad = jnp.dot(normed_two.astype(jnp.float32).T, logit_grad, precision=HIGHEST)
    normed_two_grad = normed_two_part + jnp.dot(
        logit_grad, router.astype(jnp.float32).T, precision=HIGHEST
    )
    scaled_grad = normed_two_grad * mlp_gain
    hidden_one_grad = (
        upstream
        + mlp_inv * scaled_grad
        - hidden_one * mlp_inv**3 * jnp.mean(hidden_one * scaled_grad, axis=1, keepdims=True)
    )
    mlp_gain_grad = jnp.sum(normed_two_grad * hidden_one * mlp_inv, axis=0)
    attended_grad = gather_rows(hidden_one_grad.astype(jnp.bfloat16))
    mixed_grad = jnp.einsum(
        "gd,cd->gc",
        attended_grad,
        lax.all_gather(w_out, "dp", axis=1, tiled=True),
        preferred_element_type=jnp.float32,
    )
    mixed_grad = mixed_grad.astype(jnp.bfloat16).reshape(head_shape)
    attn_probs = jnp.exp(masked_scores() - log_total)
    prob_grad = jnp.einsum(
        "qhd,khd->hqk", mixed_grad, value_heads, preferred_element_type=jnp.float32
    )
    row_dot = jnp.sum(prob_grad * attn_probs, axis=2, keepdims=True)
    score_grad = (attn_probs * (prob_grad - row_dot)).astype(jnp.bfloat16)
    query_rot_grad = (
        jnp.einsum("hqk,khd->qhd", score_grad, key_rot, preferred_element_type=jnp.float32)
        * attn_scale
    )
    key_rot_grad = (
        jnp.einsum("hqk,qhd->khd", score_grad, query_rot, preferred_element_type=jnp.float32)
        * attn_scale
    )
    value_grad = (
        jnp.einsum(
            "hqk,qhd->khd",
            attn_probs.astype(jnp.bfloat16),
            mixed_grad,
            preferred_element_type=jnp.float32,
        )
        .reshape(GROUP, head_cols)
        .astype(jnp.bfloat16)
    )
    query_norm_grad = unrotate(query_rot_grad, cosine_table, sine_table).reshape(GROUP, head_cols)
    key_norm_grad = unrotate(key_rot_grad, cosine_table, sine_table).reshape(GROUP, head_cols)
    query_scaled = query_norm_grad * q_gain_local
    key_scaled = key_norm_grad * k_gain_local
    query_dot, key_dot = tensor_total(
        (jnp.sum(queries * query_scaled, axis=1), jnp.sum(keys_raw * key_scaled, axis=1))
    )
    query_grad = (
        query_inv * query_scaled - queries * query_inv**3 * (query_dot / D)[:, None]
    ).astype(jnp.bfloat16)
    key_grad = (key_inv * key_scaled - keys_raw * key_inv**3 * (key_dot / D)[:, None]).astype(
        jnp.bfloat16
    )
    q_gain_part = jnp.sum(query_norm_grad * queries * query_inv, axis=0)
    k_gain_part = jnp.sum(key_norm_grad * keys_raw * key_inv, axis=0)
    pieces = lax.all_gather((w_query, w_key, w_value), "dp", axis=0, tiled=True)
    normed_part = (
        jnp.einsum("gc,rc->gr", query_grad, pieces[0], preferred_element_type=jnp.float32)
        + jnp.einsum("gc,rc->gr", key_grad, pieces[1], preferred_element_type=jnp.float32)
        + jnp.einsum("gc,rc->gr", value_grad, pieces[2], preferred_element_type=jnp.float32)
    )
    weight_sums = lax.psum_scatter(
        jnp.concatenate(
            [
                jnp.einsum("gr,gc->rc", normed, query_grad, preferred_element_type=jnp.float32),
                jnp.einsum("gr,gc->rc", normed, key_grad, preferred_element_type=jnp.float32),
                jnp.einsum("gr,gc->rc", normed, value_grad, preferred_element_type=jnp.float32),
                jnp.einsum(
                    "gr,gc->rc", attended_grad, mixed_heads, preferred_element_type=jnp.float32
                ),
            ],
            axis=1,
        ),
        "dp",
        scatter_dimension=0,
        tiled=True,
    )
    normed_grad = sum_rows(normed_part)
    scaled_input = normed_grad * attn_gain
    tokens_grad = (
        hidden_one_grad
        + attn_inv * scaled_input
        - inputs * attn_inv**3 * jnp.mean(inputs * scaled_input, axis=1, keepdims=True)
    )
    attn_gain_grad = jnp.sum(normed_grad * inputs * attn_inv, axis=0)
    zero_width = jnp.zeros((D,), jnp.float32)
    q_gain_full = lax.dynamic_update_slice_in_dim(zero_width, q_gain_part, col_start, 0)
    k_gain_full = lax.dynamic_update_slice_in_dim(zero_width, k_gain_part, col_start, 0)
    attn_gain_grad, q_gain_grad, k_gain_grad, mlp_gain_grad, router_grad = lax.psum(
        (attn_gain_grad, q_gain_full, k_gain_full, mlp_gain_grad, router_grad), ("dp", "tensor")
    )
    return (
        layer_out,
        tokens_grad,
        attn_gain_grad,
        q_gain_grad,
        k_gain_grad,
        weight_sums[:, :head_cols],
        weight_sums[:, head_cols : 2 * head_cols],
        weight_sums[:, 2 * head_cols : 3 * head_cols],
        jnp.transpose(weight_sums[:, 3 * head_cols :]),
        mlp_gain_grad,
        router_grad,
        gate_weight_grad[None],
        up_weight_grad[None],
        down_weight_grad[None],
    )


MESH_ID = pl.DeviceIdType.MESH
LINK_TIME = pl.CostEstimate(flops=10**11, bytes_accessed=10**8, transcendentals=0)
EVERY = ("dp", "tensor")
LANES = 128
ANYWHERE = pl.BlockSpec(memory_space=pl.ANY)
IN_VMEM = pl.BlockSpec(memory_space=pltpu.VMEM)


class Place:
    def __init__(self):
        dp = lax.axis_index("dp")
        self.y = lax.axis_index("tensor")
        self.z, self.x, self.c = dp // 4, (dp // 2) % 2, dp % 2
        self.z_count = lax.axis_size("dp") // 4

    def device(self, z=None, x=None, c=None, y=None):
        z = self.z if z is None else z
        x = self.x if x is None else x
        c = self.c if c is None else c
        y = self.y if y is None else y
        return (z * 4 + x * 2 + c, y)

    def meet(self, use_y=True, all_z=False):
        barrier = pltpu.get_barrier_semaphore()
        partners = [self.device(x=1 - self.x), self.device(c=1 - self.c)]
        if use_y:
            partners.append(self.device(y=1 - self.y))
        if all_z:
            partners += [self.device(z=(self.z + d) % self.z_count) for d in range(1, self.z_count)]
        for partner in partners:
            pl.semaphore_signal(barrier, inc=1, device_id=partner, device_id_type=MESH_ID)
        if all_z:
            pl.semaphore_wait(barrier, len(partners))
            return

        @pl.when(self.z > 0)
        def _():
            pl.semaphore_signal(
                barrier, inc=1, device_id=self.device(z=self.z - 1), device_id_type=MESH_ID
            )

        @pl.when(self.z < self.z_count - 1)
        def _():
            pl.semaphore_signal(
                barrier, inc=1, device_id=self.device(z=self.z + 1), device_id_type=MESH_ID
            )

        ends = jnp.where(self.z > 0, 1, 0) + jnp.where(self.z < self.z_count - 1, 1, 0)
        pl.semaphore_wait(barrier, len(partners) + ends)

    def far_first(self, step):
        last = self.z_count - 1
        low = jnp.where(step < last - self.z, last - step, step - (last - self.z))
        high = jnp.where(step < self.z, step, last - (step - self.z))
        return jnp.where(self.z * 2 < self.z_count, low, high)


    def near_first(self, step):
        return self.far_first(self.z_count - 1 - step)


def send(src, dst, send_sem, recv_sem, device):
    copy = pltpu.make_async_remote_copy(
        src_ref=src, dst_ref=dst, send_sem=send_sem, recv_sem=recv_sem, device_id=device, device_id_type=MESH_ID
    )
    copy.start()
    return copy


def add_rows(total, part, rows, step=16):
    def chunk(i, carry):
        here = pl.ds(pl.multiple_of(i * step, step), step)
        total[here] = total[here] + part[here]
        return carry

    lax.fori_loop(0, rows // step, chunk, 0)


class Spread:
    KINDS = 14
    ZU, ZD, XF, YF, XH, YH, CO, CX, CY, CA, CB, CC, DU, DD = range(KINDS)

    def __init__(self, place, src, whole, sent, got, kept, own_split, through_z, other_split):
        self.place, self.src, self.whole, self.sent, self.got = place, src, whole, sent, got
        rows = src.shape[0]
        self.parts = {
            True: (pl.ds(0, own_split), pl.ds(own_split, rows - own_split)),
            False: (pl.ds(through_z, other_split), pl.ds(through_z + other_split, rows - through_z - other_split)),
        }
        self.deep = pl.ds(0, through_z)
        z, x, c, y = place.z, place.x, place.c, place.y
        self.up, self.down = place.device(z=z + 1), place.device(z=z - 1)
        self.over_x, self.over_y = place.device(x=1 - x), place.device(y=1 - y)
        self.over_c = place.device(c=1 - c)
        self.keep = pltpu.make_async_copy(src, whole.at[z, x, c, y], kept)

    def push(self, kind, zz, xx, yy, rows, device, origin=None):
        ref = self.whole.at[zz, xx, self.place.c, yy, rows]
        send(
            ref if origin is None else origin,
            ref,
            self.sent.at[kind, zz],
            self.got.at[kind, zz],
            device,
        )

    def arrival(self, kind, zz, xx, yy, rows=slice(None), sibling=False):
        cc = 1 - self.place.c if sibling else self.place.c
        ref = self.whole.at[zz, xx, cc, yy, rows]
        pltpu.make_async_copy(ref, ref, self.got.at[kind, zz]).wait()

    def departure(self, kind, zz, xx, yy, rows=slice(None)):
        ref = self.whole.at[zz, xx, self.place.c, yy, rows]
        pltpu.make_async_copy(ref, ref, self.sent.at[kind, zz]).wait()

    def column(self, k, origin=None):
        x, y, every = self.place.x, self.place.y, slice(None)
        zz = self.place.near_first(k)
        self.push(self.XF, zz, x, y, every, self.over_x, origin)
        self.push(self.YF, zz, x, y, every, self.over_y, origin)
        self.push(self.CO, zz, x, y, every, self.over_c, origin)

    def begin(self):
        z, x, y, nz = self.place.z, self.place.x, self.place.y, self.place.z_count

        @pl.when(z < nz - 1)
        def _():
            self.push(self.ZU, z, x, y, slice(None), self.up, self.src)

        @pl.when(z > 0)
        def _():
            self.push(self.ZD, z, x, y, slice(None), self.down, self.src)

        self.column(0, self.src)
        self.keep.start()

    def move_z(self, d, up_kind, down_kind, xx, yy, rows, hand_over):
        z, nz = self.place.z, self.place.z_count
        below, above = z - d, z + d

        @pl.when(below >= 0)
        def _():
            self.arrival(up_kind, below, xx, yy, rows)

            @pl.when(z < nz - 1)
            def _():
                self.push(up_kind, below, xx, yy, rows, self.up)

            if hand_over:
                self.push(self.CC, below, xx, yy, rows, self.over_c)

        @pl.when(above < nz)
        def _():
            self.arrival(down_kind, above, xx, yy, rows)

            @pl.when(z > 0)
            def _():
                self.push(down_kind, above, xx, yy, rows, self.down)

            if hand_over:
                self.push(self.CC, above, xx, yy, rows, self.over_c)

    def along_z(self, d):
        self.move_z(d, self.ZU, self.ZD, self.place.x, self.place.y, slice(None), False)

    def diagonal_along_z(self, d):
        self.move_z(d, self.DU, self.DD, 1 - self.place.x, 1 - self.place.y, self.deep, True)

    def relay(self, k):
        x, y, every = self.place.x, self.place.y, slice(None)
        zz = self.place.near_first(k)
        low, high = self.parts[k == 0]
        self.arrival(self.XF, zz, 1 - x, y)
        if low.size:
            self.push(self.YH, zz, 1 - x, y, low, self.over_y)
        self.push(self.CX, zz, 1 - x, y, every, self.over_c)
        self.arrival(self.YF, zz, x, 1 - y)
        self.push(self.XH, zz, x, 1 - y, high, self.over_x)
        self.push(self.CY, zz, x, 1 - y, every, self.over_c)

    def diagonal(self, k):
        z, nz = self.place.z, self.place.z_count
        xx, yy = 1 - self.place.x, 1 - self.place.y
        zz = self.place.near_first(k)
        low, high = self.parts[k == 0]
        self.arrival(self.XH, zz, xx, yy, high)
        if low.size:
            self.arrival(self.YH, zz, xx, yy, low)
        if k == 0:

            @pl.when(z < nz - 1)
            def _():
                self.push(self.DU, z, xx, yy, self.deep, self.up)

            @pl.when(z > 0)
            def _():
                self.push(self.DD, z, xx, yy, self.deep, self.down)

        self.push(self.CB, zz, xx, yy, high, self.over_c)
        if low.size:
            self.push(self.CA, zz, xx, yy, low, self.over_c)

    def sibling_near(self, k):
        x, y = self.place.x, self.place.y
        zz = self.place.near_first(k)
        self.arrival(self.CO, zz, x, y, sibling=True)
        self.arrival(self.CY, zz, x, 1 - y, sibling=True)

    def sibling_far(self, k):
        x, y = self.place.x, self.place.y
        zz = self.place.near_first(k)
        low, high = self.parts[k == 0]
        self.arrival(self.CX, zz, 1 - x, y, sibling=True)
        self.arrival(self.CB, zz, 1 - x, 1 - y, high, sibling=True)
        if low.size:
            self.arrival(self.CA, zz, 1 - x, 1 - y, low, sibling=True)
        if k > 0:
            self.arrival(self.CC, zz, 1 - x, 1 - y, self.deep, sibling=True)

    def finish(self):
        z, x, y, nz = self.place.z, self.place.x, self.place.y, self.place.z_count
        for k in range(nz):
            zz = self.place.near_first(k)
            low, high = self.parts[k == 0]
            self.departure(self.XF, zz, x, y)
            self.departure(self.YF, zz, x, y)
            self.departure(self.CO, zz, x, y)
            self.departure(self.CX, zz, 1 - x, y)
            self.departure(self.CY, zz, x, 1 - y)
            self.departure(self.XH, zz, x, 1 - y, high)
            self.departure(self.CB, zz, 1 - x, 1 - y, high)
            if low.size:
                self.departure(self.YH, zz, 1 - x, y, low)
                self.departure(self.CA, zz, 1 - x, 1 - y, low)
            if k > 0:
                self.departure(self.CC, zz, 1 - x, 1 - y, self.deep)

            @pl.when((zz <= z) & (z < nz - 1))
            def _():
                self.departure(self.ZU, zz, x, y)
                self.departure(self.DU, zz, 1 - x, 1 - y, self.deep)

            @pl.when((zz >= z) & (z > 0))
            def _():
                self.departure(self.ZD, zz, x, y)
                self.departure(self.DD, zz, 1 - x, 1 - y, self.deep)


class Fold:
    KINDS = 12
    CD, CX, CY, CO, XH, YH, XF, YF, ZU, ZD, DU, DD = range(KINDS)
    SPOT = {CD: (1, 1), CX: (1, 0), CY: (0, 1), CO: (0, 0)}

    def __init__(
        self, place, split, parts, total, from_c, half_x, half_y, z_buf, d_buf, sent, got, loaded
    ):
        self.place, self.parts, self.total, self.from_c = place, parts, total, from_c
        self.half_x, self.half_y, self.z_buf, self.d_buf = half_x, half_y, z_buf, d_buf
        self.sent, self.got, self.loaded = sent, got, loaded
        self.rows = total.shape[3]
        self.own_split, self.through_z, self.other_split = split
        self.deep = pl.ds(0, self.through_z)
        z, x, c, y = place.z, place.x, place.c, place.y
        self.over_x, self.over_y = place.device(x=1 - x), place.device(y=1 - y)
        self.over_c = place.device(c=1 - c)

    def diagonal_parts(self, zz, own):
        if own:
            low = pl.ds(0, self.own_split)
            high = pl.ds(self.own_split, self.rows - self.own_split)
            return low, high, self.half_y.at[low], self.half_x.at[pl.ds(0, high.size)]
        low = pl.ds(self.through_z, self.other_split)
        start = self.through_z + self.other_split
        high = pl.ds(start, self.rows - start)
        y_start = pl.multiple_of(self.own_split + zz * low.size, 16)
        x_start = pl.multiple_of(self.rows - self.own_split + zz * high.size, 16)
        return (
            low,
            high,
            self.half_y.at[pl.ds(y_start, low.size)],
            self.half_x.at[pl.ds(x_start, high.size)],
        )

    def push(self, kind, zz, src, dst, device):
        send(src, dst, self.sent.at[kind, zz], self.got.at[kind, zz], device)

    def arrival(self, kind, zz, ref):
        pltpu.make_async_copy(ref, ref, self.got.at[kind, zz]).wait()

    def begin(self):
        x, c, y, nz = self.place.x, self.place.c, self.place.y, self.place.z_count

        def start(kind, i):
            dx, dy = self.SPOT[kind]
            zz = self.place.far_first(i)
            xx, yy = (1 - x if dx else x), (1 - y if dy else y)
            self.push(
                kind, zz, self.parts.at[zz, xx, 1 - c, yy], self.from_c.at[dx, dy, zz], self.over_c
            )
            pltpu.make_async_copy(
                self.parts.at[zz, xx, c, yy], self.total.at[dx, dy, zz], self.loaded.at[kind, zz]
            ).start()

        for i in range(nz):
            start(self.CD, i)
            start(self.CX, i)
            start(self.CY, i)
        for i in range(nz):
            start(self.CO, i)

    def join_cores(self, kind, zz):
        dx, dy = self.SPOT[kind]
        here, there = self.total.at[dx, dy, zz], self.from_c.at[dx, dy, zz]
        pltpu.make_async_copy(here, here, self.loaded.at[kind, zz]).wait()
        self.arrival(kind, zz, there)
        add_rows(here, there, self.rows)

    def deep_push(self, zz):
        z, nz = self.place.z, self.place.z_count
        mine = self.total.at[1, 1, zz, self.deep]

        @pl.when(zz > z)
        def _():
            self.push(self.DU, zz, mine, self.d_buf.at[zz], self.place.device(z=z + 1))

        @pl.when(zz < z)
        def _():
            landing = jnp.where(zz == z - 1, nz, zz)
            self.push(self.DD, zz, mine, self.d_buf.at[landing], self.place.device(z=z - 1))

    def at_end(self):
        return (self.place.z == 0) | (self.place.z == self.place.z_count - 1)

    def halves(self, i):
        own = i == self.place.z_count - 1
        zz = self.place.far_first(i)
        self.join_cores(self.CD, zz)
        self.join_cores(self.CX, zz)
        if own:
            return
        self.push_halves(zz, False)

        @pl.when(self.at_end())
        def _():
            self.deep_push(zz)

    def push_halves(self, zz, own):
        low, high, land_y, land_x = self.diagonal_parts(zz, own)
        self.push(self.XH, zz, self.total.at[1, 1, zz, high], land_x, self.over_x)
        self.push(self.YH, zz, self.total.at[1, 1, zz, low], land_y, self.over_y)

    def deep_on(self, i):
        z = self.place.z
        zz = self.place.far_first(i)

        @pl.when(jnp.logical_not(self.at_end()))
        def _():
            @pl.when(zz > z)
            def _():
                self.arrival(self.DU, zz, self.d_buf.at[zz])

            @pl.when(zz < z)
            def _():
                self.arrival(self.DD, zz, self.d_buf.at[zz])

            add_rows(self.total.at[1, 1, zz, self.deep], self.d_buf.at[zz], self.through_z)
            self.deep_push(zz)

    def own_halves(self):
        z, nz = self.place.z, self.place.z_count
        mine = self.total.at[1, 1, z, self.deep]

        @pl.when(z > 0)
        def _():
            self.arrival(self.DU, z, self.d_buf.at[z])
            add_rows(mine, self.d_buf.at[z], self.through_z)

        @pl.when(z < nz - 1)
        def _():
            self.arrival(self.DD, z, self.d_buf.at[nz])
            add_rows(mine, self.d_buf.at[nz], self.through_z)

        self.push_halves(z, True)

    def columns(self, i):
        zz = self.place.far_first(i)
        low, high, land_y, land_x = self.diagonal_parts(zz, i == self.place.z_count - 1)
        self.join_cores(self.CY, zz)
        self.arrival(self.XH, zz, land_x)
        add_rows(self.total.at[0, 1, zz, high], land_x, high.size)
        self.arrival(self.YH, zz, land_y)
        add_rows(self.total.at[1, 0, zz, low], land_y, low.size)
        self.push(self.XF, zz, self.total.at[1, 0, zz], self.from_c.at[1, 1, zz], self.over_x)
        self.push(self.YF, zz, self.total.at[0, 1, zz], self.from_c.at[1, 0, zz], self.over_y)

    def along_z(self, i):
        z, nz = self.place.z, self.place.z_count
        zz = self.place.far_first(i)
        mine = self.total.at[0, 0, zz]
        self.join_cores(self.CO, zz)
        self.arrival(self.XF, zz, self.from_c.at[1, 1, zz])
        add_rows(mine, self.from_c.at[1, 1, zz], self.rows)
        self.arrival(self.YF, zz, self.from_c.at[1, 0, zz])
        add_rows(mine, self.from_c.at[1, 0, zz], self.rows)
        above = jnp.where(zz == z, nz, zz)

        @pl.when((z > 0) & (zz >= z))
        def _():
            self.arrival(self.ZU, zz, self.z_buf.at[zz])
            add_rows(mine, self.z_buf.at[zz], self.rows)

        @pl.when((z < nz - 1) & (zz <= z))
        def _():
            self.arrival(self.ZD, zz, self.z_buf.at[above])
            add_rows(mine, self.z_buf.at[above], self.rows)

        @pl.when(zz > z)
        def _():
            self.push(self.ZU, zz, mine, self.z_buf.at[zz], self.place.device(z=z + 1))

        @pl.when(zz < z)
        def _():
            landing = jnp.where(zz == z - 1, nz, zz)
            self.push(self.ZD, zz, mine, self.z_buf.at[landing], self.place.device(z=z - 1))

    def opening(self):
        last = self.place.z_count - 1
        return [functools.partial(self.halves, i) for i in range(last)] + [
            functools.partial(self.columns, i) for i in range(min(1, last))
        ]

    def middle(self):
        last = self.place.z_count - 1
        steps = [functools.partial(self.deep_on, i) for i in range(last)]
        steps.insert(1, functools.partial(self.halves, last))
        steps.append(self.own_halves)
        return steps + [functools.partial(self.columns, i) for i in range(min(1, last), last + 1)]

    def result(self):
        return self.total[0, 0, self.place.z]

    def finish(self):
        z, nz = self.place.z, self.place.z_count

        def departure(kind, zz, ref):
            pltpu.make_async_copy(ref, ref, self.sent.at[kind, zz]).wait()

        for i in range(nz):
            zz = self.place.far_first(i)
            low, high, land_y, land_x = self.diagonal_parts(zz, i == nz - 1)
            for kind in (self.CD, self.CX, self.CY, self.CO, self.XF, self.YF):
                departure(kind, zz, self.total.at[0, 0, zz])
            departure(self.XH, zz, land_x)
            departure(self.YH, zz, land_y)

            @pl.when(zz > z)
            def _():
                departure(self.ZU, zz, self.total.at[0, 0, zz])
                departure(self.DU, zz, self.d_buf.at[zz])

            @pl.when(zz < z)
            def _():
                departure(self.ZD, zz, self.total.at[0, 0, zz])
                departure(self.DD, zz, self.d_buf.at[zz])


def half_rows(rows, split):
    own, deep, other = split
    return (own, other), (rows - own, rows - deep - other)


def fold_scratch(nz, rows, cols, split, dt):
    (y_own, y_other), (x_own, x_other) = half_rows(rows, split)
    return [
        pltpu.VMEM((2, 2, nz, rows, cols), dt),
        pltpu.VMEM((2, 2, nz, rows, cols), dt),
        pltpu.VMEM((x_own + nz * x_other, cols), dt),
        pltpu.VMEM((y_own + nz * y_other, cols), dt),
        pltpu.VMEM((nz + 1, rows, cols), dt),
        pltpu.VMEM((nz + 1, split[1], cols), dt),
        pltpu.SemaphoreType.DMA((Fold.KINDS, nz)),
        pltpu.SemaphoreType.DMA((Fold.KINDS, nz)),
        pltpu.SemaphoreType.DMA((4, nz)),
    ]


def scatter_kernel(parts, *refs):
    streams, refs = refs[:5], refs[5:]
    out, wg_grad, wu_grad, wd_grad = refs[:4]
    tiles, tile_sems, scratch = refs[4:9], refs[9], refs[10:]
    place = Place()
    nz = place.z_count
    fold = Fold(place, row_split(out.shape[0]), parts, *scratch)
    count = streams[0].shape[0]
    place.meet()
    fold.begin()

    def loads(t, slot):
        return [
            pltpu.make_async_copy(stream.at[t], tile.at[slot], tile_sems.at[slot, n])
            for n, (stream, tile) in enumerate(zip(streams, tiles))
        ]

    def tile_step(t, carry):
        slot = t % 2
        for copy in loads(t, slot):
            copy.wait()

        @pl.when(t + 1 < count)
        def _():
            for copy in loads(t + 1, 1 - slot):
                copy.start()

        x_tile, g_tile, hidden, gate_pre_grad, up_grad = (tile[slot] for tile in tiles)
        wg_grad[...] += dot_tn(x_tile, gate_pre_grad)
        wu_grad[...] += dot_tn(x_tile, up_grad)
        wd_grad[...] += dot_tn(hidden, g_tile)
        return carry

    for copy in loads(0, 0):
        copy.start()
    for grad in (wg_grad, wu_grad, wd_grad):
        grad[...] = jnp.zeros_like(grad)
    steps = fold.opening() + fold.middle()
    steps += [functools.partial(fold.along_z, i) for i in range(nz)]
    done = 0
    for n, step in enumerate(steps):
        until = min(count, round(count * n / (len(steps) - 1)))
        lax.fori_loop(done, until, tile_step, 0)
        done = until
        step()
    out[...] = fold.result()
    fold.finish()


def row_split(rows):
    return rows // 2, rows // 2, rows // 4


def scatter_sum(parts, streams, collective):
    nz, _, _, _, rows, cols = parts.shape
    dt = parts.dtype
    width, units = streams[0].shape[1], streams[2].shape[1]
    tile = 256 if streams[0].shape[0] % 256 == 0 else GROUP // 2
    streams = [stream.reshape(-1, tile, stream.shape[1]) for stream in streams]
    shapes = [(width, units), (width, units), (units, width)]
    return pl.pallas_call(
        scatter_kernel,
        out_shape=[jax.ShapeDtypeStruct((rows, cols), dt)]
        + [jax.ShapeDtypeStruct(shape, jnp.float32) for shape in shapes],
        in_specs=[ANYWHERE] * 6,
        out_specs=[IN_VMEM] * 4,
        scratch_shapes=[pltpu.VMEM((2,) + stream.shape[1:], stream.dtype) for stream in streams]
        + [pltpu.SemaphoreType.DMA((2, 5))]
        + fold_scratch(nz, rows, cols, row_split(rows), dt),
        cost_estimate=LINK_TIME,
        compiler_params=pltpu.CompilerParams(
            collective_id=collective, has_side_effects=True, vmem_limit_bytes=62 << 20
        ),
    )(parts, *streams)


def turn(values):
    return pltpu.roll(values, HEAD // 2, 1)


def seen_keys():
    row = lax.broadcasted_iota(jnp.int32, (GROUP, GROUP), 0)
    col = lax.broadcasted_iota(jnp.int32, (GROUP, GROUP), 1)
    return (col <= row) & ((col < PROMPT) | (col >= row - row % CONT))


def signed_rope_tables():
    cosine_table, sine_table = rope_tables()
    sign = jnp.where(jnp.arange(HEAD) < HEAD // 2, -1.0, 1.0)
    return cosine_table, sine_table * sign[None, :]


def attend_kernel(
    src,
    normed,
    w_query,
    w_key,
    w_value,
    w_out,
    q_gain,
    k_gain,
    cosine,
    sine,
    whole,
    queries,
    keys,
    values,
    q_rot,
    k_rot,
    mixed,
    q_inv,
    k_inv,
    log_total,
    attended,
    stats,
    stats_got,
    leaving,
    landed,
    swap_sems,
    sent,
    got,
    kept,
):
    place = Place()
    nz = place.z_count
    rows = leaving.shape[0]
    spread = Spread(place, src, whole, sent, got, kept, rows // 4, rows * 3 // 4, 0)
    place.meet()
    over_y = place.device(y=1 - place.y)
    spread.begin()

    lane = lax.broadcasted_iota(jnp.int32, stats.shape, 1)
    stats[...] = jnp.zeros_like(stats)
    chunk = 2 * HEAD

    def project(i, carry):
        here = pl.ds(pl.multiple_of(i * chunk, chunk), chunk)
        for index, (weight, raw) in enumerate(((w_query, queries), (w_key, keys))):
            product = dot_nn(normed[...], weight[:, here])
            raw[:, here] = product
            squares = jnp.sum(product * product, axis=1, keepdims=True)
            stats[...] += jnp.where(lane == index, squares, 0.0)
        values[:, here] = dot_nn(normed[...], w_value[:, here]).astype(jnp.bfloat16)
        return carry

    lax.fori_loop(0, queries.shape[1] // chunk, project, 0)
    stats_swap = send(stats, stats_got, swap_sems.at[0, 0], swap_sems.at[1, 0], over_y)
    spread.relay(0)
    if nz > 1:
        spread.along_z(1)
        spread.column(1)
    stats_swap.wait()
    for index, inv in enumerate((q_inv, k_inv)):
        total = stats[:, index : index + 1] + stats_got[:, index : index + 1]
        inv[...] = lax.rsqrt(total / D + EPSILON)
    visible = seen_keys()

    def head(h, carry):
        here = pl.ds(pl.multiple_of(h * HEAD, HEAD), HEAD)
        for raw, inv, gain, rotated in ((queries, q_inv, q_gain, q_rot), (keys, k_inv, k_gain, k_rot)):
            normal = raw[:, here] * inv[...] * gain[:, here]
            rotated[:, here] = (normal * cosine[...] + turn(normal) * sine[...]).astype(jnp.bfloat16)
        scores = dot_nt(q_rot[:, here], k_rot[:, here]) * HEAD**-0.5
        scores = jnp.where(visible, scores, -1e30)
        row_max = jnp.max(scores, axis=1, keepdims=True)
        exponent = jnp.exp(scores - row_max)
        row_total = jnp.sum(exponent, axis=1, keepdims=True)
        log_total[h] = row_max + jnp.log(row_total)
        weights = (exponent / row_total).astype(jnp.bfloat16)
        mixed[:, here] = dot_nn(weights, values[:, here]).astype(jnp.bfloat16)
        return carry

    heads = queries.shape[1] // HEAD
    lax.fori_loop(0, heads // 2, head, 0)
    spread.diagonal(0)
    if nz > 2:
        spread.along_z(2)
        spread.column(2)
    lax.fori_loop(heads // 2, heads, head, 0)

    def joined(target, index):
        where = pl.ds(pl.multiple_of(index * rows, rows), rows)

        def columns(b, carry):
            here = pl.ds(pl.multiple_of(b * w_out.shape[2], w_out.shape[2]), w_out.shape[2])
            target[:, here] = dot_nn(mixed[where], w_out[b]).astype(target.dtype)
            return carry

        lax.fori_loop(0, w_out.shape[0], columns, 0)

    joined(leaving, 1 - place.y)
    swap = send(leaving, landed, swap_sems.at[0, 1], swap_sems.at[1, 1], over_y)
    if nz > 1:
        spread.relay(1)
    joined(attended, place.y)
    for k in range(1, nz):
        spread.diagonal_along_z(k)
        if k + 2 < nz:
            spread.along_z(k + 2)
            spread.column(k + 2)
        if k + 1 < nz:
            spread.relay(k + 1)
        spread.diagonal(k)
    swap.wait()
    attended[...] += landed[...].astype(jnp.float32)
    spread.keep.wait()
    for k in range(nz):
        spread.sibling_near(k)
        spread.sibling_far(k)
    spread.finish()


def attend(block, normed, weights, gains, tables, collective):
    nz = lax.axis_size("dp") // 4
    rows, width = block.shape
    group, cols = normed.shape[0], weights[0].shape[1]
    half = jax.ShapeDtypeStruct((group, cols), jnp.bfloat16)
    wide = jax.ShapeDtypeStruct((group, cols), jnp.float32)
    thin = jax.ShapeDtypeStruct((group, 1), jnp.float32)
    return pl.pallas_call(
        attend_kernel,
        out_shape=[
            jax.ShapeDtypeStruct((nz, 2, 2, 2, rows, width), block.dtype),
            wide,
            wide,
            half,
            half,
            half,
            half,
            thin,
            thin,
            jax.ShapeDtypeStruct((cols // HEAD, group, 1), jnp.float32),
            jax.ShapeDtypeStruct((rows, width), jnp.float32),
        ],
        in_specs=[ANYWHERE] + [IN_VMEM] * 9,
        out_specs=[ANYWHERE] + [IN_VMEM] * 10,
        scratch_shapes=[
            pltpu.VMEM((group, LANES), jnp.float32),
            pltpu.VMEM((group, LANES), jnp.float32),
            pltpu.VMEM((rows, width), jnp.bfloat16),
            pltpu.VMEM((rows, width), jnp.bfloat16),
            pltpu.SemaphoreType.DMA((2, 2)),
            pltpu.SemaphoreType.DMA((Spread.KINDS, nz)),
            pltpu.SemaphoreType.DMA((Spread.KINDS, nz)),
            pltpu.SemaphoreType.DMA,
        ],
        cost_estimate=LINK_TIME,
        compiler_params=pltpu.CompilerParams(
            collective_id=collective, has_side_effects=True, vmem_limit_bytes=60 << 20
        ),
    )(block, normed, *weights, *gains, *tables)


def busy_y_split(rows):
    return rows // 2, rows // 2, rows // 6


def attend_back_kernel(
    parts,
    own_grad,
    w_out,
    queries,
    keys,
    q_rot,
    k_rot,
    values,
    q_inv,
    k_inv,
    log_total,
    q_gain,
    k_gain,
    cosine,
    sine,
    mixture,
    attended_grad,
    q_grad,
    k_grad,
    v_grad,
    gain_grads,
    landed,
    mixed_grad,
    q_scaled,
    k_scaled,
    dots,
    dots_got,
    swap_sems,
    *scratch,
):
    place = Place()
    nz = place.z_count
    fold = Fold(place, busy_y_split(own_grad.shape[0]), parts, *scratch)
    place.meet()
    over_y = place.device(y=1 - place.y)
    rows = own_grad.shape[0]
    swap = send(own_grad, landed, swap_sems.at[0, 0], swap_sems.at[1, 0], over_y)
    fold.begin()

    def take(block, index):
        where = pl.ds(pl.multiple_of(index * rows, rows), rows)
        attended_grad[where] = block[...]
        step = w_out.shape[2]

        def columns(b, total):
            here = pl.ds(pl.multiple_of(b * step, step), step)
            return total + dot_nt(block[:, here], w_out[b])

        total = jnp.zeros((rows, mixed_grad.shape[1]), jnp.float32)
        total = lax.fori_loop(0, w_out.shape[0], columns, total)
        mixed_grad[where] = total.astype(jnp.bfloat16)

    take(own_grad, place.y)
    for step in fold.opening():
        step()
    swap.wait()
    take(landed, 1 - place.y)
    visible = seen_keys()
    lane = lax.broadcasted_iota(jnp.int32, dots.shape, 1)
    dots[...] = jnp.zeros_like(dots)

    def head(h, carry):
        here = pl.ds(pl.multiple_of(h * HEAD, HEAD), HEAD)
        upstream = mixed_grad[:, here]
        scores = dot_nt(q_rot[:, here], k_rot[:, here]) * HEAD**-0.5
        probs = jnp.exp(jnp.where(visible, scores, -1e30) - log_total[h])
        prob_grad = dot_nt(upstream, values[:, here])
        row_dot = jnp.sum(prob_grad * probs, axis=1, keepdims=True)
        score_grad = (probs * (prob_grad - row_dot)).astype(jnp.bfloat16)
        v_grad[:, here] = dot_tn(probs.astype(jnp.bfloat16), upstream).astype(jnp.bfloat16)
        for index, (rot_grad, raw, inv, gain, scaled) in enumerate(
            (
                (dot_nn(score_grad, k_rot[:, here]), queries, q_inv, q_gain, q_scaled),
                (dot_tn(score_grad, q_rot[:, here]), keys, k_inv, k_gain, k_scaled),
            )
        ):
            rot_grad = rot_grad * HEAD**-0.5
            norm_grad = rot_grad * cosine[...] - turn(rot_grad) * sine[...]
            with_raw = norm_grad * raw[:, here]
            gain_grads[index : index + 1, here] = jnp.sum(with_raw * inv[...], axis=0, keepdims=True)
            scaled[:, here] = norm_grad * gain[:, here]
            part = jnp.sum(with_raw * gain[:, here], axis=1, keepdims=True)
            dots[...] += jnp.where(lane == index, part, 0.0)
        return carry

    heads = queries.shape[1] // HEAD
    steps = fold.middle()
    for n, step in enumerate(steps):
        step()
        lax.fori_loop(heads * n // len(steps), heads * (n + 1) // len(steps), head, 0)
    dots_swap = send(dots, dots_got, swap_sems.at[0, 1], swap_sems.at[1, 1], over_y)
    for i in range(nz):
        fold.along_z(i)
    mixture[...] = fold.result()
    dots_swap.wait()

    def grads(h, carry):
        here = pl.ds(pl.multiple_of(h * HEAD, HEAD), HEAD)
        for index, (raw, inv, scaled, grad) in enumerate(
            ((queries, q_inv, q_scaled, q_grad), (keys, k_inv, k_scaled, k_grad))
        ):
            mean = (dots[:, index : index + 1] + dots_got[:, index : index + 1]) / D
            scale = inv[...]
            grad[:, here] = (
                scale * scaled[:, here] - raw[:, here] * (scale * scale * scale * mean)
            ).astype(jnp.bfloat16)
        return carry

    lax.fori_loop(0, heads, grads, 0)
    fold.finish()


def attend_back(parts, own_grad, w_out, saved, gains, tables, collective):
    nz, _, _, _, rows, cols = parts.shape
    queries = saved[0]
    group, head_cols = queries.shape
    half = jax.ShapeDtypeStruct((group, head_cols), jnp.bfloat16)
    wide = pltpu.VMEM((group, head_cols), jnp.float32)
    return pl.pallas_call(
        attend_back_kernel,
        out_shape=[
            jax.ShapeDtypeStruct((rows, cols), jnp.bfloat16),
            jax.ShapeDtypeStruct((group, cols), jnp.bfloat16),
            half,
            half,
            half,
            jax.ShapeDtypeStruct((8, head_cols), jnp.float32),
        ],
        in_specs=[ANYWHERE] + [IN_VMEM] * 14,
        out_specs=[IN_VMEM] * 6,
        scratch_shapes=[
            pltpu.VMEM((rows, cols), jnp.bfloat16),
            pltpu.VMEM((group, head_cols), jnp.bfloat16),
            wide,
            wide,
            pltpu.VMEM((group, LANES), jnp.float32),
            pltpu.VMEM((group, LANES), jnp.float32),
            pltpu.SemaphoreType.DMA((2, 2)),
        ]
        + fold_scratch(nz, rows, cols, busy_y_split(rows), parts.dtype),
        cost_estimate=LINK_TIME,
        compiler_params=pltpu.CompilerParams(
            collective_id=collective, has_side_effects=True, vmem_limit_bytes=62 << 20
        ),
    )(parts, own_grad, w_out, *saved, *gains, *tables)


def plane_gather_kernel(count, *refs):
    srcs, block = refs[:count], refs[count]
    outs, landed = refs[count + 1 : 2 * count + 1], refs[2 * count + 1]
    sent, got, kept, swap_sems = refs[2 * count + 2 :]
    place = Place()
    z, x, c, nz = place.z, place.x, place.c, place.z_count
    ZU, ZD, XF, CO, CX = range(5)
    up, down = place.device(z=z + 1), place.device(z=z - 1)
    over_x, over_c = place.device(x=1 - x), place.device(c=1 - c)
    place.meet()
    every = range(count)
    swap = send(block, landed, swap_sems.at[0], swap_sems.at[1], place.device(y=1 - place.y))

    def push(a, kind, zz, xx, device, own=False):
        ref = outs[a].at[zz, xx, c]
        send(srcs[a] if own else ref, ref, sent.at[kind, a, zz], got.at[kind, a, zz], device)

    def arrival(a, kind, zz, xx, cc):
        ref = outs[a].at[zz, xx, cc]
        pltpu.make_async_copy(ref, ref, got.at[kind, a, zz]).wait()

    def departure(a, kind, zz, xx):
        ref = outs[a].at[zz, xx, c]
        pltpu.make_async_copy(ref, ref, sent.at[kind, a, zz]).wait()

    keeps = []
    for a in every:
        push(a, XF, z, x, over_x, own=True)

        @pl.when(z < nz - 1)
        def _():
            push(a, ZU, z, x, up, own=True)

        @pl.when(z > 0)
        def _():
            push(a, ZD, z, x, down, own=True)

        push(a, CO, z, x, over_c, own=True)
        keep = pltpu.make_async_copy(srcs[a], outs[a].at[z, x, c], kept.at[a])
        keep.start()
        keeps.append(keep)

    def relay(a, zz):
        arrival(a, XF, zz, 1 - x, c)
        push(a, CX, zz, 1 - x, over_c)

    for d in range(nz):
        below, above = z - d - 1, z + d + 1
        for a in every:
            if d < nz - 1:
                @pl.when(below >= 0)
                def _():
                    arrival(a, ZU, below, x, c)

                    @pl.when(z < nz - 1)
                    def _():
                        push(a, ZU, below, x, up)

                    push(a, XF, below, x, over_x)
                    push(a, CO, below, x, over_c)

                @pl.when(above < nz)
                def _():
                    arrival(a, ZD, above, x, c)

                    @pl.when(z > 0)
                    def _():
                        push(a, ZD, above, x, down)

                    push(a, XF, above, x, over_x)
                    push(a, CO, above, x, over_c)

    for d in range(nz):
        for a in every:
            if d == 0:
                relay(a, z)
            else:
                @pl.when(z - d >= 0)
                def _():
                    relay(a, z - d)

                @pl.when(z + d < nz)
                def _():
                    relay(a, z + d)

    for a in every:
        keeps[a].wait()
        for zz in range(nz):
            arrival(a, CO, zz, x, 1 - c)
            arrival(a, CX, zz, 1 - x, 1 - c)
            departure(a, XF, zz, x)
            departure(a, CO, zz, x)
            departure(a, CX, zz, 1 - x)

            @pl.when((zz <= z) & (z < nz - 1))
            def _():
                departure(a, ZU, zz, x)

            @pl.when((zz >= z) & (z > 0))
            def _():
                departure(a, ZD, zz, x)

    swap.wait()


def gather_in_plane(shards, block, collective):
    nz = lax.axis_size("dp") // 4
    count = len(shards)
    return pl.pallas_call(
        functools.partial(plane_gather_kernel, count),
        out_shape=[jax.ShapeDtypeStruct((nz, 2, 2) + s.shape, s.dtype) for s in shards]
        + [jax.ShapeDtypeStruct(block.shape, block.dtype)],
        in_specs=[ANYWHERE] * (count + 1),
        out_specs=[ANYWHERE] * (count + 1),
        scratch_shapes=[
            pltpu.SemaphoreType.DMA((5, count, nz)),
            pltpu.SemaphoreType.DMA((5, count, nz)),
            pltpu.SemaphoreType.DMA((count,)),
            pltpu.SemaphoreType.DMA((2,)),
        ],
        cost_estimate=LINK_TIME,
        compiler_params=pltpu.CompilerParams(collective_id=collective, has_side_effects=True),
    )(*shards, block)


def plane_scatter_kernel(count, *refs):
    lefts, rights = refs[:count], refs[count : 2 * count]
    small, row_part = refs[2 * count : 2 * count + 2]
    refs = refs[2 * count + 2 :]
    outs, small_out, row_landed = refs[:count], refs[count], refs[count + 1]
    total, leaving, from_c, full_x, z_buf, small_sum, small_got = refs[count + 2 : count + 9]
    sent, got, small_sems, row_sems = refs[count + 9 :]
    place = Place()
    z, x, c, nz = place.z, place.x, place.c, place.z_count
    rows = total.shape[3]
    C0, C1, XF, ZU, ZD = range(5)
    over_x, over_c = place.device(x=1 - x), place.device(c=1 - c)
    over_y = place.device(y=1 - place.y)
    place.meet(all_z=True)

    small_sum[0] = small[...]

    def small_start(i):
        return send(
            small_sum.at[i],
            small_got.at[i],
            small_sems.at[0, i],
            small_sems.at[1, i],
            (over_x, over_c, over_y)[i],
        )

    def small_end(i, copy):
        copy.wait()
        small_sum[i + 1] = small_sum[i] + small_got[i]

    def small_z_start():
        return [
            send(
                small_sum.at[3],
                small_got.at[2 + d],
                small_sems.at[0, 2 + d],
                small_sems.at[1, 2 + d],
                place.device(z=(z + d) % nz),
            )
            for d in range(1, nz)
        ]

    def small_z_end(copies):
        for copy in copies:
            copy.wait()
        result = jnp.zeros_like(small_out)
        for zz in range(nz):
            away = (z - zz) % nz
            result = result + jnp.where(away == 0, small_sum[3], small_got[jnp.maximum(2 + away, 3)])
        small_out[...] = result

    def arrival(a, kind, zz, ref):
        pltpu.make_async_copy(ref, ref, got.at[kind, a, zz]).wait()

    small_copy = small_start(0)

    def make(dx, i):
        zz = place.far_first(i)
        xx = 1 - x if dx else x
        for a in range(count):

            def product(cc):
                shard = (zz * 2 + xx) * 2 + cc
                here = pl.ds(pl.multiple_of(shard * rows, rows), rows)
                return dot_tn(lefts[a][:, here], rights[a][...]).astype(total.dtype)

            leaving[dx, zz, a] = product(1 - c)
            send(
                leaving.at[dx, zz, a],
                from_c.at[dx, zz, a],
                sent.at[C1 if dx else C0, a, zz],
                got.at[C1 if dx else C0, a, zz],
                over_c,
            )
            total[dx, zz, a] = product(c)

    def join_cores(a, dx, zz):
        there = from_c.at[dx, zz, a]
        arrival(a, C1 if dx else C0, zz, there)
        add_rows(total.at[dx, zz, a], there, rows)

    def over_the_x(i):
        zz = place.far_first(i)
        for a in range(count):
            join_cores(a, 1, zz)
            send(total.at[1, zz, a], full_x.at[zz, a], sent.at[XF, a, zz], got.at[XF, a, zz], over_x)

    def along_z(i):
        zz = place.far_first(i)
        above = jnp.where(zz == z, nz, zz)
        landing = jnp.where(zz == z - 1, nz, zz)
        for a in range(count):
            mine = total.at[0, zz, a]
            join_cores(a, 0, zz)
            arrival(a, XF, zz, full_x.at[zz, a])
            add_rows(mine, full_x.at[zz, a], rows)

            @pl.when((z > 0) & (zz >= z))
            def _():
                arrival(a, ZU, zz, z_buf.at[zz, a])
                add_rows(mine, z_buf.at[zz, a], rows)

            @pl.when((z < nz - 1) & (zz <= z))
            def _():
                arrival(a, ZD, zz, z_buf.at[above, a])
                add_rows(mine, z_buf.at[above, a], rows)

            @pl.when(zz > z)
            def _():
                send(
                    mine,
                    z_buf.at[zz, a],
                    sent.at[ZU, a, zz],
                    got.at[ZU, a, zz],
                    place.device(z=z + 1),
                )

            @pl.when(zz < z)
            def _():
                send(
                    mine,
                    z_buf.at[landing, a],
                    sent.at[ZD, a, zz],
                    got.at[ZD, a, zz],
                    place.device(z=z - 1),
                )

    make(1, 0)
    row_copy = send(row_part, row_landed, row_sems.at[0], row_sems.at[1], over_y)
    small_end(0, small_copy)
    small_copy = small_start(1)
    for i in range(1, nz):
        make(1, i)
        over_the_x(i - 1)
        if i == 1:
            small_end(1, small_copy)
            small_copy = small_start(2)
    over_the_x(nz - 1)

    def own_chips(i, carry):
        make(0, i)
        return carry

    lax.fori_loop(0, nz, own_chips, 0)
    small_end(2, small_copy)
    small_copies = small_z_start()
    for i in range(nz):
        along_z(i)
        if i == 0:
            small_z_end(small_copies)
    row_copy.wait()

    for a in range(count):

        def widen(i, carry):
            here = pl.ds(pl.multiple_of(i * 16, 16), 16)
            outs[a][here] = total[0, z, a, here].astype(jnp.float32)
            return carry

        lax.fori_loop(0, rows // 16, widen, 0)

    def departure(a, kind, zz):
        ref = total.at[0, 0, a]
        pltpu.make_async_copy(ref, ref, sent.at[kind, a, zz]).wait()

    for a in range(count):
        for zz in range(nz):
            departure(a, C0, zz)
            departure(a, C1, zz)
            departure(a, XF, zz)

            @pl.when(zz > z)
            def _():
                departure(a, ZU, zz)

            @pl.when(zz < z)
            def _():
                departure(a, ZD, zz)


def scatter_in_plane(lefts, rights, small, row_part, collective):
    count = len(lefts)
    nz = lax.axis_size("dp") // 4
    cols, dt = rights[0].shape[1], rights[0].dtype
    rows = lefts[0].shape[1] // (4 * nz)
    blocks = pltpu.VMEM((2, nz, count, rows, cols), dt)
    return pl.pallas_call(
        functools.partial(plane_scatter_kernel, count),
        out_shape=[jax.ShapeDtypeStruct((rows, cols), jnp.float32)] * count
        + [
            jax.ShapeDtypeStruct(small.shape, small.dtype),
            jax.ShapeDtypeStruct(row_part.shape, row_part.dtype),
        ],
        in_specs=[IN_VMEM] * (2 * count + 1) + [ANYWHERE],
        out_specs=[IN_VMEM] * (count + 1) + [ANYWHERE],
        scratch_shapes=[
            blocks,
            blocks,
            blocks,
            pltpu.VMEM((nz, count, rows, cols), dt),
            pltpu.VMEM((nz + 1, count, rows, cols), dt),
            pltpu.VMEM((4,) + small.shape, small.dtype),
            pltpu.VMEM((2 + nz,) + small.shape, small.dtype),
            pltpu.SemaphoreType.DMA((5, count, nz)),
            pltpu.SemaphoreType.DMA((5, count, nz)),
            pltpu.SemaphoreType.DMA((2, 2 + nz)),
            pltpu.SemaphoreType.DMA((2,)),
        ],
        cost_estimate=LINK_TIME,
        compiler_params=pltpu.CompilerParams(
            collective_id=collective, has_side_effects=True, vmem_limit_bytes=62 << 20
        ),
    )(*lefts, *rights, small, row_part)


def dot_nn(a, b):
    return lax.dot_general(a, b, (((1,), (0,)), ((), ())), preferred_element_type=jnp.float32)


def dot_nt(a, b):
    return lax.dot_general(a, b, (((1,), (1,)), ((), ())), preferred_element_type=jnp.float32)


def dot_tn(a, b):
    return lax.dot_general(a, b, (((0,), (0,)), ((), ())), preferred_element_type=jnp.float32)


def pick(table, index):
    return sum(jnp.where(index == i, value, 0) for i, value in enumerate(table))


def expert_kernel(
    z_count,
    src,
    g_all,
    hot_ref,
    router_ref,
    lanes_ref,
    wg_ref,
    wu_ref,
    wd_ref,
    x_all,
    y_all,
    r_all,
    hidden_all,
    gate_pre_grad_all,
    up_grad_all,
    x_tile,
    g_tile,
    y_tile,
    r_tile,
    hidden_tile,
    gate_pre_grad_tile,
    up_grad_tile,
    load_sems,
    store_sems,
    sent,
    got,
    kept,
):
    place = Place()
    place.meet()
    third = src.shape[0] // 3
    spread = Spread(place, src, x_all, sent, got, kept, src.shape[0] // 2, 2 * third, third // 2)
    spread.begin()
    width = src.shape[1]
    tile = x_tile.shape[1]
    pairs = sorted(
        ((k, dx) for k in range(z_count) for dx in (0, 1)),
        key=lambda p: p[0] + (1.3 if p[0] else 0.5) * p[1],
    )
    tiles = 2 * len(pairs)
    near_table, across_table = [p[0] for p in pairs], [p[1] for p in pairs]

    def tile_at(i):
        pair, second = i // 2, i % 2
        zz = place.near_first(pick(near_table, pair))
        xx = jnp.where(pick(across_table, pair) == 1, 1 - place.x, place.x)
        cc = jnp.where(second == 1, 1 - place.c, place.c)
        return zz, xx, cc

    stores = (
        (y_tile, y_all),
        (r_tile, r_all),
        (hidden_tile, hidden_all),
        (gate_pre_grad_tile, gate_pre_grad_all),
        (up_grad_tile, up_grad_all),
    )

    def loads(i, slot):
        zz, xx, cc = tile_at(i)
        copies = []
        for yy in range(2):
            rows = pl.ds(yy * (tile // 2), tile // 2)
            copies.append(
                pltpu.make_async_copy(
                    x_all.at[zz, xx, cc, yy], x_tile.at[slot, rows], load_sems.at[slot, yy]
                )
            )
        copies.append(
            pltpu.make_async_copy(g_all.at[zz, xx, cc], g_tile.at[slot], load_sems.at[slot, 2])
        )
        return copies

    def store(i, slot):
        zz, xx, cc = tile_at(i)
        return [
            pltpu.make_async_copy(here.at[slot], there.at[zz, xx, cc], store_sems.at[slot, n])
            for n, (here, there) in enumerate(stores)
        ]

    steps = {}
    for position, (k, dx) in enumerate(pairs):
        todo = []
        if dx == 0:
            if k == 0:
                todo.append((spread.relay, 0))
            elif k > 1:
                todo.append((spread.diagonal_along_z, k - 1))
            if k + 1 < z_count:
                todo += [(spread.along_z, k + 1), (spread.column, k + 1)]
            if k > 0:
                todo.append((spread.relay, k))
        else:
            if k == z_count - 1 and k > 0:
                todo.append((spread.diagonal_along_z, k))
            todo.append((spread.diagonal, k))
        steps[2 * position] = todo

    def prepare(i):
        for position in range(tiles):
            pair = position // 2
            k, dx = pairs[pair]

            @pl.when(i == position)
            def _():
                if position % 2 == 0:
                    for step, number in steps[position]:
                        step(number)
                    if position == 0:
                        spread.keep.wait()
                elif dx == 0:
                    spread.sibling_near(k)
                else:
                    spread.sibling_far(k)

        for copy in loads(i, i % 2):
            copy.start()

    def compute(i, carry):
        slot = i % 2
        for copy in loads(i, slot):
            copy.wait()

        @pl.when(i >= 2)
        def _():
            for copy in store(i - 2, slot):
                copy.wait()

        @pl.when(i < tiles - 1)
        def _():
            prepare(i + 1)

        zz, xx, cc = tile_at(i)
        rows = x_tile[slot]
        logits = jnp.where(lanes_ref[1:2] > 0.0, dot_nn(rows, router_ref[...]), -1e30)
        weights = jnp.exp(logits - jnp.max(logits, axis=1, keepdims=True))
        own_weight = jnp.sum(weights * lanes_ref[0:1], axis=1, keepdims=True)
        named = jnp.transpose(hot_ref[(zz * 2 + xx) * 2 + cc].astype(jnp.float32))
        hot = jnp.sum(named * lanes_ref[0:1, : named.shape[1]], axis=1, keepdims=True)
        gate = hot * own_weight / jnp.sum(weights, axis=1, keepdims=True)
        gate_pre = dot_nn(rows, wg_ref[...])
        up_pre = dot_nn(rows, wu_ref[...])
        raw_grad = dot_nt(g_tile[slot], wd_ref[...])

        sigmoid = jax.nn.sigmoid(gate_pre)
        silu = gate_pre * sigmoid
        hidden = silu * up_pre
        gate_grad = jnp.sum(hidden * raw_grad, axis=1, keepdims=True)
        coarse = gate_grad.astype(jnp.bfloat16).astype(jnp.float32)
        r_tile[slot, :, width:] = (
            coarse * lanes_ref[2:3] + (gate_grad - coarse) * lanes_ref[3:4]
        ).astype(jnp.bfloat16)
        hidden_gated = (gate * hidden).astype(jnp.bfloat16)
        hidden_tile[slot] = hidden_gated
        hidden_grad = gate * raw_grad
        up_grad = (hidden_grad * silu).astype(jnp.bfloat16)
        up_grad_tile[slot] = up_grad
        gate_pre_grad = (
            hidden_grad * up_pre * sigmoid * (1.0 + gate_pre * (1.0 - sigmoid))
        ).astype(jnp.bfloat16)
        gate_pre_grad_tile[slot] = gate_pre_grad
        y_tile[slot] = dot_nn(hidden_gated, wd_ref[...]).astype(jnp.bfloat16)
        r_tile[slot, :, :width] = (
            dot_nt(gate_pre_grad, wg_ref[...]) + dot_nt(up_grad, wu_ref[...])
        ).astype(jnp.bfloat16)
        for copy in store(i, slot):
            copy.start()
        return carry

    prepare(0)
    lax.fori_loop(0, tiles, compute, 0)
    for i in (tiles - 2, tiles - 1):
        for copy in store(i, i % 2):
            copy.wait()
    spread.finish()


def expert_pass(block, upstream, hot, router, lanes, w_gate, w_up, w_down, collective):
    rows, width = block.shape
    units = w_gate.shape[1]
    nz = lax.axis_size("dp") // 4
    tile = 2 * rows
    out = (nz, 2, 2, tile)
    return pl.pallas_call(
        functools.partial(expert_kernel, nz),
        in_specs=[ANYWHERE] * 2 + [IN_VMEM] * 6,
        out_specs=[ANYWHERE] * 6,
        out_shape=[
            jax.ShapeDtypeStruct((nz, 2, 2, 2, rows, width), jnp.bfloat16),
            jax.ShapeDtypeStruct(out + (width,), jnp.bfloat16),
            jax.ShapeDtypeStruct(out + (width + LANES,), jnp.bfloat16),
        ]
        + [jax.ShapeDtypeStruct(out + (units,), jnp.bfloat16)] * 3,
        scratch_shapes=[
            pltpu.VMEM((2, tile, width), jnp.bfloat16),
            pltpu.VMEM((2, tile, width), jnp.bfloat16),
            pltpu.VMEM((2, tile, width), jnp.bfloat16),
            pltpu.VMEM((2, tile, width + LANES), jnp.bfloat16),
            pltpu.VMEM((2, tile, units), jnp.bfloat16),
            pltpu.VMEM((2, tile, units), jnp.bfloat16),
            pltpu.VMEM((2, tile, units), jnp.bfloat16),
            pltpu.SemaphoreType.DMA((2, 3)),
            pltpu.SemaphoreType.DMA((2, 5)),
            pltpu.SemaphoreType.DMA((Spread.KINDS, nz)),
            pltpu.SemaphoreType.DMA((Spread.KINDS, nz)),
            pltpu.SemaphoreType.DMA,
        ],
        cost_estimate=LINK_TIME,
        compiler_params=pltpu.CompilerParams(
            collective_id=collective, has_side_effects=True, vmem_limit_bytes=60 << 20
        ),
    )(block, upstream.reshape(out + (width,)), hot, router, lanes, w_gate, w_up, w_down)


def dense_body(
    tokens,
    routes,
    cotangent,
    attn_gain,
    q_gain,
    k_gain,
    w_query,
    w_key,
    w_value,
    w_out,
    mlp_gain,
    router,
    w_gate,
    w_up,
    w_down,
):
    rank_index = lax.axis_index("tensor")
    own_rows = tokens.shape[0]
    head_cols = w_query.shape[1]
    col_start = rank_index * head_cols
    row_start = rank_index * own_rows
    experts = router.shape[1]
    q_gain_local = lax.dynamic_slice_in_dim(q_gain, col_start, head_cols)
    k_gain_local = lax.dynamic_slice_in_dim(k_gain, col_start, head_cols)
    expert_ids = jnp.arange(experts, dtype=jnp.int32)
    named = jnp.any(routes[None] == expert_ids[:, None, None], axis=2).astype(jnp.bfloat16)
    q_all, k_all, v_all, o_all, hot, other_tokens = gather_in_plane(
        (w_query, w_key, w_value, w_out, named), tokens, 1
    )
    hot = hot.reshape(-1, *named.shape)
    q_all, k_all, v_all = (w.reshape(D, head_cols) for w in (q_all, k_all, v_all))
    o_all = o_all.reshape(-1, *w_out.shape)
    first = rank_index == 0
    inputs_both = jnp.concatenate(
        [jnp.where(first, tokens, other_tokens), jnp.where(first, other_tokens, tokens)], axis=0
    ).astype(jnp.float32)
    unit_both = inputs_both * lax.rsqrt(
        jnp.mean(inputs_both * inputs_both, axis=1, keepdims=True) + EPSILON
    )
    normed = (unit_both * attn_gain).astype(jnp.bfloat16)
    inputs = tokens.astype(jnp.float32)
    attn_inv = lax.rsqrt(jnp.mean(inputs * inputs, axis=1, keepdims=True) + EPSILON)
    own_expert = lax.axis_index("dp")
    lane = jnp.arange(LANES)
    marked = own_expert + experts * rank_index
    lanes = jnp.stack(
        [lane == own_expert, lane < experts, lane == marked, lane == marked + 2 * experts]
        + [lane < 0] * 4
    ).astype(jnp.float32)
    router_wide = jnp.pad(router, ((0, 0), (0, LANES - experts)))
    tables = signed_rope_tables()
    gains = (q_gain_local[None], k_gain_local[None])
    (
        upstream_all,
        queries,
        keys_raw,
        values,
        query_rot,
        key_rot,
        mixed_heads,
        query_inv,
        key_inv,
        log_total,
        attended,
    ) = attend(cotangent, normed, (q_all, k_all, v_all, o_all), gains, tables, 6)
    upstream_all = upstream_all.reshape(-1, D)
    hidden_one = inputs + attended
    mlp_inv = lax.rsqrt(jnp.mean(hidden_one * hidden_one, axis=1, keepdims=True) + EPSILON)
    normed_two = (hidden_one * mlp_inv * mlp_gain).astype(jnp.bfloat16)
    own_routes = lax.dynamic_slice_in_dim(routes, row_start, own_rows, 0)
    own_hot = jnp.any(own_routes[:, :, None] == expert_ids[None, None, :], axis=1)
    own_probs = jax.nn.softmax(matmul(normed_two, router), axis=1)
    rows_all, y_part, r_part, *for_weights = expert_pass(
        normed_two, upstream_all, hot, router_wide, lanes, w_gate[0], w_up[0], w_down[0], 2
    )
    rows_all, y_part = rows_all.reshape(-1, D), y_part.reshape(-1, D)
    for_weights = [array.reshape(rows_all.shape[0], -1) for array in for_weights]
    blocks = (lax.axis_size("dp") // 4, 2, 2, 2, own_rows)
    returned, gate_weight_grad, up_weight_grad, down_weight_grad = scatter_sum(
        r_part.reshape(*blocks, D + LANES), [rows_all, upstream_all, *for_weights], 3
    )
    expert_grad = jnp.sum(
        returned[:, D : D + 4 * experts].astype(jnp.float32).reshape(own_rows, 4, experts), axis=1
    )
    expert_grad = jnp.where(own_hot, expert_grad, 0.0)
    returned = returned[:, :D]
    upstream = cotangent.astype(jnp.float32)
    logit_grad = own_probs * (expert_grad - jnp.sum(expert_grad * own_probs, axis=1, keepdims=True))
    router_grad = jnp.dot(normed_two.astype(jnp.float32).T, logit_grad, precision=HIGHEST)
    normed_two_grad = returned.astype(jnp.float32) + jnp.dot(
        logit_grad, router.astype(jnp.float32).T, precision=HIGHEST
    )
    scaled_grad = normed_two_grad * mlp_gain
    hidden_one_grad = (
        upstream
        + mlp_inv * scaled_grad
        - hidden_one * mlp_inv**3 * jnp.mean(hidden_one * scaled_grad, axis=1, keepdims=True)
    )
    mlp_gain_grad = jnp.sum(normed_two_grad * hidden_one * mlp_inv, axis=0)
    saved = (queries, keys_raw, query_rot, key_rot, values, query_inv, key_inv, log_total)
    mixture, attended_grad, query_grad, key_grad, value_grad, gain_grads = attend_back(
        y_part.reshape(*blocks, D), hidden_one_grad.astype(jnp.bfloat16), o_all, saved, gains, tables, 7
    )
    layer_out = (hidden_one + mixture.astype(jnp.float32)).astype(jnp.bfloat16)
    q_gain_part, k_gain_part = gain_grads[0], gain_grads[1]
    normed_part = (
        jnp.einsum("gc,rc->gr", query_grad, q_all, preferred_element_type=jnp.float32)
        + jnp.einsum("gc,rc->gr", key_grad, k_all, preferred_element_type=jnp.float32)
        + jnp.einsum("gc,rc->gr", value_grad, v_all, preferred_element_type=jnp.float32)
    )
    attn_gain_grad = jnp.sum(normed_part * unit_both, axis=0)
    zero_width = jnp.zeros((D,), jnp.float32)
    q_gain_full = lax.dynamic_update_slice_in_dim(zero_width, q_gain_part, col_start, 0)
    k_gain_full = lax.dynamic_update_slice_in_dim(zero_width, k_gain_part, col_start, 0)
    small_grads = jnp.concatenate(
        [
            jnp.stack([attn_gain_grad, q_gain_full, k_gain_full, mlp_gain_grad]),
            jnp.zeros((4, D), jnp.float32),
            jnp.transpose(router_grad),
        ],
        axis=0,
    )
    row_part = lax.dynamic_slice_in_dim(
        normed_part, (1 - rank_index) * own_rows, own_rows, 0
    ).astype(jnp.bfloat16)
    own_part = lax.dynamic_slice_in_dim(normed_part, row_start, own_rows, 0)
    *weight_sums, small_sums, other_part = scatter_in_plane(
        (normed, normed, normed, attended_grad),
        (query_grad, key_grad, value_grad, mixed_heads),
        small_grads,
        row_part,
        4,
    )
    normed_grad = own_part + other_part.astype(jnp.float32)
    scaled_input = normed_grad * attn_gain
    tokens_grad = (
        hidden_one_grad
        + attn_inv * scaled_input
        - inputs * attn_inv**3 * jnp.mean(inputs * scaled_input, axis=1, keepdims=True)
    )
    attn_gain_grad, q_gain_grad, k_gain_grad, mlp_gain_grad = (small_sums[i] for i in range(4))
    router_grad = jnp.transpose(small_sums[8:])
    return (
        layer_out,
        tokens_grad,
        attn_gain_grad,
        q_gain_grad,
        k_gain_grad,
        weight_sums[0],
        weight_sums[1],
        weight_sums[2],
        jnp.transpose(weight_sums[3]),
        mlp_gain_grad,
        router_grad,
        gate_weight_grad[None],
        up_weight_grad[None],
        down_weight_grad[None],
    )


def solution(mesh):
    in_specs = (
        P(("dp", "tensor"), None),
        P("dp", None),
        P(("dp", "tensor"), None),
        P(),
        P(),
        P(),
        P("dp", "tensor"),
        P("dp", "tensor"),
        P("dp", "tensor"),
        P("tensor", "dp"),
        P(),
        P(),
        P("dp", None, "tensor"),
        P("dp", None, "tensor"),
        P("dp", "tensor", None),
    )
    out_specs = (
        P(("dp", "tensor"), None),
        P(("dp", "tensor"), None),
        P(),
        P(),
        P(),
        P("dp", "tensor"),
        P("dp", "tensor"),
        P("dp", "tensor"),
        P("tensor", "dp"),
        P(),
        P(),
        P("dp", None, "tensor"),
        P("dp", None, "tensor"),
        P("dp", "tensor", None),
    )
    experts = mesh.shape["dp"]
    body = dense_body if experts <= 2 * TOPK else routed_body
    return jax.shard_map(body, mesh=mesh, in_specs=in_specs, out_specs=out_specs, check_vma=False)
```

```python
import functools

import jax
import jax.numpy as jnp
from jax import lax
from jax.experimental import pallas as pl
from jax.experimental.pallas import tpu as pltpu
from jax.sharding import PartitionSpec as P

D = 2048
HEAD = 128
TOPK = 8
PROMPT = 256
CONT = 64
GROUP = 384


EPSILON = 1e-05
ROPE_BASE = 10000.0
HIGHEST = lax.Precision.HIGHEST


def matmul(first_op, second_op):
    return jnp.dot(first_op, second_op, preferred_element_type=jnp.float32)


def gather_rows(values):
    return lax.all_gather(values, "tensor", axis=0, tiled=True)


def sum_rows(values):
    return lax.psum_scatter(values, "tensor", scatter_dimension=0, tiled=True)


def tensor_total(values):
    return lax.psum((values[0], values[1]), "tensor")


def expert_swap(values):
    return lax.all_to_all(values, "dp", split_axis=0, concat_axis=0, tiled=True)


def sum_slots(values):
    return lax.psum_scatter(values, "tensor", scatter_dimension=1, tiled=True)


def group_positions():
    position = jnp.arange(GROUP, dtype=jnp.int32)
    return jnp.where(position < PROMPT, position, PROMPT + (position - PROMPT) % CONT)


def visible_keys():
    position = jnp.arange(GROUP, dtype=jnp.int32)
    member = jnp.where(position < PROMPT, -1, (position - PROMPT) // CONT)
    causal = position[None, :] <= position[:, None]
    return causal & ((member[None, :] == -1) | (member[None, :] == member[:, None]))


def rope_tables():
    half_head = HEAD // 2
    frequency = ROPE_BASE ** (-2.0 * jnp.arange(half_head, dtype=jnp.float32) / HEAD)
    angles = group_positions().astype(jnp.float32)[:, None] * frequency[None, :]
    angles = jnp.concatenate([angles, angles], axis=1)
    return (jnp.cos(angles), jnp.sin(angles))


def rotate(values, cosine_table, sine_table):
    half_head = HEAD // 2
    turned = jnp.concatenate([-values[..., half_head:], values[..., :half_head]], axis=-1)
    return values * cosine_table[:, None, :] + turned * sine_table[:, None, :]


def unrotate(values, cosine_table, sine_table):
    half_head = HEAD // 2
    scaled = values * sine_table[:, None, :]
    turned = jnp.concatenate([scaled[..., half_head:], -scaled[..., :half_head]], axis=-1)
    return values * cosine_table[:, None, :] + turned


def gate_split(rows_in, hot_table, router):
    gates = jax.nn.softmax(matmul(rows_in, router), axis=1)
    weights = jnp.sum(jnp.where(hot_table, gates[:, None, :], 0.0), axis=2)
    return (gates, weights)


def routed_body(
    tokens,
    routes,
    cotangent,
    attn_gain,
    q_gain,
    k_gain,
    w_query,
    w_key,
    w_value,
    w_out,
    mlp_gain,
    router,
    w_gate,
    w_up,
    w_down,
):
    rank_index = lax.axis_index("tensor")
    tensor_count = lax.axis_size("tensor")
    own_rows = tokens.shape[0]
    head_cols = w_query.shape[1]
    local_heads = head_cols // HEAD
    col_start = rank_index * head_cols
    row_start = rank_index * own_rows
    experts = router.shape[1]
    half_cap = (own_rows * TOPK * 4 + 3 * experts - 1) // (3 * experts)
    capacity = tensor_count * half_cap
    attn_scale = HEAD ** (-0.5)
    head_shape = (GROUP, local_heads, HEAD)
    q_gain_local = lax.dynamic_slice_in_dim(q_gain, col_start, head_cols)
    k_gain_local = lax.dynamic_slice_in_dim(k_gain, col_start, head_cols)
    inputs = tokens.astype(jnp.float32)
    attn_inv = lax.rsqrt(jnp.mean(inputs * inputs, axis=1, keepdims=True) + EPSILON)
    normed = gather_rows((inputs * attn_inv * attn_gain).astype(jnp.bfloat16))
    pieces = (
        lax.all_gather(w_query, "dp", axis=0, tiled=True),
        lax.all_gather(w_key, "dp", axis=0, tiled=True),
        lax.all_gather(w_value, "dp", axis=0, tiled=True),
    )
    normed_part = normed
    queries = matmul(normed_part, pieces[0])
    keys_raw = matmul(normed_part, pieces[1])
    values_raw = matmul(normed_part, pieces[2])
    query_sq, key_sq = tensor_total(
        (jnp.sum(queries * queries, axis=1), jnp.sum(keys_raw * keys_raw, axis=1))
    )
    query_inv = lax.rsqrt(query_sq / D + EPSILON)[:, None]
    key_inv = lax.rsqrt(key_sq / D + EPSILON)[:, None]
    cosine_table, sine_table = rope_tables()
    query_rot = rotate(
        (queries * query_inv * q_gain_local).reshape(head_shape), cosine_table, sine_table
    ).astype(jnp.bfloat16)
    key_rot = rotate(
        (keys_raw * key_inv * k_gain_local).reshape(head_shape), cosine_table, sine_table
    ).astype(jnp.bfloat16)
    value_heads = values_raw.astype(jnp.bfloat16).reshape(head_shape)
    visible = visible_keys()[None]

    def masked_scores():
        raw_scores = (
            jnp.einsum("qhd,khd->hqk", query_rot, key_rot, preferred_element_type=jnp.float32)
            * attn_scale
        )
        return jnp.where(visible, raw_scores, -1e30)

    scores = masked_scores()
    row_max = jnp.max(scores, axis=2, keepdims=True)
    exponent = jnp.exp(scores - row_max)
    row_total = jnp.sum(exponent, axis=2, keepdims=True)
    log_total = row_max + jnp.log(row_total)
    mixed_heads = jnp.einsum(
        "hqk,khd->qhd",
        (exponent / row_total).astype(jnp.bfloat16),
        value_heads,
        preferred_element_type=jnp.float32,
    )
    mixed_heads = mixed_heads.reshape(GROUP, head_cols).astype(jnp.bfloat16)
    attn_part = matmul(mixed_heads, lax.all_gather(w_out, "dp", axis=1, tiled=True))
    attended = sum_rows(attn_part)
    hidden_one = inputs + attended
    mlp_inv = lax.rsqrt(jnp.mean(hidden_one * hidden_one, axis=1, keepdims=True) + EPSILON)
    normed_two = (hidden_one * mlp_inv * mlp_gain).astype(jnp.bfloat16)
    expert_ids = jnp.arange(experts, dtype=jnp.int32)
    route_hot = routes[:, :, None] == expert_ids[None, None, :]
    flat_hot = route_hot.astype(jnp.int32).reshape(tensor_count, own_rows * TOPK, experts)
    within = jnp.sum((jnp.cumsum(flat_hot, axis=1) - flat_hot) * flat_hot, axis=2).reshape(
        GROUP, TOPK
    )
    owner_of = (jnp.arange(GROUP, dtype=jnp.int32) // own_rows)[:, None]
    own_routes = lax.dynamic_slice_in_dim(routes, row_start, own_rows, 0)
    own_within = lax.dynamic_slice_in_dim(within, row_start, own_rows, 0)
    own_hot = lax.dynamic_slice_in_dim(route_hot, row_start, own_rows, 0)
    own_dest = own_routes * half_cap + own_within
    gate_weight = w_gate[0]
    up_weight = w_up[0]
    down_weight = w_down[0]
    normed_two_all = gather_rows(normed_two)
    gates_every, gate_every = gate_split(normed_two_all, route_hot, router)
    own_probs = lax.dynamic_slice_in_dim(gates_every, row_start, own_rows, 0)
    gate_weights = lax.dynamic_slice_in_dim(gate_every, row_start, own_rows, 0)
    destination = routes * capacity + owner_of * half_cap + within
    send_rows = (
        jnp.zeros((experts * capacity, D), jnp.bfloat16)
        .at[destination]
        .set(jnp.broadcast_to(normed_two_all[:, None, :], (GROUP, TOPK, D)))
        .reshape(experts, capacity, D)
    )
    received = lax.all_to_all(send_rows, "dp", split_axis=0, concat_axis=0, tiled=True)
    gate_pre = jnp.einsum("scd,df->scf", received, gate_weight, preferred_element_type=jnp.float32)
    up_pre = jnp.einsum("scd,df->scf", received, up_weight, preferred_element_type=jnp.float32)
    hidden = (jax.nn.silu(gate_pre) * up_pre).astype(jnp.bfloat16)
    expert_part = jnp.einsum("scf,fd->scd", hidden, down_weight, preferred_element_type=jnp.float32)
    expert_part, gate_pre, up_pre, hidden, received = (
        expert_part,
        gate_pre,
        up_pre,
        hidden,
        received,
    )
    back_rows = expert_swap(sum_slots(expert_part).astype(jnp.bfloat16)).reshape(
        experts * half_cap, D
    )
    picked = back_rows[own_dest].astype(jnp.float32)
    mixture = jnp.sum(gate_weights[:, :, None] * picked, axis=1)
    layer_out = (hidden_one + mixture).astype(jnp.bfloat16)
    upstream = cotangent.astype(jnp.float32)
    gate_grad = jnp.sum(upstream[:, None, :] * picked, axis=2)
    upstream_all = gather_rows(cotangent).astype(jnp.float32)
    send_grads = (
        jnp.zeros((experts * capacity, D), jnp.bfloat16)
        .at[destination]
        .set((gate_every[:, :, None] * upstream_all[:, None, :]).astype(jnp.bfloat16))
        .reshape(experts, capacity, D)
    )
    out_grads = expert_swap(send_grads)
    hidden_grad = jnp.einsum(
        "scd,fd->scf", out_grads, down_weight, preferred_element_type=jnp.float32
    )
    sigmoid = jax.nn.sigmoid(gate_pre)
    up_grad = (hidden_grad * gate_pre * sigmoid).astype(jnp.bfloat16)
    gate_pre_grad = (hidden_grad * up_pre * sigmoid * (1.0 + gate_pre * (1.0 - sigmoid))).astype(
        jnp.bfloat16
    )
    row_part = jnp.einsum(
        "scf,df->scd", gate_pre_grad, gate_weight, preferred_element_type=jnp.float32
    ) + jnp.einsum("scf,df->scd", up_grad, up_weight, preferred_element_type=jnp.float32)
    down_weight_grad = jnp.einsum(
        "scf,scd->fd", hidden, out_grads, preferred_element_type=jnp.float32
    )
    gate_weight_grad = jnp.einsum(
        "scd,scf->df", received, gate_pre_grad, preferred_element_type=jnp.float32
    )
    up_weight_grad = jnp.einsum(
        "scd,scf->df", received, up_grad, preferred_element_type=jnp.float32
    )
    returned_grads = expert_swap(sum_slots(row_part).astype(jnp.bfloat16)).reshape(
        experts * half_cap, D
    )
    normed_two_part = jnp.sum(returned_grads[own_dest].astype(jnp.float32), axis=1)
    expert_grad = jnp.sum(jnp.where(own_hot, gate_grad[:, :, None], 0.0), axis=1)
    logit_grad = own_probs * (expert_grad - jnp.sum(expert_grad * own_probs, axis=1, keepdims=True))
    router_grad = jnp.dot(normed_two.astype(jnp.float32).T, logit_grad, precision=HIGHEST)
    normed_two_grad = normed_two_part + jnp.dot(
        logit_grad, router.astype(jnp.float32).T, precision=HIGHEST
    )
    scaled_grad = normed_two_grad * mlp_gain
    hidden_one_grad = (
        upstream
        + mlp_inv * scaled_grad
        - hidden_one * mlp_inv**3 * jnp.mean(hidden_one * scaled_grad, axis=1, keepdims=True)
    )
    mlp_gain_grad = jnp.sum(normed_two_grad * hidden_one * mlp_inv, axis=0)
    attended_grad = gather_rows(hidden_one_grad.astype(jnp.bfloat16))
    mixed_grad = jnp.einsum(
        "gd,cd->gc",
        attended_grad,
        lax.all_gather(w_out, "dp", axis=1, tiled=True),
        preferred_element_type=jnp.float32,
    )
    mixed_grad = mixed_grad.astype(jnp.bfloat16).reshape(head_shape)
    attn_probs = jnp.exp(masked_scores() - log_total)
    prob_grad = jnp.einsum(
        "qhd,khd->hqk", mixed_grad, value_heads, preferred_element_type=jnp.float32
    )
    row_dot = jnp.sum(prob_grad * attn_probs, axis=2, keepdims=True)
    score_grad = (attn_probs * (prob_grad - row_dot)).astype(jnp.bfloat16)
    query_rot_grad = (
        jnp.einsum("hqk,khd->qhd", score_grad, key_rot, preferred_element_type=jnp.float32)
        * attn_scale
    )
    key_rot_grad = (
        jnp.einsum("hqk,qhd->khd", score_grad, query_rot, preferred_element_type=jnp.float32)
        * attn_scale
    )
    value_grad = (
        jnp.einsum(
            "hqk,qhd->khd",
            attn_probs.astype(jnp.bfloat16),
            mixed_grad,
            preferred_element_type=jnp.float32,
        )
        .reshape(GROUP, head_cols)
        .astype(jnp.bfloat16)
    )
    query_norm_grad = unrotate(query_rot_grad, cosine_table, sine_table).reshape(GROUP, head_cols)
    key_norm_grad = unrotate(key_rot_grad, cosine_table, sine_table).reshape(GROUP, head_cols)
    query_scaled = query_norm_grad * q_gain_local
    key_scaled = key_norm_grad * k_gain_local
    query_dot, key_dot = tensor_total(
        (jnp.sum(queries * query_scaled, axis=1), jnp.sum(keys_raw * key_scaled, axis=1))
    )
    query_grad = (
        query_inv * query_scaled - queries * query_inv**3 * (query_dot / D)[:, None]
    ).astype(jnp.bfloat16)
    key_grad = (key_inv * key_scaled - keys_raw * key_inv**3 * (key_dot / D)[:, None]).astype(
        jnp.bfloat16
    )
    q_gain_part = jnp.sum(query_norm_grad * queries * query_inv, axis=0)
    k_gain_part = jnp.sum(key_norm_grad * keys_raw * key_inv, axis=0)
    pieces = lax.all_gather((w_query, w_key, w_value), "dp", axis=0, tiled=True)
    normed_part = (
        jnp.einsum("gc,rc->gr", query_grad, pieces[0], preferred_element_type=jnp.float32)
        + jnp.einsum("gc,rc->gr", key_grad, pieces[1], preferred_element_type=jnp.float32)
        + jnp.einsum("gc,rc->gr", value_grad, pieces[2], preferred_element_type=jnp.float32)
    )
    weight_sums = lax.psum_scatter(
        jnp.concatenate(
            [
                jnp.einsum("gr,gc->rc", normed, query_grad, preferred_element_type=jnp.float32),
                jnp.einsum("gr,gc->rc", normed, key_grad, preferred_element_type=jnp.float32),
                jnp.einsum("gr,gc->rc", normed, value_grad, preferred_element_type=jnp.float32),
                jnp.einsum(
                    "gr,gc->rc", attended_grad, mixed_heads, preferred_element_type=jnp.float32
                ),
            ],
            axis=1,
        ),
        "dp",
        scatter_dimension=0,
        tiled=True,
    )
    normed_grad = sum_rows(normed_part)
    scaled_input = normed_grad * attn_gain
    tokens_grad = (
        hidden_one_grad
        + attn_inv * scaled_input
        - inputs * attn_inv**3 * jnp.mean(inputs * scaled_input, axis=1, keepdims=True)
    )
    attn_gain_grad = jnp.sum(normed_grad * inputs * attn_inv, axis=0)
    zero_width = jnp.zeros((D,), jnp.float32)
    q_gain_full = lax.dynamic_update_slice_in_dim(zero_width, q_gain_part, col_start, 0)
    k_gain_full = lax.dynamic_update_slice_in_dim(zero_width, k_gain_part, col_start, 0)
    attn_gain_grad, q_gain_grad, k_gain_grad, mlp_gain_grad, router_grad = lax.psum(
        (attn_gain_grad, q_gain_full, k_gain_full, mlp_gain_grad, router_grad), ("dp", "tensor")
    )
    return (
        layer_out,
        tokens_grad,
        attn_gain_grad,
        q_gain_grad,
        k_gain_grad,
        weight_sums[:, :head_cols],
        weight_sums[:, head_cols : 2 * head_cols],
        weight_sums[:, 2 * head_cols : 3 * head_cols],
        jnp.transpose(weight_sums[:, 3 * head_cols :]),
        mlp_gain_grad,
        router_grad,
        gate_weight_grad[None],
        up_weight_grad[None],
        down_weight_grad[None],
    )


MESH_ID = pl.DeviceIdType.MESH
LINK_TIME = pl.CostEstimate(flops=10**11, bytes_accessed=10**8, transcendentals=0)
EVERY = ("dp", "tensor")
LANES = 128
ANYWHERE = pl.BlockSpec(memory_space=pl.ANY)
IN_VMEM = pl.BlockSpec(memory_space=pltpu.VMEM)


class Place:
    def __init__(self):
        dp = lax.axis_index("dp")
        self.y = lax.axis_index("tensor")
        self.z, self.x, self.c = dp // 4, (dp // 2) % 2, dp % 2
        self.z_count = lax.axis_size("dp") // 4

    def device(self, z=None, x=None, c=None, y=None):
        z = self.z if z is None else z
        x = self.x if x is None else x
        c = self.c if c is None else c
        y = self.y if y is None else y
        return (z * 4 + x * 2 + c, y)

    def meet(self, use_y=True, all_z=False):
        barrier = pltpu.get_barrier_semaphore()
        partners = [self.device(x=1 - self.x), self.device(c=1 - self.c)]
        if use_y:
            partners.append(self.device(y=1 - self.y))
        if all_z:
            partners += [self.device(z=(self.z + d) % self.z_count) for d in range(1, self.z_count)]
        for partner in partners:
            pl.semaphore_signal(barrier, inc=1, device_id=partner, device_id_type=MESH_ID)
        if all_z:
            pl.semaphore_wait(barrier, len(partners))
            return

        @pl.when(self.z > 0)
        def _():
            pl.semaphore_signal(
                barrier, inc=1, device_id=self.device(z=self.z - 1), device_id_type=MESH_ID
            )

        @pl.when(self.z < self.z_count - 1)
        def _():
            pl.semaphore_signal(
                barrier, inc=1, device_id=self.device(z=self.z + 1), device_id_type=MESH_ID
            )

        ends = jnp.where(self.z > 0, 1, 0) + jnp.where(self.z < self.z_count - 1, 1, 0)
        pl.semaphore_wait(barrier, len(partners) + ends)

    def far_first(self, step):
        last = self.z_count - 1
        low = jnp.where(step < last - self.z, last - step, step - (last - self.z))
        high = jnp.where(step < self.z, step, last - (step - self.z))
        return jnp.where(self.z * 2 < self.z_count, low, high)


    def near_first(self, step):
        return self.far_first(self.z_count - 1 - step)


def send(src, dst, send_sem, recv_sem, device):
    copy = pltpu.make_async_remote_copy(
        src_ref=src, dst_ref=dst, send_sem=send_sem, recv_sem=recv_sem, device_id=device, device_id_type=MESH_ID
    )
    copy.start()
    return copy


def fetch(sources, targets, sems):
    copies = [
        pltpu.make_async_copy(source, target, sems.at[n])
        for n, (source, target) in enumerate(zip(sources, targets))
    ]
    for copy in copies:
        copy.start()
    return copies


def add_rows(total, part, rows, step=16):
    def chunk(i, carry):
        here = pl.ds(pl.multiple_of(i * step, step), step)
        total[here] = total[here] + part[here]
        return carry

    lax.fori_loop(0, rows // step, chunk, 0)


class Spread:
    KINDS = 14
    ZU, ZD, XF, YF, XH, YH, CO, CX, CY, CA, CB, CC, DU, DD = range(KINDS)

    def __init__(self, place, src, whole, sent, got, kept, own_split, through_z, other_split):
        self.place, self.src, self.whole, self.sent, self.got = place, src, whole, sent, got
        rows = src.shape[0]
        self.parts = {
            True: (pl.ds(0, own_split), pl.ds(own_split, rows - own_split)),
            False: (pl.ds(through_z, other_split), pl.ds(through_z + other_split, rows - through_z - other_split)),
        }
        self.deep = pl.ds(0, through_z)
        z, x, c, y = place.z, place.x, place.c, place.y
        self.up, self.down = place.device(z=z + 1), place.device(z=z - 1)
        self.over_x, self.over_y = place.device(x=1 - x), place.device(y=1 - y)
        self.over_c = place.device(c=1 - c)
        self.keep = pltpu.make_async_copy(src, whole.at[z, x, c, y], kept)

    def push(self, kind, zz, xx, yy, rows, device, origin=None):
        ref = self.whole.at[zz, xx, self.place.c, yy, rows]
        send(
            ref if origin is None else origin,
            ref,
            self.sent.at[kind, zz],
            self.got.at[kind, zz],
            device,
        )

    def arrival(self, kind, zz, xx, yy, rows=slice(None), sibling=False):
        cc = 1 - self.place.c if sibling else self.place.c
        ref = self.whole.at[zz, xx, cc, yy, rows]
        pltpu.make_async_copy(ref, ref, self.got.at[kind, zz]).wait()

    def departure(self, kind, zz, xx, yy, rows=slice(None)):
        ref = self.whole.at[zz, xx, self.place.c, yy, rows]
        pltpu.make_async_copy(ref, ref, self.sent.at[kind, zz]).wait()

    def column(self, k, origin=None):
        x, y, every = self.place.x, self.place.y, slice(None)
        zz = self.place.near_first(k)
        self.push(self.XF, zz, x, y, every, self.over_x, origin)
        self.push(self.YF, zz, x, y, every, self.over_y, origin)
        self.push(self.CO, zz, x, y, every, self.over_c, origin)

    def begin(self):
        z, x, y, nz = self.place.z, self.place.x, self.place.y, self.place.z_count

        @pl.when(z < nz - 1)
        def _():
            self.push(self.ZU, z, x, y, slice(None), self.up, self.src)

        @pl.when(z > 0)
        def _():
            self.push(self.ZD, z, x, y, slice(None), self.down, self.src)

        self.column(0, self.src)
        self.keep.start()

    def move_z(self, d, up_kind, down_kind, xx, yy, rows, hand_over):
        z, nz = self.place.z, self.place.z_count
        below, above = z - d, z + d

        @pl.when(below >= 0)
        def _():
            self.arrival(up_kind, below, xx, yy, rows)

            @pl.when(z < nz - 1)
            def _():
                self.push(up_kind, below, xx, yy, rows, self.up)

            if hand_over:
                self.push(self.CC, below, xx, yy, rows, self.over_c)

        @pl.when(above < nz)
        def _():
            self.arrival(down_kind, above, xx, yy, rows)

            @pl.when(z > 0)
            def _():
                self.push(down_kind, above, xx, yy, rows, self.down)

            if hand_over:
                self.push(self.CC, above, xx, yy, rows, self.over_c)

    def along_z(self, d):
        self.move_z(d, self.ZU, self.ZD, self.place.x, self.place.y, slice(None), False)

    def diagonal_along_z(self, d):
        self.move_z(d, self.DU, self.DD, 1 - self.place.x, 1 - self.place.y, self.deep, True)

    def relay(self, k):
        x, y, every = self.place.x, self.place.y, slice(None)
        zz = self.place.near_first(k)
        low, high = self.parts[k == 0]
        self.arrival(self.XF, zz, 1 - x, y)
        if low.size:
            self.push(self.YH, zz, 1 - x, y, low, self.over_y)
        self.push(self.CX, zz, 1 - x, y, every, self.over_c)
        self.arrival(self.YF, zz, x, 1 - y)
        self.push(self.XH, zz, x, 1 - y, high, self.over_x)
        self.push(self.CY, zz, x, 1 - y, every, self.over_c)

    def diagonal(self, k):
        z, nz = self.place.z, self.place.z_count
        xx, yy = 1 - self.place.x, 1 - self.place.y
        zz = self.place.near_first(k)
        low, high = self.parts[k == 0]
        self.arrival(self.XH, zz, xx, yy, high)
        if low.size:
            self.arrival(self.YH, zz, xx, yy, low)
        if k == 0:

            @pl.when(z < nz - 1)
            def _():
                self.push(self.DU, z, xx, yy, self.deep, self.up)

            @pl.when(z > 0)
            def _():
                self.push(self.DD, z, xx, yy, self.deep, self.down)

        self.push(self.CB, zz, xx, yy, high, self.over_c)
        if low.size:
            self.push(self.CA, zz, xx, yy, low, self.over_c)

    def sibling_near(self, k):
        x, y = self.place.x, self.place.y
        zz = self.place.near_first(k)
        self.arrival(self.CO, zz, x, y, sibling=True)
        self.arrival(self.CY, zz, x, 1 - y, sibling=True)

    def sibling_far(self, k):
        x, y = self.place.x, self.place.y
        zz = self.place.near_first(k)
        low, high = self.parts[k == 0]
        self.arrival(self.CX, zz, 1 - x, y, sibling=True)
        self.arrival(self.CB, zz, 1 - x, 1 - y, high, sibling=True)
        if low.size:
            self.arrival(self.CA, zz, 1 - x, 1 - y, low, sibling=True)
        if k > 0:
            self.arrival(self.CC, zz, 1 - x, 1 - y, self.deep, sibling=True)

    def finish(self):
        z, x, y, nz = self.place.z, self.place.x, self.place.y, self.place.z_count
        for k in range(nz):
            zz = self.place.near_first(k)
            low, high = self.parts[k == 0]
            self.departure(self.XF, zz, x, y)
            self.departure(self.YF, zz, x, y)
            self.departure(self.CO, zz, x, y)
            self.departure(self.CX, zz, 1 - x, y)
            self.departure(self.CY, zz, x, 1 - y)
            self.departure(self.XH, zz, x, 1 - y, high)
            self.departure(self.CB, zz, 1 - x, 1 - y, high)
            if low.size:
                self.departure(self.YH, zz, 1 - x, y, low)
                self.departure(self.CA, zz, 1 - x, 1 - y, low)
            if k > 0:
                self.departure(self.CC, zz, 1 - x, 1 - y, self.deep)

            @pl.when((zz <= z) & (z < nz - 1))
            def _():
                self.departure(self.ZU, zz, x, y)
                self.departure(self.DU, zz, 1 - x, 1 - y, self.deep)

            @pl.when((zz >= z) & (z > 0))
            def _():
                self.departure(self.ZD, zz, x, y)
                self.departure(self.DD, zz, 1 - x, 1 - y, self.deep)


class Fold:
    KINDS = 12
    CD, CX, CY, CO, XH, YH, XF, YF, ZU, ZD, DU, DD = range(KINDS)
    SPOT = {CD: (1, 1), CX: (1, 0), CY: (0, 1), CO: (0, 0)}

    def __init__(
        self, place, split, parts, total, from_c, half_x, half_y, z_buf, d_buf, sent, got, loaded
    ):
        self.place, self.parts, self.total, self.from_c = place, parts, total, from_c
        self.half_x, self.half_y, self.z_buf, self.d_buf = half_x, half_y, z_buf, d_buf
        self.sent, self.got, self.loaded = sent, got, loaded
        self.rows = total.shape[3]
        self.own_split, self.through_z, self.other_split = split
        self.deep = pl.ds(0, self.through_z)
        z, x, c, y = place.z, place.x, place.c, place.y
        self.over_x, self.over_y = place.device(x=1 - x), place.device(y=1 - y)
        self.over_c = place.device(c=1 - c)

    def diagonal_parts(self, zz, own):
        if own:
            low = pl.ds(0, self.own_split)
            high = pl.ds(self.own_split, self.rows - self.own_split)
            return low, high, self.half_y.at[low], self.half_x.at[pl.ds(0, high.size)]
        low = pl.ds(self.through_z, self.other_split)
        start = self.through_z + self.other_split
        high = pl.ds(start, self.rows - start)
        y_start = pl.multiple_of(self.own_split + zz * low.size, 16)
        x_start = pl.multiple_of(self.rows - self.own_split + zz * high.size, 16)
        return (
            low,
            high,
            self.half_y.at[pl.ds(y_start, low.size)],
            self.half_x.at[pl.ds(x_start, high.size)],
        )

    def push(self, kind, zz, src, dst, device):
        send(src, dst, self.sent.at[kind, zz], self.got.at[kind, zz], device)

    def arrival(self, kind, zz, ref):
        pltpu.make_async_copy(ref, ref, self.got.at[kind, zz]).wait()

    def begin(self):
        x, c, y, nz = self.place.x, self.place.c, self.place.y, self.place.z_count

        def start(kind, i):
            dx, dy = self.SPOT[kind]
            zz = self.place.far_first(i)
            xx, yy = (1 - x if dx else x), (1 - y if dy else y)
            self.push(
                kind, zz, self.parts.at[zz, xx, 1 - c, yy], self.from_c.at[dx, dy, zz], self.over_c
            )
            pltpu.make_async_copy(
                self.parts.at[zz, xx, c, yy], self.total.at[dx, dy, zz], self.loaded.at[kind, zz]
            ).start()

        for i in range(nz):
            start(self.CD, i)
            start(self.CX, i)
            start(self.CY, i)
        for i in range(nz):
            start(self.CO, i)

    def join_cores(self, kind, zz):
        dx, dy = self.SPOT[kind]
        here, there = self.total.at[dx, dy, zz], self.from_c.at[dx, dy, zz]
        pltpu.make_async_copy(here, here, self.loaded.at[kind, zz]).wait()
        self.arrival(kind, zz, there)
        add_rows(here, there, self.rows)

    def deep_push(self, zz):
        z, nz = self.place.z, self.place.z_count
        mine = self.total.at[1, 1, zz, self.deep]

        @pl.when(zz > z)
        def _():
            self.push(self.DU, zz, mine, self.d_buf.at[zz], self.place.device(z=z + 1))

        @pl.when(zz < z)
        def _():
            landing = jnp.where(zz == z - 1, nz, zz)
            self.push(self.DD, zz, mine, self.d_buf.at[landing], self.place.device(z=z - 1))

    def at_end(self):
        return (self.place.z == 0) | (self.place.z == self.place.z_count - 1)

    def halves(self, i):
        own = i == self.place.z_count - 1
        zz = self.place.far_first(i)
        self.join_cores(self.CD, zz)
        self.join_cores(self.CX, zz)
        if own:
            return
        self.push_halves(zz, False)

        @pl.when(self.at_end())
        def _():
            self.deep_push(zz)

    def push_halves(self, zz, own):
        low, high, land_y, land_x = self.diagonal_parts(zz, own)
        self.push(self.XH, zz, self.total.at[1, 1, zz, high], land_x, self.over_x)
        self.push(self.YH, zz, self.total.at[1, 1, zz, low], land_y, self.over_y)

    def deep_on(self, i):
        z = self.place.z
        zz = self.place.far_first(i)

        @pl.when(jnp.logical_not(self.at_end()))
        def _():
            @pl.when(zz > z)
            def _():
                self.arrival(self.DU, zz, self.d_buf.at[zz])

            @pl.when(zz < z)
            def _():
                self.arrival(self.DD, zz, self.d_buf.at[zz])

            add_rows(self.total.at[1, 1, zz, self.deep], self.d_buf.at[zz], self.through_z)
            self.deep_push(zz)

    def own_halves(self):
        z, nz = self.place.z, self.place.z_count
        mine = self.total.at[1, 1, z, self.deep]

        @pl.when(z > 0)
        def _():
            self.arrival(self.DU, z, self.d_buf.at[z])
            add_rows(mine, self.d_buf.at[z], self.through_z)

        @pl.when(z < nz - 1)
        def _():
            self.arrival(self.DD, z, self.d_buf.at[nz])
            add_rows(mine, self.d_buf.at[nz], self.through_z)

        self.push_halves(z, True)

    def columns(self, i):
        zz = self.place.far_first(i)
        low, high, land_y, land_x = self.diagonal_parts(zz, i == self.place.z_count - 1)
        self.join_cores(self.CY, zz)
        self.arrival(self.XH, zz, land_x)
        add_rows(self.total.at[0, 1, zz, high], land_x, high.size)
        self.arrival(self.YH, zz, land_y)
        add_rows(self.total.at[1, 0, zz, low], land_y, low.size)
        self.push(self.XF, zz, self.total.at[1, 0, zz], self.from_c.at[1, 1, zz], self.over_x)
        self.push(self.YF, zz, self.total.at[0, 1, zz], self.from_c.at[1, 0, zz], self.over_y)

    def along_z(self, i):
        z, nz = self.place.z, self.place.z_count
        zz = self.place.far_first(i)
        mine = self.total.at[0, 0, zz]
        self.join_cores(self.CO, zz)
        self.arrival(self.XF, zz, self.from_c.at[1, 1, zz])
        add_rows(mine, self.from_c.at[1, 1, zz], self.rows)
        self.arrival(self.YF, zz, self.from_c.at[1, 0, zz])
        add_rows(mine, self.from_c.at[1, 0, zz], self.rows)
        above = jnp.where(zz == z, nz, zz)

        @pl.when((z > 0) & (zz >= z))
        def _():
            self.arrival(self.ZU, zz, self.z_buf.at[zz])
            add_rows(mine, self.z_buf.at[zz], self.rows)

        @pl.when((z < nz - 1) & (zz <= z))
        def _():
            self.arrival(self.ZD, zz, self.z_buf.at[above])
            add_rows(mine, self.z_buf.at[above], self.rows)

        @pl.when(zz > z)
        def _():
            self.push(self.ZU, zz, mine, self.z_buf.at[zz], self.place.device(z=z + 1))

        @pl.when(zz < z)
        def _():
            landing = jnp.where(zz == z - 1, nz, zz)
            self.push(self.ZD, zz, mine, self.z_buf.at[landing], self.place.device(z=z - 1))

    def opening(self):
        last = self.place.z_count - 1
        return [functools.partial(self.halves, i) for i in range(last)] + [
            functools.partial(self.columns, i) for i in range(min(1, last))
        ]

    def middle(self):
        last = self.place.z_count - 1
        steps = [functools.partial(self.deep_on, i) for i in range(last)]
        steps.insert(1, functools.partial(self.halves, last))
        steps.append(self.own_halves)
        return steps + [functools.partial(self.columns, i) for i in range(min(1, last), last + 1)]

    def result(self):
        return self.total[0, 0, self.place.z]

    def finish(self):
        z, nz = self.place.z, self.place.z_count

        def departure(kind, zz, ref):
            pltpu.make_async_copy(ref, ref, self.sent.at[kind, zz]).wait()

        for i in range(nz):
            zz = self.place.far_first(i)
            low, high, land_y, land_x = self.diagonal_parts(zz, i == nz - 1)
            for kind in (self.CD, self.CX, self.CY, self.CO, self.XF, self.YF):
                departure(kind, zz, self.total.at[0, 0, zz])
            departure(self.XH, zz, land_x)
            departure(self.YH, zz, land_y)

            @pl.when(zz > z)
            def _():
                departure(self.ZU, zz, self.total.at[0, 0, zz])
                departure(self.DU, zz, self.d_buf.at[zz])

            @pl.when(zz < z)
            def _():
                departure(self.ZD, zz, self.total.at[0, 0, zz])
                departure(self.DD, zz, self.d_buf.at[zz])


def half_rows(rows, split):
    own, deep, other = split
    return (own, other), (rows - own, rows - deep - other)


def fold_scratch(nz, rows, cols, split, dt):
    (y_own, y_other), (x_own, x_other) = half_rows(rows, split)
    return [
        pltpu.VMEM((2, 2, nz, rows, cols), dt),
        pltpu.VMEM((2, 2, nz, rows, cols), dt),
        pltpu.VMEM((x_own + nz * x_other, cols), dt),
        pltpu.VMEM((y_own + nz * y_other, cols), dt),
        pltpu.VMEM((nz + 1, rows, cols), dt),
        pltpu.VMEM((nz + 1, split[1], cols), dt),
        pltpu.SemaphoreType.DMA((Fold.KINDS, nz)),
        pltpu.SemaphoreType.DMA((Fold.KINDS, nz)),
        pltpu.SemaphoreType.DMA((4, nz)),
    ]


def scatter_kernel(parts, *refs):
    streams, refs = refs[:5], refs[5:]
    out, wg_grad, wu_grad, wd_grad = refs[:4]
    tiles, tile_sems, scratch = refs[4:9], refs[9], refs[10:]
    place = Place()
    nz = place.z_count
    fold = Fold(place, row_split(out.shape[0]), parts, *scratch)
    count = streams[0].shape[0]
    place.meet()
    fold.begin()

    def loads(t, slot):
        return [
            pltpu.make_async_copy(stream.at[t], tile.at[slot], tile_sems.at[slot, n])
            for n, (stream, tile) in enumerate(zip(streams, tiles))
        ]

    def tile_step(t, carry):
        slot = t % 2
        for copy in loads(t, slot):
            copy.wait()

        @pl.when(t + 1 < count)
        def _():
            for copy in loads(t + 1, 1 - slot):
                copy.start()

        x_tile, g_tile, hidden, gate_pre_grad, up_grad = (tile[slot] for tile in tiles)
        wg_grad[...] += dot_tn(x_tile, gate_pre_grad)
        wu_grad[...] += dot_tn(x_tile, up_grad)
        wd_grad[...] += dot_tn(hidden, g_tile)
        return carry

    for copy in loads(0, 0):
        copy.start()
    for grad in (wg_grad, wu_grad, wd_grad):
        grad[...] = jnp.zeros_like(grad)
    steps = fold.opening() + fold.middle()
    steps += [functools.partial(fold.along_z, i) for i in range(nz)]
    done = 0
    for n, step in enumerate(steps):
        until = min(count, round(count * n / (len(steps) - 1)))
        lax.fori_loop(done, until, tile_step, 0)
        done = until
        step()
    out[...] = fold.result()
    fold.finish()


def row_split(rows):
    return rows // 2, rows // 2, rows // 4


def scatter_sum(parts, streams, collective):
    nz, _, _, _, rows, cols = parts.shape
    dt = parts.dtype
    width, units = streams[0].shape[1], streams[2].shape[1]
    tile = 256 if streams[0].shape[0] % 256 == 0 else GROUP // 2
    streams = [stream.reshape(-1, tile, stream.shape[1]) for stream in streams]
    shapes = [(width, units), (width, units), (units, width)]
    return pl.pallas_call(
        scatter_kernel,
        out_shape=[jax.ShapeDtypeStruct((rows, cols), dt)]
        + [jax.ShapeDtypeStruct(shape, jnp.float32) for shape in shapes],
        in_specs=[ANYWHERE] * 6,
        out_specs=[IN_VMEM] * 4,
        scratch_shapes=[pltpu.VMEM((2,) + stream.shape[1:], stream.dtype) for stream in streams]
        + [pltpu.SemaphoreType.DMA((2, 5))]
        + fold_scratch(nz, rows, cols, row_split(rows), dt),
        cost_estimate=LINK_TIME,
        compiler_params=pltpu.CompilerParams(
            collective_id=collective, has_side_effects=True, vmem_limit_bytes=62 << 20
        ),
    )(parts, *streams)


def turn(values):
    return pltpu.roll(values, HEAD // 2, 1)


def seen_keys():
    row = lax.broadcasted_iota(jnp.int32, (GROUP, GROUP), 0)
    col = lax.broadcasted_iota(jnp.int32, (GROUP, GROUP), 1)
    return (col <= row) & ((col < PROMPT) | (col >= row - row % CONT))


def signed_rope_tables():
    cosine_table, sine_table = rope_tables()
    sign = jnp.where(jnp.arange(HEAD) < HEAD // 2, -1.0, 1.0)
    return cosine_table, sine_table * sign[None, :]


def attend_kernel(
    src,
    normed_source,
    w_query_source,
    w_key_source,
    w_value_source,
    w_out_source,
    q_gain,
    k_gain,
    cosine,
    sine,
    whole,
    queries,
    keys,
    values,
    q_rot,
    k_rot,
    mixed,
    q_inv,
    k_inv,
    log_total,
    attended,
    stats,
    stats_got,
    leaving,
    landed,
    normed,
    w_query,
    w_key,
    w_value,
    w_out,
    fetch_sems,
    swap_sems,
    sent,
    got,
    kept,
):
    sources = (normed_source, w_query_source, w_key_source, w_value_source, w_out_source)
    fetched = fetch(sources, (normed, w_query, w_key, w_value, w_out), fetch_sems)
    place = Place()
    nz = place.z_count
    rows = leaving.shape[0]
    spread = Spread(place, src, whole, sent, got, kept, rows // 4, rows * 3 // 4, 0)
    place.meet()
    over_y = place.device(y=1 - place.y)
    spread.begin()

    lane = lax.broadcasted_iota(jnp.int32, stats.shape, 1)
    stats[...] = jnp.zeros_like(stats)
    chunk = 2 * HEAD

    def project(i, carry):
        here = pl.ds(pl.multiple_of(i * chunk, chunk), chunk)
        for index, (weight, raw) in enumerate(((w_query, queries), (w_key, keys))):
            product = dot_nn(normed[...], weight[:, here])
            raw[:, here] = product
            squares = jnp.sum(product * product, axis=1, keepdims=True)
            stats[...] += jnp.where(lane == index, squares, 0.0)
        values[:, here] = dot_nn(normed[...], w_value[:, here]).astype(jnp.bfloat16)
        return carry

    for copy in fetched[:4]:
        copy.wait()
    lax.fori_loop(0, queries.shape[1] // chunk, project, 0)
    stats_swap = send(stats, stats_got, swap_sems.at[0, 0], swap_sems.at[1, 0], over_y)
    spread.relay(0)
    if nz > 1:
        spread.along_z(1)
        spread.column(1)
    stats_swap.wait()
    for index, inv in enumerate((q_inv, k_inv)):
        total = stats[:, index : index + 1] + stats_got[:, index : index + 1]
        inv[...] = lax.rsqrt(total / D + EPSILON)
    visible = seen_keys()

    def head(h, carry):
        here = pl.ds(pl.multiple_of(h * HEAD, HEAD), HEAD)
        for raw, inv, gain, rotated in ((queries, q_inv, q_gain, q_rot), (keys, k_inv, k_gain, k_rot)):
            normal = raw[:, here] * inv[...] * gain[:, here]
            rotated[:, here] = (normal * cosine[...] + turn(normal) * sine[...]).astype(jnp.bfloat16)
        scores = dot_nt(q_rot[:, here], k_rot[:, here]) * HEAD**-0.5
        scores = jnp.where(visible, scores, -1e30)
        row_max = jnp.max(scores, axis=1, keepdims=True)
        exponent = jnp.exp(scores - row_max)
        row_total = jnp.sum(exponent, axis=1, keepdims=True)
        log_total[h] = row_max + jnp.log(row_total)
        weights = (exponent / row_total).astype(jnp.bfloat16)
        mixed[:, here] = dot_nn(weights, values[:, here]).astype(jnp.bfloat16)
        return carry

    heads = queries.shape[1] // HEAD
    lax.fori_loop(0, heads // 2, head, 0)
    spread.diagonal(0)
    if nz > 2:
        spread.along_z(2)
        spread.column(2)
    lax.fori_loop(heads // 2, heads, head, 0)

    def joined(target, index):
        where = pl.ds(pl.multiple_of(index * rows, rows), rows)

        def columns(b, carry):
            here = pl.ds(pl.multiple_of(b * w_out.shape[2], w_out.shape[2]), w_out.shape[2])
            target[:, here] = dot_nn(mixed[where], w_out[b]).astype(target.dtype)
            return carry

        lax.fori_loop(0, w_out.shape[0], columns, 0)

    fetched[4].wait()
    joined(leaving, 1 - place.y)
    swap = send(leaving, landed, swap_sems.at[0, 1], swap_sems.at[1, 1], over_y)
    if nz > 1:
        spread.relay(1)
    joined(attended, place.y)
    for k in range(1, nz):
        spread.diagonal_along_z(k)
        if k + 2 < nz:
            spread.along_z(k + 2)
            spread.column(k + 2)
        if k + 1 < nz:
            spread.relay(k + 1)
        spread.diagonal(k)
    swap.wait()
    attended[...] += landed[...].astype(jnp.float32)
    spread.keep.wait()
    for k in range(nz):
        spread.sibling_near(k)
        spread.sibling_far(k)
    spread.finish()


def attend(block, normed, weights, gains, tables, collective):
    nz = lax.axis_size("dp") // 4
    rows, width = block.shape
    group, cols = normed.shape[0], weights[0].shape[1]
    half = jax.ShapeDtypeStruct((group, cols), jnp.bfloat16)
    wide = jax.ShapeDtypeStruct((group, cols), jnp.float32)
    thin = jax.ShapeDtypeStruct((group, 1), jnp.float32)
    return pl.pallas_call(
        attend_kernel,
        out_shape=[
            jax.ShapeDtypeStruct((nz, 2, 2, 2, rows, width), block.dtype),
            wide,
            wide,
            half,
            half,
            half,
            half,
            thin,
            thin,
            jax.ShapeDtypeStruct((cols // HEAD, group, 1), jnp.float32),
            jax.ShapeDtypeStruct((rows, width), jnp.float32),
        ],
        in_specs=[ANYWHERE] * 6 + [IN_VMEM] * 4,
        out_specs=[ANYWHERE] + [IN_VMEM] * 10,
        scratch_shapes=[
            pltpu.VMEM((group, LANES), jnp.float32),
            pltpu.VMEM((group, LANES), jnp.float32),
            pltpu.VMEM((rows, width), jnp.bfloat16),
            pltpu.VMEM((rows, width), jnp.bfloat16),
        ]
        + [pltpu.VMEM(array.shape, array.dtype) for array in (normed, *weights)]
        + [
            pltpu.SemaphoreType.DMA((5,)),
            pltpu.SemaphoreType.DMA((2, 2)),
            pltpu.SemaphoreType.DMA((Spread.KINDS, nz)),
            pltpu.SemaphoreType.DMA((Spread.KINDS, nz)),
            pltpu.SemaphoreType.DMA,
        ],
        cost_estimate=LINK_TIME,
        compiler_params=pltpu.CompilerParams(
            collective_id=collective, has_side_effects=True, vmem_limit_bytes=60 << 20
        ),
    )(block, normed, *weights, *gains, *tables)


def busy_y_split(rows):
    return rows // 2, rows // 2, rows // 6


def attend_back_kernel(
    parts,
    own_grad,
    w_out_source,
    queries_source,
    keys_source,
    q_rot_source,
    k_rot_source,
    values_source,
    q_inv,
    k_inv,
    log_total_source,
    q_gain,
    k_gain,
    cosine,
    sine,
    mixture,
    attended_grad,
    q_grad,
    k_grad,
    v_grad,
    gain_grads,
    landed,
    mixed_grad,
    q_scaled,
    k_scaled,
    dots,
    dots_got,
    w_out,
    queries,
    keys,
    q_rot,
    k_rot,
    values,
    log_total,
    fetch_sems,
    swap_sems,
    *scratch,
):
    sources = (
        w_out_source,
        queries_source,
        keys_source,
        q_rot_source,
        k_rot_source,
        values_source,
        log_total_source,
    )
    targets = (w_out, queries, keys, q_rot, k_rot, values, log_total)
    fetched = fetch(sources, targets, fetch_sems)
    place = Place()
    nz = place.z_count
    fold = Fold(place, busy_y_split(own_grad.shape[0]), parts, *scratch)
    place.meet()
    over_y = place.device(y=1 - place.y)
    rows = own_grad.shape[0]
    swap = send(own_grad, landed, swap_sems.at[0, 0], swap_sems.at[1, 0], over_y)
    fold.begin()

    def take(block, index):
        where = pl.ds(pl.multiple_of(index * rows, rows), rows)
        attended_grad[where] = block[...]
        step = w_out.shape[2]

        def columns(b, total):
            here = pl.ds(pl.multiple_of(b * step, step), step)
            return total + dot_nt(block[:, here], w_out[b])

        total = jnp.zeros((rows, mixed_grad.shape[1]), jnp.float32)
        total = lax.fori_loop(0, w_out.shape[0], columns, total)
        mixed_grad[where] = total.astype(jnp.bfloat16)

    fetched[0].wait()
    take(own_grad, place.y)
    for step in fold.opening():
        step()
    swap.wait()
    take(landed, 1 - place.y)
    for copy in fetched[1:]:
        copy.wait()
    visible = seen_keys()
    lane = lax.broadcasted_iota(jnp.int32, dots.shape, 1)
    dots[...] = jnp.zeros_like(dots)

    def head(h, carry):
        here = pl.ds(pl.multiple_of(h * HEAD, HEAD), HEAD)
        upstream = mixed_grad[:, here]
        scores = dot_nt(q_rot[:, here], k_rot[:, here]) * HEAD**-0.5
        probs = jnp.exp(jnp.where(visible, scores, -1e30) - log_total[h])
        prob_grad = dot_nt(upstream, values[:, here])
        row_dot = jnp.sum(prob_grad * probs, axis=1, keepdims=True)
        score_grad = (probs * (prob_grad - row_dot)).astype(jnp.bfloat16)
        v_grad[:, here] = dot_tn(probs.astype(jnp.bfloat16), upstream).astype(jnp.bfloat16)
        for index, (rot_grad, raw, inv, gain, scaled) in enumerate(
            (
                (dot_nn(score_grad, k_rot[:, here]), queries, q_inv, q_gain, q_scaled),
                (dot_tn(score_grad, q_rot[:, here]), keys, k_inv, k_gain, k_scaled),
            )
        ):
            rot_grad = rot_grad * HEAD**-0.5
            norm_grad = rot_grad * cosine[...] - turn(rot_grad) * sine[...]
            with_raw = norm_grad * raw[:, here]
            gain_grads[index : index + 1, here] = jnp.sum(with_raw * inv[...], axis=0, keepdims=True)
            scaled[:, here] = norm_grad * gain[:, here]
            part = jnp.sum(with_raw * gain[:, here], axis=1, keepdims=True)
            dots[...] += jnp.where(lane == index, part, 0.0)
        return carry

    heads = queries.shape[1] // HEAD
    steps = fold.middle()
    for n, step in enumerate(steps):
        step()
        lax.fori_loop(heads * n // len(steps), heads * (n + 1) // len(steps), head, 0)
    dots_swap = send(dots, dots_got, swap_sems.at[0, 1], swap_sems.at[1, 1], over_y)
    for i in range(nz):
        fold.along_z(i)
    mixture[...] = fold.result()
    dots_swap.wait()

    def grads(h, carry):
        here = pl.ds(pl.multiple_of(h * HEAD, HEAD), HEAD)
        for index, (raw, inv, scaled, grad) in enumerate(
            ((queries, q_inv, q_scaled, q_grad), (keys, k_inv, k_scaled, k_grad))
        ):
            mean = (dots[:, index : index + 1] + dots_got[:, index : index + 1]) / D
            scale = inv[...]
            grad[:, here] = (
                scale * scaled[:, here] - raw[:, here] * (scale * scale * scale * mean)
            ).astype(jnp.bfloat16)
        return carry

    lax.fori_loop(0, heads, grads, 0)
    fold.finish()


def attend_back(parts, own_grad, w_out, saved, gains, tables, collective):
    nz, _, _, _, rows, cols = parts.shape
    queries = saved[0]
    group, head_cols = queries.shape
    half = jax.ShapeDtypeStruct((group, head_cols), jnp.bfloat16)
    wide = pltpu.VMEM((group, head_cols), jnp.float32)
    return pl.pallas_call(
        attend_back_kernel,
        out_shape=[
            jax.ShapeDtypeStruct((rows, cols), jnp.bfloat16),
            jax.ShapeDtypeStruct((group, cols), jnp.bfloat16),
            half,
            half,
            half,
            jax.ShapeDtypeStruct((8, head_cols), jnp.float32),
        ],
        in_specs=[ANYWHERE, IN_VMEM] + [ANYWHERE] * 6 + [IN_VMEM] * 2 + [ANYWHERE] + [IN_VMEM] * 4,
        out_specs=[IN_VMEM] * 6,
        scratch_shapes=[
            pltpu.VMEM((rows, cols), jnp.bfloat16),
            pltpu.VMEM((group, head_cols), jnp.bfloat16),
            wide,
            wide,
            pltpu.VMEM((group, LANES), jnp.float32),
            pltpu.VMEM((group, LANES), jnp.float32),
        ]
        + [pltpu.VMEM(array.shape, array.dtype) for array in (w_out, *saved[:5], saved[7])]
        + [pltpu.SemaphoreType.DMA((7,)), pltpu.SemaphoreType.DMA((2, 2))]
        + fold_scratch(nz, rows, cols, busy_y_split(rows), parts.dtype),
        cost_estimate=LINK_TIME,
        compiler_params=pltpu.CompilerParams(
            collective_id=collective, has_side_effects=True, vmem_limit_bytes=62 << 20
        ),
    )(parts, own_grad, w_out, *saved, *gains, *tables)


def plane_gather_kernel(count, *refs):
    srcs, block = refs[:count], refs[count]
    outs, landed = refs[count + 1 : 2 * count + 1], refs[2 * count + 1]
    sent, got, kept, swap_sems = refs[2 * count + 2 :]
    place = Place()
    z, x, c, nz = place.z, place.x, place.c, place.z_count
    ZU, ZD, XF, CO, CX = range(5)
    up, down = place.device(z=z + 1), place.device(z=z - 1)
    over_x, over_c = place.device(x=1 - x), place.device(c=1 - c)
    place.meet()
    every = range(count)
    swap = send(block, landed, swap_sems.at[0], swap_sems.at[1], place.device(y=1 - place.y))

    def push(a, kind, zz, xx, device, own=False):
        ref = outs[a].at[zz, xx, c]
        send(srcs[a] if own else ref, ref, sent.at[kind, a, zz], got.at[kind, a, zz], device)

    def arrival(a, kind, zz, xx, cc):
        ref = outs[a].at[zz, xx, cc]
        pltpu.make_async_copy(ref, ref, got.at[kind, a, zz]).wait()

    def departure(a, kind, zz, xx):
        ref = outs[a].at[zz, xx, c]
        pltpu.make_async_copy(ref, ref, sent.at[kind, a, zz]).wait()

    keeps = []
    for a in every:
        push(a, XF, z, x, over_x, own=True)

        @pl.when(z < nz - 1)
        def _():
            push(a, ZU, z, x, up, own=True)

        @pl.when(z > 0)
        def _():
            push(a, ZD, z, x, down, own=True)

        push(a, CO, z, x, over_c, own=True)
        keep = pltpu.make_async_copy(srcs[a], outs[a].at[z, x, c], kept.at[a])
        keep.start()
        keeps.append(keep)

    def relay(a, zz):
        arrival(a, XF, zz, 1 - x, c)
        push(a, CX, zz, 1 - x, over_c)

    for d in range(nz):
        below, above = z - d - 1, z + d + 1
        for a in every:
            if d < nz - 1:
                @pl.when(below >= 0)
                def _():
                    arrival(a, ZU, below, x, c)

                    @pl.when(z < nz - 1)
                    def _():
                        push(a, ZU, below, x, up)

                    push(a, XF, below, x, over_x)
                    push(a, CO, below, x, over_c)

                @pl.when(above < nz)
                def _():
                    arrival(a, ZD, above, x, c)

                    @pl.when(z > 0)
                    def _():
                        push(a, ZD, above, x, down)

                    push(a, XF, above, x, over_x)
                    push(a, CO, above, x, over_c)

    for d in range(nz):
        for a in every:
            if d == 0:
                relay(a, z)
            else:
                @pl.when(z - d >= 0)
                def _():
                    relay(a, z - d)

                @pl.when(z + d < nz)
                def _():
                    relay(a, z + d)

    for a in every:
        keeps[a].wait()
        for zz in range(nz):
            arrival(a, CO, zz, x, 1 - c)
            arrival(a, CX, zz, 1 - x, 1 - c)
            departure(a, XF, zz, x)
            departure(a, CO, zz, x)
            departure(a, CX, zz, 1 - x)

            @pl.when((zz <= z) & (z < nz - 1))
            def _():
                departure(a, ZU, zz, x)

            @pl.when((zz >= z) & (z > 0))
            def _():
                departure(a, ZD, zz, x)

    swap.wait()


def gather_in_plane(shards, block, collective):
    nz = lax.axis_size("dp") // 4
    count = len(shards)
    return pl.pallas_call(
        functools.partial(plane_gather_kernel, count),
        out_shape=[jax.ShapeDtypeStruct((nz, 2, 2) + s.shape, s.dtype) for s in shards]
        + [jax.ShapeDtypeStruct(block.shape, block.dtype)],
        in_specs=[ANYWHERE] * (count + 1),
        out_specs=[ANYWHERE] * (count + 1),
        scratch_shapes=[
            pltpu.SemaphoreType.DMA((5, count, nz)),
            pltpu.SemaphoreType.DMA((5, count, nz)),
            pltpu.SemaphoreType.DMA((count,)),
            pltpu.SemaphoreType.DMA((2,)),
        ],
        cost_estimate=LINK_TIME,
        compiler_params=pltpu.CompilerParams(collective_id=collective, has_side_effects=True),
    )(*shards, block)


def plane_scatter_kernel(count, *refs):
    lefts, rights = refs[:count], refs[count : 2 * count]
    small, row_part = refs[2 * count : 2 * count + 2]
    refs = refs[2 * count + 2 :]
    outs, small_out, row_landed = refs[:count], refs[count], refs[count + 1]
    total, leaving, from_c, full_x, z_buf, small_sum, small_got = refs[count + 2 : count + 9]
    sent, got, small_sems, row_sems = refs[count + 9 :]
    place = Place()
    z, x, c, nz = place.z, place.x, place.c, place.z_count
    rows = total.shape[3]
    C0, C1, XF, ZU, ZD = range(5)
    over_x, over_c = place.device(x=1 - x), place.device(c=1 - c)
    over_y = place.device(y=1 - place.y)
    place.meet(all_z=True)

    small_sum[0] = small[...]

    def small_start(i):
        return send(
            small_sum.at[i],
            small_got.at[i],
            small_sems.at[0, i],
            small_sems.at[1, i],
            (over_x, over_c, over_y)[i],
        )

    def small_end(i, copy):
        copy.wait()
        small_sum[i + 1] = small_sum[i] + small_got[i]

    def small_z_start():
        return [
            send(
                small_sum.at[3],
                small_got.at[2 + d],
                small_sems.at[0, 2 + d],
                small_sems.at[1, 2 + d],
                place.device(z=(z + d) % nz),
            )
            for d in range(1, nz)
        ]

    def small_z_end(copies):
        for copy in copies:
            copy.wait()
        result = jnp.zeros_like(small_out)
        for zz in range(nz):
            away = (z - zz) % nz
            result = result + jnp.where(away == 0, small_sum[3], small_got[jnp.maximum(2 + away, 3)])
        small_out[...] = result

    def arrival(a, kind, zz, ref):
        pltpu.make_async_copy(ref, ref, got.at[kind, a, zz]).wait()

    small_copy = small_start(0)

    def make(dx, i):
        zz = place.far_first(i)
        xx = 1 - x if dx else x
        for a in range(count):

            def product(cc):
                shard = (zz * 2 + xx) * 2 + cc
                here = pl.ds(pl.multiple_of(shard * rows, rows), rows)
                return dot_tn(lefts[a][:, here], rights[a][...]).astype(total.dtype)

            leaving[dx, zz, a] = product(1 - c)
            send(
                leaving.at[dx, zz, a],
                from_c.at[dx, zz, a],
                sent.at[C1 if dx else C0, a, zz],
                got.at[C1 if dx else C0, a, zz],
                over_c,
            )
            total[dx, zz, a] = product(c)

    def join_cores(a, dx, zz):
        there = from_c.at[dx, zz, a]
        arrival(a, C1 if dx else C0, zz, there)
        add_rows(total.at[dx, zz, a], there, rows)

    def over_the_x(i):
        zz = place.far_first(i)
        for a in range(count):
            join_cores(a, 1, zz)
            send(total.at[1, zz, a], full_x.at[zz, a], sent.at[XF, a, zz], got.at[XF, a, zz], over_x)

    def along_z(i):
        zz = place.far_first(i)
        above = jnp.where(zz == z, nz, zz)
        landing = jnp.where(zz == z - 1, nz, zz)
        for a in range(count):
            mine = total.at[0, zz, a]
            join_cores(a, 0, zz)
            arrival(a, XF, zz, full_x.at[zz, a])
            add_rows(mine, full_x.at[zz, a], rows)

            @pl.when((z > 0) & (zz >= z))
            def _():
                arrival(a, ZU, zz, z_buf.at[zz, a])
                add_rows(mine, z_buf.at[zz, a], rows)

            @pl.when((z < nz - 1) & (zz <= z))
            def _():
                arrival(a, ZD, zz, z_buf.at[above, a])
                add_rows(mine, z_buf.at[above, a], rows)

            @pl.when(zz > z)
            def _():
                send(
                    mine,
                    z_buf.at[zz, a],
                    sent.at[ZU, a, zz],
                    got.at[ZU, a, zz],
                    place.device(z=z + 1),
                )

            @pl.when(zz < z)
            def _():
                send(
                    mine,
                    z_buf.at[landing, a],
                    sent.at[ZD, a, zz],
                    got.at[ZD, a, zz],
                    place.device(z=z - 1),
                )

    make(1, 0)
    row_copy = send(row_part, row_landed, row_sems.at[0], row_sems.at[1], over_y)
    small_end(0, small_copy)
    small_copy = small_start(1)
    for i in range(1, nz):
        make(1, i)
        over_the_x(i - 1)
        if i == 1:
            small_end(1, small_copy)
            small_copy = small_start(2)
    over_the_x(nz - 1)

    def own_chips(i, carry):
        make(0, i)
        return carry

    lax.fori_loop(0, nz, own_chips, 0)
    small_end(2, small_copy)
    small_copies = small_z_start()
    for i in range(nz):
        along_z(i)
        if i == 0:
            small_z_end(small_copies)
    row_copy.wait()

    for a in range(count):

        def widen(i, carry):
            here = pl.ds(pl.multiple_of(i * 16, 16), 16)
            outs[a][here] = total[0, z, a, here].astype(jnp.float32)
            return carry

        lax.fori_loop(0, rows // 16, widen, 0)

    def departure(a, kind, zz):
        ref = total.at[0, 0, a]
        pltpu.make_async_copy(ref, ref, sent.at[kind, a, zz]).wait()

    for a in range(count):
        for zz in range(nz):
            departure(a, C0, zz)
            departure(a, C1, zz)
            departure(a, XF, zz)

            @pl.when(zz > z)
            def _():
                departure(a, ZU, zz)

            @pl.when(zz < z)
            def _():
                departure(a, ZD, zz)


def scatter_in_plane(lefts, rights, small, row_part, collective):
    count = len(lefts)
    nz = lax.axis_size("dp") // 4
    cols, dt = rights[0].shape[1], rights[0].dtype
    rows = lefts[0].shape[1] // (4 * nz)
    blocks = pltpu.VMEM((2, nz, count, rows, cols), dt)
    return pl.pallas_call(
        functools.partial(plane_scatter_kernel, count),
        out_shape=[jax.ShapeDtypeStruct((rows, cols), jnp.float32)] * count
        + [
            jax.ShapeDtypeStruct(small.shape, small.dtype),
            jax.ShapeDtypeStruct(row_part.shape, row_part.dtype),
        ],
        in_specs=[IN_VMEM] * (2 * count + 1) + [ANYWHERE],
        out_specs=[IN_VMEM] * (count + 1) + [ANYWHERE],
        scratch_shapes=[
            blocks,
            blocks,
            blocks,
            pltpu.VMEM((nz, count, rows, cols), dt),
            pltpu.VMEM((nz + 1, count, rows, cols), dt),
            pltpu.VMEM((4,) + small.shape, small.dtype),
            pltpu.VMEM((2 + nz,) + small.shape, small.dtype),
            pltpu.SemaphoreType.DMA((5, count, nz)),
            pltpu.SemaphoreType.DMA((5, count, nz)),
            pltpu.SemaphoreType.DMA((2, 2 + nz)),
            pltpu.SemaphoreType.DMA((2,)),
        ],
        cost_estimate=LINK_TIME,
        compiler_params=pltpu.CompilerParams(
            collective_id=collective, has_side_effects=True, vmem_limit_bytes=62 << 20
        ),
    )(*lefts, *rights, small, row_part)


def dot_nn(a, b):
    return lax.dot_general(a, b, (((1,), (0,)), ((), ())), preferred_element_type=jnp.float32)


def dot_nt(a, b):
    return lax.dot_general(a, b, (((1,), (1,)), ((), ())), preferred_element_type=jnp.float32)


def dot_tn(a, b):
    return lax.dot_general(a, b, (((0,), (0,)), ((), ())), preferred_element_type=jnp.float32)


def pick(table, index):
    return sum(jnp.where(index == i, value, 0) for i, value in enumerate(table))


def expert_kernel(
    z_count,
    src,
    g_all,
    hot_ref,
    router_ref,
    lanes_ref,
    wg_source,
    wu_source,
    wd_source,
    x_all,
    y_all,
    r_all,
    hidden_all,
    gate_pre_grad_all,
    up_grad_all,
    x_tile,
    g_tile,
    y_tile,
    r_tile,
    hidden_tile,
    gate_pre_grad_tile,
    up_grad_tile,
    wg_ref,
    wu_ref,
    wd_ref,
    fetch_sems,
    load_sems,
    store_sems,
    sent,
    got,
    kept,
):
    fetched = fetch((wg_source, wu_source, wd_source), (wg_ref, wu_ref, wd_ref), fetch_sems)
    place = Place()
    place.meet()
    third = src.shape[0] // 3
    spread = Spread(place, src, x_all, sent, got, kept, src.shape[0] // 2, 2 * third, third // 2)
    spread.begin()
    width = src.shape[1]
    tile = x_tile.shape[1]
    pairs = sorted(
        ((k, dx) for k in range(z_count) for dx in (0, 1)),
        key=lambda p: p[0] + (1.3 if p[0] else 0.5) * p[1],
    )
    tiles = 2 * len(pairs)
    near_table, across_table = [p[0] for p in pairs], [p[1] for p in pairs]

    def tile_at(i):
        pair, second = i // 2, i % 2
        zz = place.near_first(pick(near_table, pair))
        xx = jnp.where(pick(across_table, pair) == 1, 1 - place.x, place.x)
        cc = jnp.where(second == 1, 1 - place.c, place.c)
        return zz, xx, cc

    stores = (
        (y_tile, y_all),
        (r_tile, r_all),
        (hidden_tile, hidden_all),
        (gate_pre_grad_tile, gate_pre_grad_all),
        (up_grad_tile, up_grad_all),
    )

    def loads(i, slot):
        zz, xx, cc = tile_at(i)
        copies = []
        for yy in range(2):
            rows = pl.ds(yy * (tile // 2), tile // 2)
            copies.append(
                pltpu.make_async_copy(
                    x_all.at[zz, xx, cc, yy], x_tile.at[slot, rows], load_sems.at[slot, yy]
                )
            )
        copies.append(
            pltpu.make_async_copy(g_all.at[zz, xx, cc], g_tile.at[slot], load_sems.at[slot, 2])
        )
        return copies

    def store(i, slot):
        zz, xx, cc = tile_at(i)
        return [
            pltpu.make_async_copy(here.at[slot], there.at[zz, xx, cc], store_sems.at[slot, n])
            for n, (here, there) in enumerate(stores)
        ]

    steps = {}
    for position, (k, dx) in enumerate(pairs):
        todo = []
        if dx == 0:
            if k == 0:
                todo.append((spread.relay, 0))
            elif k > 1:
                todo.append((spread.diagonal_along_z, k - 1))
            if k + 1 < z_count:
                todo += [(spread.along_z, k + 1), (spread.column, k + 1)]
            if k > 0:
                todo.append((spread.relay, k))
        else:
            if k == z_count - 1 and k > 0:
                todo.append((spread.diagonal_along_z, k))
            todo.append((spread.diagonal, k))
        steps[2 * position] = todo

    def prepare(i):
        for position in range(tiles):
            pair = position // 2
            k, dx = pairs[pair]

            @pl.when(i == position)
            def _():
                if position % 2 == 0:
                    for step, number in steps[position]:
                        step(number)
                    if position == 0:
                        spread.keep.wait()
                elif dx == 0:
                    spread.sibling_near(k)
                else:
                    spread.sibling_far(k)

        for copy in loads(i, i % 2):
            copy.start()

    def compute(i, carry):
        slot = i % 2
        for copy in loads(i, slot):
            copy.wait()

        @pl.when(i >= 2)
        def _():
            for copy in store(i - 2, slot):
                copy.wait()

        @pl.when(i < tiles - 1)
        def _():
            prepare(i + 1)

        zz, xx, cc = tile_at(i)
        rows = x_tile[slot]
        logits = jnp.where(lanes_ref[1:2] > 0.0, dot_nn(rows, router_ref[...]), -1e30)
        weights = jnp.exp(logits - jnp.max(logits, axis=1, keepdims=True))
        own_weight = jnp.sum(weights * lanes_ref[0:1], axis=1, keepdims=True)
        named = jnp.transpose(hot_ref[(zz * 2 + xx) * 2 + cc].astype(jnp.float32))
        hot = jnp.sum(named * lanes_ref[0:1, : named.shape[1]], axis=1, keepdims=True)
        gate = hot * own_weight / jnp.sum(weights, axis=1, keepdims=True)
        gate_pre = dot_nn(rows, wg_ref[...])
        up_pre = dot_nn(rows, wu_ref[...])
        raw_grad = dot_nt(g_tile[slot], wd_ref[...])

        sigmoid = jax.nn.sigmoid(gate_pre)
        silu = gate_pre * sigmoid
        hidden = silu * up_pre
        gate_grad = jnp.sum(hidden * raw_grad, axis=1, keepdims=True)
        coarse = gate_grad.astype(jnp.bfloat16).astype(jnp.float32)
        r_tile[slot, :, width:] = (
            coarse * lanes_ref[2:3] + (gate_grad - coarse) * lanes_ref[3:4]
        ).astype(jnp.bfloat16)
        hidden_gated = (gate * hidden).astype(jnp.bfloat16)
        hidden_tile[slot] = hidden_gated
        hidden_grad = gate * raw_grad
        up_grad = (hidden_grad * silu).astype(jnp.bfloat16)
        up_grad_tile[slot] = up_grad
        gate_pre_grad = (
            hidden_grad * up_pre * sigmoid * (1.0 + gate_pre * (1.0 - sigmoid))
        ).astype(jnp.bfloat16)
        gate_pre_grad_tile[slot] = gate_pre_grad
        y_tile[slot] = dot_nn(hidden_gated, wd_ref[...]).astype(jnp.bfloat16)
        r_tile[slot, :, :width] = (
            dot_nt(gate_pre_grad, wg_ref[...]) + dot_nt(up_grad, wu_ref[...])
        ).astype(jnp.bfloat16)
        for copy in store(i, slot):
            copy.start()
        return carry

    prepare(0)
    for copy in fetched:
        copy.wait()
    lax.fori_loop(0, tiles, compute, 0)
    for i in (tiles - 2, tiles - 1):
        for copy in store(i, i % 2):
            copy.wait()
    spread.finish()


def expert_pass(block, upstream, hot, router, lanes, w_gate, w_up, w_down, collective):
    rows, width = block.shape
    units = w_gate.shape[1]
    nz = lax.axis_size("dp") // 4
    tile = 2 * rows
    out = (nz, 2, 2, tile)
    return pl.pallas_call(
        functools.partial(expert_kernel, nz),
        in_specs=[ANYWHERE] * 2 + [IN_VMEM] * 3 + [ANYWHERE] * 3,
        out_specs=[ANYWHERE] * 6,
        out_shape=[
            jax.ShapeDtypeStruct((nz, 2, 2, 2, rows, width), jnp.bfloat16),
            jax.ShapeDtypeStruct(out + (width,), jnp.bfloat16),
            jax.ShapeDtypeStruct(out + (width + LANES,), jnp.bfloat16),
        ]
        + [jax.ShapeDtypeStruct(out + (units,), jnp.bfloat16)] * 3,
        scratch_shapes=[
            pltpu.VMEM((2, tile, width), jnp.bfloat16),
            pltpu.VMEM((2, tile, width), jnp.bfloat16),
            pltpu.VMEM((2, tile, width), jnp.bfloat16),
            pltpu.VMEM((2, tile, width + LANES), jnp.bfloat16),
            pltpu.VMEM((2, tile, units), jnp.bfloat16),
            pltpu.VMEM((2, tile, units), jnp.bfloat16),
            pltpu.VMEM((2, tile, units), jnp.bfloat16),
            pltpu.VMEM(w_gate.shape, w_gate.dtype),
            pltpu.VMEM(w_up.shape, w_up.dtype),
            pltpu.VMEM(w_down.shape, w_down.dtype),
            pltpu.SemaphoreType.DMA((3,)),
            pltpu.SemaphoreType.DMA((2, 3)),
            pltpu.SemaphoreType.DMA((2, 5)),
            pltpu.SemaphoreType.DMA((Spread.KINDS, nz)),
            pltpu.SemaphoreType.DMA((Spread.KINDS, nz)),
            pltpu.SemaphoreType.DMA,
        ],
        cost_estimate=LINK_TIME,
        compiler_params=pltpu.CompilerParams(
            collective_id=collective, has_side_effects=True, vmem_limit_bytes=60 << 20
        ),
    )(block, upstream.reshape(out + (width,)), hot, router, lanes, w_gate, w_up, w_down)


def dense_body(
    tokens,
    routes,
    cotangent,
    attn_gain,
    q_gain,
    k_gain,
    w_query,
    w_key,
    w_value,
    w_out,
    mlp_gain,
    router,
    w_gate,
    w_up,
    w_down,
):
    rank_index = lax.axis_index("tensor")
    own_rows = tokens.shape[0]
    head_cols = w_query.shape[1]
    col_start = rank_index * head_cols
    row_start = rank_index * own_rows
    experts = router.shape[1]
    q_gain_local = lax.dynamic_slice_in_dim(q_gain, col_start, head_cols)
    k_gain_local = lax.dynamic_slice_in_dim(k_gain, col_start, head_cols)
    expert_ids = jnp.arange(experts, dtype=jnp.int32)
    named = jnp.any(routes[None] == expert_ids[:, None, None], axis=2).astype(jnp.bfloat16)
    q_all, k_all, v_all, o_all, hot, other_tokens = gather_in_plane(
        (w_query, w_key, w_value, w_out, named), tokens, 1
    )
    hot = hot.reshape(-1, *named.shape)
    q_all, k_all, v_all = (w.reshape(D, head_cols) for w in (q_all, k_all, v_all))
    o_all = o_all.reshape(-1, *w_out.shape)
    first = rank_index == 0
    inputs_both = jnp.concatenate(
        [jnp.where(first, tokens, other_tokens), jnp.where(first, other_tokens, tokens)], axis=0
    ).astype(jnp.float32)
    unit_both = inputs_both * lax.rsqrt(
        jnp.mean(inputs_both * inputs_both, axis=1, keepdims=True) + EPSILON
    )
    normed = (unit_both * attn_gain).astype(jnp.bfloat16)
    inputs = tokens.astype(jnp.float32)
    attn_inv = lax.rsqrt(jnp.mean(inputs * inputs, axis=1, keepdims=True) + EPSILON)
    own_expert = lax.axis_index("dp")
    lane = jnp.arange(LANES)
    marked = own_expert + experts * rank_index
    lanes = jnp.stack(
        [lane == own_expert, lane < experts, lane == marked, lane == marked + 2 * experts]
        + [lane < 0] * 4
    ).astype(jnp.float32)
    router_wide = jnp.pad(router, ((0, 0), (0, LANES - experts)))
    tables = signed_rope_tables()
    gains = (q_gain_local[None], k_gain_local[None])
    (
        upstream_all,
        queries,
        keys_raw,
        values,
        query_rot,
        key_rot,
        mixed_heads,
        query_inv,
        key_inv,
        log_total,
        attended,
    ) = attend(cotangent, normed, (q_all, k_all, v_all, o_all), gains, tables, 6)
    upstream_all = upstream_all.reshape(-1, D)
    hidden_one = inputs + attended
    mlp_inv = lax.rsqrt(jnp.mean(hidden_one * hidden_one, axis=1, keepdims=True) + EPSILON)
    normed_two = (hidden_one * mlp_inv * mlp_gain).astype(jnp.bfloat16)
    own_routes = lax.dynamic_slice_in_dim(routes, row_start, own_rows, 0)
    own_hot = jnp.any(own_routes[:, :, None] == expert_ids[None, None, :], axis=1)
    own_probs = jax.nn.softmax(matmul(normed_two, router), axis=1)
    rows_all, y_part, r_part, *for_weights = expert_pass(
        normed_two, upstream_all, hot, router_wide, lanes, w_gate[0], w_up[0], w_down[0], 2
    )
    rows_all, y_part = rows_all.reshape(-1, D), y_part.reshape(-1, D)
    for_weights = [array.reshape(rows_all.shape[0], -1) for array in for_weights]
    blocks = (lax.axis_size("dp") // 4, 2, 2, 2, own_rows)
    returned, gate_weight_grad, up_weight_grad, down_weight_grad = scatter_sum(
        r_part.reshape(*blocks, D + LANES), [rows_all, upstream_all, *for_weights], 3
    )
    expert_grad = jnp.sum(
        returned[:, D : D + 4 * experts].astype(jnp.float32).reshape(own_rows, 4, experts), axis=1
    )
    expert_grad = jnp.where(own_hot, expert_grad, 0.0)
    returned = returned[:, :D]
    upstream = cotangent.astype(jnp.float32)
    logit_grad = own_probs * (expert_grad - jnp.sum(expert_grad * own_probs, axis=1, keepdims=True))
    router_grad = jnp.dot(normed_two.astype(jnp.float32).T, logit_grad, precision=HIGHEST)
    normed_two_grad = returned.astype(jnp.float32) + jnp.dot(
        logit_grad, router.astype(jnp.float32).T, precision=HIGHEST
    )
    scaled_grad = normed_two_grad * mlp_gain
    hidden_one_grad = (
        upstream
        + mlp_inv * scaled_grad
        - hidden_one * mlp_inv**3 * jnp.mean(hidden_one * scaled_grad, axis=1, keepdims=True)
    )
    mlp_gain_grad = jnp.sum(normed_two_grad * hidden_one * mlp_inv, axis=0)
    saved = (queries, keys_raw, query_rot, key_rot, values, query_inv, key_inv, log_total)
    mixture, attended_grad, query_grad, key_grad, value_grad, gain_grads = attend_back(
        y_part.reshape(*blocks, D), hidden_one_grad.astype(jnp.bfloat16), o_all, saved, gains, tables, 7
    )
    layer_out = (hidden_one + mixture.astype(jnp.float32)).astype(jnp.bfloat16)
    q_gain_part, k_gain_part = gain_grads[0], gain_grads[1]
    normed_part = (
        jnp.einsum("gc,rc->gr", query_grad, q_all, preferred_element_type=jnp.float32)
        + jnp.einsum("gc,rc->gr", key_grad, k_all, preferred_element_type=jnp.float32)
        + jnp.einsum("gc,rc->gr", value_grad, v_all, preferred_element_type=jnp.float32)
    )
    attn_gain_grad = jnp.sum(normed_part * unit_both, axis=0)
    zero_width = jnp.zeros((D,), jnp.float32)
    q_gain_full = lax.dynamic_update_slice_in_dim(zero_width, q_gain_part, col_start, 0)
    k_gain_full = lax.dynamic_update_slice_in_dim(zero_width, k_gain_part, col_start, 0)
    small_grads = jnp.concatenate(
        [
            jnp.stack([attn_gain_grad, q_gain_full, k_gain_full, mlp_gain_grad]),
            jnp.zeros((4, D), jnp.float32),
            jnp.transpose(router_grad),
        ],
        axis=0,
    )
    row_part = lax.dynamic_slice_in_dim(
        normed_part, (1 - rank_index) * own_rows, own_rows, 0
    ).astype(jnp.bfloat16)
    own_part = lax.dynamic_slice_in_dim(normed_part, row_start, own_rows, 0)
    *weight_sums, small_sums, other_part = scatter_in_plane(
        (normed, normed, normed, attended_grad),
        (query_grad, key_grad, value_grad, mixed_heads),
        small_grads,
        row_part,
        4,
    )
    normed_grad = own_part + other_part.astype(jnp.float32)
    scaled_input = normed_grad * attn_gain
    tokens_grad = (
        hidden_one_grad
        + attn_inv * scaled_input
        - inputs * attn_inv**3 * jnp.mean(inputs * scaled_input, axis=1, keepdims=True)
    )
    attn_gain_grad, q_gain_grad, k_gain_grad, mlp_gain_grad = (small_sums[i] for i in range(4))
    router_grad = jnp.transpose(small_sums[8:])
    return (
        layer_out,
        tokens_grad,
        attn_gain_grad,
        q_gain_grad,
        k_gain_grad,
        weight_sums[0],
        weight_sums[1],
        weight_sums[2],
        jnp.transpose(weight_sums[3]),
        mlp_gain_grad,
        router_grad,
        gate_weight_grad[None],
        up_weight_grad[None],
        down_weight_grad[None],
    )


def solution(mesh):
    in_specs = (
        P(("dp", "tensor"), None),
        P("dp", None),
        P(("dp", "tensor"), None),
        P(),
        P(),
        P(),
        P("dp", "tensor"),
        P("dp", "tensor"),
        P("dp", "tensor"),
        P("tensor", "dp"),
        P(),
        P(),
        P("dp", None, "tensor"),
        P("dp", None, "tensor"),
        P("dp", "tensor", None),
    )
    out_specs = (
        P(("dp", "tensor"), None),
        P(("dp", "tensor"), None),
        P(),
        P(),
        P(),
        P("dp", "tensor"),
        P("dp", "tensor"),
        P("dp", "tensor"),
        P("tensor", "dp"),
        P(),
        P(),
        P("dp", None, "tensor"),
        P("dp", None, "tensor"),
        P("dp", "tensor", None),
    )
    experts = mesh.shape["dp"]
    body = dense_body if experts <= 2 * TOPK else routed_body
    return jax.shard_map(body, mesh=mesh, in_specs=in_specs, out_specs=out_specs, check_vma=False)
```

```python
import functools

import jax
import jax.numpy as jnp
from jax import lax
from jax.experimental import pallas as pl
from jax.experimental.pallas import tpu as pltpu
from jax.sharding import PartitionSpec as P

D = 2048
HEAD = 128
TOPK = 8
PROMPT = 256
CONT = 64
GROUP = 384


EPSILON = 1e-05
ROPE_BASE = 10000.0
HIGHEST = lax.Precision.HIGHEST


def matmul(first_op, second_op):
    return jnp.dot(first_op, second_op, preferred_element_type=jnp.float32)


def gather_rows(values):
    return lax.all_gather(values, "tensor", axis=0, tiled=True)


def sum_rows(values):
    return lax.psum_scatter(values, "tensor", scatter_dimension=0, tiled=True)


def tensor_total(values):
    return lax.psum((values[0], values[1]), "tensor")


def expert_swap(values):
    return lax.all_to_all(values, "dp", split_axis=0, concat_axis=0, tiled=True)


def sum_slots(values):
    return lax.psum_scatter(values, "tensor", scatter_dimension=1, tiled=True)


def group_positions():
    position = jnp.arange(GROUP, dtype=jnp.int32)
    return jnp.where(position < PROMPT, position, PROMPT + (position - PROMPT) % CONT)


def visible_keys():
    position = jnp.arange(GROUP, dtype=jnp.int32)
    member = jnp.where(position < PROMPT, -1, (position - PROMPT) // CONT)
    causal = position[None, :] <= position[:, None]
    return causal & ((member[None, :] == -1) | (member[None, :] == member[:, None]))


def rope_tables():
    half_head = HEAD // 2
    frequency = ROPE_BASE ** (-2.0 * jnp.arange(half_head, dtype=jnp.float32) / HEAD)
    angles = group_positions().astype(jnp.float32)[:, None] * frequency[None, :]
    angles = jnp.concatenate([angles, angles], axis=1)
    return (jnp.cos(angles), jnp.sin(angles))


def rotate(values, cosine_table, sine_table):
    half_head = HEAD // 2
    turned = jnp.concatenate([-values[..., half_head:], values[..., :half_head]], axis=-1)
    return values * cosine_table[:, None, :] + turned * sine_table[:, None, :]


def unrotate(values, cosine_table, sine_table):
    half_head = HEAD // 2
    scaled = values * sine_table[:, None, :]
    turned = jnp.concatenate([scaled[..., half_head:], -scaled[..., :half_head]], axis=-1)
    return values * cosine_table[:, None, :] + turned


def gate_split(rows_in, hot_table, router):
    gates = jax.nn.softmax(matmul(rows_in, router), axis=1)
    weights = jnp.sum(jnp.where(hot_table, gates[:, None, :], 0.0), axis=2)
    return (gates, weights)


def routed_body(
    tokens,
    routes,
    cotangent,
    attn_gain,
    q_gain,
    k_gain,
    w_query,
    w_key,
    w_value,
    w_out,
    mlp_gain,
    router,
    w_gate,
    w_up,
    w_down,
):
    rank_index = lax.axis_index("tensor")
    tensor_count = lax.axis_size("tensor")
    own_rows = tokens.shape[0]
    head_cols = w_query.shape[1]
    local_heads = head_cols // HEAD
    col_start = rank_index * head_cols
    row_start = rank_index * own_rows
    experts = router.shape[1]
    half_cap = (own_rows * TOPK * 4 + 3 * experts - 1) // (3 * experts)
    capacity = tensor_count * half_cap
    attn_scale = HEAD ** (-0.5)
    head_shape = (GROUP, local_heads, HEAD)
    q_gain_local = lax.dynamic_slice_in_dim(q_gain, col_start, head_cols)
    k_gain_local = lax.dynamic_slice_in_dim(k_gain, col_start, head_cols)
    inputs = tokens.astype(jnp.float32)
    attn_inv = lax.rsqrt(jnp.mean(inputs * inputs, axis=1, keepdims=True) + EPSILON)
    normed = gather_rows((inputs * attn_inv * attn_gain).astype(jnp.bfloat16))
    pieces = (
        lax.all_gather(w_query, "dp", axis=0, tiled=True),
        lax.all_gather(w_key, "dp", axis=0, tiled=True),
        lax.all_gather(w_value, "dp", axis=0, tiled=True),
    )
    normed_part = normed
    queries = matmul(normed_part, pieces[0])
    keys_raw = matmul(normed_part, pieces[1])
    values_raw = matmul(normed_part, pieces[2])
    query_sq, key_sq = tensor_total(
        (jnp.sum(queries * queries, axis=1), jnp.sum(keys_raw * keys_raw, axis=1))
    )
    query_inv = lax.rsqrt(query_sq / D + EPSILON)[:, None]
    key_inv = lax.rsqrt(key_sq / D + EPSILON)[:, None]
    cosine_table, sine_table = rope_tables()
    query_rot = rotate(
        (queries * query_inv * q_gain_local).reshape(head_shape), cosine_table, sine_table
    ).astype(jnp.bfloat16)
    key_rot = rotate(
        (keys_raw * key_inv * k_gain_local).reshape(head_shape), cosine_table, sine_table
    ).astype(jnp.bfloat16)
    value_heads = values_raw.astype(jnp.bfloat16).reshape(head_shape)
    visible = visible_keys()[None]

    def masked_scores():
        raw_scores = (
            jnp.einsum("qhd,khd->hqk", query_rot, key_rot, preferred_element_type=jnp.float32)
            * attn_scale
        )
        return jnp.where(visible, raw_scores, -1e30)

    scores = masked_scores()
    row_max = jnp.max(scores, axis=2, keepdims=True)
    exponent = jnp.exp(scores - row_max)
    row_total = jnp.sum(exponent, axis=2, keepdims=True)
    log_total = row_max + jnp.log(row_total)
    mixed_heads = jnp.einsum(
        "hqk,khd->qhd",
        (exponent / row_total).astype(jnp.bfloat16),
        value_heads,
        preferred_element_type=jnp.float32,
    )
    mixed_heads = mixed_heads.reshape(GROUP, head_cols).astype(jnp.bfloat16)
    attn_part = matmul(mixed_heads, lax.all_gather(w_out, "dp", axis=1, tiled=True))
    attended = sum_rows(attn_part)
    hidden_one = inputs + attended
    mlp_inv = lax.rsqrt(jnp.mean(hidden_one * hidden_one, axis=1, keepdims=True) + EPSILON)
    normed_two = (hidden_one * mlp_inv * mlp_gain).astype(jnp.bfloat16)
    expert_ids = jnp.arange(experts, dtype=jnp.int32)
    route_hot = routes[:, :, None] == expert_ids[None, None, :]
    flat_hot = route_hot.astype(jnp.int32).reshape(tensor_count, own_rows * TOPK, experts)
    within = jnp.sum((jnp.cumsum(flat_hot, axis=1) - flat_hot) * flat_hot, axis=2).reshape(
        GROUP, TOPK
    )
    owner_of = (jnp.arange(GROUP, dtype=jnp.int32) // own_rows)[:, None]
    own_routes = lax.dynamic_slice_in_dim(routes, row_start, own_rows, 0)
    own_within = lax.dynamic_slice_in_dim(within, row_start, own_rows, 0)
    own_hot = lax.dynamic_slice_in_dim(route_hot, row_start, own_rows, 0)
    own_dest = own_routes * half_cap + own_within
    gate_weight = w_gate[0]
    up_weight = w_up[0]
    down_weight = w_down[0]
    normed_two_all = gather_rows(normed_two)
    gates_every, gate_every = gate_split(normed_two_all, route_hot, router)
    own_probs = lax.dynamic_slice_in_dim(gates_every, row_start, own_rows, 0)
    gate_weights = lax.dynamic_slice_in_dim(gate_every, row_start, own_rows, 0)
    destination = routes * capacity + owner_of * half_cap + within
    send_rows = (
        jnp.zeros((experts * capacity, D), jnp.bfloat16)
        .at[destination]
        .set(jnp.broadcast_to(normed_two_all[:, None, :], (GROUP, TOPK, D)))
        .reshape(experts, capacity, D)
    )
    received = lax.all_to_all(send_rows, "dp", split_axis=0, concat_axis=0, tiled=True)
    gate_pre = jnp.einsum("scd,df->scf", received, gate_weight, preferred_element_type=jnp.float32)
    up_pre = jnp.einsum("scd,df->scf", received, up_weight, preferred_element_type=jnp.float32)
    hidden = (jax.nn.silu(gate_pre) * up_pre).astype(jnp.bfloat16)
    expert_part = jnp.einsum("scf,fd->scd", hidden, down_weight, preferred_element_type=jnp.float32)
    expert_part, gate_pre, up_pre, hidden, received = (
        expert_part,
        gate_pre,
        up_pre,
        hidden,
        received,
    )
    back_rows = expert_swap(sum_slots(expert_part).astype(jnp.bfloat16)).reshape(
        experts * half_cap, D
    )
    picked = back_rows[own_dest].astype(jnp.float32)
    mixture = jnp.sum(gate_weights[:, :, None] * picked, axis=1)
    layer_out = (hidden_one + mixture).astype(jnp.bfloat16)
    upstream = cotangent.astype(jnp.float32)
    gate_grad = jnp.sum(upstream[:, None, :] * picked, axis=2)
    upstream_all = gather_rows(cotangent).astype(jnp.float32)
    send_grads = (
        jnp.zeros((experts * capacity, D), jnp.bfloat16)
        .at[destination]
        .set((gate_every[:, :, None] * upstream_all[:, None, :]).astype(jnp.bfloat16))
        .reshape(experts, capacity, D)
    )
    out_grads = expert_swap(send_grads)
    hidden_grad = jnp.einsum(
        "scd,fd->scf", out_grads, down_weight, preferred_element_type=jnp.float32
    )
    sigmoid = jax.nn.sigmoid(gate_pre)
    up_grad = (hidden_grad * gate_pre * sigmoid).astype(jnp.bfloat16)
    gate_pre_grad = (hidden_grad * up_pre * sigmoid * (1.0 + gate_pre * (1.0 - sigmoid))).astype(
        jnp.bfloat16
    )
    row_part = jnp.einsum(
        "scf,df->scd", gate_pre_grad, gate_weight, preferred_element_type=jnp.float32
    ) + jnp.einsum("scf,df->scd", up_grad, up_weight, preferred_element_type=jnp.float32)
    down_weight_grad = jnp.einsum(
        "scf,scd->fd", hidden, out_grads, preferred_element_type=jnp.float32
    )
    gate_weight_grad = jnp.einsum(
        "scd,scf->df", received, gate_pre_grad, preferred_element_type=jnp.float32
    )
    up_weight_grad = jnp.einsum(
        "scd,scf->df", received, up_grad, preferred_element_type=jnp.float32
    )
    returned_grads = expert_swap(sum_slots(row_part).astype(jnp.bfloat16)).reshape(
        experts * half_cap, D
    )
    normed_two_part = jnp.sum(returned_grads[own_dest].astype(jnp.float32), axis=1)
    expert_grad = jnp.sum(jnp.where(own_hot, gate_grad[:, :, None], 0.0), axis=1)
    logit_grad = own_probs * (expert_grad - jnp.sum(expert_grad * own_probs, axis=1, keepdims=True))
    router_grad = jnp.dot(normed_two.astype(jnp.float32).T, logit_grad, precision=HIGHEST)
    normed_two_grad = normed_two_part + jnp.dot(
        logit_grad, router.astype(jnp.float32).T, precision=HIGHEST
    )
    scaled_grad = normed_two_grad * mlp_gain
    hidden_one_grad = (
        upstream
        + mlp_inv * scaled_grad
        - hidden_one * mlp_inv**3 * jnp.mean(hidden_one * scaled_grad, axis=1, keepdims=True)
    )
    mlp_gain_grad = jnp.sum(normed_two_grad * hidden_one * mlp_inv, axis=0)
    attended_grad = gather_rows(hidden_one_grad.astype(jnp.bfloat16))
    mixed_grad = jnp.einsum(
        "gd,cd->gc",
        attended_grad,
        lax.all_gather(w_out, "dp", axis=1, tiled=True),
        preferred_element_type=jnp.float32,
    )
    mixed_grad = mixed_grad.astype(jnp.bfloat16).reshape(head_shape)
    attn_probs = jnp.exp(masked_scores() - log_total)
    prob_grad = jnp.einsum(
        "qhd,khd->hqk", mixed_grad, value_heads, preferred_element_type=jnp.float32
    )
    row_dot = jnp.sum(prob_grad * attn_probs, axis=2, keepdims=True)
    score_grad = (attn_probs * (prob_grad - row_dot)).astype(jnp.bfloat16)
    query_rot_grad = (
        jnp.einsum("hqk,khd->qhd", score_grad, key_rot, preferred_element_type=jnp.float32)
        * attn_scale
    )
    key_rot_grad = (
        jnp.einsum("hqk,qhd->khd", score_grad, query_rot, preferred_element_type=jnp.float32)
        * attn_scale
    )
    value_grad = (
        jnp.einsum(
            "hqk,qhd->khd",
            attn_probs.astype(jnp.bfloat16),
            mixed_grad,
            preferred_element_type=jnp.float32,
        )
        .reshape(GROUP, head_cols)
        .astype(jnp.bfloat16)
    )
    query_norm_grad = unrotate(query_rot_grad, cosine_table, sine_table).reshape(GROUP, head_cols)
    key_norm_grad = unrotate(key_rot_grad, cosine_table, sine_table).reshape(GROUP, head_cols)
    query_scaled = query_norm_grad * q_gain_local
    key_scaled = key_norm_grad * k_gain_local
    query_dot, key_dot = tensor_total(
        (jnp.sum(queries * query_scaled, axis=1), jnp.sum(keys_raw * key_scaled, axis=1))
    )
    query_grad = (
        query_inv * query_scaled - queries * query_inv**3 * (query_dot / D)[:, None]
    ).astype(jnp.bfloat16)
    key_grad = (key_inv * key_scaled - keys_raw * key_inv**3 * (key_dot / D)[:, None]).astype(
        jnp.bfloat16
    )
    q_gain_part = jnp.sum(query_norm_grad * queries * query_inv, axis=0)
    k_gain_part = jnp.sum(key_norm_grad * keys_raw * key_inv, axis=0)
    pieces = lax.all_gather((w_query, w_key, w_value), "dp", axis=0, tiled=True)
    normed_part = (
        jnp.einsum("gc,rc->gr", query_grad, pieces[0], preferred_element_type=jnp.float32)
        + jnp.einsum("gc,rc->gr", key_grad, pieces[1], preferred_element_type=jnp.float32)
        + jnp.einsum("gc,rc->gr", value_grad, pieces[2], preferred_element_type=jnp.float32)
    )
    weight_sums = lax.psum_scatter(
        jnp.concatenate(
            [
                jnp.einsum("gr,gc->rc", normed, query_grad, preferred_element_type=jnp.float32),
                jnp.einsum("gr,gc->rc", normed, key_grad, preferred_element_type=jnp.float32),
                jnp.einsum("gr,gc->rc", normed, value_grad, preferred_element_type=jnp.float32),
                jnp.einsum(
                    "gr,gc->rc", attended_grad, mixed_heads, preferred_element_type=jnp.float32
                ),
            ],
            axis=1,
        ),
        "dp",
        scatter_dimension=0,
        tiled=True,
    )
    normed_grad = sum_rows(normed_part)
    scaled_input = normed_grad * attn_gain
    tokens_grad = (
        hidden_one_grad
        + attn_inv * scaled_input
        - inputs * attn_inv**3 * jnp.mean(inputs * scaled_input, axis=1, keepdims=True)
    )
    attn_gain_grad = jnp.sum(normed_grad * inputs * attn_inv, axis=0)
    zero_width = jnp.zeros((D,), jnp.float32)
    q_gain_full = lax.dynamic_update_slice_in_dim(zero_width, q_gain_part, col_start, 0)
    k_gain_full = lax.dynamic_update_slice_in_dim(zero_width, k_gain_part, col_start, 0)
    attn_gain_grad, q_gain_grad, k_gain_grad, mlp_gain_grad, router_grad = lax.psum(
        (attn_gain_grad, q_gain_full, k_gain_full, mlp_gain_grad, router_grad), ("dp", "tensor")
    )
    return (
        layer_out,
        tokens_grad,
        attn_gain_grad,
        q_gain_grad,
        k_gain_grad,
        weight_sums[:, :head_cols],
        weight_sums[:, head_cols : 2 * head_cols],
        weight_sums[:, 2 * head_cols : 3 * head_cols],
        jnp.transpose(weight_sums[:, 3 * head_cols :]),
        mlp_gain_grad,
        router_grad,
        gate_weight_grad[None],
        up_weight_grad[None],
        down_weight_grad[None],
    )


MESH_ID = pl.DeviceIdType.MESH
LINK_TIME = pl.CostEstimate(flops=10**11, bytes_accessed=10**8, transcendentals=0)
EVERY = ("dp", "tensor")
LANES = 128
ANYWHERE = pl.BlockSpec(memory_space=pl.ANY)
IN_VMEM = pl.BlockSpec(memory_space=pltpu.VMEM)


class Place:
    def __init__(self):
        dp = lax.axis_index("dp")
        self.y = lax.axis_index("tensor")
        self.z, self.x, self.c = dp // 4, (dp // 2) % 2, dp % 2
        self.z_count = lax.axis_size("dp") // 4

    def device(self, z=None, x=None, c=None, y=None):
        z = self.z if z is None else z
        x = self.x if x is None else x
        c = self.c if c is None else c
        y = self.y if y is None else y
        return (z * 4 + x * 2 + c, y)

    def meet(self, use_y=True, all_z=False):
        barrier = pltpu.get_barrier_semaphore()
        partners = [self.device(x=1 - self.x), self.device(c=1 - self.c)]
        if use_y:
            partners.append(self.device(y=1 - self.y))
        if all_z:
            partners += [self.device(z=(self.z + d) % self.z_count) for d in range(1, self.z_count)]
        for partner in partners:
            pl.semaphore_signal(barrier, inc=1, device_id=partner, device_id_type=MESH_ID)
        if all_z:
            pl.semaphore_wait(barrier, len(partners))
            return

        @pl.when(self.z > 0)
        def _():
            pl.semaphore_signal(
                barrier, inc=1, device_id=self.device(z=self.z - 1), device_id_type=MESH_ID
            )

        @pl.when(self.z < self.z_count - 1)
        def _():
            pl.semaphore_signal(
                barrier, inc=1, device_id=self.device(z=self.z + 1), device_id_type=MESH_ID
            )

        ends = jnp.where(self.z > 0, 1, 0) + jnp.where(self.z < self.z_count - 1, 1, 0)
        pl.semaphore_wait(barrier, len(partners) + ends)

    def far_first(self, step):
        last = self.z_count - 1
        low = jnp.where(step < last - self.z, last - step, step - (last - self.z))
        high = jnp.where(step < self.z, step, last - (step - self.z))
        return jnp.where(self.z * 2 < self.z_count, low, high)


    def near_first(self, step):
        return self.far_first(self.z_count - 1 - step)


def send(src, dst, send_sem, recv_sem, device):
    copy = pltpu.make_async_remote_copy(
        src_ref=src, dst_ref=dst, send_sem=send_sem, recv_sem=recv_sem, device_id=device, device_id_type=MESH_ID
    )
    copy.start()
    return copy


def fetch(sources, targets, sems):
    copies = [
        pltpu.make_async_copy(source, target, sems.at[n])
        for n, (source, target) in enumerate(zip(sources, targets))
    ]
    for copy in copies:
        copy.start()
    return copies


def add_rows(total, part, rows, step=16):
    def chunk(i, carry):
        here = pl.ds(pl.multiple_of(i * step, step), step)
        total[here] = total[here] + part[here]
        return carry

    lax.fori_loop(0, rows // step, chunk, 0)


class Spread:
    KINDS = 14
    ZU, ZD, XF, YF, XH, YH, CO, CX, CY, CA, CB, CC, DU, DD = range(KINDS)

    def __init__(self, place, src, whole, sent, got, kept, own_split, through_z, other_split):
        self.place, self.src, self.whole, self.sent, self.got = place, src, whole, sent, got
        rows = src.shape[0]
        self.parts = {
            True: (pl.ds(0, own_split), pl.ds(own_split, rows - own_split)),
            False: (pl.ds(through_z, other_split), pl.ds(through_z + other_split, rows - through_z - other_split)),
        }
        self.deep = pl.ds(0, through_z)
        z, x, c, y = place.z, place.x, place.c, place.y
        self.up, self.down = place.device(z=z + 1), place.device(z=z - 1)
        self.over_x, self.over_y = place.device(x=1 - x), place.device(y=1 - y)
        self.over_c = place.device(c=1 - c)
        self.keep = pltpu.make_async_copy(src, whole.at[z, x, c, y], kept)

    def push(self, kind, zz, xx, yy, rows, device, origin=None):
        ref = self.whole.at[zz, xx, self.place.c, yy, rows]
        send(
            ref if origin is None else origin,
            ref,
            self.sent.at[kind, zz],
            self.got.at[kind, zz],
            device,
        )

    def arrival(self, kind, zz, xx, yy, rows=slice(None), sibling=False):
        cc = 1 - self.place.c if sibling else self.place.c
        ref = self.whole.at[zz, xx, cc, yy, rows]
        pltpu.make_async_copy(ref, ref, self.got.at[kind, zz]).wait()

    def departure(self, kind, zz, xx, yy, rows=slice(None)):
        ref = self.whole.at[zz, xx, self.place.c, yy, rows]
        pltpu.make_async_copy(ref, ref, self.sent.at[kind, zz]).wait()

    def column(self, k, origin=None):
        x, y, every = self.place.x, self.place.y, slice(None)
        zz = self.place.near_first(k)
        self.push(self.XF, zz, x, y, every, self.over_x, origin)
        self.push(self.YF, zz, x, y, every, self.over_y, origin)
        self.push(self.CO, zz, x, y, every, self.over_c, origin)

    def begin(self):
        z, x, y, nz = self.place.z, self.place.x, self.place.y, self.place.z_count

        @pl.when(z < nz - 1)
        def _():
            self.push(self.ZU, z, x, y, slice(None), self.up, self.src)

        @pl.when(z > 0)
        def _():
            self.push(self.ZD, z, x, y, slice(None), self.down, self.src)

        self.column(0, self.src)
        self.keep.start()

    def move_z(self, d, up_kind, down_kind, xx, yy, rows, hand_over):
        z, nz = self.place.z, self.place.z_count
        below, above = z - d, z + d

        @pl.when(below >= 0)
        def _():
            self.arrival(up_kind, below, xx, yy, rows)

            @pl.when(z < nz - 1)
            def _():
                self.push(up_kind, below, xx, yy, rows, self.up)

            if hand_over:
                self.push(self.CC, below, xx, yy, rows, self.over_c)

        @pl.when(above < nz)
        def _():
            self.arrival(down_kind, above, xx, yy, rows)

            @pl.when(z > 0)
            def _():
                self.push(down_kind, above, xx, yy, rows, self.down)

            if hand_over:
                self.push(self.CC, above, xx, yy, rows, self.over_c)

    def along_z(self, d):
        self.move_z(d, self.ZU, self.ZD, self.place.x, self.place.y, slice(None), False)

    def diagonal_along_z(self, d):
        self.move_z(d, self.DU, self.DD, 1 - self.place.x, 1 - self.place.y, self.deep, True)

    def relay(self, k):
        x, y, every = self.place.x, self.place.y, slice(None)
        zz = self.place.near_first(k)
        low, high = self.parts[k == 0]
        self.arrival(self.XF, zz, 1 - x, y)
        if low.size:
            self.push(self.YH, zz, 1 - x, y, low, self.over_y)
        self.push(self.CX, zz, 1 - x, y, every, self.over_c)
        self.arrival(self.YF, zz, x, 1 - y)
        self.push(self.XH, zz, x, 1 - y, high, self.over_x)
        self.push(self.CY, zz, x, 1 - y, every, self.over_c)

    def diagonal(self, k):
        z, nz = self.place.z, self.place.z_count
        xx, yy = 1 - self.place.x, 1 - self.place.y
        zz = self.place.near_first(k)
        low, high = self.parts[k == 0]
        self.arrival(self.XH, zz, xx, yy, high)
        if low.size:
            self.arrival(self.YH, zz, xx, yy, low)
        if k == 0:

            @pl.when(z < nz - 1)
            def _():
                self.push(self.DU, z, xx, yy, self.deep, self.up)

            @pl.when(z > 0)
            def _():
                self.push(self.DD, z, xx, yy, self.deep, self.down)

        self.push(self.CB, zz, xx, yy, high, self.over_c)
        if low.size:
            self.push(self.CA, zz, xx, yy, low, self.over_c)

    def sibling_near(self, k):
        x, y = self.place.x, self.place.y
        zz = self.place.near_first(k)
        self.arrival(self.CO, zz, x, y, sibling=True)
        self.arrival(self.CY, zz, x, 1 - y, sibling=True)

    def sibling_far(self, k):
        x, y = self.place.x, self.place.y
        zz = self.place.near_first(k)
        low, high = self.parts[k == 0]
        self.arrival(self.CX, zz, 1 - x, y, sibling=True)
        self.arrival(self.CB, zz, 1 - x, 1 - y, high, sibling=True)
        if low.size:
            self.arrival(self.CA, zz, 1 - x, 1 - y, low, sibling=True)
        if k > 0:
            self.arrival(self.CC, zz, 1 - x, 1 - y, self.deep, sibling=True)

    def finish(self):
        z, x, y, nz = self.place.z, self.place.x, self.place.y, self.place.z_count
        for k in range(nz):
            zz = self.place.near_first(k)
            low, high = self.parts[k == 0]
            self.departure(self.XF, zz, x, y)
            self.departure(self.YF, zz, x, y)
            self.departure(self.CO, zz, x, y)
            self.departure(self.CX, zz, 1 - x, y)
            self.departure(self.CY, zz, x, 1 - y)
            self.departure(self.XH, zz, x, 1 - y, high)
            self.departure(self.CB, zz, 1 - x, 1 - y, high)
            if low.size:
                self.departure(self.YH, zz, 1 - x, y, low)
                self.departure(self.CA, zz, 1 - x, 1 - y, low)
            if k > 0:
                self.departure(self.CC, zz, 1 - x, 1 - y, self.deep)

            @pl.when((zz <= z) & (z < nz - 1))
            def _():
                self.departure(self.ZU, zz, x, y)
                self.departure(self.DU, zz, 1 - x, 1 - y, self.deep)

            @pl.when((zz >= z) & (z > 0))
            def _():
                self.departure(self.ZD, zz, x, y)
                self.departure(self.DD, zz, 1 - x, 1 - y, self.deep)


class Fold:
    KINDS = 12
    CD, CX, CY, CO, XH, YH, XF, YF, ZU, ZD, DU, DD = range(KINDS)
    SPOT = {CD: (1, 1), CX: (1, 0), CY: (0, 1), CO: (0, 0)}

    def __init__(
        self, place, split, parts, total, from_c, half_x, half_y, z_buf, d_buf, sent, got, loaded
    ):
        self.place, self.parts, self.total, self.from_c = place, parts, total, from_c
        self.half_x, self.half_y, self.z_buf, self.d_buf = half_x, half_y, z_buf, d_buf
        self.sent, self.got, self.loaded = sent, got, loaded
        self.rows = total.shape[3]
        self.own_split, self.through_z, self.other_split = split
        self.deep = pl.ds(0, self.through_z)
        z, x, c, y = place.z, place.x, place.c, place.y
        self.over_x, self.over_y = place.device(x=1 - x), place.device(y=1 - y)
        self.over_c = place.device(c=1 - c)

    def diagonal_parts(self, zz, own):
        if own:
            low = pl.ds(0, self.own_split)
            high = pl.ds(self.own_split, self.rows - self.own_split)
            return low, high, self.half_y.at[low], self.half_x.at[pl.ds(0, high.size)]
        low = pl.ds(self.through_z, self.other_split)
        start = self.through_z + self.other_split
        high = pl.ds(start, self.rows - start)
        y_start = pl.multiple_of(self.own_split + zz * low.size, 16)
        x_start = pl.multiple_of(self.rows - self.own_split + zz * high.size, 16)
        return (
            low,
            high,
            self.half_y.at[pl.ds(y_start, low.size)],
            self.half_x.at[pl.ds(x_start, high.size)],
        )

    def push(self, kind, zz, src, dst, device):
        send(src, dst, self.sent.at[kind, zz], self.got.at[kind, zz], device)

    def arrival(self, kind, zz, ref):
        pltpu.make_async_copy(ref, ref, self.got.at[kind, zz]).wait()

    def begin(self):
        x, c, y, nz = self.place.x, self.place.c, self.place.y, self.place.z_count

        def start(kind, i):
            dx, dy = self.SPOT[kind]
            zz = self.place.far_first(i)
            xx, yy = (1 - x if dx else x), (1 - y if dy else y)
            self.push(
                kind, zz, self.parts.at[zz, xx, 1 - c, yy], self.from_c.at[dx, dy, zz], self.over_c
            )
            pltpu.make_async_copy(
                self.parts.at[zz, xx, c, yy], self.total.at[dx, dy, zz], self.loaded.at[kind, zz]
            ).start()

        for i in range(nz):
            start(self.CD, i)
            start(self.CX, i)
            start(self.CY, i)
        for i in range(nz):
            start(self.CO, i)

    def join_cores(self, kind, zz):
        dx, dy = self.SPOT[kind]
        here, there = self.total.at[dx, dy, zz], self.from_c.at[dx, dy, zz]
        pltpu.make_async_copy(here, here, self.loaded.at[kind, zz]).wait()
        self.arrival(kind, zz, there)
        add_rows(here, there, self.rows)

    def deep_push(self, zz):
        z, nz = self.place.z, self.place.z_count
        mine = self.total.at[1, 1, zz, self.deep]

        @pl.when(zz > z)
        def _():
            self.push(self.DU, zz, mine, self.d_buf.at[zz], self.place.device(z=z + 1))

        @pl.when(zz < z)
        def _():
            landing = jnp.where(zz == z - 1, nz, zz)
            self.push(self.DD, zz, mine, self.d_buf.at[landing], self.place.device(z=z - 1))

    def at_end(self):
        return (self.place.z == 0) | (self.place.z == self.place.z_count - 1)

    def halves(self, i):
        own = i == self.place.z_count - 1
        zz = self.place.far_first(i)
        self.join_cores(self.CD, zz)
        self.join_cores(self.CX, zz)
        if own:
            return
        self.push_halves(zz, False)

        @pl.when(self.at_end())
        def _():
            self.deep_push(zz)

    def push_halves(self, zz, own):
        low, high, land_y, land_x = self.diagonal_parts(zz, own)
        self.push(self.XH, zz, self.total.at[1, 1, zz, high], land_x, self.over_x)
        self.push(self.YH, zz, self.total.at[1, 1, zz, low], land_y, self.over_y)

    def deep_on(self, i):
        z = self.place.z
        zz = self.place.far_first(i)

        @pl.when(jnp.logical_not(self.at_end()))
        def _():
            @pl.when(zz > z)
            def _():
                self.arrival(self.DU, zz, self.d_buf.at[zz])

            @pl.when(zz < z)
            def _():
                self.arrival(self.DD, zz, self.d_buf.at[zz])

            add_rows(self.total.at[1, 1, zz, self.deep], self.d_buf.at[zz], self.through_z)
            self.deep_push(zz)

    def own_halves(self):
        z, nz = self.place.z, self.place.z_count
        mine = self.total.at[1, 1, z, self.deep]

        @pl.when(z > 0)
        def _():
            self.arrival(self.DU, z, self.d_buf.at[z])
            add_rows(mine, self.d_buf.at[z], self.through_z)

        @pl.when(z < nz - 1)
        def _():
            self.arrival(self.DD, z, self.d_buf.at[nz])
            add_rows(mine, self.d_buf.at[nz], self.through_z)

        self.push_halves(z, True)

    def columns(self, i):
        zz = self.place.far_first(i)
        low, high, land_y, land_x = self.diagonal_parts(zz, i == self.place.z_count - 1)
        self.join_cores(self.CY, zz)
        self.arrival(self.XH, zz, land_x)
        add_rows(self.total.at[0, 1, zz, high], land_x, high.size)
        self.arrival(self.YH, zz, land_y)
        add_rows(self.total.at[1, 0, zz, low], land_y, low.size)
        self.push(self.XF, zz, self.total.at[1, 0, zz], self.from_c.at[1, 1, zz], self.over_x)
        self.push(self.YF, zz, self.total.at[0, 1, zz], self.from_c.at[1, 0, zz], self.over_y)

    def along_z(self, i):
        z, nz = self.place.z, self.place.z_count
        zz = self.place.far_first(i)
        mine = self.total.at[0, 0, zz]
        self.join_cores(self.CO, zz)
        self.arrival(self.XF, zz, self.from_c.at[1, 1, zz])
        add_rows(mine, self.from_c.at[1, 1, zz], self.rows)
        self.arrival(self.YF, zz, self.from_c.at[1, 0, zz])
        add_rows(mine, self.from_c.at[1, 0, zz], self.rows)
        above = jnp.where(zz == z, nz, zz)

        @pl.when((z > 0) & (zz >= z))
        def _():
            self.arrival(self.ZU, zz, self.z_buf.at[zz])
            add_rows(mine, self.z_buf.at[zz], self.rows)

        @pl.when((z < nz - 1) & (zz <= z))
        def _():
            self.arrival(self.ZD, zz, self.z_buf.at[above])
            add_rows(mine, self.z_buf.at[above], self.rows)

        @pl.when(zz > z)
        def _():
            self.push(self.ZU, zz, mine, self.z_buf.at[zz], self.place.device(z=z + 1))

        @pl.when(zz < z)
        def _():
            landing = jnp.where(zz == z - 1, nz, zz)
            self.push(self.ZD, zz, mine, self.z_buf.at[landing], self.place.device(z=z - 1))

    def opening(self):
        last = self.place.z_count - 1
        return [functools.partial(self.halves, i) for i in range(last)] + [
            functools.partial(self.columns, i) for i in range(min(1, last))
        ]

    def middle(self):
        last = self.place.z_count - 1
        steps = [functools.partial(self.deep_on, i) for i in range(last)]
        steps.insert(1, functools.partial(self.halves, last))
        steps.append(self.own_halves)
        return steps + [functools.partial(self.columns, i) for i in range(min(1, last), last + 1)]

    def result(self):
        return self.total[0, 0, self.place.z]

    def finish(self):
        z, nz = self.place.z, self.place.z_count

        def departure(kind, zz, ref):
            pltpu.make_async_copy(ref, ref, self.sent.at[kind, zz]).wait()

        for i in range(nz):
            zz = self.place.far_first(i)
            low, high, land_y, land_x = self.diagonal_parts(zz, i == nz - 1)
            for kind in (self.CD, self.CX, self.CY, self.CO, self.XF, self.YF):
                departure(kind, zz, self.total.at[0, 0, zz])
            departure(self.XH, zz, land_x)
            departure(self.YH, zz, land_y)

            @pl.when(zz > z)
            def _():
                departure(self.ZU, zz, self.total.at[0, 0, zz])
                departure(self.DU, zz, self.d_buf.at[zz])

            @pl.when(zz < z)
            def _():
                departure(self.ZD, zz, self.total.at[0, 0, zz])
                departure(self.DD, zz, self.d_buf.at[zz])


def half_rows(rows, split):
    own, deep, other = split
    return (own, other), (rows - own, rows - deep - other)


def fold_scratch(nz, rows, cols, split, dt):
    (y_own, y_other), (x_own, x_other) = half_rows(rows, split)
    return [
        pltpu.VMEM((2, 2, nz, rows, cols), dt),
        pltpu.VMEM((2, 2, nz, rows, cols), dt),
        pltpu.VMEM((x_own + nz * x_other, cols), dt),
        pltpu.VMEM((y_own + nz * y_other, cols), dt),
        pltpu.VMEM((nz + 1, rows, cols), dt),
        pltpu.VMEM((nz + 1, split[1], cols), dt),
        pltpu.SemaphoreType.DMA((Fold.KINDS, nz)),
        pltpu.SemaphoreType.DMA((Fold.KINDS, nz)),
        pltpu.SemaphoreType.DMA((4, nz)),
    ]


def scatter_kernel(parts, *refs):
    streams, refs = refs[:5], refs[5:]
    out, wg_grad, wu_grad, wd_grad = refs[:4]
    tiles, tile_sems, scratch = refs[4:9], refs[9], refs[10:]
    place = Place()
    nz = place.z_count
    fold = Fold(place, row_split(out.shape[0]), parts, *scratch)
    count = streams[0].shape[0]
    place.meet()
    fold.begin()

    def loads(t, slot):
        return [
            pltpu.make_async_copy(stream.at[t], tile.at[slot], tile_sems.at[slot, n])
            for n, (stream, tile) in enumerate(zip(streams, tiles))
        ]

    def tile_step(t, carry):
        slot = t % 2
        for copy in loads(t, slot):
            copy.wait()

        @pl.when(t + 1 < count)
        def _():
            for copy in loads(t + 1, 1 - slot):
                copy.start()

        x_tile, g_tile, hidden, gate_pre_grad, up_grad = (tile[slot] for tile in tiles)
        wg_grad[...] += dot_tn(x_tile, gate_pre_grad)
        wu_grad[...] += dot_tn(x_tile, up_grad)
        wd_grad[...] += dot_tn(hidden, g_tile)
        return carry

    for copy in loads(0, 0):
        copy.start()
    for grad in (wg_grad, wu_grad, wd_grad):
        grad[...] = jnp.zeros_like(grad)
    steps = fold.opening() + fold.middle()
    steps += [functools.partial(fold.along_z, i) for i in range(nz)]
    done = 0
    for n, step in enumerate(steps):
        until = min(count, round(count * n / (len(steps) - 1)))
        lax.fori_loop(done, until, tile_step, 0)
        done = until
        step()
    out[...] = fold.result()
    fold.finish()


def row_split(rows):
    return rows // 2, rows // 2, rows // 4


def scatter_sum(parts, streams, collective):
    nz, _, _, _, rows, cols = parts.shape
    dt = parts.dtype
    width, units = streams[0].shape[1], streams[2].shape[1]
    tile = 256 if streams[0].shape[0] % 256 == 0 else GROUP // 2
    streams = [stream.reshape(-1, tile, stream.shape[1]) for stream in streams]
    shapes = [(width, units), (width, units), (units, width)]
    return pl.pallas_call(
        scatter_kernel,
        out_shape=[jax.ShapeDtypeStruct((rows, cols), dt)]
        + [jax.ShapeDtypeStruct(shape, jnp.float32) for shape in shapes],
        in_specs=[ANYWHERE] * 6,
        out_specs=[IN_VMEM] * 4,
        scratch_shapes=[pltpu.VMEM((2,) + stream.shape[1:], stream.dtype) for stream in streams]
        + [pltpu.SemaphoreType.DMA((2, 5))]
        + fold_scratch(nz, rows, cols, row_split(rows), dt),
        cost_estimate=LINK_TIME,
        compiler_params=pltpu.CompilerParams(
            collective_id=collective, has_side_effects=True, vmem_limit_bytes=62 << 20
        ),
    )(parts, *streams)


def turn(values):
    return pltpu.roll(values, HEAD // 2, 1)


def seen_keys():
    row = lax.broadcasted_iota(jnp.int32, (GROUP, GROUP), 0)
    col = lax.broadcasted_iota(jnp.int32, (GROUP, GROUP), 1)
    return (col <= row) & ((col < PROMPT) | (col >= row - row % CONT))


def signed_rope_tables():
    cosine_table, sine_table = rope_tables()
    sign = jnp.where(jnp.arange(HEAD) < HEAD // 2, -1.0, 1.0)
    return cosine_table, sine_table * sign[None, :]


def attend_kernel(
    src,
    normed_source,
    w_query_source,
    w_key_source,
    w_value_source,
    w_out_source,
    q_gain,
    k_gain,
    cosine,
    sine,
    whole,
    queries,
    keys,
    values,
    q_rot,
    k_rot,
    mixed,
    q_inv,
    k_inv,
    log_total,
    attended,
    stats,
    stats_got,
    leaving,
    landed,
    normed,
    w_query,
    w_key,
    w_value,
    w_out,
    fetch_sems,
    swap_sems,
    sent,
    got,
    kept,
):
    sources = (normed_source, w_query_source, w_key_source, w_value_source, w_out_source)
    fetched = fetch(sources, (normed, w_query, w_key, w_value, w_out), fetch_sems)
    place = Place()
    nz = place.z_count
    rows = leaving.shape[0]
    spread = Spread(place, src, whole, sent, got, kept, rows // 4, rows * 3 // 4, 0)
    place.meet()
    over_y = place.device(y=1 - place.y)
    spread.begin()

    lane = lax.broadcasted_iota(jnp.int32, stats.shape, 1)
    stats[...] = jnp.zeros_like(stats)
    chunk = 2 * HEAD

    def project(i, carry):
        here = pl.ds(pl.multiple_of(i * chunk, chunk), chunk)
        for index, (weight, raw) in enumerate(((w_query, queries), (w_key, keys))):
            product = dot_nn(normed[...], weight[:, here])
            raw[:, here] = product
            squares = jnp.sum(product * product, axis=1, keepdims=True)
            stats[...] += jnp.where(lane == index, squares, 0.0)
        values[:, here] = dot_nn(normed[...], w_value[:, here]).astype(jnp.bfloat16)
        return carry

    for copy in fetched[:4]:
        copy.wait()
    lax.fori_loop(0, queries.shape[1] // chunk, project, 0)
    stats_swap = send(stats, stats_got, swap_sems.at[0, 0], swap_sems.at[1, 0], over_y)
    spread.relay(0)
    if nz > 1:
        spread.along_z(1)
        spread.column(1)
    stats_swap.wait()
    for index, inv in enumerate((q_inv, k_inv)):
        total = stats[:, index : index + 1] + stats_got[:, index : index + 1]
        inv[...] = lax.rsqrt(total / D + EPSILON)
    visible = seen_keys()

    def head(h, carry):
        here = pl.ds(pl.multiple_of(h * HEAD, HEAD), HEAD)
        for raw, inv, gain, rotated in ((queries, q_inv, q_gain, q_rot), (keys, k_inv, k_gain, k_rot)):
            normal = raw[:, here] * inv[...] * gain[:, here]
            rotated[:, here] = (normal * cosine[...] + turn(normal) * sine[...]).astype(jnp.bfloat16)
        scores = dot_nt(q_rot[:, here], k_rot[:, here]) * HEAD**-0.5
        scores = jnp.where(visible, scores, -1e30)
        row_max = jnp.max(scores, axis=1, keepdims=True)
        exponent = jnp.exp(scores - row_max)
        row_total = jnp.sum(exponent, axis=1, keepdims=True)
        log_total[h] = row_max + jnp.log(row_total)
        weights = (exponent / row_total).astype(jnp.bfloat16)
        mixed[:, here] = dot_nn(weights, values[:, here]).astype(jnp.bfloat16)
        return carry

    heads = queries.shape[1] // HEAD
    lax.fori_loop(0, heads // 2, head, 0)
    spread.diagonal(0)
    if nz > 2:
        spread.along_z(2)
        spread.column(2)
    lax.fori_loop(heads // 2, heads, head, 0)

    def joined(target, index):
        where = pl.ds(pl.multiple_of(index * rows, rows), rows)

        def columns(b, carry):
            here = pl.ds(pl.multiple_of(b * w_out.shape[2], w_out.shape[2]), w_out.shape[2])
            target[:, here] = dot_nn(mixed[where], w_out[b]).astype(target.dtype)
            return carry

        lax.fori_loop(0, w_out.shape[0], columns, 0)

    fetched[4].wait()
    joined(leaving, 1 - place.y)
    swap = send(leaving, landed, swap_sems.at[0, 1], swap_sems.at[1, 1], over_y)
    if nz > 1:
        spread.relay(1)
    joined(attended, place.y)
    for k in range(1, nz):
        spread.diagonal_along_z(k)
        if k + 2 < nz:
            spread.along_z(k + 2)
            spread.column(k + 2)
        if k + 1 < nz:
            spread.relay(k + 1)
        spread.diagonal(k)
    swap.wait()
    attended[...] += landed[...].astype(jnp.float32)
    spread.keep.wait()
    for k in range(nz):
        spread.sibling_near(k)
        spread.sibling_far(k)
    spread.finish()


def attend(block, normed, weights, gains, tables, collective):
    nz = lax.axis_size("dp") // 4
    rows, width = block.shape
    group, cols = normed.shape[0], weights[0].shape[1]
    half = jax.ShapeDtypeStruct((group, cols), jnp.bfloat16)
    wide = jax.ShapeDtypeStruct((group, cols), jnp.float32)
    thin = jax.ShapeDtypeStruct((group, 1), jnp.float32)
    return pl.pallas_call(
        attend_kernel,
        out_shape=[
            jax.ShapeDtypeStruct((nz, 2, 2, 2, rows, width), block.dtype),
            wide,
            wide,
            half,
            half,
            half,
            half,
            thin,
            thin,
            jax.ShapeDtypeStruct((cols // HEAD, group, 1), jnp.float32),
            jax.ShapeDtypeStruct((rows, width), jnp.float32),
        ],
        in_specs=[ANYWHERE] * 6 + [IN_VMEM] * 4,
        out_specs=[ANYWHERE] + [IN_VMEM] * 10,
        scratch_shapes=[
            pltpu.VMEM((group, LANES), jnp.float32),
            pltpu.VMEM((group, LANES), jnp.float32),
            pltpu.VMEM((rows, width), jnp.bfloat16),
            pltpu.VMEM((rows, width), jnp.bfloat16),
        ]
        + [pltpu.VMEM(array.shape, array.dtype) for array in (normed, *weights)]
        + [
            pltpu.SemaphoreType.DMA((5,)),
            pltpu.SemaphoreType.DMA((2, 2)),
            pltpu.SemaphoreType.DMA((Spread.KINDS, nz)),
            pltpu.SemaphoreType.DMA((Spread.KINDS, nz)),
            pltpu.SemaphoreType.DMA,
        ],
        cost_estimate=LINK_TIME,
        compiler_params=pltpu.CompilerParams(
            collective_id=collective, has_side_effects=True, vmem_limit_bytes=60 << 20
        ),
    )(block, normed, *weights, *gains, *tables)


def busy_y_split(rows):
    return rows // 2, rows // 2, rows // 6


def attend_back_kernel(
    parts,
    own_grad,
    w_out_source,
    queries_source,
    keys_source,
    q_rot_source,
    k_rot_source,
    values_source,
    q_inv,
    k_inv,
    log_total_source,
    q_gain,
    k_gain,
    cosine,
    sine,
    mixture,
    attended_grad,
    q_grad,
    k_grad,
    v_grad,
    gain_grads,
    landed,
    mixed_grad,
    q_scaled,
    k_scaled,
    dots,
    dots_got,
    w_out,
    queries,
    keys,
    q_rot,
    k_rot,
    values,
    log_total,
    fetch_sems,
    swap_sems,
    *scratch,
):
    sources = (
        w_out_source,
        queries_source,
        keys_source,
        q_rot_source,
        k_rot_source,
        values_source,
        log_total_source,
    )
    targets = (w_out, queries, keys, q_rot, k_rot, values, log_total)
    fetched = fetch(sources, targets, fetch_sems)
    place = Place()
    nz = place.z_count
    fold = Fold(place, busy_y_split(own_grad.shape[0]), parts, *scratch)
    place.meet()
    over_y = place.device(y=1 - place.y)
    rows = own_grad.shape[0]
    swap = send(own_grad, landed, swap_sems.at[0, 0], swap_sems.at[1, 0], over_y)
    fold.begin()

    def take(block, index):
        where = pl.ds(pl.multiple_of(index * rows, rows), rows)
        attended_grad[where] = block[...]
        step = w_out.shape[2]

        def columns(b, total):
            here = pl.ds(pl.multiple_of(b * step, step), step)
            return total + dot_nt(block[:, here], w_out[b])

        total = jnp.zeros((rows, mixed_grad.shape[1]), jnp.float32)
        total = lax.fori_loop(0, w_out.shape[0], columns, total)
        mixed_grad[where] = total.astype(jnp.bfloat16)

    fetched[0].wait()
    take(own_grad, place.y)
    for step in fold.opening():
        step()
    swap.wait()
    take(landed, 1 - place.y)
    for copy in fetched[1:]:
        copy.wait()
    visible = seen_keys()
    lane = lax.broadcasted_iota(jnp.int32, dots.shape, 1)
    dots[...] = jnp.zeros_like(dots)

    def head(h, carry):
        here = pl.ds(pl.multiple_of(h * HEAD, HEAD), HEAD)
        upstream = mixed_grad[:, here]
        scores = dot_nt(q_rot[:, here], k_rot[:, here]) * HEAD**-0.5
        probs = jnp.exp(jnp.where(visible, scores, -1e30) - log_total[h])
        prob_grad = dot_nt(upstream, values[:, here])
        row_dot = jnp.sum(prob_grad * probs, axis=1, keepdims=True)
        score_grad = (probs * (prob_grad - row_dot)).astype(jnp.bfloat16)
        v_grad[:, here] = dot_tn(probs.astype(jnp.bfloat16), upstream).astype(jnp.bfloat16)
        for index, (rot_grad, raw, inv, gain, scaled) in enumerate(
            (
                (dot_nn(score_grad, k_rot[:, here]), queries, q_inv, q_gain, q_scaled),
                (dot_tn(score_grad, q_rot[:, here]), keys, k_inv, k_gain, k_scaled),
            )
        ):
            rot_grad = rot_grad * HEAD**-0.5
            norm_grad = rot_grad * cosine[...] - turn(rot_grad) * sine[...]
            with_raw = norm_grad * raw[:, here]
            gain_grads[index : index + 1, here] = jnp.sum(with_raw * inv[...], axis=0, keepdims=True)
            scaled[:, here] = norm_grad * gain[:, here]
            part = jnp.sum(with_raw * gain[:, here], axis=1, keepdims=True)
            dots[...] += jnp.where(lane == index, part, 0.0)
        return carry

    heads = queries.shape[1] // HEAD
    steps = fold.middle()
    for n, step in enumerate(steps):
        step()
        lax.fori_loop(heads * n // len(steps), heads * (n + 1) // len(steps), head, 0)
    dots_swap = send(dots, dots_got, swap_sems.at[0, 1], swap_sems.at[1, 1], over_y)
    for i in range(nz):
        fold.along_z(i)
    mixture[...] = fold.result()
    dots_swap.wait()

    def grads(h, carry):
        here = pl.ds(pl.multiple_of(h * HEAD, HEAD), HEAD)
        for index, (raw, inv, scaled, grad) in enumerate(
            ((queries, q_inv, q_scaled, q_grad), (keys, k_inv, k_scaled, k_grad))
        ):
            mean = (dots[:, index : index + 1] + dots_got[:, index : index + 1]) / D
            scale = inv[...]
            grad[:, here] = (
                scale * scaled[:, here] - raw[:, here] * (scale * scale * scale * mean)
            ).astype(jnp.bfloat16)
        return carry

    lax.fori_loop(0, heads, grads, 0)
    fold.finish()


def attend_back(parts, own_grad, w_out, saved, gains, tables, collective):
    nz, _, _, _, rows, cols = parts.shape
    queries = saved[0]
    group, head_cols = queries.shape
    half = jax.ShapeDtypeStruct((group, head_cols), jnp.bfloat16)
    wide = pltpu.VMEM((group, head_cols), jnp.float32)
    return pl.pallas_call(
        attend_back_kernel,
        out_shape=[
            jax.ShapeDtypeStruct((rows, cols), jnp.bfloat16),
            jax.ShapeDtypeStruct((group, cols), jnp.bfloat16),
            half,
            half,
            half,
            jax.ShapeDtypeStruct((8, head_cols), jnp.float32),
        ],
        in_specs=[ANYWHERE, IN_VMEM] + [ANYWHERE] * 6 + [IN_VMEM] * 2 + [ANYWHERE] + [IN_VMEM] * 4,
        out_specs=[IN_VMEM] * 6,
        scratch_shapes=[
            pltpu.VMEM((rows, cols), jnp.bfloat16),
            pltpu.VMEM((group, head_cols), jnp.bfloat16),
            wide,
            wide,
            pltpu.VMEM((group, LANES), jnp.float32),
            pltpu.VMEM((group, LANES), jnp.float32),
        ]
        + [pltpu.VMEM(array.shape, array.dtype) for array in (w_out, *saved[:5], saved[7])]
        + [pltpu.SemaphoreType.DMA((7,)), pltpu.SemaphoreType.DMA((2, 2))]
        + fold_scratch(nz, rows, cols, busy_y_split(rows), parts.dtype),
        cost_estimate=LINK_TIME,
        compiler_params=pltpu.CompilerParams(
            collective_id=collective, has_side_effects=True, vmem_limit_bytes=62 << 20
        ),
    )(parts, own_grad, w_out, *saved, *gains, *tables)


def plane_gather_kernel(count, *refs):
    srcs, block = refs[:count], refs[count]
    outs, landed = refs[count + 1 : 2 * count + 1], refs[2 * count + 1]
    sent, got, kept, swap_sems = refs[2 * count + 2 :]
    place = Place()
    z, x, c, nz = place.z, place.x, place.c, place.z_count
    ZU, ZD, XF, CO, CX, EU, ED, CE = range(8)
    up, down = place.device(z=z + 1), place.device(z=z - 1)
    over_x, over_c = place.device(x=1 - x), place.device(c=1 - c)
    place.meet()
    every = range(count)
    swap = send(block, landed, swap_sems.at[0], swap_sems.at[1], place.device(y=1 - place.y))

    lengths = [src.shape[0] for src in srcs]
    deep = [3 * n // 4 if n == max(lengths) else 0 for n in lengths]

    def rest(a, own):
        return slice(None) if own or not deep[a] else pl.ds(deep[a], lengths[a] - deep[a])

    def view(a, zz, xx, cc, rows):
        block = outs[a].at[zz, xx, cc]
        return block if rows == slice(None) else block.at[rows]

    def push(a, kind, zz, xx, device, own=False, rows=slice(None)):
        ref = view(a, zz, xx, c, rows)
        send(srcs[a] if own else ref, ref, sent.at[kind, a, zz], got.at[kind, a, zz], device)

    def arrival(a, kind, zz, xx, cc, rows=slice(None)):
        ref = view(a, zz, xx, cc, rows)
        pltpu.make_async_copy(ref, ref, got.at[kind, a, zz]).wait()

    def departure(a, kind, zz, xx, rows=slice(None)):
        ref = view(a, zz, xx, c, rows)
        pltpu.make_async_copy(ref, ref, sent.at[kind, a, zz]).wait()

    keeps = []
    for a in every:
        push(a, XF, z, x, over_x, own=True)

        @pl.when(z < nz - 1)
        def _():
            push(a, ZU, z, x, up, own=True)

        @pl.when(z > 0)
        def _():
            push(a, ZD, z, x, down, own=True)

        push(a, CO, z, x, over_c, own=True)
        keep = pltpu.make_async_copy(srcs[a], outs[a].at[z, x, c], kept.at[a])
        keep.start()
        keeps.append(keep)

    def relay(a, zz, own):
        rows = rest(a, own)
        arrival(a, XF, zz, 1 - x, c, rows)
        if own and deep[a]:
            some = pl.ds(0, deep[a])

            @pl.when(z < nz - 1)
            def _():
                push(a, EU, z, 1 - x, up, rows=some)

            @pl.when(z > 0)
            def _():
                push(a, ED, z, 1 - x, down, rows=some)

        push(a, CX, zz, 1 - x, over_c, rows=rows)

    def deep_along_z(a, d):
        some = pl.ds(0, deep[a])

        @pl.when(z - d >= 0)
        def _():
            arrival(a, EU, z - d, 1 - x, c, some)

            @pl.when(z < nz - 1)
            def _():
                push(a, EU, z - d, 1 - x, up, rows=some)

            push(a, CE, z - d, 1 - x, over_c, rows=some)

        @pl.when(z + d < nz)
        def _():
            arrival(a, ED, z + d, 1 - x, c, some)

            @pl.when(z > 0)
            def _():
                push(a, ED, z + d, 1 - x, down, rows=some)

            push(a, CE, z + d, 1 - x, over_c, rows=some)

    for d in range(nz):
        below, above = z - d - 1, z + d + 1
        for a in every:
            if d < nz - 1:
                @pl.when(below >= 0)
                def _():
                    arrival(a, ZU, below, x, c)

                    @pl.when(z < nz - 1)
                    def _():
                        push(a, ZU, below, x, up)

                    push(a, XF, below, x, over_x, rows=rest(a, False))
                    push(a, CO, below, x, over_c)

                @pl.when(above < nz)
                def _():
                    arrival(a, ZD, above, x, c)

                    @pl.when(z > 0)
                    def _():
                        push(a, ZD, above, x, down)

                    push(a, XF, above, x, over_x, rows=rest(a, False))
                    push(a, CO, above, x, over_c)

    for d in range(nz):
        for a in every:
            if d == 0:
                relay(a, z, True)
            else:
                @pl.when(z - d >= 0)
                def _():
                    relay(a, z - d, False)

                @pl.when(z + d < nz)
                def _():
                    relay(a, z + d, False)

                if deep[a]:
                    deep_along_z(a, d)

    for a in every:
        keeps[a].wait()
        for near in range(nz):
            zz = place.near_first(near)
            rows, some = rest(a, near == 0), pl.ds(0, deep[a])
            arrival(a, CO, zz, x, 1 - c)
            arrival(a, CX, zz, 1 - x, 1 - c, rows)
            departure(a, XF, zz, x, rows)
            departure(a, CO, zz, x)
            departure(a, CX, zz, 1 - x, rows)
            if near and deep[a]:
                arrival(a, CE, zz, 1 - x, 1 - c, some)
                departure(a, CE, zz, 1 - x, some)

            @pl.when((zz <= z) & (z < nz - 1))
            def _():
                departure(a, ZU, zz, x)
                if deep[a]:
                    departure(a, EU, zz, 1 - x, some)

            @pl.when((zz >= z) & (z > 0))
            def _():
                departure(a, ZD, zz, x)
                if deep[a]:
                    departure(a, ED, zz, 1 - x, some)

    swap.wait()


def gather_in_plane(shards, block, collective):
    nz = lax.axis_size("dp") // 4
    count = len(shards)
    return pl.pallas_call(
        functools.partial(plane_gather_kernel, count),
        out_shape=[jax.ShapeDtypeStruct((nz, 2, 2) + s.shape, s.dtype) for s in shards]
        + [jax.ShapeDtypeStruct(block.shape, block.dtype)],
        in_specs=[ANYWHERE] * (count + 1),
        out_specs=[ANYWHERE] * (count + 1),
        scratch_shapes=[
            pltpu.SemaphoreType.DMA((8, count, nz)),
            pltpu.SemaphoreType.DMA((8, count, nz)),
            pltpu.SemaphoreType.DMA((count,)),
            pltpu.SemaphoreType.DMA((2,)),
        ],
        cost_estimate=LINK_TIME,
        compiler_params=pltpu.CompilerParams(collective_id=collective, has_side_effects=True),
    )(*shards, block)


def plane_scatter_kernel(count, *refs):
    lefts, rights = refs[:count], refs[count : 2 * count]
    small, row_part = refs[2 * count : 2 * count + 2]
    refs = refs[2 * count + 2 :]
    outs, small_out, row_landed = refs[:count], refs[count], refs[count + 1]
    total, leaving, from_c, full_x, z_buf, small_sum, small_got = refs[count + 2 : count + 9]
    sent, got, small_sems, row_sems = refs[count + 9 :]
    place = Place()
    z, x, c, nz = place.z, place.x, place.c, place.z_count
    rows = total.shape[3]
    C0, C1, XF, ZU, ZD = range(5)
    over_x, over_c = place.device(x=1 - x), place.device(c=1 - c)
    over_y = place.device(y=1 - place.y)
    place.meet(all_z=True)

    small_sum[0] = small[...]

    def small_start(i):
        return send(
            small_sum.at[i],
            small_got.at[i],
            small_sems.at[0, i],
            small_sems.at[1, i],
            (over_x, over_c, over_y)[i],
        )

    def small_end(i, copy):
        copy.wait()
        small_sum[i + 1] = small_sum[i] + small_got[i]

    def small_z_start():
        return [
            send(
                small_sum.at[3],
                small_got.at[2 + d],
                small_sems.at[0, 2 + d],
                small_sems.at[1, 2 + d],
                place.device(z=(z + d) % nz),
            )
            for d in range(1, nz)
        ]

    def small_z_end(copies):
        for copy in copies:
            copy.wait()
        result = jnp.zeros_like(small_out)
        for zz in range(nz):
            away = (z - zz) % nz
            result = result + jnp.where(away == 0, small_sum[3], small_got[jnp.maximum(2 + away, 3)])
        small_out[...] = result

    def arrival(a, kind, zz, ref):
        pltpu.make_async_copy(ref, ref, got.at[kind, a, zz]).wait()

    small_copy = small_start(0)

    def make(dx, i):
        zz = place.far_first(i)
        xx = 1 - x if dx else x
        for a in range(count):

            def product(cc):
                shard = (zz * 2 + xx) * 2 + cc
                here = pl.ds(pl.multiple_of(shard * rows, rows), rows)
                return dot_tn(lefts[a][:, here], rights[a][...]).astype(total.dtype)

            leaving[dx, zz, a] = product(1 - c)
            send(
                leaving.at[dx, zz, a],
                from_c.at[dx, zz, a],
                sent.at[C1 if dx else C0, a, zz],
                got.at[C1 if dx else C0, a, zz],
                over_c,
            )
            total[dx, zz, a] = product(c)

    def join_cores(a, dx, zz):
        there = from_c.at[dx, zz, a]
        arrival(a, C1 if dx else C0, zz, there)
        add_rows(total.at[dx, zz, a], there, rows)

    def over_the_x(i):
        zz = place.far_first(i)
        for a in range(count):
            join_cores(a, 1, zz)
            send(total.at[1, zz, a], full_x.at[zz, a], sent.at[XF, a, zz], got.at[XF, a, zz], over_x)

    def along_z(i):
        zz = place.far_first(i)
        above = jnp.where(zz == z, nz, zz)
        landing = jnp.where(zz == z - 1, nz, zz)
        for a in range(count):
            mine = total.at[0, zz, a]
            join_cores(a, 0, zz)
            arrival(a, XF, zz, full_x.at[zz, a])
            add_rows(mine, full_x.at[zz, a], rows)

            @pl.when((z > 0) & (zz >= z))
            def _():
                arrival(a, ZU, zz, z_buf.at[zz, a])
                add_rows(mine, z_buf.at[zz, a], rows)

            @pl.when((z < nz - 1) & (zz <= z))
            def _():
                arrival(a, ZD, zz, z_buf.at[above, a])
                add_rows(mine, z_buf.at[above, a], rows)

            @pl.when(zz > z)
            def _():
                send(
                    mine,
                    z_buf.at[zz, a],
                    sent.at[ZU, a, zz],
                    got.at[ZU, a, zz],
                    place.device(z=z + 1),
                )

            @pl.when(zz < z)
            def _():
                send(
                    mine,
                    z_buf.at[landing, a],
                    sent.at[ZD, a, zz],
                    got.at[ZD, a, zz],
                    place.device(z=z - 1),
                )

    make(1, 0)
    row_copy = send(row_part, row_landed, row_sems.at[0], row_sems.at[1], over_y)
    small_end(0, small_copy)
    small_copy = small_start(1)
    for i in range(1, nz):
        make(1, i)
        over_the_x(i - 1)
        if i == 1:
            small_end(1, small_copy)
            small_copy = small_start(2)
    over_the_x(nz - 1)

    def own_chips(i, carry):
        make(0, i)
        return carry

    lax.fori_loop(0, nz, own_chips, 0)
    small_end(2, small_copy)
    small_copies = small_z_start()
    for i in range(nz):
        along_z(i)
        if i == 0:
            small_z_end(small_copies)
    row_copy.wait()

    for a in range(count):

        def widen(i, carry):
            here = pl.ds(pl.multiple_of(i * 16, 16), 16)
            outs[a][here] = total[0, z, a, here].astype(jnp.float32)
            return carry

        lax.fori_loop(0, rows // 16, widen, 0)

    def departure(a, kind, zz):
        ref = total.at[0, 0, a]
        pltpu.make_async_copy(ref, ref, sent.at[kind, a, zz]).wait()

    for a in range(count):
        for zz in range(nz):
            departure(a, C0, zz)
            departure(a, C1, zz)
            departure(a, XF, zz)

            @pl.when(zz > z)
            def _():
                departure(a, ZU, zz)

            @pl.when(zz < z)
            def _():
                departure(a, ZD, zz)


def scatter_in_plane(lefts, rights, small, row_part, collective):
    count = len(lefts)
    nz = lax.axis_size("dp") // 4
    cols, dt = rights[0].shape[1], rights[0].dtype
    rows = lefts[0].shape[1] // (4 * nz)
    blocks = pltpu.VMEM((2, nz, count, rows, cols), dt)
    return pl.pallas_call(
        functools.partial(plane_scatter_kernel, count),
        out_shape=[jax.ShapeDtypeStruct((rows, cols), jnp.float32)] * count
        + [
            jax.ShapeDtypeStruct(small.shape, small.dtype),
            jax.ShapeDtypeStruct(row_part.shape, row_part.dtype),
        ],
        in_specs=[IN_VMEM] * (2 * count + 1) + [ANYWHERE],
        out_specs=[IN_VMEM] * (count + 1) + [ANYWHERE],
        scratch_shapes=[
            blocks,
            blocks,
            blocks,
            pltpu.VMEM((nz, count, rows, cols), dt),
            pltpu.VMEM((nz + 1, count, rows, cols), dt),
            pltpu.VMEM((4,) + small.shape, small.dtype),
            pltpu.VMEM((2 + nz,) + small.shape, small.dtype),
            pltpu.SemaphoreType.DMA((5, count, nz)),
            pltpu.SemaphoreType.DMA((5, count, nz)),
            pltpu.SemaphoreType.DMA((2, 2 + nz)),
            pltpu.SemaphoreType.DMA((2,)),
        ],
        cost_estimate=LINK_TIME,
        compiler_params=pltpu.CompilerParams(
            collective_id=collective, has_side_effects=True, vmem_limit_bytes=62 << 20
        ),
    )(*lefts, *rights, small, row_part)


def dot_nn(a, b):
    return lax.dot_general(a, b, (((1,), (0,)), ((), ())), preferred_element_type=jnp.float32)


def dot_nt(a, b):
    return lax.dot_general(a, b, (((1,), (1,)), ((), ())), preferred_element_type=jnp.float32)


def dot_tn(a, b):
    return lax.dot_general(a, b, (((0,), (0,)), ((), ())), preferred_element_type=jnp.float32)


def pick(table, index):
    return sum(jnp.where(index == i, value, 0) for i, value in enumerate(table))


def expert_kernel(
    z_count,
    src,
    g_all,
    hot_ref,
    router_ref,
    lanes_ref,
    wg_source,
    wu_source,
    wd_source,
    x_all,
    y_all,
    r_all,
    hidden_all,
    gate_pre_grad_all,
    up_grad_all,
    x_tile,
    g_tile,
    y_tile,
    r_tile,
    hidden_tile,
    gate_pre_grad_tile,
    up_grad_tile,
    wg_ref,
    wu_ref,
    wd_ref,
    fetch_sems,
    load_sems,
    store_sems,
    sent,
    got,
    kept,
):
    fetched = fetch((wg_source, wu_source, wd_source), (wg_ref, wu_ref, wd_ref), fetch_sems)
    place = Place()
    place.meet()
    third = src.shape[0] // 3
    spread = Spread(place, src, x_all, sent, got, kept, src.shape[0] // 2, 2 * third, third // 2)
    spread.begin()
    width = src.shape[1]
    tile = x_tile.shape[1]
    pairs = sorted(
        ((k, dx) for k in range(z_count) for dx in (0, 1)),
        key=lambda p: p[0] + (1.3 if p[0] else 0.5) * p[1],
    )
    tiles = 2 * len(pairs)
    near_table, across_table = [p[0] for p in pairs], [p[1] for p in pairs]

    def tile_at(i):
        pair, second = i // 2, i % 2
        zz = place.near_first(pick(near_table, pair))
        xx = jnp.where(pick(across_table, pair) == 1, 1 - place.x, place.x)
        cc = jnp.where(second == 1, 1 - place.c, place.c)
        return zz, xx, cc

    stores = (
        (y_tile, y_all),
        (r_tile, r_all),
        (hidden_tile, hidden_all),
        (gate_pre_grad_tile, gate_pre_grad_all),
        (up_grad_tile, up_grad_all),
    )

    def loads(i, slot):
        zz, xx, cc = tile_at(i)
        copies = []
        for yy in range(2):
            rows = pl.ds(yy * (tile // 2), tile // 2)
            copies.append(
                pltpu.make_async_copy(
                    x_all.at[zz, xx, cc, yy], x_tile.at[slot, rows], load_sems.at[slot, yy]
                )
            )
        copies.append(
            pltpu.make_async_copy(g_all.at[zz, xx, cc], g_tile.at[slot], load_sems.at[slot, 2])
        )
        return copies

    def store(i, slot):
        zz, xx, cc = tile_at(i)
        return [
            pltpu.make_async_copy(here.at[slot], there.at[zz, xx, cc], store_sems.at[slot, n])
            for n, (here, there) in enumerate(stores)
        ]

    steps = {}
    for position, (k, dx) in enumerate(pairs):
        todo = []
        if dx == 0:
            if k == 0:
                todo.append((spread.relay, 0))
            elif k > 1:
                todo.append((spread.diagonal_along_z, k - 1))
            if k + 1 < z_count:
                todo += [(spread.along_z, k + 1), (spread.column, k + 1)]
            if k > 0:
                todo.append((spread.relay, k))
        else:
            if k == z_count - 1 and k > 0:
                todo.append((spread.diagonal_along_z, k))
            todo.append((spread.diagonal, k))
        steps[2 * position] = todo

    def prepare(i):
        for position in range(tiles):
            pair = position // 2
            k, dx = pairs[pair]

            @pl.when(i == position)
            def _():
                if position % 2 == 0:
                    for step, number in steps[position]:
                        step(number)
                    if position == 0:
                        spread.keep.wait()
                elif dx == 0:
                    spread.sibling_near(k)
                else:
                    spread.sibling_far(k)

        for copy in loads(i, i % 2):
            copy.start()

    def compute(i, carry):
        slot = i % 2
        for copy in loads(i, slot):
            copy.wait()

        @pl.when(i >= 2)
        def _():
            for copy in store(i - 2, slot):
                copy.wait()

        @pl.when(i < tiles - 1)
        def _():
            prepare(i + 1)

        zz, xx, cc = tile_at(i)
        rows = x_tile[slot]
        logits = jnp.where(lanes_ref[1:2] > 0.0, dot_nn(rows, router_ref[...]), -1e30)
        weights = jnp.exp(logits - jnp.max(logits, axis=1, keepdims=True))
        own_weight = jnp.sum(weights * lanes_ref[0:1], axis=1, keepdims=True)
        named = jnp.transpose(hot_ref[(zz * 2 + xx) * 2 + cc].astype(jnp.float32))
        hot = jnp.sum(named * lanes_ref[0:1, : named.shape[1]], axis=1, keepdims=True)
        gate = hot * own_weight / jnp.sum(weights, axis=1, keepdims=True)
        gate_pre = dot_nn(rows, wg_ref[...])
        up_pre = dot_nn(rows, wu_ref[...])
        raw_grad = dot_nt(g_tile[slot], wd_ref[...])

        sigmoid = jax.nn.sigmoid(gate_pre)
        silu = gate_pre * sigmoid
        hidden = silu * up_pre
        gate_grad = jnp.sum(hidden * raw_grad, axis=1, keepdims=True)
        coarse = gate_grad.astype(jnp.bfloat16).astype(jnp.float32)
        r_tile[slot, :, width:] = (
            coarse * lanes_ref[2:3] + (gate_grad - coarse) * lanes_ref[3:4]
        ).astype(jnp.bfloat16)
        hidden_gated = (gate * hidden).astype(jnp.bfloat16)
        hidden_tile[slot] = hidden_gated
        hidden_grad = gate * raw_grad
        up_grad = (hidden_grad * silu).astype(jnp.bfloat16)
        up_grad_tile[slot] = up_grad
        gate_pre_grad = (
            hidden_grad * up_pre * sigmoid * (1.0 + gate_pre * (1.0 - sigmoid))
        ).astype(jnp.bfloat16)
        gate_pre_grad_tile[slot] = gate_pre_grad
        y_tile[slot] = dot_nn(hidden_gated, wd_ref[...]).astype(jnp.bfloat16)
        r_tile[slot, :, :width] = (
            dot_nt(gate_pre_grad, wg_ref[...]) + dot_nt(up_grad, wu_ref[...])
        ).astype(jnp.bfloat16)
        for copy in store(i, slot):
            copy.start()
        return carry

    prepare(0)
    for copy in fetched:
        copy.wait()
    lax.fori_loop(0, tiles, compute, 0)
    for i in (tiles - 2, tiles - 1):
        for copy in store(i, i % 2):
            copy.wait()
    spread.finish()


def expert_pass(block, upstream, hot, router, lanes, w_gate, w_up, w_down, collective):
    rows, width = block.shape
    units = w_gate.shape[1]
    nz = lax.axis_size("dp") // 4
    tile = 2 * rows
    out = (nz, 2, 2, tile)
    return pl.pallas_call(
        functools.partial(expert_kernel, nz),
        in_specs=[ANYWHERE] * 2 + [IN_VMEM] * 3 + [ANYWHERE] * 3,
        out_specs=[ANYWHERE] * 6,
        out_shape=[
            jax.ShapeDtypeStruct((nz, 2, 2, 2, rows, width), jnp.bfloat16),
            jax.ShapeDtypeStruct(out + (width,), jnp.bfloat16),
            jax.ShapeDtypeStruct(out + (width + LANES,), jnp.bfloat16),
        ]
        + [jax.ShapeDtypeStruct(out + (units,), jnp.bfloat16)] * 3,
        scratch_shapes=[
            pltpu.VMEM((2, tile, width), jnp.bfloat16),
            pltpu.VMEM((2, tile, width), jnp.bfloat16),
            pltpu.VMEM((2, tile, width), jnp.bfloat16),
            pltpu.VMEM((2, tile, width + LANES), jnp.bfloat16),
            pltpu.VMEM((2, tile, units), jnp.bfloat16),
            pltpu.VMEM((2, tile, units), jnp.bfloat16),
            pltpu.VMEM((2, tile, units), jnp.bfloat16),
            pltpu.VMEM(w_gate.shape, w_gate.dtype),
            pltpu.VMEM(w_up.shape, w_up.dtype),
            pltpu.VMEM(w_down.shape, w_down.dtype),
            pltpu.SemaphoreType.DMA((3,)),
            pltpu.SemaphoreType.DMA((2, 3)),
            pltpu.SemaphoreType.DMA((2, 5)),
            pltpu.SemaphoreType.DMA((Spread.KINDS, nz)),
            pltpu.SemaphoreType.DMA((Spread.KINDS, nz)),
            pltpu.SemaphoreType.DMA,
        ],
        cost_estimate=LINK_TIME,
        compiler_params=pltpu.CompilerParams(
            collective_id=collective, has_side_effects=True, vmem_limit_bytes=60 << 20
        ),
    )(block, upstream.reshape(out + (width,)), hot, router, lanes, w_gate, w_up, w_down)


def dense_body(
    tokens,
    routes,
    cotangent,
    attn_gain,
    q_gain,
    k_gain,
    w_query,
    w_key,
    w_value,
    w_out,
    mlp_gain,
    router,
    w_gate,
    w_up,
    w_down,
):
    rank_index = lax.axis_index("tensor")
    own_rows = tokens.shape[0]
    head_cols = w_query.shape[1]
    col_start = rank_index * head_cols
    row_start = rank_index * own_rows
    experts = router.shape[1]
    q_gain_local = lax.dynamic_slice_in_dim(q_gain, col_start, head_cols)
    k_gain_local = lax.dynamic_slice_in_dim(k_gain, col_start, head_cols)
    expert_ids = jnp.arange(experts, dtype=jnp.int32)
    named = jnp.any(routes[None] == expert_ids[:, None, None], axis=2).astype(jnp.bfloat16)
    q_all, k_all, v_all, o_all, hot, other_tokens = gather_in_plane(
        (w_query, w_key, w_value, w_out, named), tokens, 1
    )
    hot = hot.reshape(-1, *named.shape)
    q_all, k_all, v_all = (w.reshape(D, head_cols) for w in (q_all, k_all, v_all))
    o_all = o_all.reshape(-1, *w_out.shape)
    first = rank_index == 0
    inputs_both = jnp.concatenate(
        [jnp.where(first, tokens, other_tokens), jnp.where(first, other_tokens, tokens)], axis=0
    ).astype(jnp.float32)
    unit_both = inputs_both * lax.rsqrt(
        jnp.mean(inputs_both * inputs_both, axis=1, keepdims=True) + EPSILON
    )
    normed = (unit_both * attn_gain).astype(jnp.bfloat16)
    inputs = tokens.astype(jnp.float32)
    attn_inv = lax.rsqrt(jnp.mean(inputs * inputs, axis=1, keepdims=True) + EPSILON)
    own_expert = lax.axis_index("dp")
    lane = jnp.arange(LANES)
    marked = own_expert + experts * rank_index
    lanes = jnp.stack(
        [lane == own_expert, lane < experts, lane == marked, lane == marked + 2 * experts]
        + [lane < 0] * 4
    ).astype(jnp.float32)
    router_wide = jnp.pad(router, ((0, 0), (0, LANES - experts)))
    tables = signed_rope_tables()
    gains = (q_gain_local[None], k_gain_local[None])
    (
        upstream_all,
        queries,
        keys_raw,
        values,
        query_rot,
        key_rot,
        mixed_heads,
        query_inv,
        key_inv,
        log_total,
        attended,
    ) = attend(cotangent, normed, (q_all, k_all, v_all, o_all), gains, tables, 6)
    upstream_all = upstream_all.reshape(-1, D)
    hidden_one = inputs + attended
    mlp_inv = lax.rsqrt(jnp.mean(hidden_one * hidden_one, axis=1, keepdims=True) + EPSILON)
    normed_two = (hidden_one * mlp_inv * mlp_gain).astype(jnp.bfloat16)
    own_routes = lax.dynamic_slice_in_dim(routes, row_start, own_rows, 0)
    own_hot = jnp.any(own_routes[:, :, None] == expert_ids[None, None, :], axis=1)
    own_probs = jax.nn.softmax(matmul(normed_two, router), axis=1)
    rows_all, y_part, r_part, *for_weights = expert_pass(
        normed_two, upstream_all, hot, router_wide, lanes, w_gate[0], w_up[0], w_down[0], 2
    )
    rows_all, y_part = rows_all.reshape(-1, D), y_part.reshape(-1, D)
    for_weights = [array.reshape(rows_all.shape[0], -1) for array in for_weights]
    blocks = (lax.axis_size("dp") // 4, 2, 2, 2, own_rows)
    returned, gate_weight_grad, up_weight_grad, down_weight_grad = scatter_sum(
        r_part.reshape(*blocks, D + LANES), [rows_all, upstream_all, *for_weights], 3
    )
    expert_grad = jnp.sum(
        returned[:, D : D + 4 * experts].astype(jnp.float32).reshape(own_rows, 4, experts), axis=1
    )
    expert_grad = jnp.where(own_hot, expert_grad, 0.0)
    returned = returned[:, :D]
    upstream = cotangent.astype(jnp.float32)
    logit_grad = own_probs * (expert_grad - jnp.sum(expert_grad * own_probs, axis=1, keepdims=True))
    router_grad = jnp.dot(normed_two.astype(jnp.float32).T, logit_grad, precision=HIGHEST)
    normed_two_grad = returned.astype(jnp.float32) + jnp.dot(
        logit_grad, router.astype(jnp.float32).T, precision=HIGHEST
    )
    scaled_grad = normed_two_grad * mlp_gain
    hidden_one_grad = (
        upstream
        + mlp_inv * scaled_grad
        - hidden_one * mlp_inv**3 * jnp.mean(hidden_one * scaled_grad, axis=1, keepdims=True)
    )
    mlp_gain_grad = jnp.sum(normed_two_grad * hidden_one * mlp_inv, axis=0)
    saved = (queries, keys_raw, query_rot, key_rot, values, query_inv, key_inv, log_total)
    mixture, attended_grad, query_grad, key_grad, value_grad, gain_grads = attend_back(
        y_part.reshape(*blocks, D), hidden_one_grad.astype(jnp.bfloat16), o_all, saved, gains, tables, 7
    )
    layer_out = (hidden_one + mixture.astype(jnp.float32)).astype(jnp.bfloat16)
    q_gain_part, k_gain_part = gain_grads[0], gain_grads[1]
    normed_part = (
        jnp.einsum("gc,rc->gr", query_grad, q_all, preferred_element_type=jnp.float32)
        + jnp.einsum("gc,rc->gr", key_grad, k_all, preferred_element_type=jnp.float32)
        + jnp.einsum("gc,rc->gr", value_grad, v_all, preferred_element_type=jnp.float32)
    )
    attn_gain_grad = jnp.sum(normed_part * unit_both, axis=0)
    zero_width = jnp.zeros((D,), jnp.float32)
    q_gain_full = lax.dynamic_update_slice_in_dim(zero_width, q_gain_part, col_start, 0)
    k_gain_full = lax.dynamic_update_slice_in_dim(zero_width, k_gain_part, col_start, 0)
    small_grads = jnp.concatenate(
        [
            jnp.stack([attn_gain_grad, q_gain_full, k_gain_full, mlp_gain_grad]),
            jnp.zeros((4, D), jnp.float32),
            jnp.transpose(router_grad),
        ],
        axis=0,
    )
    row_part = lax.dynamic_slice_in_dim(
        normed_part, (1 - rank_index) * own_rows, own_rows, 0
    ).astype(jnp.bfloat16)
    own_part = lax.dynamic_slice_in_dim(normed_part, row_start, own_rows, 0)
    *weight_sums, small_sums, other_part = scatter_in_plane(
        (normed, normed, normed, attended_grad),
        (query_grad, key_grad, value_grad, mixed_heads),
        small_grads,
        row_part,
        4,
    )
    normed_grad = own_part + other_part.astype(jnp.float32)
    scaled_input = normed_grad * attn_gain
    tokens_grad = (
        hidden_one_grad
        + attn_inv * scaled_input
        - inputs * attn_inv**3 * jnp.mean(inputs * scaled_input, axis=1, keepdims=True)
    )
    attn_gain_grad, q_gain_grad, k_gain_grad, mlp_gain_grad = (small_sums[i] for i in range(4))
    router_grad = jnp.transpose(small_sums[8:])
    return (
        layer_out,
        tokens_grad,
        attn_gain_grad,
        q_gain_grad,
        k_gain_grad,
        weight_sums[0],
        weight_sums[1],
        weight_sums[2],
        jnp.transpose(weight_sums[3]),
        mlp_gain_grad,
        router_grad,
        gate_weight_grad[None],
        up_weight_grad[None],
        down_weight_grad[None],
    )


def solution(mesh):
    in_specs = (
        P(("dp", "tensor"), None),
        P("dp", None),
        P(("dp", "tensor"), None),
        P(),
        P(),
        P(),
        P("dp", "tensor"),
        P("dp", "tensor"),
        P("dp", "tensor"),
        P("tensor", "dp"),
        P(),
        P(),
        P("dp", None, "tensor"),
        P("dp", None, "tensor"),
        P("dp", "tensor", None),
    )
    out_specs = (
        P(("dp", "tensor"), None),
        P(("dp", "tensor"), None),
        P(),
        P(),
        P(),
        P("dp", "tensor"),
        P("dp", "tensor"),
        P("dp", "tensor"),
        P("tensor", "dp"),
        P(),
        P(),
        P("dp", None, "tensor"),
        P("dp", None, "tensor"),
        P("dp", "tensor", None),
    )
    experts = mesh.shape["dp"]
    body = dense_body if experts <= 2 * TOPK else routed_body
    return jax.shard_map(body, mesh=mesh, in_specs=in_specs, out_specs=out_specs, check_vma=False)
```
